32 devices in a mesh: shard: 8 (over z, x), ctx: 2 (over y), tp: 2 (over core).
Axes of the slice: x: 2, y: 2, z: 4, core: 2. Of those that a mesh axis runs over, the one named last changes fastest.
Arguments:
- video_clips: bfloat16 [16, 8, 196, 768], P('shard', 'ctx', 'tp'), may hold values from -6 to 6
- cotangent: float32 [16, 8, 196, 768], P('shard', 'ctx', 'tp'), may hold values from -6 to 6
- slot_clip: int32 [16], P('shard'), may hold values from -1 to 9, as said below
- valid_places: int32 [10], replicated, may hold values from 49 to 196, as said below
- norm_gain: float32 [2, 3, 768], replicated, may hold values from 0.5 to 1.5
- norm_bias: float32 [2, 3, 768], replicated, may hold values from -1 to 1
- triple_weight: bfloat16 [2, 2, 768, 3, 768], P(None, None, ('shard', 'ctx'), None, 'tp'), may hold values from -0.21875 to 0.21875
- entry_bias: float32 [2, 2, 2, 768], P(None, None, None, 'tp'), may hold values from -1.5 to 1.5
- merge_weight: bfloat16 [2, 2, 768, 768], P(None, None, 'tp', ('shard', 'ctx')), may hold values from -0.625 to 0.625
- branch_bias: float32 [2, 4, 768], replicated, may hold values from -1.5 to 1.5
- mixing_weight: bfloat16 [2, 768, 768], P(None, ('shard', 'ctx', 'tp')), may hold values from -0.21875 to 0.21875
- up_weight: bfloat16 [2, 768, 3072], P(None, ('shard', 'ctx'), 'tp'), may hold values from -0.21875 to 0.21875
- up_bias: float32 [2, 3072], P(None, 'tp'), may hold values from -1.5 to 1.5
- down_weight: bfloat16 [2, 3072, 768], P(None, 'tp', ('shard', 'ctx')), may hold values from -0.109375 to 0.109375
Outputs:
- block_output: bfloat16 [16, 8, 196, 768], P('shard', 'ctx', 'tp')
- input_grad: float32 [16, 8, 196, 768], P('shard', 'ctx', 'tp')
- gain_grad: float32 [2, 3, 768], replicated
- shift_grad: float32 [2, 3, 768], replicated
- triple_grad: float32 [2, 2, 768, 3, 768], P(None, None, ('shard', 'ctx'), None, 'tp')
- entry_grad: float32 [2, 2, 2, 768], P(None, None, None, 'tp')
- merge_grad: float32 [2, 2, 768, 768], P(None, None, 'tp', ('shard', 'ctx'))
- branch_grad: float32 [2, 4, 768], replicated
- mixing_grad: float32 [2, 768, 768], P(None, ('shard', 'ctx', 'tp'))
- up_grad: float32 [2, 768, 3072], P(None, ('shard', 'ctx'), 'tp')
- up_bias_grad: float32 [2, 3072], P(None, 'tp')
- down_grad: float32 [2, 3072, 768], P(None, 'tp', ('shard', 'ctx'))
- root_squares: float32 [2, 4], replicated
The draws below stay inside these ranges and needn't reach their ends.
Inputs may be any that keep to these rules, and one draw needn't show every extreme that they name: `slot_clip`: each of the 10 clips stands in exactly one slot. Slots 2 s and 2 s + 1 belong to index s of shard; the first always holds a clip, the second for 2 indices drawn from the seed; -1 marks an empty slot. `valid_places`: the first that many places of every frame of a clip are valid; at least one clip has all 196 valid.
All inputs are finite; a program needn't handle non-finite values.
Results may differ from the reference program's by a relative error of at most 0.03.
Values may be sent and summed in bfloat16 or wider, within the bound.
A program may use at most 384 MiB of HBM per device.

```python
import jax
import jax.numpy as jnp
from jax import lax

WIDTH = 768
HEADS = 12
HEAD_DIM = 64
HIDDEN_SIZE = 3072
FRAMES = 8
PLACES = 196
LAYERS = 2
SLOTS = 16
CLIPS = 10


def draw_slot_clip(key, part):
    shards = SLOTS // 2
    extra = CLIPS - shards
    order = jax.random.permutation(jax.random.fold_in(key, 11), shards)
    doubled = (order < extra).astype(jnp.int32)
    occupied = jnp.stack([jnp.ones((shards,), jnp.int32), doubled], axis=1).reshape(SLOTS)
    rank = jnp.cumsum(occupied) - 1
    names = jax.random.permutation(jax.random.fold_in(key, 12), CLIPS).astype(jnp.int32)
    picked = names[jnp.clip(rank, 0, CLIPS - 1)]
    return jnp.where(occupied > 0, picked, -1).astype(jnp.int32)


def draw_valid_places(key, part):
    counts = jax.random.randint(jax.random.fold_in(key, 21), (CLIPS,), PLACES // 4, PLACES + 1)
    chosen = jax.random.randint(jax.random.fold_in(key, 22), (), 0, CLIPS)
    return jnp.where(jnp.arange(CLIPS) == chosen, PLACES, counts).astype(jnp.int32)


def shard_levels(key, dims, cuts, low, high):
    def one(dim, shards_of):
        steps = jax.random.uniform(jax.random.fold_in(jax.random.fold_in(key, 6), dim), (shards_of,), jnp.float32, low / len(cuts), high / len(cuts))
        return jnp.repeat(jnp.exp(steps), dims[dim] // shards_of).reshape((-1,) + (1,) * (len(dims) - dim - 1))

    level = one(*cuts[0])
    for cut in cuts[1:]:
        level = level * one(*cut)
    return level


def noise(rng, shape, width, limit, cuts=(), kind=jnp.bfloat16):
    level = shard_levels(rng, shape, cuts, -0.22, 0.18) if cuts else 1.0
    array = jax.random.normal(rng, shape, jnp.float32) * width * level
    return jnp.minimum(jnp.maximum(array, -limit), limit).astype(kind)


def setup_inputs(seed: int = 0) -> dict:
    key_list = jax.random.split(jax.random.key(seed), 15)
    video_clips = noise(key_list[0], (SLOTS, FRAMES, PLACES, WIDTH), 1.0, 6.0, ((0, 8), (1, 2), (2, 2)))
    cotangent = noise(key_list[1], (SLOTS, FRAMES, PLACES, WIDTH), 1.0, 6.0, ((0, 8), (1, 2), (2, 2)), jnp.float32)
    slot_clip = draw_slot_clip(jax.random.fold_in(key_list[14], 71), 0)
    valid_places = draw_valid_places(jax.random.fold_in(key_list[14], 71), 0)
    norm_gain = jnp.clip(1.0 + 0.1 * jax.random.normal(key_list[4], (LAYERS, 3, WIDTH), jnp.float32), 0.5, 1.5)
    norm_bias = noise(key_list[5], (LAYERS, 3, WIDTH), 0.2, 1.0, (), jnp.float32)
    triple_weight = noise(key_list[6], (LAYERS, 2, WIDTH, 3, WIDTH), WIDTH ** -0.5, 0.21875, ((2, 16), (4, 2)))
    entry_bias = noise(key_list[7], (LAYERS, 2, 2, WIDTH), 0.3, 1.5, ((3, 2),), jnp.float32)
    merge_weight = noise(key_list[8], (LAYERS, 2, WIDTH, WIDTH), (WIDTH // 8) ** -0.5, 0.625, ((2, 2), (3, 16)))
    branch_bias = noise(key_list[9], (LAYERS, 4, WIDTH), 0.3, 1.5, (), jnp.float32)
    mixing_weight = noise(key_list[10], (LAYERS, WIDTH, WIDTH), WIDTH ** -0.5, 0.21875, ((1, 32),))
    up_weight = noise(key_list[11], (LAYERS, WIDTH, HIDDEN_SIZE), WIDTH ** -0.5, 0.21875, ((1, 16), (2, 2)))
    up_bias = noise(key_list[12], (LAYERS, HIDDEN_SIZE), 0.3, 1.5, ((1, 2),), jnp.float32)
    down_weight = noise(key_list[13], (LAYERS, HIDDEN_SIZE, WIDTH), HIDDEN_SIZE ** -0.5, 0.109375, ((1, 2), (2, 16)))
    return {"video_clips": video_clips, "cotangent": cotangent, "slot_clip": slot_clip, "valid_places": valid_places, "norm_gain": norm_gain, "norm_bias": norm_bias, "triple_weight": triple_weight, "entry_bias": entry_bias, "merge_weight": merge_weight, "branch_bias": branch_bias, "mixing_weight": mixing_weight, "up_weight": up_weight, "up_bias": up_bias, "down_weight": down_weight}


highest = lax.Precision.HIGHEST
far_below = -1000000000.0
epsilon = 1e-06

@jax.custom_vjp
def low(v):
    return lax.optimization_barrier(v.astype(jnp.bfloat16)).astype(jnp.float32)

@jax.custom_vjp
def low_back(v):
    return v

def low_keep(v):
    return (low(v), None)

def low_pass(kept, grad):
    return (grad,)

def back_keep(v):
    return (v, None)

def back_low(kept, grad):
    return (low(grad),)
low.defvjp(low_keep, low_pass)
low_back.defvjp(back_keep, back_low)

def product(left, right):
    return jnp.matmul(left, right, precision=highest)

def layer_norm(value, gain, shift):
    center = value - lax.optimization_barrier(jnp.mean(value, axis=-1, keepdims=True))
    spread = lax.optimization_barrier(jnp.mean(center * center, axis=-1, keepdims=True))
    return center * lax.rsqrt(spread + epsilon) * gain + shift

def soft_rows(scores):
    top = lax.optimization_barrier(jnp.max(scores, axis=-1, keepdims=True))
    raised = jnp.exp(scores - top)
    return raised / lax.optimization_barrier(jnp.sum(raised, axis=-1, keepdims=True))

def project_heads(normed, triple, entry):
    shape = (FRAMES, PLACES, HEADS, HEAD_DIM)
    query = low_back(low(product(normed, triple[:, 0]) + entry[0])).reshape(shape)
    keys = low_back(low(product(normed, triple[:, 1]))).reshape(shape)
    values = low_back(low(product(normed, triple[:, 2]) + entry[1])).reshape(shape)
    return (query, keys, values)

def temporal_mix(normed, triple, entry):
    query, keys, values = project_heads(normed, triple, entry)
    scores = low_back(jnp.einsum('fphd,gphd->phfg', query, keys, precision=highest) * HEAD_DIM ** (-0.5))
    shares = soft_rows(scores)
    mixed = jnp.einsum('phfg,gphd->fphd', low(shares), values, precision=highest)
    return low_back(low(mixed.reshape(FRAMES, PLACES, WIDTH)))

def spatial_mix(normed, triple, entry, allowed):
    query, keys, values = project_heads(normed, triple, entry)
    scores = low_back(jnp.einsum('fphd,fqhd->fhpq', query, keys, precision=highest) * HEAD_DIM ** (-0.5))
    scores = jnp.where(allowed, scores, far_below)
    shares = soft_rows(scores)
    mixed = jnp.einsum('fhpq,fqhd->fphd', low(shares), values, precision=highest)
    return low_back(low(mixed.reshape(FRAMES, PLACES, WIDTH)))

def one_layer(state, layer_weights, allowed):
    gain, shift, triple, entry, merge, bias, mixing, upward, upward_bias, downward = layer_weights
    normed = low(layer_norm(state, gain[0], shift[0]))
    mixed = temporal_mix(normed, triple[0], entry[0])
    joined = low_back(low(product(mixed, merge[0]) + bias[0]))
    temporal = low_back(product(joined, mixing) + bias[1])
    state = state + temporal
    normed = low(layer_norm(state, gain[1], shift[1]))
    mixed = spatial_mix(normed, triple[1], entry[1], allowed)
    spatial = low_back(product(mixed, merge[1]) + bias[2])
    state = state + spatial
    normed = low(layer_norm(state, gain[2], shift[2]))
    hidden = low_back(product(normed, upward) + upward_bias)
    active = low(jax.nn.gelu(hidden, approximate=False))
    dense_out = low_back(product(active, downward) + bias[3])
    state = state + dense_out
    return (state, (temporal, spatial, dense_out))

def forward_slot(state, parameters, allowed, valid_rows):
    squares = []
    for layer in range(LAYERS):
        layer_weights = tuple((item[layer] for item in parameters))
        state, branches = one_layer(state, layer_weights, allowed)
        squares.append(jnp.stack([jnp.sum(jnp.square(item) * valid_rows) for item in branches + (state,)]))
    return (state, jnp.stack(squares))

def reference(video_clips, cotangent, slot_clip, valid_places, norm_gain, norm_bias, triple_weight, entry_bias, merge_weight, branch_bias, mixing_weight, up_weight, up_bias, down_weight):
    parameters = tuple((item.astype(jnp.float32) for item in (norm_gain, norm_bias, triple_weight, entry_bias, merge_weight, branch_bias, mixing_weight, up_weight, up_bias, down_weight)))
    clip_ids = jnp.arange(CLIPS, dtype=jnp.int32)
    chosen = slot_clip[:, None] == clip_ids[None, :]
    counts = lax.optimization_barrier(jnp.sum(jnp.where(chosen, valid_places[None, :], 0), axis=1)).astype(jnp.int32)
    place_ids = jnp.arange(PLACES, dtype=jnp.int32)
    zero_grads = tuple((jnp.zeros_like(item) for item in parameters))

    def per_slot(carry, inputs):
        grads_sum, squares_sum = carry
        state, outer_grad, count = inputs
        allowed = place_ids < count
        valid_rows = allowed.astype(jnp.float32)[None, :, None]

        def forward_run(start, weights_all):
            return forward_slot(start, weights_all, allowed, valid_rows)
        result, pullback, slot_squares = jax.vjp(forward_run, state.astype(jnp.float32), parameters, has_aux=True)
        state_grad, weight_grads = pullback(outer_grad.astype(result.dtype) * valid_rows)
        grads_sum = jax.tree.map(jnp.add, grads_sum, weight_grads)
        return ((grads_sum, squares_sum + slot_squares), (result.astype(jnp.bfloat16), state_grad))
    start_squares = jnp.zeros((LAYERS, 4), jnp.float32)
    (grads, squares), (block_output, input_grad) = lax.scan(per_slot, (zero_grads, start_squares), (video_clips, cotangent, counts))
    total = FRAMES * WIDTH * jnp.sum(valid_places).astype(jnp.float32)
    root_squares = jnp.sqrt(squares / total)
    return (block_output, input_grad, grads[0], grads[1], grads[2], grads[3], grads[4], grads[5], grads[6], grads[7], grads[8], grads[9], root_squares)
```

```python
import functools

import jax
import jax.numpy as jnp
from jax import lax
from jax.experimental import pallas as pl
from jax.experimental.pallas import tpu as pltpu
from jax.sharding import PartitionSpec as P

HEAD_DIM = 64
FRAMES = 8
LAYERS = 2
AXES = ("shard", "ctx", "tp")
BF = jnp.bfloat16
F32 = jnp.float32

far_below = -1000000000.0
epsilon = 1e-06
root_half = 0.7071067811865476
gauss_scale = 0.3989422804014327


def dot_nn(left, right):
    return lax.dot_general(left, right, (((1,), (0,)), ((), ())), preferred_element_type=F32)


def dot_nt(left, right):
    return lax.dot_general(left, right, (((1,), (1,)), ((), ())), preferred_element_type=F32)


def dot_tn(left, right):
    return lax.dot_general(left, right, (((0,), (0,)), ((), ())), preferred_element_type=F32)


def rows(value):
    return value.reshape(-1, value.shape[-1])


def row_total(value):
    return jnp.sum(rows(value).astype(F32), axis=0)


def lane_masks(shape):
    lane = lax.broadcasted_iota(jnp.int32, shape, 1)
    return lane < HEAD_DIM


def softmax_rows(scores):
    top = jnp.max(scores, axis=-1, keepdims=True)
    raised = jnp.exp(scores - top)
    total = jnp.sum(raised, axis=-1, keepdims=True)
    return raised * (1.0 / total)


def sides(value, first):
    zero = jnp.zeros_like(value)
    return [jnp.where(first, value, zero), jnp.where(first, zero, value)]


def heads_forward(qkv, fix, scale, put):
    first = lane_masks(qkv(0, 0).shape)
    scores = []
    for pair in range(3):
        k = qkv(1, pair)
        scores.append([dot_nt(q, k) for q in sides(qkv(0, pair), first)])
    shares = [[softmax_rows(fix(item * scale)).astype(BF) for item in both] for both in scores]
    for pair in range(3):
        v = qkv(2, pair)
        outs = [dot_nn(item, v) for item in shares[pair]]
        put(pair, jnp.where(first, outs[0], outs[1]).astype(BF))


def heads_backward(qkv, back, fix, scale, put):
    first = lane_masks(qkv(0, 0).shape)
    scores, backs = [], []
    for pair in range(3):
        k, v = qkv(1, pair), qkv(2, pair)
        scores.append([dot_nt(q, k) for q in sides(qkv(0, pair), first)])
        backs.append([dot_nt(b, v) for b in sides(back(pair), first)])
    low_shares, low_scores = [], []
    for pair in range(3):
        low_shares.append([])
        low_scores.append([])
        for side in range(2):
            shares = softmax_rows(fix(scores[pair][side] * scale))
            back_shares = backs[pair][side]
            inner = jnp.sum(back_shares * shares, axis=-1, keepdims=True)
            low_scores[pair].append((shares * (back_shares - inner)).astype(BF))
            low_shares[pair].append(shares.astype(BF))
    for pair in range(3):
        q, k, bm = qkv(0, pair), qkv(1, pair), back(pair)
        gq = [dot_nn(item, k) for item in low_scores[pair]]
        gk = [dot_tn(item, q) for item in low_scores[pair]]
        gv = [dot_tn(item, bm) for item in low_shares[pair]]
        put(0, pair, (jnp.where(first, gq[0], gq[1]) * scale).astype(BF))
        put(1, pair, (jnp.where(first, gk[0], gk[1]) * scale).astype(BF))
        put(2, pair, jnp.where(first, gv[0], gv[1]).astype(BF))


def column(part, pair):
    start = part * 384 + pair * 128
    return slice(start, start + 128)


def spatial_fix(count_ref, padded, places):
    col = lax.broadcasted_iota(jnp.int32, (padded, padded), 1)
    floor = jnp.where(col < places, far_below, 3.0 * far_below)
    allowed = col < jnp.minimum(count_ref[0], places)
    return lambda scores: jnp.where(allowed, scores, floor)


def spatial_fwd_body(places, scale, count_ref, own_ref, oth_ref, own_out, oth_out):
    fix = spatial_fix(count_ref, own_ref.shape[1], places)
    for src, dst in ((own_ref, own_out), (oth_ref, oth_out)):

        def put(pair, value, dst=dst):
            dst[0, :, pair * 128 : pair * 128 + 128] = value

        heads_forward(lambda part, pair, src=src: src[0, :, column(part, pair)], fix, scale, put)


def spatial_bwd_body(
    places, scale, count_ref, own_ref, oth_ref, bown_ref, both_ref, own_out, oth_out
):
    fix = spatial_fix(count_ref, own_ref.shape[1], places)
    for src, back, dst in ((own_ref, bown_ref, own_out), (oth_ref, both_ref, oth_out)):

        def put(part, pair, value, dst=dst):
            dst[0, :, column(part, pair)] = value

        heads_backward(
            lambda part, pair, src=src: src[0, :, column(part, pair)],
            lambda pair, back=back: back[0, :, pair * 128 : pair * 128 + 128],
            fix,
            scale,
            put,
        )


def temporal_fix(tile):
    size = FRAMES * tile
    row = lax.broadcasted_iota(jnp.int32, (size, size), 0)
    col = lax.broadcasted_iota(jnp.int32, (size, size), 1)
    same = (row & (tile - 1)) == (col & (tile - 1))
    return lambda scores: jnp.where(same, scores, 3.0 * far_below)


def temporal_fwd_body(scale, src, dst):
    tile = src.shape[1]
    fix = temporal_fix(tile)

    def put(pair, value):
        dst[:, :, pair * 128 : pair * 128 + 128] = value.reshape(FRAMES, tile, 128)

    heads_forward(
        lambda part, pair: src[:, :, column(part, pair)].reshape(FRAMES * tile, 128),
        fix,
        scale,
        put,
    )


def temporal_bwd_body(scale, src, back, dst):
    tile = src.shape[1]
    fix = temporal_fix(tile)

    def put(part, pair, value):
        dst[:, :, column(part, pair)] = value.reshape(FRAMES, tile, 128)

    heads_backward(
        lambda part, pair: src[:, :, column(part, pair)].reshape(FRAMES * tile, 128),
        lambda pair: back[:, :, pair * 128 : pair * 128 + 128].reshape(FRAMES * tile, 128),
        fix,
        scale,
        put,
    )


def spatial_call(count, ins, widths, places, scale, backward):
    frames, padded, _ = ins[0].shape
    spec = lambda width: pl.BlockSpec((1, padded, width), lambda f: (f, 0, 0))
    body = spatial_bwd_body if backward else spatial_fwd_body
    work = frames * 12 * padded * 256 * 128 * 2 * (5 if backward else 2)
    return pl.pallas_call(
        functools.partial(body, places, scale),
        grid=(frames,),
        in_specs=[pl.BlockSpec(memory_space=pltpu.SMEM)] + [spec(x.shape[-1]) for x in ins],
        out_specs=[spec(width) for width in widths],
        out_shape=[jax.ShapeDtypeStruct((frames, padded, width), BF) for width in widths],
        cost_estimate=pl.CostEstimate(
            flops=work * 4, bytes_accessed=8 * frames * padded * 2304, transcendentals=0
        ),
        name="spatial_back" if backward else "spatial_mix",
    )(count, *ins)


def temporal_call(ins, width, scale, backward):
    frames, padded, _ = ins[0].shape
    tile = 16
    spec = lambda lanes: pl.BlockSpec((frames, tile, lanes), lambda i: (0, i, 0))
    body = temporal_bwd_body if backward else temporal_fwd_body
    work = padded // tile * 6 * 128 * 128 * 128 * 2 * (5 if backward else 2)
    return pl.pallas_call(
        functools.partial(body, scale),
        grid=(padded // tile,),
        in_specs=[spec(x.shape[-1]) for x in ins],
        out_specs=spec(width),
        out_shape=jax.ShapeDtypeStruct((frames, padded, width), BF),
        cost_estimate=pl.CostEstimate(
            flops=work * 8, bytes_accessed=4 * frames * padded * 1152, transcendentals=0
        ),
        name="temporal_back" if backward else "temporal_mix",
    )(*ins)


class Grid:
    def __init__(self):
        self.shards = lax.axis_size("shard")
        self.depth = self.shards // 2
        shard = lax.axis_index("shard")
        self.z = shard // 2
        self.x = shard % 2
        self.y = lax.axis_index("ctx")
        self.t = lax.axis_index("tp")
        self.direct = self.depth == 4

    def perm(self, move):
        pairs = []
        for z in range(self.depth):
            for x in range(2):
                for y in range(2):
                    for t in range(2):
                        tz, tx, ty, tt = move(z, x, y, t)
                        pairs.append(
                            (((z * 2 + x) * 2 + y) * 2 + t, ((tz * 2 + tx) * 2 + ty) * 2 + tt)
                        )
        return pairs

    def over_x(self, value):
        return lax.ppermute(value, AXES, self.perm(lambda z, x, y, t: (z, 1 - x, y, t)))

    def over_y(self, value):
        return lax.ppermute(value, AXES, self.perm(lambda z, x, y, t: (z, x, 1 - y, t)))

    def over_t(self, value):
        return lax.ppermute(value, AXES, self.perm(lambda z, x, y, t: (z, x, y, 1 - t)))

    def over_z(self, value, step):
        depth = self.depth
        return lax.ppermute(
            value, AXES, self.perm(lambda z, x, y, t: ((z + step) % depth, x, y, t))
        )

    def over_bit(self, value, bit):
        pairs = []
        for s in range(self.shards):
            for y in range(2):
                for t in range(2):
                    pairs.append(((s * 2 + y) * 2 + t, ((s ^ bit) * 2 + y) * 2 + t))
        return lax.ppermute(value, AXES, pairs)

    def total(self, value, across):
        if across:
            value = value + self.over_t(value)
        value = value + self.over_y(value)
        bit = 1
        while bit < self.shards:
            value = value + self.over_bit(value, bit)
            bit *= 2
        return value


def place_body(widths, step_rows, half, at_ref, own, xn, yn, da, db, *outs):
    back = pl.program_id(0)
    x, y = at_ref[1], at_ref[2]

    def put(dx, dy, piece):
        bx = x if dx == 0 else 1 - x
        by = y if dy == 0 else 1 - y
        row = pl.multiple_of((bx * 2 + by) * step_rows, 16)
        start = 0
        for number, width in enumerate(widths):
            outs[number][pl.ds(row, step_rows), :] = piece[0, :, start : start + width]
            start += width

    put(0, 0, own)
    put(1, 0, xn)
    put(0, 1, yn)

    @pl.when(back < half)
    def _():
        put(1, 1, da)

    @pl.when(back >= half)
    def _():
        put(1, 1, db)


def gather_rows(grid, block, widths):
    step_rows, lanes = block.shape
    if not grid.direct:
        full = lax.all_gather(block, ("shard", "ctx"), axis=0, tiled=True)
        outs, start = [], 0
        for width in widths:
            outs.append(full[:, start : start + width])
            start += width
        return outs
    depth = grid.depth
    half = depth // 2
    own = jnp.stack([block] + [grid.over_z(block, k) for k in range(1, depth)])
    xn = grid.over_x(own)
    yn = grid.over_y(own)
    da = grid.over_y(xn[:half])
    db = grid.over_x(yn[half:])
    at = jnp.stack([grid.z, grid.x, grid.y]).astype(jnp.int32)
    piece = lambda index: pl.BlockSpec((1, step_rows, lanes), index)
    straight = piece(lambda k, at_ref: (k, 0, 0))
    return pl.pallas_call(
        functools.partial(place_body, tuple(widths), step_rows, half),
        grid_spec=pltpu.PrefetchScalarGridSpec(
            num_scalar_prefetch=1,
            grid=(depth,),
            in_specs=[
                straight,
                straight,
                straight,
                piece(lambda k, at_ref: (jnp.minimum(k, half - 1), 0, 0)),
                piece(lambda k, at_ref: (jnp.maximum(k - half, 0), 0, 0)),
            ],
            out_specs=[
                pl.BlockSpec(
                    (4 * step_rows, width),
                    lambda k, at_ref: (lax.rem(at_ref[0] - k + depth, depth), 0),
                )
                for width in widths
            ],
        ),
        out_shape=[
            jax.ShapeDtypeStruct((depth * 4 * step_rows, width), block.dtype) for width in widths
        ],
        cost_estimate=pl.CostEstimate(
            flops=0, bytes_accessed=depth * 4 * step_rows * lanes * 4, transcendentals=0
        ),
        name="place_rows",
    )(at, own, xn, yn, da, db)


def scatter_rows(grid, parts):
    if not grid.direct:
        whole = jnp.concatenate(parts, axis=1).astype(F32)
        return lax.psum_scatter(whole, ("shard", "ctx"), scatter_dimension=0, tiled=True)
    depth = grid.depth
    half = depth // 2

    def pick(dx, dy):
        out = []
        for part in parts:
            step_rows = part.shape[0] // (depth * 4)
            cube = part.reshape(depth, 2, 2, step_rows, part.shape[1])
            bx = grid.x if dx == 0 else 1 - grid.x
            by = grid.y if dy == 0 else 1 - grid.y
            out.append(
                lax.dynamic_slice(
                    cube, (0, bx, by, 0, 0), (depth, 1, 1, step_rows, part.shape[1])
                ).reshape(depth, step_rows, part.shape[1])
            )
        return jnp.concatenate(out, axis=-1)

    far = pick(1, 1)
    ra = grid.over_y(far[:half])
    rb = grid.over_x(far[half:])
    sx = pick(1, 0)
    sy = pick(0, 1)
    sx = jnp.concatenate([(sx[:half].astype(F32) + ra.astype(F32)).astype(BF), sx[half:]])
    sy = jnp.concatenate([sy[:half], (sy[half:].astype(F32) + rb.astype(F32)).astype(BF)])
    rx = grid.over_x(sx)
    ry = grid.over_y(sy)
    kept = pick(0, 0).astype(F32) + rx.astype(F32) + ry.astype(F32)
    own = lax.dynamic_index_in_dim(kept, grid.z, 0, keepdims=False)
    low = kept.astype(BF)
    for k in range(1, depth):
        block = lax.dynamic_index_in_dim(low, (grid.z + k) % depth, 0, keepdims=False)
        own = own + grid.over_z(block, k).astype(F32)
    return own


def split_columns(value, widths):
    outs, start = [], 0
    for width in widths:
        outs.append(value[..., start : start + width])
        start += width
    return outs


def norm_forward(state, gain, shift):
    center = state - jnp.mean(state, axis=-1, keepdims=True)
    scale = lax.rsqrt(jnp.mean(center * center, axis=-1, keepdims=True) + epsilon)
    unit = center * scale
    return ((unit * gain + shift).astype(BF), unit, scale)


def norm_backward(incoming, unit, scale, gain):
    along = incoming * gain
    back = scale * (
        along
        - jnp.mean(along, axis=-1, keepdims=True)
        - unit * jnp.mean(along * unit, axis=-1, keepdims=True)
    )
    return (back, row_total(incoming * unit), row_total(incoming))


def per_device(
    video_clips,
    cotangent,
    slot_clip,
    valid_places,
    norm_gain,
    norm_bias,
    triple_weight,
    entry_bias,
    merge_weight,
    branch_bias,
    mixing_weight,
    up_weight,
    up_bias,
    down_weight,
):
    grid = Grid()
    slots, frames_here, places_here, width = video_clips.shape
    places = places_here * 2
    padded = -(-places // 16) * 16
    scale = HEAD_DIM ** (-0.5)
    step_rows = triple_weight.shape[2]
    half_rows = step_rows // 2
    own_first = grid.t == 0
    straight = grid.t == grid.y

    clip_ids = jnp.arange(valid_places.shape[0], dtype=jnp.int32)
    my_clip = lax.dynamic_index_in_dim(slot_clip, grid.y, 0, keepdims=False)
    count = jnp.sum(jnp.where(my_clip == clip_ids, valid_places, 0)).astype(jnp.int32)
    valid_here = (jnp.arange(padded, dtype=jnp.int32) < count).astype(F32)[None, :, None]
    count_ref = count.reshape(1)

    def spread_in(value):
        mine = lax.dynamic_index_in_dim(value, grid.y, 0, keepdims=False)
        theirs = lax.dynamic_index_in_dim(value, 1 - grid.y, 0, keepdims=False)
        got = grid.over_y(theirs)
        keep = jnp.where(straight, mine, got)
        send = jnp.where(straight, got, mine)
        swap = grid.over_t(send)
        low = jnp.where(own_first, keep, swap)
        high = jnp.where(own_first, swap, keep)
        gap = jnp.zeros((frames_here, padded - places, width), value.dtype)
        return jnp.concatenate([low, high, gap], axis=1)

    def spread_out(value):
        low = value[:, :places_here]
        high = value[:, places_here:places]
        keep = jnp.where(own_first, low, high)
        send = jnp.where(own_first, high, low)
        swap = grid.over_t(send)
        mine = jnp.where(straight, keep, swap)
        away = jnp.where(straight, swap, keep)
        got = grid.over_y(away)
        first = jnp.where(grid.y == 0, mine, got)
        second = jnp.where(grid.y == 0, got, mine)
        return jnp.stack([first, second])

    def pack_mix(item):
        return jnp.concatenate([item[..., : width // 2], item[..., width // 2 :]], axis=-2)

    def block_t(layer):
        return jnp.concatenate(
            [triple_weight[layer, 0, :, i] for i in range(3)]
            + [merge_weight[layer, 0].T, pack_mix(mixing_weight[layer])],
            axis=1,
        )

    def block_s(layer):
        return jnp.concatenate(
            [triple_weight[layer, 1, :, i] for i in range(3)] + [merge_weight[layer, 1].T], axis=1
        )

    def block_m(layer):
        return jnp.concatenate([up_weight[layer], down_weight[layer].T], axis=1)

    split = triple_weight.shape[-1]
    hid = up_weight.shape[-1]
    wide_t = (3 * split, split, width // 2)
    wide_s = (3 * split, split)
    wide_m = (hid, hid)

    start_clips = spread_in(video_clips)
    gathered = [None] * LAYERS
    for layer in range(LAYERS):
        if layer == 0:
            got = gather_rows(grid, block_t(layer), wide_t)
            got += gather_rows(
                grid, jnp.concatenate([block_s(layer), block_m(layer)], axis=1), wide_s + wide_m
            )
        else:
            got = gather_rows(
                grid,
                jnp.concatenate([block_t(layer), block_s(layer), block_m(layer)], axis=1),
                wide_t + wide_s + wide_m,
            )
        triple_t, merge_t, mix, triple_s, merge_s, upward, downward = got
        other = [grid.over_t(item) for item in (merge_t, mix, triple_s, merge_s, upward, downward)]

        def unpack_mix(item):
            cube = item.reshape(-1, 2, half_rows, width // 2)
            return jnp.concatenate([cube[:, 0], cube[:, 1]], axis=-1)

        mix_own, mix_oth = unpack_mix(mix), unpack_mix(other[1])
        mixing = jnp.stack(
            [jnp.where(own_first, mix_own, mix_oth), jnp.where(own_first, mix_oth, mix_own)],
            axis=1,
        ).reshape(width, width)
        gathered[layer] = dict(
            triple_t=triple_t,
            mixing=mixing,
            merge_t=(merge_t, other[0]),
            triple_s=(triple_s, other[2]),
            merge_s=(merge_s, other[3]),
            up=(upward, other[4]),
            down=(downward, other[5]),
        )

    small = jnp.concatenate([entry_bias[:, 1].reshape(-1), up_bias.reshape(-1)])
    small_oth = grid.over_t(small)
    entry_count = LAYERS * 2 * split
    entry_s = (
        small[:entry_count].reshape(LAYERS, 2, split),
        small_oth[:entry_count].reshape(LAYERS, 2, split),
    )
    up_bias2 = (
        small[entry_count:].reshape(LAYERS, hid),
        small_oth[entry_count:].reshape(LAYERS, hid),
    )

    def triple_bias(pair):
        return jnp.concatenate([pair[0], jnp.zeros((split,), F32), pair[1]])

    def cube(value):
        return value.reshape(-1, padded, value.shape[-1])

    state = start_clips.astype(F32)
    upstream = spread_in(cotangent.astype(BF)).astype(F32) * valid_here
    stored = []
    squares = []
    for layer in range(LAYERS):
        w = gathered[layer]
        gain, shift, bias = norm_gain[layer], norm_bias[layer], branch_bias[layer]
        normed, unit_t, scale_t = norm_forward(state, gain[0], shift[0])
        normed_t = jnp.concatenate([normed, grid.over_t(normed)], axis=0)
        qkv_t = cube(
            (dot_nn(rows(normed_t), w["triple_t"]) + triple_bias(entry_bias[layer, 0])).astype(BF)
        )
        mixed = temporal_call([qkv_t], split, scale, False)
        mine = mixed[:frames_here]
        swap = grid.over_t(mixed[frames_here:])
        joined = (
            dot_nt(rows(mine), w["merge_t"][0]) + dot_nt(rows(swap), w["merge_t"][1]) + bias[0]
        ).astype(BF)
        temporal = cube(dot_nn(joined, w["mixing"]) + bias[1])
        state = state + temporal
        normed_s, unit_s, scale_s = norm_forward(state, gain[1], shift[1])
        qkv_s = [
            cube(
                (
                    dot_nn(rows(normed_s), w["triple_s"][i]) + triple_bias(entry_s[i][layer])
                ).astype(BF)
            )
            for i in range(2)
        ]
        mixed_s = spatial_call(count_ref, qkv_s, (split, split), places, scale, False)
        spatial = cube(
            dot_nt(rows(mixed_s[0]), w["merge_s"][0])
            + dot_nt(rows(mixed_s[1]), w["merge_s"][1])
            + bias[2]
        )
        state = state + spatial
        normed_m, unit_m, scale_m = norm_forward(state, gain[2], shift[2])
        active, slope = [], []
        for i in range(2):
            hidden = dot_nn(rows(normed_m), w["up"][i]) + up_bias2[i][layer]
            below = 0.5 * (1.0 + lax.erf(hidden * root_half))
            active.append((hidden * below).astype(BF))
            slope.append(
                (below + hidden * gauss_scale * jnp.exp(-0.5 * hidden * hidden)).astype(BF)
            )
        dense = cube(
            dot_nt(active[0], w["down"][0]) + dot_nt(active[1], w["down"][1]) + bias[3]
        )
        state = state + dense
        squares.append(
            jnp.stack(
                [
                    jnp.sum(jnp.square(item) * valid_here)
                    for item in (temporal, spatial, dense, state)
                ]
            )
        )
        stored.append(
            dict(
                unit_t=unit_t,
                scale_t=scale_t,
                normed_t=normed_t,
                qkv_t=qkv_t,
                mixed_t=(mine, swap),
                joined=joined,
                unit_s=unit_s,
                scale_s=scale_s,
                normed_s=normed_s,
                qkv_s=qkv_s,
                mixed_s=mixed_s,
                unit_m=unit_m,
                scale_m=scale_m,
                normed_m=normed_m,
                active=active,
                slope=slope,
            )
        )
    block_output = spread_out(state.astype(BF))

    whole_sums = [None] * LAYERS
    half_sums = [None] * LAYERS
    shards = [None] * LAYERS

    def join_halves(mine, theirs):
        return (mine + grid.over_t(theirs.astype(BF)).astype(F32)).astype(BF)

    for layer in range(LAYERS - 1, -1, -1):
        w, kept = gathered[layer], stored[layer]
        gain = norm_gain[layer]
        r = rows(upstream).astype(BF)
        down_bias_part = row_total(r)
        back_hidden = [
            (dot_nn(r, w["down"][i]) * kept["slope"][i].astype(F32)).astype(BF) for i in range(2)
        ]
        down_part = join_halves(*[dot_tn(r, kept["active"][i]) for i in range(2)])
        up_part = join_halves(
            *[dot_tn(rows(kept["normed_m"]), back_hidden[i]) for i in range(2)]
        )
        hidden_part = [row_total(back_hidden[i]) for i in range(2)]
        back_normed = cube(
            dot_nt(back_hidden[0], w["up"][0]) + dot_nt(back_hidden[1], w["up"][1])
        )
        back_state, gain_m, shift_m = norm_backward(
            back_normed, kept["unit_m"], kept["scale_m"], gain[2]
        )
        upstream = upstream + back_state
        r = rows(upstream).astype(BF)
        spatial_bias_part = row_total(r)
        merge_s_part = join_halves(*[dot_tn(r, rows(kept["mixed_s"][i])) for i in range(2)])
        back_mixed = [cube(dot_nn(r, w["merge_s"][i]).astype(BF)) for i in range(2)]
        back_qkv = spatial_call(
            count_ref,
            list(kept["qkv_s"]) + back_mixed,
            (3 * split, 3 * split),
            places,
            scale,
            True,
        )
        triple_s_part = join_halves(
            *[dot_tn(rows(kept["normed_s"]), rows(back_qkv[i])) for i in range(2)]
        )
        qkv_sums = [row_total(back_qkv[i]) for i in range(2)]
        entry_s_part = [jnp.stack([q[:split], q[2 * split :]]) for q in qkv_sums]
        back_normed = cube(
            dot_nt(rows(back_qkv[0]), w["triple_s"][0])
            + dot_nt(rows(back_qkv[1]), w["triple_s"][1])
        )
        back_state, gain_s, shift_s = norm_backward(
            back_normed, kept["unit_s"], kept["scale_s"], gain[1]
        )
        upstream = upstream + back_state
        r = rows(upstream).astype(BF)
        mixing_bias_part = row_total(r)
        mixing_part = dot_tn(kept["joined"], r).reshape(-1, 2, half_rows, width)
        mix_mine = lax.dynamic_index_in_dim(mixing_part, grid.t, 1, keepdims=False)
        mix_theirs = lax.dynamic_index_in_dim(mixing_part, 1 - grid.t, 1, keepdims=False)
        mixing_part = pack_mix(join_halves(mix_mine, mix_theirs)).reshape(width, width // 2)
        back_joined = dot_nt(r, w["mixing"]).astype(BF)
        merge_bias_part = row_total(back_joined)
        merge_t_part = join_halves(
            *[dot_tn(back_joined, rows(kept["mixed_t"][i])) for i in range(2)]
        )
        back_mine, back_away = [
            cube(dot_nn(back_joined, w["merge_t"][i]).astype(BF)) for i in range(2)
        ]
        back_mixed = jnp.concatenate([back_mine, grid.over_t(back_away)], axis=0)
        back_qkv = temporal_call([kept["qkv_t"], back_mixed], 3 * split, scale, True)
        triple_t_part = dot_tn(rows(kept["normed_t"]), rows(back_qkv)).astype(BF)
        qkv_sum = row_total(back_qkv)
        entry_t_part = jnp.stack([qkv_sum[:split], qkv_sum[2 * split :]])
        back_own = dot_nt(rows(back_qkv[:frames_here]), w["triple_t"])
        back_oth = dot_nt(rows(back_qkv[frames_here:]), w["triple_t"]).astype(BF)
        back_normed = cube(back_own + grid.over_t(back_oth).astype(F32))
        back_state, gain_t, shift_t = norm_backward(
            back_normed, kept["unit_t"], kept["scale_t"], gain[0]
        )
        upstream = upstream + back_state

        parts_t = [triple_t_part, merge_t_part, mixing_part]
        parts_sm = [triple_s_part, merge_s_part, up_part, down_part]
        if layer == 0:
            late = scatter_rows(grid, parts_sm)
            early = scatter_rows(grid, parts_t)
            shards[layer] = split_columns(early, wide_t) + split_columns(late, wide_s + wide_m)
        else:
            shards[layer] = split_columns(
                scatter_rows(grid, parts_t + parts_sm), wide_t + wide_s + wide_m
            )
        whole_sums[layer] = jnp.concatenate(
            [
                gain_t,
                gain_s,
                gain_m,
                shift_t,
                shift_s,
                shift_m,
                merge_bias_part,
                mixing_bias_part,
                spatial_bias_part,
                down_bias_part,
                squares[layer],
            ]
        )
        theirs = jnp.concatenate([entry_s_part[1].reshape(-1), hidden_part[1]])
        mine = jnp.concatenate([entry_s_part[0].reshape(-1), hidden_part[0]])
        half_sums[layer] = jnp.concatenate(
            [entry_t_part.reshape(-1), mine + grid.over_t(theirs)]
        )

    input_grad = spread_out(upstream.astype(BF)).astype(F32)
    whole = jnp.stack(whole_sums)
    halves = jnp.stack(half_sums)
    whole = whole + grid.over_t(whole)
    both = grid.total(jnp.concatenate([whole, halves], axis=1), False)
    whole, halves = both[:, : whole.shape[1]], both[:, whole.shape[1] :]
    gain_sum = whole[:, : 3 * width].reshape(LAYERS, 3, width)
    shift_sum = whole[:, 3 * width : 6 * width].reshape(LAYERS, 3, width)
    bias_sum = whole[:, 6 * width : 10 * width].reshape(LAYERS, 4, width)
    square_sum = whole[:, 10 * width :]
    entry_sum = halves[:, : 4 * split].reshape(LAYERS, 2, 2, split)
    hidden_sum = halves[:, 4 * split :]
    tokens = FRAMES * width * jnp.sum(valid_places).astype(F32)
    root_squares = jnp.sqrt(square_sum / tokens)

    def unpack_rows(item):
        return jnp.concatenate([item[:half_rows], item[half_rows:]], axis=-1)

    def triple_shape(item):
        return item.reshape(step_rows, 3, split)

    return (
        block_output,
        input_grad,
        gain_sum,
        shift_sum,
        jnp.stack([jnp.stack([triple_shape(s[0]), triple_shape(s[3])]) for s in shards]),
        entry_sum,
        jnp.stack([jnp.stack([s[1].T, s[4].T]) for s in shards]),
        bias_sum,
        jnp.stack([unpack_rows(s[2]) for s in shards]),
        jnp.stack([s[5] for s in shards]),
        hidden_sum,
        jnp.stack([s[6].T for s in shards]),
        root_squares,
    )


def solution(mesh):
    return jax.shard_map(
        per_device,
        mesh=mesh,
        in_specs=(
            P("shard", "ctx", "tp", None),
            P("shard", "ctx", "tp", None),
            P("shard"),
            P(),
            P(),
            P(),
            P(None, None, ("shard", "ctx"), None, "tp"),
            P(None, None, None, "tp"),
            P(None, None, "tp", ("shard", "ctx")),
            P(),
            P(None, ("shard", "ctx", "tp"), None),
            P(None, ("shard", "ctx"), "tp"),
            P(None, "tp"),
            P(None, "tp", ("shard", "ctx")),
        ),
        out_specs=(
            P("shard", "ctx", "tp", None),
            P("shard", "ctx", "tp", None),
            P(),
            P(),
            P(None, None, ("shard", "ctx"), None, "tp"),
            P(None, None, None, "tp"),
            P(None, None, "tp", ("shard", "ctx")),
            P(),
            P(None, ("shard", "ctx", "tp"), None),
            P(None, ("shard", "ctx"), "tp"),
            P(None, "tp"),
            P(None, "tp", ("shard", "ctx")),
            P(),
        ),
        check_vma=False,
    )
```

```python
import functools

import jax
import jax.numpy as jnp
from jax import lax
from jax.experimental import pallas as pl
from jax.experimental.pallas import tpu as pltpu
from jax.sharding import PartitionSpec as P

HEAD_DIM = 64
FRAMES = 8
LAYERS = 2
AXES = ("shard", "ctx", "tp")
BF = jnp.bfloat16
F32 = jnp.float32

far_below = -1000000000.0
epsilon = 1e-06
root_half = 0.7071067811865476
gauss_scale = 0.3989422804014327


def dot_nn(left, right):
    return lax.dot_general(left, right, (((1,), (0,)), ((), ())), preferred_element_type=F32)


def dot_nt(left, right):
    return lax.dot_general(left, right, (((1,), (1,)), ((), ())), preferred_element_type=F32)


def dot_tn(left, right):
    return lax.dot_general(left, right, (((0,), (0,)), ((), ())), preferred_element_type=F32)


def rows(value):
    return value.reshape(-1, value.shape[-1])


def row_total(value):
    return jnp.sum(rows(value).astype(F32), axis=0)


def lane_masks(shape):
    lane = lax.broadcasted_iota(jnp.int32, shape, 1)
    return lane < HEAD_DIM


def softmax_rows(scores):
    top = jnp.max(scores, axis=-1, keepdims=True)
    raised = jnp.exp(scores - top)
    total = jnp.sum(raised, axis=-1, keepdims=True)
    return raised * (1.0 / total)


def sides(value, first):
    zero = jnp.zeros_like(value)
    return [jnp.where(first, value, zero), jnp.where(first, zero, value)]


def heads_forward(qkv, fix, scale, put):
    first = lane_masks(qkv(0, 0).shape)
    scores = []
    for pair in range(3):
        k = qkv(1, pair)
        scores.append([dot_nt(q, k) for q in sides(qkv(0, pair), first)])
    shares = [[softmax_rows(fix(item * scale)).astype(BF) for item in both] for both in scores]
    for pair in range(3):
        v = qkv(2, pair)
        outs = [dot_nn(item, v) for item in shares[pair]]
        put(pair, jnp.where(first, outs[0], outs[1]).astype(BF))


def heads_backward(qkv, back, fix, scale, put):
    first = lane_masks(qkv(0, 0).shape)
    scores, backs = [], []
    for pair in range(3):
        k, v = qkv(1, pair), qkv(2, pair)
        scores.append([dot_nt(q, k) for q in sides(qkv(0, pair), first)])
        backs.append([dot_nt(b, v) for b in sides(back(pair), first)])
    low_shares, low_scores = [], []
    for pair in range(3):
        low_shares.append([])
        low_scores.append([])
        for side in range(2):
            shares = softmax_rows(fix(scores[pair][side] * scale))
            back_shares = backs[pair][side]
            inner = jnp.sum(back_shares * shares, axis=-1, keepdims=True)
            low_scores[pair].append((shares * (back_shares - inner)).astype(BF))
            low_shares[pair].append(shares.astype(BF))
    for pair in range(3):
        q, k, bm = qkv(0, pair), qkv(1, pair), back(pair)
        gq = [dot_nn(item, k) for item in low_scores[pair]]
        gk = [dot_tn(item, q) for item in low_scores[pair]]
        gv = [dot_tn(item, bm) for item in low_shares[pair]]
        put(0, pair, (jnp.where(first, gq[0], gq[1]) * scale).astype(BF))
        put(1, pair, (jnp.where(first, gk[0], gk[1]) * scale).astype(BF))
        put(2, pair, jnp.where(first, gv[0], gv[1]).astype(BF))


def column(part, pair):
    start = part * 384 + pair * 128
    return slice(start, start + 128)


def spatial_fix(count_ref, padded, places):
    col = lax.broadcasted_iota(jnp.int32, (padded, padded), 1)
    floor = jnp.where(col < places, far_below, 3.0 * far_below)
    allowed = col < jnp.minimum(count_ref[0], places)
    return lambda scores: jnp.where(allowed, scores, floor)


def spatial_fwd_body(places, scale, count_ref, own_ref, oth_ref, own_out, oth_out):
    fix = spatial_fix(count_ref, own_ref.shape[1], places)
    for src, dst in ((own_ref, own_out), (oth_ref, oth_out)):

        def put(pair, value, dst=dst):
            dst[0, :, pair * 128 : pair * 128 + 128] = value

        heads_forward(lambda part, pair, src=src: src[0, :, column(part, pair)], fix, scale, put)


def spatial_bwd_body(
    places, scale, count_ref, own_ref, oth_ref, bown_ref, both_ref, own_out, oth_out
):
    fix = spatial_fix(count_ref, own_ref.shape[1], places)
    for src, back, dst in ((own_ref, bown_ref, own_out), (oth_ref, both_ref, oth_out)):

        def put(part, pair, value, dst=dst):
            dst[0, :, column(part, pair)] = value

        heads_backward(
            lambda part, pair, src=src: src[0, :, column(part, pair)],
            lambda pair, back=back: back[0, :, pair * 128 : pair * 128 + 128],
            fix,
            scale,
            put,
        )


def temporal_fix(tile):
    size = FRAMES * tile
    row = lax.broadcasted_iota(jnp.int32, (size, size), 0)
    col = lax.broadcasted_iota(jnp.int32, (size, size), 1)
    same = (row & (tile - 1)) == (col & (tile - 1))
    return lambda scores: jnp.where(same, scores, 3.0 * far_below)


def temporal_fwd_body(scale, src, dst):
    tile = src.shape[1]
    fix = temporal_fix(tile)

    def put(pair, value):
        dst[:, :, pair * 128 : pair * 128 + 128] = value.reshape(FRAMES, tile, 128)

    heads_forward(
        lambda part, pair: src[:, :, column(part, pair)].reshape(FRAMES * tile, 128),
        fix,
        scale,
        put,
    )


def temporal_bwd_body(scale, src, back, dst):
    tile = src.shape[1]
    fix = temporal_fix(tile)

    def put(part, pair, value):
        dst[:, :, column(part, pair)] = value.reshape(FRAMES, tile, 128)

    heads_backward(
        lambda part, pair: src[:, :, column(part, pair)].reshape(FRAMES * tile, 128),
        lambda pair: back[:, :, pair * 128 : pair * 128 + 128].reshape(FRAMES * tile, 128),
        fix,
        scale,
        put,
    )


def spatial_call(count, ins, widths, places, scale, backward):
    frames, padded, _ = ins[0].shape
    spec = lambda width: pl.BlockSpec((1, padded, width), lambda f: (f, 0, 0))
    body = spatial_bwd_body if backward else spatial_fwd_body
    work = frames * 12 * padded * 256 * 128 * 2 * (5 if backward else 2)
    return pl.pallas_call(
        functools.partial(body, places, scale),
        grid=(frames,),
        in_specs=[pl.BlockSpec(memory_space=pltpu.SMEM)] + [spec(x.shape[-1]) for x in ins],
        out_specs=[spec(width) for width in widths],
        out_shape=[jax.ShapeDtypeStruct((frames, padded, width), BF) for width in widths],
        cost_estimate=pl.CostEstimate(
            flops=work * 4, bytes_accessed=8 * frames * padded * 2304, transcendentals=0
        ),
        name="spatial_back" if backward else "spatial_mix",
    )(count, *ins)


def temporal_call(ins, width, scale, backward):
    frames, padded, _ = ins[0].shape
    tile = 16
    spec = lambda lanes: pl.BlockSpec((frames, tile, lanes), lambda i: (0, i, 0))
    body = temporal_bwd_body if backward else temporal_fwd_body
    work = padded // tile * 6 * 128 * 128 * 128 * 2 * (5 if backward else 2)
    return pl.pallas_call(
        functools.partial(body, scale),
        grid=(padded // tile,),
        in_specs=[spec(x.shape[-1]) for x in ins],
        out_specs=spec(width),
        out_shape=jax.ShapeDtypeStruct((frames, padded, width), BF),
        cost_estimate=pl.CostEstimate(
            flops=work * 8, bytes_accessed=4 * frames * padded * 1152, transcendentals=0
        ),
        name="temporal_back" if backward else "temporal_mix",
    )(*ins)


class Grid:
    def __init__(self):
        self.shards = lax.axis_size("shard")
        self.depth = self.shards // 2
        shard = lax.axis_index("shard")
        self.z = shard // 2
        self.x = shard % 2
        self.y = lax.axis_index("ctx")
        self.t = lax.axis_index("tp")
        self.direct = self.depth == 4

    def perm(self, move):
        pairs = []
        for z in range(self.depth):
            for x in range(2):
                for y in range(2):
                    for t in range(2):
                        tz, tx, ty, tt = move(z, x, y, t)
                        pairs.append(
                            (((z * 2 + x) * 2 + y) * 2 + t, ((tz * 2 + tx) * 2 + ty) * 2 + tt)
                        )
        return pairs

    def send(self, value, pairs):
        return lax.ppermute(value, AXES, pairs)

    def over_x(self, value):
        return self.send(value, self.perm(lambda z, x, y, t: (z, 1 - x, y, t)))

    def over_y(self, value):
        return self.send(value, self.perm(lambda z, x, y, t: (z, x, 1 - y, t)))

    def over_t(self, value):
        return self.send(value, self.perm(lambda z, x, y, t: (z, x, y, 1 - t)))

    def over_z(self, value, step):
        depth = self.depth
        return self.send(value, self.perm(lambda z, x, y, t: ((z + step) % depth, x, y, t)))

    def over_bit(self, value, bit):
        pairs = []
        for s in range(self.shards):
            for y in range(2):
                for t in range(2):
                    pairs.append(((s * 2 + y) * 2 + t, ((s ^ bit) * 2 + y) * 2 + t))
        return self.send(value, pairs)

    def total(self, value, across):
        if across:
            value = value + self.over_t(value)
        value = value + self.over_y(value)
        bit = 1
        while bit < self.shards:
            value = value + self.over_bit(value, bit)
            bit *= 2
        return value


def place_body(widths, step_rows, half, at_ref, own, xn, yn, da, db, *outs):
    back = pl.program_id(0)
    x, y = at_ref[1], at_ref[2]

    def put(dx, dy, piece):
        bx = x if dx == 0 else 1 - x
        by = y if dy == 0 else 1 - y
        row = pl.multiple_of((bx * 2 + by) * step_rows, 16)
        start = 0
        for number, width in enumerate(widths):
            outs[number][pl.ds(row, step_rows), :] = piece[0, :, start : start + width]
            start += width

    put(0, 0, own)
    put(1, 0, xn)
    put(0, 1, yn)

    @pl.when(back < half)
    def _():
        put(1, 1, da)

    @pl.when(back >= half)
    def _():
        put(1, 1, db)


def tie(value, *others):
    return lax.optimization_barrier((value, *others))[0]


class Feed:
    def __init__(self, grid, items, widths, *behind):
        self.grid, self.widths = grid, widths
        block = tie(jnp.concatenate(items, axis=1), *behind)
        if grid.direct:
            self.blocks = [block] + [grid.over_z(block, k) for k in range(1, grid.depth)]
        else:
            self.blocks = [block]

    def near(self, *behind):
        grid = self.grid
        if grid.direct:
            self.own = tie(jnp.stack(self.blocks), *behind)
            self.xn = grid.over_x(self.own)
            self.yn = grid.over_y(self.own)
        return self

    def far(self, *behind):
        grid = self.grid
        if grid.direct:
            half = grid.depth // 2
            xn, yn = tie(self.xn[:half], *behind), tie(self.yn[half:], *behind)
            self.last = (grid.over_y(xn), grid.over_x(yn))
        return self

    def done(self):
        grid = self.grid
        if not grid.direct:
            full = lax.all_gather(self.blocks[0], ("shard", "ctx"), axis=0, tiled=True)
            return split_columns(full, self.widths)
        at = jnp.stack([grid.z, grid.x, grid.y]).astype(jnp.int32)
        return place_rows(grid, at, self.own, self.xn, self.yn, *self.last, self.widths)

    def near_parts(self):
        return (self.xn, self.yn) if self.grid.direct else ()

    def far_parts(self):
        return self.last if self.grid.direct else ()


def place_rows(grid, at, own, xn, yn, da, db, widths):
    depth, step_rows, lanes = own.shape
    half = depth // 2
    piece = lambda index: pl.BlockSpec((1, step_rows, lanes), index)
    straight = piece(lambda k, at_ref: (k, 0, 0))
    return pl.pallas_call(
        functools.partial(place_body, tuple(widths), step_rows, half),
        grid_spec=pltpu.PrefetchScalarGridSpec(
            num_scalar_prefetch=1,
            grid=(depth,),
            in_specs=[
                straight,
                straight,
                straight,
                piece(lambda k, at_ref: (jnp.minimum(k, half - 1), 0, 0)),
                piece(lambda k, at_ref: (jnp.maximum(k - half, 0), 0, 0)),
            ],
            out_specs=[
                pl.BlockSpec(
                    (4 * step_rows, width),
                    lambda k, at_ref: (lax.rem(at_ref[0] - k + depth, depth), 0),
                )
                for width in widths
            ],
        ),
        out_shape=[
            jax.ShapeDtypeStruct((depth * 4 * step_rows, width), own.dtype) for width in widths
        ],
        cost_estimate=pl.CostEstimate(
            flops=0, bytes_accessed=depth * 4 * step_rows * lanes * 4, transcendentals=0
        ),
        compiler_params=pltpu.CompilerParams(vmem_limit_bytes=48 << 20),
        name="place_rows",
    )(at, own, xn, yn, da, db)


class Sums:
    def __init__(self, place, part, own, ra, rb, sx, sy, rx, ry, low, gz, send, recv):
        self.place, self.part, self.own = place, part, own
        self.ra, self.rb, self.sx, self.sy = ra, rb, sx, sy
        self.rx, self.ry, self.low, self.gz = rx, ry, low, gz
        self.send, self.recv = send, recv
        self.half = part.shape[0] // 2

    def copy(self, number, src, dst, target):
        return pltpu.make_async_remote_copy(
            src_ref=src,
            dst_ref=dst,
            send_sem=self.send.at[number],
            recv_sem=self.recv.at[number],
            device_id=target,
            device_id_type=pl.DeviceIdType.MESH,
        )

    def first(self):
        z, x, y = self.place.z, self.place.x, self.place.y
        low, high = pl.ds(0, self.half), pl.ds(self.half, self.half)
        self.far = [
            self.copy(0, self.part.at[low, 1 - x, 1 - y], self.ra, self.place.over_y()),
            self.copy(1, self.part.at[high, 1 - x, 1 - y], self.rb, self.place.over_x()),
        ]
        for item in self.far:
            item.start()

    def second(self):
        x, y, half = self.place.x, self.place.y, self.half
        for item in self.far:
            item.wait()
        for k in range(2 * half):
            toward_x, toward_y = self.part[k, 1 - x, y], self.part[k, x, 1 - y]
            if k < half:
                toward_x = (toward_x.astype(F32) + self.ra[k].astype(F32)).astype(BF)
            else:
                toward_y = (toward_y.astype(F32) + self.rb[k - half].astype(F32)).astype(BF)
            self.sx[k] = toward_x
            self.sy[k] = toward_y
        self.near = [
            self.copy(2, self.sx, self.rx, self.place.over_x()),
            self.copy(3, self.sy, self.ry, self.place.over_y()),
        ]
        for item in self.near:
            item.start()

    def kept(self, k):
        mine = self.part[k, self.place.x, self.place.y].astype(F32)
        return mine + self.rx[k].astype(F32) + self.ry[k].astype(F32)

    def third(self):
        depth = 2 * self.half
        for item in self.near:
            item.wait()
        for k in range(depth):
            self.low[k] = self.kept(k).astype(BF)
        self.deep = [
            self.copy(
                3 + k,
                self.low.at[lax.rem(self.place.z + k, depth)],
                self.gz.at[k - 1],
                self.place.over_z(k),
            )
            for k in range(1, depth)
        ]
        for item in self.deep:
            item.start()

    def last(self):
        for item in self.deep:
            item.wait()
        total = self.kept(self.place.z)
        for k in range(2 * self.half - 1):
            total = total + self.gz[k].astype(F32)
        self.own[...] = total


class Place:
    def __init__(self, depth):
        self.depth = depth
        shard = lax.axis_index("shard")
        self.z = shard // 2
        self.x = lax.rem(shard, 2)
        self.y = lax.axis_index("ctx")

    def over_x(self):
        return {"shard": self.z * 2 + 1 - self.x}

    def over_y(self):
        return {"ctx": 1 - self.y}

    def over_z(self, step):
        return {"shard": lax.rem(self.z + step, self.depth) * 2 + self.x}

    def meet(self):
        barrier = pltpu.get_barrier_semaphore()
        targets = [self.over_x(), self.over_y()]
        targets += [self.over_z(k) for k in range(1, self.depth)]
        for target in targets:
            pl.semaphore_signal(
                barrier, inc=1, device_id=target, device_id_type=pl.DeviceIdType.MESH
            )
        pl.semaphore_wait(barrier, len(targets))


def sum_body(depth, ins, parts, outs, payload, *refs):
    refs = list(refs)
    take = lambda count: [refs.pop(0) for _ in range(count)]
    in_refs, part_refs, out_refs, own_refs = take(ins), take(parts), take(outs), take(parts)
    place = Place(depth)
    sums = [
        Sums(place, part, own, *take(10)) for part, own in zip(part_refs, own_refs)
    ]
    place.meet()
    for item in sums:
        item.first()
    payload(0, in_refs, out_refs)
    for item in sums:
        item.second()
    payload(1, in_refs, out_refs)
    for item in sums:
        item.third()
    for item in sums:
        item.last()


def no_payload(stage, in_refs, out_refs):
    return None


def sum_rows(grid, number, parts, payload=no_payload, ins=(), outs=(), smem=0):
    depth = grid.depth
    step_rows = parts[0].shape[0] // (depth * 4)
    cubes = [part.reshape(depth, 2, 2, step_rows, part.shape[1]) for part in parts]
    scratch = []
    for part in parts:
        block = lambda count, lanes=part.shape[1]: pltpu.VMEM((count, step_rows, lanes), BF)
        scratch += [block(depth // 2)] * 2 + [block(depth)] * 5 + [block(depth - 1)]
        scratch += [pltpu.SemaphoreType.DMA((3 + depth,))] * 2
    vmem = pl.BlockSpec(memory_space=pltpu.VMEM)
    results = pl.pallas_call(
        functools.partial(sum_body, depth, len(ins), len(parts), len(outs), payload),
        in_specs=[pl.BlockSpec(memory_space=pltpu.SMEM)] * smem
        + [vmem] * (len(ins) - smem + len(parts)),
        out_specs=[vmem] * (len(outs) + len(parts)),
        out_shape=list(outs)
        + [jax.ShapeDtypeStruct((step_rows, part.shape[1]), F32) for part in parts],
        scratch_shapes=scratch,
        compiler_params=pltpu.CompilerParams(
            collective_id=number, has_side_effects=True, vmem_limit_bytes=56 << 20
        ),
        cost_estimate=pl.CostEstimate(
            flops=20000000000, bytes_accessed=50000000, transcendentals=0
        ),
        name="sum_rows",
    )(*ins, *cubes)
    return results[: len(outs)], results[len(outs) :]


def plain_sums(parts):
    return [
        lax.psum_scatter(part.astype(F32), ("shard", "ctx"), scatter_dimension=0, tiled=True)
        for part in parts
    ]


def spatial_back_payload(places, scale, stage, ins, outs):
    count_ref, own_ref, oth_ref, bown_ref, both_ref = ins
    frames = own_ref.shape[0]
    fix = spatial_fix(count_ref, own_ref.shape[1], places)

    def frame(f, carry):
        for src, back, dst in ((own_ref, bown_ref, outs[0]), (oth_ref, both_ref, outs[1])):

            def put(part, pair, value, dst=dst):
                dst[f, :, column(part, pair)] = value

            heads_backward(
                lambda part, pair, src=src: src[f, :, column(part, pair)],
                lambda pair, back=back: back[f, :, pair * 128 : pair * 128 + 128],
                fix,
                scale,
                put,
            )
        return carry

    half = frames // 2
    lax.fori_loop(stage * half, half if stage == 0 else frames, frame, 0)


def temporal_back_payload(scale, stage, ins, outs):
    src, back = ins
    dst = outs[0]
    tile = 16
    tiles = src.shape[1] // tile
    fix = temporal_fix(tile)

    def one(i, carry):
        at = pl.ds(pl.multiple_of(i * tile, tile), tile)

        def put(part, pair, value):
            dst[:, at, column(part, pair)] = value.reshape(FRAMES, tile, 128)

        heads_backward(
            lambda part, pair: src[:, at, column(part, pair)].reshape(FRAMES * tile, 128),
            lambda pair: back[:, at, pair * 128 : pair * 128 + 128].reshape(FRAMES * tile, 128),
            fix,
            scale,
            put,
        )
        return carry

    half = tiles // 2
    lax.fori_loop(stage * half, half if stage == 0 else tiles, one, 0)


def split_columns(value, widths):
    outs, start = [], 0
    for width in widths:
        outs.append(value[..., start : start + width])
        start += width
    return outs


def norm_forward(state, gain, shift):
    center = state - jnp.mean(state, axis=-1, keepdims=True)
    scale = lax.rsqrt(jnp.mean(center * center, axis=-1, keepdims=True) + epsilon)
    unit = center * scale
    return ((unit * gain + shift).astype(BF), unit, scale)


def norm_backward(incoming, unit, scale, gain):
    along = incoming * gain
    back = scale * (
        along
        - jnp.mean(along, axis=-1, keepdims=True)
        - unit * jnp.mean(along * unit, axis=-1, keepdims=True)
    )
    return (back, row_total(incoming * unit), row_total(incoming))


def per_device(
    video_clips,
    cotangent,
    slot_clip,
    valid_places,
    norm_gain,
    norm_bias,
    triple_weight,
    entry_bias,
    merge_weight,
    branch_bias,
    mixing_weight,
    up_weight,
    up_bias,
    down_weight,
):
    grid = Grid()
    slots, frames_here, places_here, width = video_clips.shape
    places = places_here * 2
    padded = -(-places // 16) * 16
    scale = HEAD_DIM ** (-0.5)
    step_rows = triple_weight.shape[2]
    half_rows = step_rows // 2
    own_first = grid.t == 0
    straight = grid.t == grid.y

    clip_ids = jnp.arange(valid_places.shape[0], dtype=jnp.int32)
    my_clip = lax.dynamic_index_in_dim(slot_clip, grid.y, 0, keepdims=False)
    count = jnp.sum(jnp.where(my_clip == clip_ids, valid_places, 0)).astype(jnp.int32)
    valid_here = (jnp.arange(padded, dtype=jnp.int32) < count).astype(F32)[None, :, None]
    count_ref = count.reshape(1)

    def spread_in(value):
        mine = lax.dynamic_index_in_dim(value, grid.y, 0, keepdims=False)
        theirs = lax.dynamic_index_in_dim(value, 1 - grid.y, 0, keepdims=False)
        got = grid.over_y(theirs)
        keep = jnp.where(straight, mine, got)
        send = jnp.where(straight, got, mine)
        swap = grid.over_t(send)
        low = jnp.where(own_first, keep, swap)
        high = jnp.where(own_first, swap, keep)
        gap = jnp.zeros((frames_here, padded - places, width), value.dtype)
        return jnp.concatenate([low, high, gap], axis=1)

    def spread_out(value):
        low = value[:, :places_here]
        high = value[:, places_here:places]
        keep = jnp.where(own_first, low, high)
        send = jnp.where(own_first, high, low)
        swap = grid.over_t(send)
        mine = jnp.where(straight, keep, swap)
        away = jnp.where(straight, swap, keep)
        got = grid.over_y(away)
        first = jnp.where(grid.y == 0, mine, got)
        second = jnp.where(grid.y == 0, got, mine)
        return jnp.stack([first, second])

    def pack_mix(item):
        return jnp.concatenate([item[..., : width // 2], item[..., width // 2 :]], axis=-2)

    def block_triple(layer, part):
        return [triple_weight[layer, part, :, i] for i in range(3)]

    def block_out(layer):
        return [merge_weight[layer, 0].T, pack_mix(mixing_weight[layer])]

    def block_s(layer):
        return block_triple(layer, 1) + [merge_weight[layer, 1].T]

    def block_m(layer):
        return [up_weight[layer], down_weight[layer].T]

    split = triple_weight.shape[-1]
    hid = up_weight.shape[-1]
    wide_t = (3 * split, split, width // 2)
    wide_s = (3 * split, split)
    wide_m = (hid, hid)

    def unpack_mix(item):
        cube = item.reshape(-1, 2, half_rows, width // 2)
        return jnp.concatenate([cube[:, 0], cube[:, 1]], axis=-1)

    def with_other(item):
        return (item, grid.over_t(item))

    def out_weights(merge_t, mix):
        mix_own, mix_oth = [unpack_mix(item) for item in with_other(mix)]
        mixing = jnp.stack(
            [jnp.where(own_first, mix_own, mix_oth), jnp.where(own_first, mix_oth, mix_own)],
            axis=1,
        ).reshape(width, width)
        return dict(merge_t=with_other(merge_t), mixing=mixing)

    small = jnp.concatenate([entry_bias[:, 1].reshape(-1), up_bias.reshape(-1)])
    small_oth = grid.over_t(small)
    entry_count = LAYERS * 2 * split
    entry_s = (
        small[:entry_count].reshape(LAYERS, 2, split),
        small_oth[:entry_count].reshape(LAYERS, 2, split),
    )
    up_bias2 = (
        small[entry_count:].reshape(LAYERS, hid),
        small_oth[entry_count:].reshape(LAYERS, hid),
    )

    def triple_bias(pair):
        return jnp.concatenate([pair[0], jnp.zeros((split,), F32), pair[1]])

    def cube(value):
        return value.reshape(-1, padded, value.shape[-1])

    gathered = [dict() for _ in range(LAYERS)]
    feed1 = Feed(grid, block_triple(0, 0), wide_t[:1]).near().far()
    gathered[0]["triple_t"] = feed1.done()[0]
    feed2 = Feed(grid, block_out(0) + block_s(0), wide_t[1:] + wide_s, *feed1.near_parts())
    state = spread_in(video_clips).astype(F32)

    def corner(value):
        return value[(slice(0, 1),) * (value.ndim - 2) + (slice(0, 8), slice(0, 128))]
    stored = []
    squares = []
    for layer in range(LAYERS):
        w = gathered[layer]
        gain, shift, bias = norm_gain[layer], norm_bias[layer], branch_bias[layer]
        normed, unit_t, scale_t = norm_forward(state, gain[0], shift[0])
        normed_t = jnp.concatenate([normed, grid.over_t(normed)], axis=0)
        qkv_t = cube(
            (dot_nn(rows(normed_t), w["triple_t"]) + triple_bias(entry_bias[layer, 0])).astype(BF)
        )
        if layer == 0:
            feed2.near(*feed1.far_parts(), corner(normed_t)).far(corner(qkv_t))
            merge_t, mix, triple_s, merge_s = feed2.done()
            w.update(out_weights(merge_t, mix))
            w.update(triple_s=with_other(triple_s), merge_s=with_other(merge_s))
            feed3 = Feed(grid, block_m(0), wide_m, corner(qkv_t))
        mixed = temporal_call([qkv_t], split, scale, False)
        if layer == 0:
            feed3.near(*feed2.far_parts(), corner(mixed))
        elif layer == 1:
            feed5.far(corner(mixed))
            triple_s, merge_s, upward, downward = feed5.done()
            w.update(triple_s=with_other(triple_s), merge_s=with_other(merge_s))
            w.update(up=with_other(upward), down=with_other(downward))
        mine = mixed[:frames_here]
        swap = grid.over_t(mixed[frames_here:])
        joined = (
            dot_nt(rows(mine), w["merge_t"][0]) + dot_nt(rows(swap), w["merge_t"][1]) + bias[0]
        ).astype(BF)
        temporal = cube(dot_nn(joined, w["mixing"]) + bias[1])
        state = state + temporal
        normed_s, unit_s, scale_s = norm_forward(state, gain[1], shift[1])
        qkv_s = [
            cube(
                (
                    dot_nn(rows(normed_s), w["triple_s"][i]) + triple_bias(entry_s[i][layer])
                ).astype(BF)
            )
            for i in range(2)
        ]
        if layer == 0:
            upward, downward = feed3.far(corner(qkv_s[0])).done()
            w.update(up=with_other(upward), down=with_other(downward))
            feed4 = Feed(grid, block_triple(1, 0) + block_out(1), wide_t, corner(joined))
        mixed_s = spatial_call(count_ref, qkv_s, (split, split), places, scale, False)
        if layer == 0:
            feed4.near(*feed3.far_parts(), corner(mixed_s[0]))
            feed5 = Feed(grid, block_s(1) + block_m(1), wide_s + wide_m, corner(mixed_s[0]))
            late_cotangent = tie(cotangent, corner(mixed_s[0]))
            upstream = spread_in(late_cotangent.astype(BF)).astype(F32) * valid_here
        spatial = cube(
            dot_nt(rows(mixed_s[0]), w["merge_s"][0])
            + dot_nt(rows(mixed_s[1]), w["merge_s"][1])
            + bias[2]
        )
        state = state + spatial
        normed_m, unit_m, scale_m = norm_forward(state, gain[2], shift[2])
        active, slope = [], []
        for i in range(2):
            hidden = dot_nn(rows(normed_m), w["up"][i]) + up_bias2[i][layer]
            below = 0.5 * (1.0 + lax.erf(hidden * root_half))
            active.append((hidden * below).astype(BF))
            slope.append(
                (below + hidden * gauss_scale * jnp.exp(-0.5 * hidden * hidden)).astype(BF)
            )
        if layer == 0:
            triple_t, merge_t, mix = feed4.far(corner(active[0])).done()
            gathered[1].update(triple_t=triple_t, **out_weights(merge_t, mix))
            feed5.near(*feed4.far_parts(), corner(active[1]))
        dense = cube(
            dot_nt(active[0], w["down"][0]) + dot_nt(active[1], w["down"][1]) + bias[3]
        )
        state = state + dense
        squares.append(
            jnp.stack(
                [
                    jnp.sum(jnp.square(item) * valid_here)
                    for item in (temporal, spatial, dense, state)
                ]
            )
        )
        stored.append(
            dict(
                unit_t=unit_t,
                scale_t=scale_t,
                normed_t=normed_t,
                qkv_t=qkv_t,
                mixed_t=(mine, swap),
                joined=joined,
                unit_s=unit_s,
                scale_s=scale_s,
                normed_s=normed_s,
                qkv_s=qkv_s,
                mixed_s=mixed_s,
                unit_m=unit_m,
                scale_m=scale_m,
                normed_m=normed_m,
                active=active,
                slope=slope,
            )
        )
    block_output = spread_out(state.astype(BF))

    shards = [None] * LAYERS
    whole_early, half_early = [], []
    sums = {}

    def add_up(wholes, halves):
        whole = jnp.concatenate(wholes)
        whole = whole + grid.over_t(whole)
        return grid.total(jnp.concatenate([whole] + halves), False)

    def join(make):
        got = grid.over_t(make(1).astype(BF))
        return (make(0) + got.astype(F32)).astype(BF)

    for layer in range(LAYERS - 1, -1, -1):
        w, kept = gathered[layer], stored[layer]
        gain = norm_gain[layer]
        r = rows(upstream).astype(BF)
        down_bias_part = row_total(r)
        back_active = [dot_nn(r, w["down"][i]) for i in range(2)]
        back_hidden = [
            (back_active[i] * kept["slope"][i].astype(F32)).astype(BF) for i in range(2)
        ]
        hidden_part = [row_total(back_hidden[i]) for i in range(2)]
        back_sides = [dot_nt(back_hidden[i], w["up"][i]) for i in range(2)]
        back_normed = cube(back_sides[0] + back_sides[1])
        back_state, gain_m, shift_m = norm_backward(
            back_normed, kept["unit_m"], kept["scale_m"], gain[2]
        )
        upstream = upstream + back_state
        parts_m = [
            join(lambda i: dot_tn(rows(kept["normed_m"]), back_hidden[i])),
            join(lambda i: dot_tn(r, kept["active"][i])),
        ]
        rs = rows(upstream).astype(BF)
        r = rs
        spatial_bias_part = row_total(r)
        back_mixed = [cube(dot_nn(r, w["merge_s"][i]).astype(BF)) for i in range(2)]
        spatial_ins = list(kept["qkv_s"]) + back_mixed
        if grid.direct:
            back_qkv, sums["m", layer] = sum_rows(
                grid,
                layer,
                parts_m,
                functools.partial(spatial_back_payload, places, scale),
                [count_ref] + spatial_ins,
                [jax.ShapeDtypeStruct(item.shape, BF) for item in kept["qkv_s"]],
                1,
            )
        else:
            back_qkv = spatial_call(
                count_ref, spatial_ins, (3 * split, 3 * split), places, scale, True
            )
            sums["m", layer] = plain_sums(parts_m)
        qkv_sums = [row_total(back_qkv[i]) for i in range(2)]
        entry_s_part = [jnp.stack([q[:split], q[2 * split :]]) for q in qkv_sums]
        back_sides = [dot_nt(rows(back_qkv[i]), w["triple_s"][i]) for i in range(2)]
        back_normed = cube(back_sides[0] + back_sides[1])
        back_state, gain_s, shift_s = norm_backward(
            back_normed, kept["unit_s"], kept["scale_s"], gain[1]
        )
        upstream = upstream + back_state
        parts_s = [
            join(lambda i: dot_tn(rows(kept["normed_s"]), rows(back_qkv[i]))),
            join(lambda i: dot_tn(rs, rows(kept["mixed_s"][i]))),
        ]
        theirs = jnp.concatenate([entry_s_part[1].reshape(-1), hidden_part[1]])
        mine = jnp.concatenate([entry_s_part[0].reshape(-1), hidden_part[0]])
        half_early.append(mine + grid.over_t(theirs))
        whole_early.append(
            jnp.concatenate(
                [gain_s, gain_m, shift_s, shift_m, spatial_bias_part, down_bias_part]
                + [squares[layer], jnp.zeros((124,), F32)]
            )
        )
        r = rows(upstream).astype(BF)
        mixing_bias_part = row_total(r)
        back_joined = dot_nt(r, w["mixing"]).astype(BF)
        merge_bias_part = row_total(back_joined)
        back_mine, back_away = [
            cube(dot_nn(back_joined, w["merge_t"][i]).astype(BF)) for i in range(2)
        ]
        back_mixed = jnp.concatenate([back_mine, grid.over_t(back_away)], axis=0)
        mix_part = dot_tn(kept["joined"], r).reshape(-1, 2, half_rows, width)

        def mix_half(i, mix_part=mix_part):
            chosen = grid.t if i == 0 else 1 - grid.t
            half = lax.dynamic_index_in_dim(mix_part, chosen, 1, keepdims=False)
            return pack_mix(half).reshape(width, width // 2)

        parts_o = [
            join(lambda i: dot_tn(back_joined, rows(kept["mixed_t"][i]))),
            join(mix_half),
        ]
        if grid.direct:
            (back_qkv,), sums["s", layer] = sum_rows(
                grid,
                2 + layer,
                parts_s,
                functools.partial(temporal_back_payload, scale),
                [kept["qkv_t"], back_mixed],
                [jax.ShapeDtypeStruct(kept["qkv_t"].shape, BF)],
            )
        else:
            back_qkv = temporal_call([kept["qkv_t"], back_mixed], 3 * split, scale, True)
            sums["s", layer] = plain_sums(parts_s)
        parts_t = [dot_tn(rows(kept["normed_t"]), rows(back_qkv)).astype(BF)] + parts_o
        if grid.direct:
            sums["t", layer] = sum_rows(grid, 4 + layer, parts_t)[1]
        else:
            sums["t", layer] = plain_sums(parts_t)
        qkv_sum = row_total(back_qkv)
        entry_t_part = jnp.stack([qkv_sum[:split], qkv_sum[2 * split :]])
        back_own = dot_nt(rows(back_qkv[:frames_here]), w["triple_t"])
        back_oth = dot_nt(rows(back_qkv[frames_here:]), w["triple_t"]).astype(BF)
        back_normed = cube(back_own + grid.over_t(back_oth).astype(F32))
        back_state, gain_t, shift_t = norm_backward(
            back_normed, kept["unit_t"], kept["scale_t"], gain[0]
        )
        upstream = upstream + back_state
        late_whole = jnp.concatenate([gain_t, shift_t, merge_bias_part, mixing_bias_part])
        late_half = entry_t_part.reshape(-1)
        if layer > 0:
            whole_early.append(late_whole)
            half_early.append(late_half)
        else:
            early = add_up(whole_early, half_early)
            late = add_up([late_whole], [late_half])

    input_grad = spread_out(upstream.astype(BF)).astype(F32)
    for layer in range(LAYERS):
        shards[layer] = [
            *sums["t", layer],
            *sums["s", layer],
            *sums["m", layer],
        ]
    size_s = 6 * width + 128
    tail_t = 4 * width
    size_h = 2 * split + hid
    gains, shifts, biases, square_sums, entries, hiddens = [], [], [], [], [], []
    start = 0
    tails = []
    wholes = []
    for layer in range(LAYERS - 1, -1, -1):
        wholes.insert(0, early[start : start + size_s])
        start += size_s
        if layer > 0:
            tails.insert(0, early[start : start + tail_t])
            start += tail_t
    tails.insert(0, late[:tail_t])
    half_parts, half_tails = [], []
    for layer in range(LAYERS - 1, -1, -1):
        half_parts.insert(0, early[start : start + size_h])
        start += size_h
        if layer > 0:
            half_tails.insert(0, early[start : start + 2 * split])
            start += 2 * split
    half_tails.insert(0, late[tail_t:])
    for layer in range(LAYERS):
        six = wholes[layer][: 6 * width].reshape(6, width)
        four = tails[layer].reshape(4, width)
        gains.append(jnp.stack([four[0], six[0], six[1]]))
        shifts.append(jnp.stack([four[1], six[2], six[3]]))
        biases.append(jnp.stack([four[2], four[3], six[4], six[5]]))
        square_sums.append(wholes[layer][6 * width : 6 * width + 4])
        entries.append(
            jnp.stack(
                [
                    half_tails[layer].reshape(2, split),
                    half_parts[layer][: 2 * split].reshape(2, split),
                ]
            )
        )
        hiddens.append(half_parts[layer][2 * split :])
    gain_sum, shift_sum, bias_sum = jnp.stack(gains), jnp.stack(shifts), jnp.stack(biases)
    square_sum, entry_sum, hidden_sum = (
        jnp.stack(square_sums),
        jnp.stack(entries),
        jnp.stack(hiddens),
    )
    tokens = FRAMES * width * jnp.sum(valid_places).astype(F32)
    root_squares = jnp.sqrt(square_sum / tokens)

    def unpack_rows(item):
        return jnp.concatenate([item[:half_rows], item[half_rows:]], axis=-1)

    def triple_shape(item):
        return item.reshape(step_rows, 3, split)

    return (
        block_output,
        input_grad,
        gain_sum,
        shift_sum,
        jnp.stack([jnp.stack([triple_shape(s[0]), triple_shape(s[3])]) for s in shards]),
        entry_sum,
        jnp.stack([jnp.stack([s[1].T, s[4].T]) for s in shards]),
        bias_sum,
        jnp.stack([unpack_rows(s[2]) for s in shards]),
        jnp.stack([s[5] for s in shards]),
        hidden_sum,
        jnp.stack([s[6].T for s in shards]),
        root_squares,
    )


def solution(mesh):
    return jax.shard_map(
        per_device,
        mesh=mesh,
        in_specs=(
            P("shard", "ctx", "tp", None),
            P("shard", "ctx", "tp", None),
            P("shard"),
            P(),
            P(),
            P(),
            P(None, None, ("shard", "ctx"), None, "tp"),
            P(None, None, None, "tp"),
            P(None, None, "tp", ("shard", "ctx")),
            P(),
            P(None, ("shard", "ctx", "tp"), None),
            P(None, ("shard", "ctx"), "tp"),
            P(None, "tp"),
            P(None, "tp", ("shard", "ctx")),
        ),
        out_specs=(
            P("shard", "ctx", "tp", None),
            P("shard", "ctx", "tp", None),
            P(),
            P(),
            P(None, None, ("shard", "ctx"), None, "tp"),
            P(None, None, None, "tp"),
            P(None, None, "tp", ("shard", "ctx")),
            P(),
            P(None, ("shard", "ctx", "tp"), None),
            P(None, ("shard", "ctx"), "tp"),
            P(None, "tp"),
            P(None, "tp", ("shard", "ctx")),
            P(),
        ),
        check_vma=False,
    )
```

```python
import functools

import jax
import jax.numpy as jnp
from jax import lax
from jax.experimental import pallas as pl
from jax.experimental.pallas import tpu as pltpu
from jax.sharding import PartitionSpec as P

HEAD_DIM = 64
FRAMES = 8
LAYERS = 2
AXES = ("shard", "ctx", "tp")
BF = jnp.bfloat16
F32 = jnp.float32

far_below = -1000000000.0
epsilon = 1e-06
root_half = 0.7071067811865476
gauss_scale = 0.3989422804014327


def dot_nn(left, right):
    return lax.dot_general(left, right, (((1,), (0,)), ((), ())), preferred_element_type=F32)


def dot_nt(left, right):
    return lax.dot_general(left, right, (((1,), (1,)), ((), ())), preferred_element_type=F32)


def dot_tn(left, right):
    return lax.dot_general(left, right, (((0,), (0,)), ((), ())), preferred_element_type=F32)


def rows(value):
    return value.reshape(-1, value.shape[-1])


def row_total(value):
    return jnp.sum(rows(value).astype(F32), axis=0)


def lane_masks(shape):
    lane = lax.broadcasted_iota(jnp.int32, shape, 1)
    return lane < HEAD_DIM


def softmax_rows(scores):
    top = jnp.max(scores, axis=-1, keepdims=True)
    raised = jnp.exp(scores - top)
    total = jnp.sum(raised, axis=-1, keepdims=True)
    return raised * (1.0 / total)


def sides(value, first):
    zero = jnp.zeros_like(value)
    return [jnp.where(first, value, zero), jnp.where(first, zero, value)]


def heads_forward(qkv, fix, scale, put):
    first = lane_masks(qkv(0, 0).shape)
    scores = []
    for pair in range(3):
        k = qkv(1, pair)
        scores.append([dot_nt(q, k) for q in sides(qkv(0, pair), first)])
    shares = [[softmax_rows(fix(item * scale)).astype(BF) for item in both] for both in scores]
    for pair in range(3):
        v = qkv(2, pair)
        outs = [dot_nn(item, v) for item in shares[pair]]
        put(pair, jnp.where(first, outs[0], outs[1]).astype(BF))


def heads_backward(qkv, back, fix, scale, put):
    first = lane_masks(qkv(0, 0).shape)
    scores, backs = [], []
    for pair in range(3):
        k, v = qkv(1, pair), qkv(2, pair)
        scores.append([dot_nt(q, k) for q in sides(qkv(0, pair), first)])
        backs.append([dot_nt(b, v) for b in sides(back(pair), first)])
    low_shares, low_scores = [], []
    for pair in range(3):
        low_shares.append([])
        low_scores.append([])
        for side in range(2):
            shares = softmax_rows(fix(scores[pair][side] * scale))
            back_shares = backs[pair][side]
            inner = jnp.sum(back_shares * shares, axis=-1, keepdims=True)
            low_scores[pair].append((shares * (back_shares - inner)).astype(BF))
            low_shares[pair].append(shares.astype(BF))
    for pair in range(3):
        q, k, bm = qkv(0, pair), qkv(1, pair), back(pair)
        gq = [dot_nn(item, k) for item in low_scores[pair]]
        gk = [dot_tn(item, q) for item in low_scores[pair]]
        gv = [dot_tn(item, bm) for item in low_shares[pair]]
        put(0, pair, (jnp.where(first, gq[0], gq[1]) * scale).astype(BF))
        put(1, pair, (jnp.where(first, gk[0], gk[1]) * scale).astype(BF))
        put(2, pair, jnp.where(first, gv[0], gv[1]).astype(BF))


def column(part, pair):
    start = part * 384 + pair * 128
    return slice(start, start + 128)


def spatial_fix(count_ref, padded, places):
    col = lax.broadcasted_iota(jnp.int32, (padded, padded), 1)
    floor = jnp.where(col < places, far_below, 3.0 * far_below)
    allowed = col < jnp.minimum(count_ref[0], places)
    return lambda scores: jnp.where(allowed, scores, floor)


def spatial_fwd_body(places, scale, count_ref, own_ref, oth_ref, own_out, oth_out):
    fix = spatial_fix(count_ref, own_ref.shape[1], places)
    for src, dst in ((own_ref, own_out), (oth_ref, oth_out)):

        def put(pair, value, dst=dst):
            dst[0, :, pair * 128 : pair * 128 + 128] = value

        heads_forward(lambda part, pair, src=src: src[0, :, column(part, pair)], fix, scale, put)


def spatial_bwd_body(
    places, scale, count_ref, own_ref, oth_ref, bown_ref, both_ref, own_out, oth_out
):
    fix = spatial_fix(count_ref, own_ref.shape[1], places)
    for src, back, dst in ((own_ref, bown_ref, own_out), (oth_ref, both_ref, oth_out)):

        def put(part, pair, value, dst=dst):
            dst[0, :, column(part, pair)] = value

        heads_backward(
            lambda part, pair, src=src: src[0, :, column(part, pair)],
            lambda pair, back=back: back[0, :, pair * 128 : pair * 128 + 128],
            fix,
            scale,
            put,
        )


def temporal_fix(tile):
    size = FRAMES * tile
    row = lax.broadcasted_iota(jnp.int32, (size, size), 0)
    col = lax.broadcasted_iota(jnp.int32, (size, size), 1)
    same = (row & (tile - 1)) == (col & (tile - 1))
    return lambda scores: jnp.where(same, scores, 3.0 * far_below)


def temporal_fwd_body(scale, src, dst):
    tile = src.shape[1]
    fix = temporal_fix(tile)

    def put(pair, value):
        dst[:, :, pair * 128 : pair * 128 + 128] = value.reshape(FRAMES, tile, 128)

    heads_forward(
        lambda part, pair: src[:, :, column(part, pair)].reshape(FRAMES * tile, 128),
        fix,
        scale,
        put,
    )


def temporal_bwd_body(scale, src, back, dst):
    tile = src.shape[1]
    fix = temporal_fix(tile)

    def put(part, pair, value):
        dst[:, :, column(part, pair)] = value.reshape(FRAMES, tile, 128)

    heads_backward(
        lambda part, pair: src[:, :, column(part, pair)].reshape(FRAMES * tile, 128),
        lambda pair: back[:, :, pair * 128 : pair * 128 + 128].reshape(FRAMES * tile, 128),
        fix,
        scale,
        put,
    )


def spatial_call(count, ins, widths, places, scale, backward):
    frames, padded, _ = ins[0].shape
    spec = lambda width: pl.BlockSpec((1, padded, width), lambda f: (f, 0, 0))
    body = spatial_bwd_body if backward else spatial_fwd_body
    work = frames * 12 * padded * 256 * 128 * 2 * (5 if backward else 2)
    return pl.pallas_call(
        functools.partial(body, places, scale),
        grid=(frames,),
        in_specs=[pl.BlockSpec(memory_space=pltpu.SMEM)] + [spec(x.shape[-1]) for x in ins],
        out_specs=[spec(width) for width in widths],
        out_shape=[jax.ShapeDtypeStruct((frames, padded, width), BF) for width in widths],
        cost_estimate=pl.CostEstimate(
            flops=work * 4, bytes_accessed=8 * frames * padded * 2304, transcendentals=0
        ),
        name="spatial_back" if backward else "spatial_mix",
    )(count, *ins)


def temporal_call(ins, width, scale, backward):
    frames, padded, _ = ins[0].shape
    tile = 16
    spec = lambda lanes: pl.BlockSpec((frames, tile, lanes), lambda i: (0, i, 0))
    body = temporal_bwd_body if backward else temporal_fwd_body
    work = padded // tile * 6 * 128 * 128 * 128 * 2 * (5 if backward else 2)
    return pl.pallas_call(
        functools.partial(body, scale),
        grid=(padded // tile,),
        in_specs=[spec(x.shape[-1]) for x in ins],
        out_specs=spec(width),
        out_shape=jax.ShapeDtypeStruct((frames, padded, width), BF),
        cost_estimate=pl.CostEstimate(
            flops=work * 8, bytes_accessed=4 * frames * padded * 1152, transcendentals=0
        ),
        name="temporal_back" if backward else "temporal_mix",
    )(*ins)


class Grid:
    def __init__(self):
        self.shards = lax.axis_size("shard")
        self.depth = self.shards // 2
        shard = lax.axis_index("shard")
        self.z = shard // 2
        self.x = shard % 2
        self.y = lax.axis_index("ctx")
        self.t = lax.axis_index("tp")
        self.direct = self.depth == 4

    def perm(self, move):
        pairs = []
        for z in range(self.depth):
            for x in range(2):
                for y in range(2):
                    for t in range(2):
                        tz, tx, ty, tt = move(z, x, y, t)
                        pairs.append(
                            (((z * 2 + x) * 2 + y) * 2 + t, ((tz * 2 + tx) * 2 + ty) * 2 + tt)
                        )
        return pairs

    def send(self, value, pairs):
        return lax.ppermute(value, AXES, pairs)

    def over_x(self, value):
        return self.send(value, self.perm(lambda z, x, y, t: (z, 1 - x, y, t)))

    def over_y(self, value):
        return self.send(value, self.perm(lambda z, x, y, t: (z, x, 1 - y, t)))

    def over_t(self, value):
        return self.send(value, self.perm(lambda z, x, y, t: (z, x, y, 1 - t)))

    def over_z(self, value, step):
        depth = self.depth
        return self.send(value, self.perm(lambda z, x, y, t: ((z + step) % depth, x, y, t)))

    def over_bit(self, value, bit):
        pairs = []
        for s in range(self.shards):
            for y in range(2):
                for t in range(2):
                    pairs.append(((s * 2 + y) * 2 + t, ((s ^ bit) * 2 + y) * 2 + t))
        return self.send(value, pairs)

    def total(self, value, across):
        if across:
            value = value + self.over_t(value)
        value = value + self.over_y(value)
        bit = 1
        while bit < self.shards:
            value = value + self.over_bit(value, bit)
            bit *= 2
        return value


def place_body(widths, step_rows, half, at_ref, own, xn, yn, da, db, *outs):
    back = pl.program_id(0)
    x, y = at_ref[1], at_ref[2]

    def put(dx, dy, piece):
        bx = x if dx == 0 else 1 - x
        by = y if dy == 0 else 1 - y
        row = pl.multiple_of((bx * 2 + by) * step_rows, 16)
        start = 0
        for number, width in enumerate(widths):
            outs[number][pl.ds(row, step_rows), :] = piece[0, :, start : start + width]
            start += width

    put(0, 0, own)
    put(1, 0, xn)
    put(0, 1, yn)

    @pl.when(back < half)
    def _():
        put(1, 1, da)

    @pl.when(back >= half)
    def _():
        put(1, 1, db)


def tie(value, *others):
    return lax.optimization_barrier((value, *others))[0]


class Feed:
    def __init__(self, grid, items, widths, *behind):
        self.grid, self.widths = grid, widths
        block = tie(jnp.concatenate(items, axis=1), *behind)
        if grid.direct:
            self.blocks = [block] + [grid.over_z(block, k) for k in range(1, grid.depth)]
        else:
            self.blocks = [block]

    def near(self, *behind):
        grid = self.grid
        if grid.direct:
            self.own = tie(jnp.stack(self.blocks), *behind)
            self.xn = grid.over_x(self.own)
            self.yn = grid.over_y(self.own)
        return self

    def far(self, *behind):
        grid = self.grid
        if grid.direct:
            half = grid.depth // 2
            xn, yn = tie(self.xn[:half], *behind), tie(self.yn[half:], *behind)
            self.last = (grid.over_y(xn), grid.over_x(yn))
        return self

    def done(self):
        grid = self.grid
        if not grid.direct:
            full = lax.all_gather(self.blocks[0], ("shard", "ctx"), axis=0, tiled=True)
            return split_columns(full, self.widths)
        at = jnp.stack([grid.z, grid.x, grid.y]).astype(jnp.int32)
        return place_rows(grid, at, self.own, self.xn, self.yn, *self.last, self.widths)

    def near_parts(self):
        return (self.xn, self.yn) if self.grid.direct else ()

    def far_parts(self):
        return self.last if self.grid.direct else ()


def place_rows(grid, at, own, xn, yn, da, db, widths):
    depth, step_rows, lanes = own.shape
    half = depth // 2
    piece = lambda index: pl.BlockSpec((1, step_rows, lanes), index)
    straight = piece(lambda k, at_ref: (k, 0, 0))
    return pl.pallas_call(
        functools.partial(place_body, tuple(widths), step_rows, half),
        grid_spec=pltpu.PrefetchScalarGridSpec(
            num_scalar_prefetch=1,
            grid=(depth,),
            in_specs=[
                straight,
                straight,
                straight,
                piece(lambda k, at_ref: (jnp.minimum(k, half - 1), 0, 0)),
                piece(lambda k, at_ref: (jnp.maximum(k - half, 0), 0, 0)),
            ],
            out_specs=[
                pl.BlockSpec(
                    (4 * step_rows, width),
                    lambda k, at_ref: (lax.rem(at_ref[0] - k + depth, depth), 0),
                )
                for width in widths
            ],
        ),
        out_shape=[
            jax.ShapeDtypeStruct((depth * 4 * step_rows, width), own.dtype) for width in widths
        ],
        cost_estimate=pl.CostEstimate(
            flops=0, bytes_accessed=depth * 4 * step_rows * lanes * 4, transcendentals=0
        ),
        compiler_params=pltpu.CompilerParams(vmem_limit_bytes=48 << 20),
        name="place_rows",
    )(at, own, xn, yn, da, db)


class Sums:
    def __init__(self, place, part, own, ra, rb, sx, sy, rx, ry, low, gz, send, recv):
        self.place, self.part, self.own = place, part, own
        self.ra, self.rb, self.sx, self.sy = ra, rb, sx, sy
        self.rx, self.ry, self.low, self.gz = rx, ry, low, gz
        self.send, self.recv = send, recv
        self.depth = part.shape[0]
        self.half = part.shape[0] // 2

    def copy(self, number, src, dst, target):
        return remote(src, dst, self.send.at[number], self.recv.at[number], target)

    def far(self):
        x, y = self.place.x, self.place.y
        low, high = pl.ds(0, self.half), pl.ds(self.half, self.half)
        return [
            self.copy(0, self.part.at[low, 1 - x, 1 - y], self.ra, self.place.over_y()),
            self.copy(1, self.part.at[high, 1 - x, 1 - y], self.rb, self.place.over_x()),
        ]

    def near(self):
        return [
            self.copy(2, self.sx, self.rx, self.place.over_x()),
            self.copy(3, self.sy, self.ry, self.place.over_y()),
        ]

    def deep(self):
        return [
            self.copy(
                3 + k,
                self.low.at[lax.rem(self.place.z + k, self.depth)],
                self.gz.at[k - 1],
                self.place.over_z(k),
            )
            for k in range(1, self.depth)
        ]

    def first(self):
        for item in self.far():
            item.start()

    def second(self):
        x, y, half = self.place.x, self.place.y, self.half
        for item in self.far():
            item.wait()
        for k in range(2 * half):
            toward_x, toward_y = self.part[k, 1 - x, y], self.part[k, x, 1 - y]
            if k < half:
                toward_x = (toward_x.astype(F32) + self.ra[k].astype(F32)).astype(BF)
            else:
                toward_y = (toward_y.astype(F32) + self.rb[k - half].astype(F32)).astype(BF)
            self.sx[k] = toward_x
            self.sy[k] = toward_y
        for item in self.near():
            item.start()

    def kept(self, k):
        mine = self.part[k, self.place.x, self.place.y].astype(F32)
        return mine + self.rx[k].astype(F32) + self.ry[k].astype(F32)

    def third(self):
        for item in self.near():
            item.wait()
        for k in range(self.depth):
            self.low[k] = self.kept(k).astype(BF)
        for item in self.deep():
            item.start()

    def last(self):
        for item in self.deep():
            item.wait()
        total = self.kept(self.place.z)
        for k in range(self.depth - 1):
            total = total + self.gz[k].astype(F32)
        self.own[...] = total


def remote(src, dst, send, recv, target):
    return pltpu.make_async_remote_copy(
        src_ref=src,
        dst_ref=dst,
        send_sem=send,
        recv_sem=recv,
        device_id=target,
        device_id_type=pl.DeviceIdType.MESH,
    )


class Place:
    def __init__(self, depth):
        self.depth = depth
        shard = lax.axis_index("shard")
        self.z = shard // 2
        self.x = lax.rem(shard, 2)
        self.y = lax.axis_index("ctx")
        self.t = lax.axis_index("tp")

    def over_x(self):
        return {"shard": self.z * 2 + 1 - self.x}

    def over_y(self):
        return {"ctx": 1 - self.y}

    def over_t(self):
        return {"tp": 1 - self.t}

    def over_z(self, step):
        return {"shard": lax.rem(self.z + step, self.depth) * 2 + self.x}

    def meet(self, chips, cores):
        barrier = pltpu.get_barrier_semaphore()
        targets = [self.over_t()] if cores else []
        if chips:
            targets += [self.over_x(), self.over_y()]
            targets += [self.over_z(k) for k in range(1, self.depth)]
        for target in targets:
            pl.semaphore_signal(
                barrier, inc=1, device_id=target, device_id_type=pl.DeviceIdType.MESH
            )
        pl.semaphore_wait(barrier, len(targets))


class Carrier:
    def __init__(self, place, cores, parts, owns, scratch):
        self.place, self.cores = place, cores
        self.sums = [
            Sums(place, part, own, *scratch[10 * i : 10 * i + 10])
            for i, (part, own) in enumerate(zip(parts, owns))
        ]

    def step(self, number):
        lead, rest = self.sums[:1], self.sums[1:]
        if number == 0:
            self.place.meet(bool(self.sums), self.cores)
            for item in lead + rest:
                item.first()
        elif number == 1:
            for item in lead:
                item.second()
        elif number == 2:
            for item in lead:
                item.third()
            for item in rest:
                item.second()
        elif number == 3:
            for item in rest:
                item.third()
        else:
            for item in lead + rest:
                item.last()


def carried(grid, parts):
    depth = grid.depth
    cubes, shapes, scratch = [], [], []
    for part in parts:
        step_rows, lanes = part.shape[0] // (depth * 4), part.shape[1]
        block = lambda count: pltpu.VMEM((count, step_rows, lanes), BF)
        cubes.append(part.reshape(depth, 2, 2, step_rows, lanes))
        shapes.append(jax.ShapeDtypeStruct((step_rows, lanes), F32))
        scratch += [block(depth // 2)] * 2 + [block(depth)] * 5 + [block(depth - 1)]
        scratch += [pltpu.SemaphoreType.DMA((3 + depth,))] * 2
    return cubes, shapes, scratch


def stage_params(number, vmem=58):
    return pltpu.CompilerParams(
        collective_id=number, has_side_effects=True, vmem_limit_bytes=vmem << 20
    )


def stage_cost(flops):
    return pl.CostEstimate(flops=flops, bytes_accessed=30000000, transcendentals=0)


VMEM_SPEC = pl.BlockSpec(memory_space=pltpu.VMEM)
SMEM_SPEC = pl.BlockSpec(memory_space=pltpu.SMEM)


def splitter(refs):
    refs = list(refs)
    return lambda count: [refs.pop(0) for _ in range(count)]


def tail_body(depth, count, *refs):
    take = splitter(refs)
    parts, owns, scratch = take(count), take(count), take(10 * count)
    carrier = Carrier(Place(depth), False, parts, owns, scratch)
    for number in range(5):
        carrier.step(number)


def tail_sums(grid, number, parts):
    cubes, shapes, scratch = carried(grid, parts)
    return pl.pallas_call(
        functools.partial(tail_body, grid.depth, len(parts)),
        in_specs=[VMEM_SPEC] * len(parts),
        out_specs=[VMEM_SPEC] * len(parts),
        out_shape=shapes,
        scratch_shapes=scratch,
        compiler_params=stage_params(number),
        cost_estimate=stage_cost(20000000000),
        name="sum_rows",
    )(*cubes)


def norm_back_rows(e, unit, scale, gain):
    along = e * gain
    lanes = e.shape[-1]
    mean_along = jnp.sum(along, axis=-1, keepdims=True) * (1.0 / lanes)
    mean_unit = jnp.sum(along * unit, axis=-1, keepdims=True) * (1.0 / lanes)
    return scale * (along - mean_along - unit * mean_unit)


def column_sum(value):
    return jnp.sum(value, axis=0, keepdims=True)


def feed_back_body(depth, count, steps, *refs):
    take = splitter(refs)
    state, normed, unit, scale, gain = take(5)
    oth, own = take(4), take(4)
    parts = take(count)
    out, sums, g_up, g_down, h_own, h_oth = take(6)
    owns = take(count)
    r, rt, nt, bh, s_up, s_down, r_up, r_down, send, recv = take(10)
    place = Place(depth)
    carrier = Carrier(place, True, parts, owns, take(10 * count))
    frames, padded, width = state.shape
    rows_all = frames * padded
    i = pl.program_id(0)

    @pl.when(i == 0)
    def _():
        carrier.step(0)
        sums[...] = jnp.zeros_like(sums)

        def begin(f, carry):
            low = state[f].astype(BF)
            r[f] = low
            out[f] = jnp.zeros((padded, width), F32)
            return carry + column_sum(low.astype(F32))

        sums[0:1] = lax.fori_loop(0, frames, begin, jnp.zeros((1, width), F32))
        rt[...] = r[...].reshape(rows_all, width).T
        nt[...] = normed[...].reshape(rows_all, width).T

    def work(down, up, active, slope, h_sum):
        lanes = down.shape[1]

        def one(f, carry):
            value = (dot_nn(r[f], down[...]) * slope[f].astype(F32)).astype(BF)
            bh[f] = value
            out[f] += dot_nt(value, up[...])
            return carry + column_sum(value.astype(F32))

        h_sum[...] = lax.fori_loop(0, frames, one, jnp.zeros((1, lanes), F32))
        return (
            dot_nn(nt[...], bh[...].reshape(rows_all, lanes)),
            dot_nn(rt[...], active[...].reshape(rows_all, lanes)),
        )

    def swaps(j):
        return [
            remote(s_up.at[j], r_up.at[j], send.at[0, j], recv.at[0, j], place.over_t()),
            remote(s_down.at[j], r_down.at[j], send.at[1, j], recv.at[1, j], place.over_t()),
        ]

    @pl.when(i < steps)
    def _():
        up_part, down_part = work(*oth, h_oth)
        s_up[i] = up_part.astype(BF)
        s_down[i] = down_part.astype(BF)
        for item in swaps(i):
            item.start()

    for number, at in ((1, 1), (2, 3), (3, 4)):
        if count:

            @pl.when(i == at)
            def _(number=number):
                carrier.step(number)

    @pl.when(i >= steps)
    def _():
        j = i - steps
        up_part, down_part = work(*own, h_own)
        for item in swaps(j):
            item.wait()
        g_up[...] = (up_part + r_up[j].astype(F32)).astype(BF)
        g_down[...] = (down_part + r_down[j].astype(F32)).astype(BF)

    @pl.when(i == 2 * steps - 1)
    def _():
        def finish(f, carry):
            e, u = out[f], unit[f]
            out[f] = state[f] + norm_back_rows(e, u, scale[f], gain[...])
            return (carry[0] + column_sum(e * u), carry[1] + column_sum(e))

        zero = jnp.zeros((1, width), F32)
        sums[1:2], sums[2:3] = lax.fori_loop(0, frames, finish, (zero, zero))
        carrier.step(4)


def feed_back(grid, number, state, kept, gain, w, parts):
    frames, padded, width = state.shape
    hid = w["up"][0].shape[1]
    steps = 3
    lanes = hid // steps
    cubes, shapes, scratch = carried(grid, parts)
    whole = lambda item: pl.BlockSpec(
        item.shape, lambda i: (0,) * item.ndim, pipeline_mode=pl.Buffered(1)
    )
    first = lambda i: jnp.minimum(i, steps - 1)
    later = lambda i: jnp.maximum(i - steps, 0)

    def side(at):
        weight = pl.BlockSpec((width, lanes), lambda i: (0, at(i)))
        token = pl.BlockSpec((frames, padded, lanes), lambda i: (0, 0, at(i)))
        return [weight, weight, token, token]

    tokens = lambda item: item.reshape(frames, padded, hid)
    sides = [
        [w["down"][k], w["up"][k], tokens(kept["active"][k]), tokens(kept["slope"][k])]
        for k in (1, 0)
    ]
    fixed = [state, kept["normed_m"], kept["unit_m"], kept["scale_m"], gain]
    vec = lambda at: pl.BlockSpec((1, lanes), lambda i: (0, at(i)))
    result = pl.pallas_call(
        functools.partial(feed_back_body, grid.depth, len(parts), steps),
        grid=(2 * steps,),
        in_specs=[whole(item) for item in fixed]
        + side(first)
        + side(later)
        + [whole(item) for item in cubes],
        out_specs=[
            pl.BlockSpec((frames, padded, width), lambda i: (0, 0, 0)),
            pl.BlockSpec((8, width), lambda i: (0, 0)),
            pl.BlockSpec((width, lanes), lambda i: (0, later(i))),
            pl.BlockSpec((width, lanes), lambda i: (0, later(i))),
            vec(later),
            vec(first),
        ]
        + [pl.BlockSpec(item.shape, lambda i: (0, 0)) for item in shapes],
        out_shape=[
            jax.ShapeDtypeStruct((frames, padded, width), F32),
            jax.ShapeDtypeStruct((8, width), F32),
            jax.ShapeDtypeStruct((width, hid), BF),
            jax.ShapeDtypeStruct((width, hid), BF),
            jax.ShapeDtypeStruct((1, hid), F32),
            jax.ShapeDtypeStruct((1, hid), F32),
        ]
        + shapes,
        scratch_shapes=[
            pltpu.VMEM((frames, padded, width), BF),
            pltpu.VMEM((width, frames * padded), BF),
            pltpu.VMEM((width, frames * padded), BF),
            pltpu.VMEM((frames, padded, lanes), BF),
        ]
        + [pltpu.VMEM((steps, width, lanes), BF)] * 4
        + [pltpu.SemaphoreType.DMA((2, steps))] * 2
        + scratch,
        compiler_params=stage_params(number),
        cost_estimate=stage_cost(24000000000),
        name="feed_back",
    )(*fixed, *sides[0], *sides[1], *cubes)
    return result[0], result[1], result[2:4], (result[4], result[5]), result[6:]


def spatial_back_body(depth, count, places, att_scale, *refs):
    take = splitter(refs)
    (count_ref, state, merge0, merge1, mixed0, mixed1, qkv0, qkv1) = take(8)
    tri0, tri1, normed, unit, scale, gain = take(6)
    parts = take(count)
    out, sums, q_sums, g_tri, g_merge = take(5)
    owns = take(count)
    r, bm0, bm1, b0, b1, rt, nt, s_tri, r_tri, s_merge, r_merge, send, recv = take(13)
    place = Place(depth)
    carrier = Carrier(place, True, parts, owns, take(10 * count))
    frames, padded, width = state.shape
    rows_all = frames * padded
    split = merge0.shape[1]
    fix = spatial_fix(count_ref, padded, places)
    carrier.step(0)

    def one(f, carry):
        low = state[f].astype(BF)
        r[f] = low
        for merge, bm, src, dst in ((merge0, bm0, qkv0, b0), (merge1, bm1, qkv1, b1)):
            bm[...] = dot_nn(low, merge[...]).astype(BF)

            def put(part, pair, value, dst=dst):
                dst[f, :, column(part, pair)] = value

            heads_backward(
                lambda part, pair, src=src: src[f, :, column(part, pair)],
                lambda pair, bm=bm: bm[:, pair * 128 : pair * 128 + 128],
                fix,
                att_scale,
                put,
            )
        return carry + column_sum(low.astype(F32))

    sums[...] = jnp.zeros_like(sums)
    q_sums[...] = jnp.zeros_like(q_sums)
    half = frames // 2
    total = lax.fori_loop(0, half, one, jnp.zeros((1, width), F32))
    carrier.step(1)
    sums[0:1] = lax.fori_loop(half, frames, one, total)
    carrier.step(2)
    rt[...] = r[...].reshape(rows_all, width).T
    nt[...] = normed[...].reshape(rows_all, width).T
    flat = lambda ref, part: ref[:, :, part * split : (part + 1) * split].reshape(rows_all, split)
    swap_tri = remote(s_tri, r_tri, send.at[0], recv.at[0], place.over_t())
    swap_merge = remote(s_merge, r_merge, send.at[1], recv.at[1], place.over_t())
    s_merge[...] = dot_nn(rt[...], mixed1[...]).astype(BF)
    swap_merge.start()
    for part in range(3):
        cols = slice(part * split, (part + 1) * split)
        s_tri[:, cols] = dot_nn(nt[...], flat(b1, part)).astype(BF)
    swap_tri.start()
    carrier.step(3)

    def finish(f, carry):
        e = dot_nt(b0[f], tri0[...]) + dot_nt(b1[f], tri1[...])
        u = unit[f]
        out[f] = state[f] + norm_back_rows(e, u, scale[f], gain[...])
        return (
            carry[0] + column_sum(e * u),
            carry[1] + column_sum(e),
            carry[2] + column_sum(b0[f].astype(F32)),
            carry[3] + column_sum(b1[f].astype(F32)),
        )

    zero, wide = jnp.zeros((1, width), F32), jnp.zeros((1, 3 * split), F32)
    sums[1:2], sums[2:3], q_sums[0:1], q_sums[1:2] = lax.fori_loop(
        0, frames, finish, (zero, zero, wide, wide)
    )
    swap_merge.wait()
    g_merge[...] = (dot_nn(rt[...], mixed0[...]) + r_merge[...].astype(F32)).astype(BF)
    swap_tri.wait()
    for part in range(3):
        cols = slice(part * split, (part + 1) * split)
        mine = dot_nn(nt[...], flat(b0, part))
        g_tri[:, cols] = (mine + r_tri[:, cols].astype(F32)).astype(BF)
    carrier.step(4)


def spatial_back(grid, number, count_ref, state, kept, gain, w, parts, places, att_scale):
    frames, padded, width = state.shape
    split = w["merge_s"][0].shape[1]
    cubes, shapes, scratch = carried(grid, parts)
    flat = [item.reshape(frames * padded, split) for item in kept["mixed_s"]]
    fixed = [count_ref, state, *w["merge_s"], *flat, *kept["qkv_s"], *w["triple_s"]]
    fixed += [kept["normed_s"], kept["unit_s"], kept["scale_s"], gain]
    result = pl.pallas_call(
        functools.partial(spatial_back_body, grid.depth, len(parts), places, att_scale),
        in_specs=[SMEM_SPEC] + [VMEM_SPEC] * (len(fixed) - 1 + len(parts)),
        out_specs=[VMEM_SPEC] * (5 + len(parts)),
        out_shape=[
            jax.ShapeDtypeStruct((frames, padded, width), F32),
            jax.ShapeDtypeStruct((8, width), F32),
            jax.ShapeDtypeStruct((8, 3 * split), F32),
            jax.ShapeDtypeStruct((width, 3 * split), BF),
            jax.ShapeDtypeStruct((width, split), BF),
        ]
        + shapes,
        scratch_shapes=[pltpu.VMEM((frames, padded, width), BF)]
        + [pltpu.VMEM((padded, split), BF)] * 2
        + [pltpu.VMEM((frames, padded, 3 * split), BF)] * 2
        + [pltpu.VMEM((width, frames * padded), BF)] * 2
        + [pltpu.VMEM((width, 3 * split), BF)] * 2
        + [pltpu.VMEM((width, split), BF)] * 2
        + [pltpu.SemaphoreType.DMA((2,))] * 2
        + scratch,
        compiler_params=stage_params(number),
        cost_estimate=stage_cost(24000000000),
        name="spatial_stage",
    )(*fixed, *cubes)
    return result[0], result[1], result[2], result[3:5], result[5:]


def temporal_back_body(depth, count, att_scale, *refs):
    take = splitter(refs)
    state, mixing, joined, merge0, merge1, mine, swap, qkv, tri = take(9)
    normed, unit, scale, gain = take(4)
    parts = take(count)
    out, sums, q_sums, g_tri, g_merge, g_mix = take(6)
    owns = take(count)
    r, bj, away, bm, b, nt, rt, s_merge, r_merge, s_back, r_back, send, recv = take(13)
    place = Place(depth)
    carrier = Carrier(place, True, parts, owns, take(10 * count))
    frames, padded, width = state.shape
    rows_all = frames * padded
    split = merge0.shape[1]
    carrier.step(0)

    def begin(f, carry):
        low = state[f].astype(BF)
        r[f] = low
        value = dot_nt(low, mixing[...]).astype(BF)
        bj[f] = value
        bm[f] = dot_nn(value, merge0[...]).astype(BF)
        away[f] = dot_nn(value, merge1[...]).astype(BF)
        return (carry[0] + column_sum(low.astype(F32)), carry[1] + column_sum(value.astype(F32)))

    sums[...] = jnp.zeros_like(sums)
    q_sums[...] = jnp.zeros_like(q_sums)
    zero = jnp.zeros((1, width), F32)
    sums[0:1], sums[1:2] = lax.fori_loop(0, frames, begin, (zero, zero))
    swap_bm = remote(
        away, bm.at[pl.ds(frames, frames)], send.at[0], recv.at[0], place.over_t()
    )
    swap_bm.start()
    rt[...] = bj[...].reshape(rows_all, width).T
    s_merge[...] = dot_nn(rt[...], swap[...]).astype(BF)
    swap_merge = remote(s_merge, r_merge, send.at[1], recv.at[1], place.over_t())
    swap_merge.start()
    carrier.step(1)
    rt[...] = joined[...].T
    for half in range(2):
        cols = slice(half * split, (half + 1) * split)
        g_mix[:, cols] = dot_nn(rt[...], r[:, :, cols].reshape(rows_all, split))
    rt[...] = bj[...].reshape(rows_all, width).T
    swap_merge.wait()
    g_merge[...] = (dot_nn(rt[...], mine[...]) + r_merge[...].astype(F32)).astype(BF)
    swap_bm.wait()
    tile = 16
    fix = temporal_fix(tile)

    def one(i, carry):
        at = pl.ds(pl.multiple_of(i * tile, tile), tile)

        def put(part, pair, value):
            b[:, at, column(part, pair)] = value.reshape(FRAMES, tile, 128)

        heads_backward(
            lambda part, pair: qkv[:, at, column(part, pair)].reshape(FRAMES * tile, 128),
            lambda pair: bm[:, at, pair * 128 : pair * 128 + 128].reshape(FRAMES * tile, 128),
            fix,
            att_scale,
            put,
        )
        return carry

    tiles = padded // tile
    lax.fori_loop(0, tiles // 2, one, 0)
    carrier.step(2)
    lax.fori_loop(tiles // 2, tiles, one, 0)
    carrier.step(3)

    def toward(f, carry):
        s_back[f] = dot_nt(b[f + frames], tri[...]).astype(BF)
        return carry

    lax.fori_loop(0, frames, toward, 0)
    swap_back = remote(s_back, r_back, send.at[2], recv.at[2], place.over_t())
    swap_back.start()
    nt[...] = normed[...].T
    for part in range(3):
        cols = slice(part * split, (part + 1) * split)
        g_tri[:, cols] = dot_nn(
            nt[...], b[:, :, cols].reshape(2 * rows_all, split)
        ).astype(BF)
    swap_back.wait()

    def finish(f, carry):
        e = dot_nt(b[f], tri[...]) + r_back[f].astype(F32)
        u = unit[f]
        out[f] = state[f] + norm_back_rows(e, u, scale[f], gain[...])
        both = column_sum(b[f].astype(F32)) + column_sum(b[f + frames].astype(F32))
        return (carry[0] + column_sum(e * u), carry[1] + column_sum(e), carry[2] + both)

    sums[2:3], sums[3:4], q_sums[0:1] = lax.fori_loop(
        0, frames, finish, (zero, zero, jnp.zeros((1, 3 * split), F32))
    )
    carrier.step(4)


def temporal_back(grid, number, state, kept, gain, w, parts, att_scale):
    frames, padded, width = state.shape
    split = w["merge_t"][0].shape[1]
    cubes, shapes, scratch = carried(grid, parts)
    flat = [item.reshape(frames * padded, split) for item in kept["mixed_t"]]
    fixed = [state, w["mixing"], kept["joined"], *w["merge_t"], *flat, kept["qkv_t"]]
    fixed += [w["triple_t"], rows(kept["normed_t"]), kept["unit_t"], kept["scale_t"], gain]
    result = pl.pallas_call(
        functools.partial(temporal_back_body, grid.depth, len(parts), att_scale),
        in_specs=[VMEM_SPEC] * (len(fixed) + len(parts)),
        out_specs=[VMEM_SPEC] * (6 + len(parts)),
        out_shape=[
            jax.ShapeDtypeStruct((frames, padded, width), F32),
            jax.ShapeDtypeStruct((8, width), F32),
            jax.ShapeDtypeStruct((8, 3 * split), F32),
            jax.ShapeDtypeStruct((width, 3 * split), BF),
            jax.ShapeDtypeStruct((width, split), BF),
            jax.ShapeDtypeStruct((width, width), F32),
        ]
        + shapes,
        scratch_shapes=[pltpu.VMEM((frames, padded, width), BF)] * 2
        + [pltpu.VMEM((frames, padded, split), BF)]
        + [pltpu.VMEM((2 * frames, padded, split), BF)]
        + [pltpu.VMEM((2 * frames, padded, 3 * split), BF)]
        + [pltpu.VMEM((width, 2 * frames * padded), BF)]
        + [pltpu.VMEM((width, frames * padded), BF)]
        + [pltpu.VMEM((width, split), BF)] * 2
        + [pltpu.VMEM((frames, padded, width), BF)] * 2
        + [pltpu.SemaphoreType.DMA((3,))] * 2
        + scratch,
        compiler_params=stage_params(number),
        cost_estimate=stage_cost(24000000000),
        name="temporal_stage",
    )(*fixed, *cubes)
    return result[0], result[1], result[2], result[3:6], result[6:]


def plain_sums(parts):
    return [
        lax.psum_scatter(part.astype(F32), ("shard", "ctx"), scatter_dimension=0, tiled=True)
        for part in parts
    ]


def split_columns(value, widths):
    outs, start = [], 0
    for width in widths:
        outs.append(value[..., start : start + width])
        start += width
    return outs


def norm_forward(state, gain, shift):
    center = state - jnp.mean(state, axis=-1, keepdims=True)
    scale = lax.rsqrt(jnp.mean(center * center, axis=-1, keepdims=True) + epsilon)
    unit = center * scale
    return ((unit * gain + shift).astype(BF), unit, scale)


def norm_backward(incoming, unit, scale, gain):
    along = incoming * gain
    back = scale * (
        along
        - jnp.mean(along, axis=-1, keepdims=True)
        - unit * jnp.mean(along * unit, axis=-1, keepdims=True)
    )
    return (back, row_total(incoming * unit), row_total(incoming))


def per_device(
    video_clips,
    cotangent,
    slot_clip,
    valid_places,
    norm_gain,
    norm_bias,
    triple_weight,
    entry_bias,
    merge_weight,
    branch_bias,
    mixing_weight,
    up_weight,
    up_bias,
    down_weight,
):
    grid = Grid()
    slots, frames_here, places_here, width = video_clips.shape
    places = places_here * 2
    padded = -(-places // 16) * 16
    scale = HEAD_DIM ** (-0.5)
    step_rows = triple_weight.shape[2]
    half_rows = step_rows // 2
    own_first = grid.t == 0
    straight = grid.t == grid.y

    clip_ids = jnp.arange(valid_places.shape[0], dtype=jnp.int32)
    my_clip = lax.dynamic_index_in_dim(slot_clip, grid.y, 0, keepdims=False)
    count = jnp.sum(jnp.where(my_clip == clip_ids, valid_places, 0)).astype(jnp.int32)
    valid_here = (jnp.arange(padded, dtype=jnp.int32) < count).astype(F32)[None, :, None]
    count_ref = count.reshape(1)

    def spread_in(value):
        mine = lax.dynamic_index_in_dim(value, grid.y, 0, keepdims=False)
        theirs = lax.dynamic_index_in_dim(value, 1 - grid.y, 0, keepdims=False)
        got = grid.over_y(theirs)
        keep = jnp.where(straight, mine, got)
        send = jnp.where(straight, got, mine)
        swap = grid.over_t(send)
        low = jnp.where(own_first, keep, swap)
        high = jnp.where(own_first, swap, keep)
        gap = jnp.zeros((frames_here, padded - places, width), value.dtype)
        return jnp.concatenate([low, high, gap], axis=1)

    def spread_out(value):
        low = value[:, :places_here]
        high = value[:, places_here:places]
        keep = jnp.where(own_first, low, high)
        send = jnp.where(own_first, high, low)
        swap = grid.over_t(send)
        mine = jnp.where(straight, keep, swap)
        away = jnp.where(straight, swap, keep)
        got = grid.over_y(away)
        first = jnp.where(grid.y == 0, mine, got)
        second = jnp.where(grid.y == 0, got, mine)
        return jnp.stack([first, second])

    def pack_mix(item):
        return jnp.concatenate([item[..., : width // 2], item[..., width // 2 :]], axis=-2)

    def block_triple(layer, part):
        return [triple_weight[layer, part, :, i] for i in range(3)]

    def block_out(layer):
        return [merge_weight[layer, 0].T, pack_mix(mixing_weight[layer])]

    def block_s(layer):
        return block_triple(layer, 1) + [merge_weight[layer, 1].T]

    def block_m(layer):
        return [up_weight[layer], down_weight[layer].T]

    split = triple_weight.shape[-1]
    hid = up_weight.shape[-1]
    wide_t = (3 * split, split, width // 2)
    wide_s = (3 * split, split)
    wide_m = (hid, hid)

    def unpack_mix(item):
        cube = item.reshape(-1, 2, half_rows, width // 2)
        return jnp.concatenate([cube[:, 0], cube[:, 1]], axis=-1)

    def with_other(item):
        return (item, grid.over_t(item))

    def out_weights(merge_t, mix):
        mix_own, mix_oth = [unpack_mix(item) for item in with_other(mix)]
        mixing = jnp.stack(
            [jnp.where(own_first, mix_own, mix_oth), jnp.where(own_first, mix_oth, mix_own)],
            axis=1,
        ).reshape(width, width)
        return dict(merge_t=with_other(merge_t), mixing=mixing)

    small = jnp.concatenate([entry_bias[:, 1].reshape(-1), up_bias.reshape(-1)])
    small_oth = grid.over_t(small)
    entry_count = LAYERS * 2 * split
    entry_s = (
        small[:entry_count].reshape(LAYERS, 2, split),
        small_oth[:entry_count].reshape(LAYERS, 2, split),
    )
    up_bias2 = (
        small[entry_count:].reshape(LAYERS, hid),
        small_oth[entry_count:].reshape(LAYERS, hid),
    )

    def triple_bias(pair):
        return jnp.concatenate([pair[0], jnp.zeros((split,), F32), pair[1]])

    def cube(value):
        return value.reshape(-1, padded, value.shape[-1])

    gathered = [dict() for _ in range(LAYERS)]
    feed1 = Feed(grid, block_triple(0, 0), wide_t[:1]).near().far()
    gathered[0]["triple_t"] = feed1.done()[0]
    feed2 = Feed(grid, block_out(0) + block_s(0), wide_t[1:] + wide_s, *feed1.near_parts())
    state = spread_in(video_clips).astype(F32)

    def corner(value):
        return value[(slice(0, 1),) * (value.ndim - 2) + (slice(0, 8), slice(0, 128))]
    stored = []
    squares = []
    for layer in range(LAYERS):
        w = gathered[layer]
        gain, shift, bias = norm_gain[layer], norm_bias[layer], branch_bias[layer]
        normed, unit_t, scale_t = norm_forward(state, gain[0], shift[0])
        normed_t = jnp.concatenate([normed, grid.over_t(normed)], axis=0)
        qkv_t = cube(
            (dot_nn(rows(normed_t), w["triple_t"]) + triple_bias(entry_bias[layer, 0])).astype(BF)
        )
        if layer == 0:
            feed2.near(*feed1.far_parts(), corner(normed_t)).far(corner(qkv_t))
            merge_t, mix, triple_s, merge_s = feed2.done()
            w.update(out_weights(merge_t, mix))
            w.update(triple_s=with_other(triple_s), merge_s=with_other(merge_s))
            feed3 = Feed(grid, block_m(0), wide_m, corner(qkv_t))
        mixed = temporal_call([qkv_t], split, scale, False)
        if layer == 0:
            feed3.near(*feed2.far_parts(), corner(mixed))
        elif layer == 1:
            feed5.far(corner(mixed))
            triple_s, merge_s, upward, downward = feed5.done()
            w.update(triple_s=with_other(triple_s), merge_s=with_other(merge_s))
            w.update(up=with_other(upward), down=with_other(downward))
        mine = mixed[:frames_here]
        swap = grid.over_t(mixed[frames_here:])
        joined = (
            dot_nt(rows(mine), w["merge_t"][0]) + dot_nt(rows(swap), w["merge_t"][1]) + bias[0]
        ).astype(BF)
        temporal = cube(dot_nn(joined, w["mixing"]) + bias[1])
        state = state + temporal
        normed_s, unit_s, scale_s = norm_forward(state, gain[1], shift[1])
        qkv_s = [
            cube(
                (
                    dot_nn(rows(normed_s), w["triple_s"][i]) + triple_bias(entry_s[i][layer])
                ).astype(BF)
            )
            for i in range(2)
        ]
        if layer == 0:
            upward, downward = feed3.far(corner(qkv_s[0])).done()
            w.update(up=with_other(upward), down=with_other(downward))
            feed4 = Feed(grid, block_triple(1, 0) + block_out(1), wide_t, corner(joined))
        mixed_s = spatial_call(count_ref, qkv_s, (split, split), places, scale, False)
        if layer == 0:
            feed4.near(*feed3.far_parts(), corner(mixed_s[0]))
            feed5 = Feed(grid, block_s(1) + block_m(1), wide_s + wide_m, corner(mixed_s[0]))
            late_cotangent = tie(cotangent, corner(mixed_s[0]))
            upstream = spread_in(late_cotangent.astype(BF)).astype(F32) * valid_here
        spatial = cube(
            dot_nt(rows(mixed_s[0]), w["merge_s"][0])
            + dot_nt(rows(mixed_s[1]), w["merge_s"][1])
            + bias[2]
        )
        state = state + spatial
        normed_m, unit_m, scale_m = norm_forward(state, gain[2], shift[2])
        active, slope = [], []
        for i in range(2):
            hidden = dot_nn(rows(normed_m), w["up"][i]) + up_bias2[i][layer]
            below = 0.5 * (1.0 + lax.erf(hidden * root_half))
            active.append((hidden * below).astype(BF))
            slope.append(
                (below + hidden * gauss_scale * jnp.exp(-0.5 * hidden * hidden)).astype(BF)
            )
        if layer == 0:
            triple_t, merge_t, mix = feed4.far(corner(active[0])).done()
            gathered[1].update(triple_t=triple_t, **out_weights(merge_t, mix))
            feed5.near(*feed4.far_parts(), corner(active[1]))
        dense = cube(
            dot_nt(active[0], w["down"][0]) + dot_nt(active[1], w["down"][1]) + bias[3]
        )
        state = state + dense
        squares.append(
            jnp.stack(
                [
                    jnp.sum(jnp.square(item) * valid_here)
                    for item in (temporal, spatial, dense, state)
                ]
            )
        )
        stored.append(
            dict(
                unit_t=unit_t,
                scale_t=scale_t,
                normed_t=normed_t,
                qkv_t=qkv_t,
                mixed_t=(mine, swap),
                joined=joined,
                unit_s=unit_s,
                scale_s=scale_s,
                normed_s=normed_s,
                qkv_s=qkv_s,
                mixed_s=mixed_s,
                unit_m=unit_m,
                scale_m=scale_m,
                normed_m=normed_m,
                active=active,
                slope=slope,
            )
        )
    block_output = spread_out(state.astype(BF))

    shards = [None] * LAYERS
    whole_early, half_early = [], []
    sums = {}

    def add_up(wholes, halves):
        whole = jnp.concatenate(wholes)
        whole = whole + grid.over_t(whole)
        return grid.total(jnp.concatenate([whole] + halves), False)

    waiting = None

    def carry_sums(name, parts):
        nonlocal waiting
        if not grid.direct:
            sums[name] = plain_sums(parts)
            return
        waiting = (name, parts)

    def carried_parts():
        return waiting[1] if waiting else []

    def arrived_sums(result):
        nonlocal waiting
        if waiting:
            sums[waiting[0]] = list(result)
        waiting = None

    for layer in range(LAYERS - 1, -1, -1):
        w, kept = gathered[layer], stored[layer]
        gain = [norm_gain[layer, part : part + 1] for part in range(3)]
        upstream, vec_m, parts_m, hidden_part, got = feed_back(
            grid, layer, upstream, kept, gain[2], w, carried_parts()
        )
        arrived_sums(got)
        carry_sums(("m", layer), parts_m)
        upstream, vec_s, q_sums, parts_s, got = spatial_back(
            grid, 2 + layer, count_ref, upstream, kept, gain[1], w, carried_parts(), places, scale
        )
        arrived_sums(got)
        carry_sums(("s", layer), parts_s)
        entry_of = lambda row: jnp.stack([row[:split], row[2 * split :]]).reshape(-1)
        theirs = jnp.concatenate([entry_of(q_sums[1]), hidden_part[1][0]])
        mine = jnp.concatenate([entry_of(q_sums[0]), hidden_part[0][0]])
        half_early.append(mine + grid.over_t(theirs))
        whole_early.append(
            jnp.concatenate(
                [vec_s[1], vec_m[1], vec_s[2], vec_m[2], vec_s[0], vec_m[0]]
                + [squares[layer], jnp.zeros((124,), F32)]
            )
        )
        upstream, vec_t, q_sums, parts_t, got = temporal_back(
            grid, 4 + layer, upstream, kept, gain[0], w, carried_parts(), scale
        )
        arrived_sums(got)
        mix_part = parts_t[2].reshape(-1, 2, half_rows, width)
        mix_mine = lax.dynamic_index_in_dim(mix_part, grid.t, 1, keepdims=False)
        mix_theirs = lax.dynamic_index_in_dim(mix_part, 1 - grid.t, 1, keepdims=False)
        mix_got = grid.over_t(mix_theirs.astype(BF)).astype(F32)
        mix_sum = pack_mix((mix_mine + mix_got).astype(BF)).reshape(width, width // 2)
        carry_sums(("t", layer), [parts_t[0], parts_t[1], mix_sum])
        late_whole = jnp.concatenate([vec_t[2], vec_t[3], vec_t[1], vec_t[0]])
        late_half = entry_of(q_sums[0])
        if layer > 0:
            whole_early.append(late_whole)
            half_early.append(late_half)
        else:
            early = add_up(whole_early, half_early)
            late = add_up([late_whole], [late_half])

    if waiting:
        arrived_sums(tail_sums(grid, 6, carried_parts()))
    input_grad = spread_out(upstream.astype(BF)).astype(F32)
    for layer in range(LAYERS):
        shards[layer] = [
            *sums["t", layer],
            *sums["s", layer],
            *sums["m", layer],
        ]
    size_s = 6 * width + 128
    tail_t = 4 * width
    size_h = 2 * split + hid
    gains, shifts, biases, square_sums, entries, hiddens = [], [], [], [], [], []
    start = 0
    tails = []
    wholes = []
    for layer in range(LAYERS - 1, -1, -1):
        wholes.insert(0, early[start : start + size_s])
        start += size_s
        if layer > 0:
            tails.insert(0, early[start : start + tail_t])
            start += tail_t
    tails.insert(0, late[:tail_t])
    half_parts, half_tails = [], []
    for layer in range(LAYERS - 1, -1, -1):
        half_parts.insert(0, early[start : start + size_h])
        start += size_h
        if layer > 0:
            half_tails.insert(0, early[start : start + 2 * split])
            start += 2 * split
    half_tails.insert(0, late[tail_t:])
    for layer in range(LAYERS):
        six = wholes[layer][: 6 * width].reshape(6, width)
        four = tails[layer].reshape(4, width)
        gains.append(jnp.stack([four[0], six[0], six[1]]))
        shifts.append(jnp.stack([four[1], six[2], six[3]]))
        biases.append(jnp.stack([four[2], four[3], six[4], six[5]]))
        square_sums.append(wholes[layer][6 * width : 6 * width + 4])
        entries.append(
            jnp.stack(
                [
                    half_tails[layer].reshape(2, split),
                    half_parts[layer][: 2 * split].reshape(2, split),
                ]
            )
        )
        hiddens.append(half_parts[layer][2 * split :])
    gain_sum, shift_sum, bias_sum = jnp.stack(gains), jnp.stack(shifts), jnp.stack(biases)
    square_sum, entry_sum, hidden_sum = (
        jnp.stack(square_sums),
        jnp.stack(entries),
        jnp.stack(hiddens),
    )
    tokens = FRAMES * width * jnp.sum(valid_places).astype(F32)
    root_squares = jnp.sqrt(square_sum / tokens)

    def unpack_rows(item):
        return jnp.concatenate([item[:half_rows], item[half_rows:]], axis=-1)

    def triple_shape(item):
        return item.reshape(step_rows, 3, split)

    return (
        block_output,
        input_grad,
        gain_sum,
        shift_sum,
        jnp.stack([jnp.stack([triple_shape(s[0]), triple_shape(s[3])]) for s in shards]),
        entry_sum,
        jnp.stack([jnp.stack([s[1].T, s[4].T]) for s in shards]),
        bias_sum,
        jnp.stack([unpack_rows(s[2]) for s in shards]),
        jnp.stack([s[5] for s in shards]),
        hidden_sum,
        jnp.stack([s[6].T for s in shards]),
        root_squares,
    )


def solution(mesh):
    return jax.shard_map(
        per_device,
        mesh=mesh,
        in_specs=(
            P("shard", "ctx", "tp", None),
            P("shard", "ctx", "tp", None),
            P("shard"),
            P(),
            P(),
            P(),
            P(None, None, ("shard", "ctx"), None, "tp"),
            P(None, None, None, "tp"),
            P(None, None, "tp", ("shard", "ctx")),
            P(),
            P(None, ("shard", "ctx", "tp"), None),
            P(None, ("shard", "ctx"), "tp"),
            P(None, "tp"),
            P(None, "tp", ("shard", "ctx")),
        ),
        out_specs=(
            P("shard", "ctx", "tp", None),
            P("shard", "ctx", "tp", None),
            P(),
            P(),
            P(None, None, ("shard", "ctx"), None, "tp"),
            P(None, None, None, "tp"),
            P(None, None, "tp", ("shard", "ctx")),
            P(),
            P(None, ("shard", "ctx", "tp"), None),
            P(None, ("shard", "ctx"), "tp"),
            P(None, "tp"),
            P(None, "tp", ("shard", "ctx")),
            P(),
        ),
        check_vma=False,
    )
```

```python
import functools
import math

import jax
import jax.numpy as jnp
from jax import lax
from jax.experimental import pallas as pl
from jax.experimental.pallas import tpu as pltpu
from jax.sharding import PartitionSpec as P

HEAD_DIM = 64
FRAMES = 8
LAYERS = 2
AXES = ("shard", "ctx", "tp")
BF = jnp.bfloat16
F32 = jnp.float32

far_below = -1000000000.0
epsilon = 1e-06
root_half = 0.7071067811865476
gauss_scale = 0.3989422804014327


def dot_nn(left, right):
    return lax.dot_general(left, right, (((1,), (0,)), ((), ())), preferred_element_type=F32)


def dot_nt(left, right):
    return lax.dot_general(left, right, (((1,), (1,)), ((), ())), preferred_element_type=F32)


def dot_tn(left, right):
    return lax.dot_general(left, right, (((0,), (0,)), ((), ())), preferred_element_type=F32)


def rows(value):
    return value.reshape(-1, value.shape[-1])


def row_total(value):
    return jnp.sum(rows(value).astype(F32), axis=0)


def lane_masks(shape):
    lane = lax.broadcasted_iota(jnp.int32, shape, 1)
    return lane < HEAD_DIM


def softmax_rows(scores):
    top = jnp.max(scores, axis=-1, keepdims=True)
    raised = jnp.exp(scores - top)
    total = jnp.sum(raised, axis=-1, keepdims=True)
    return raised * (1.0 / total)


def sides(value, first):
    zero = jnp.zeros_like(value)
    return [jnp.where(first, value, zero), jnp.where(first, zero, value)]


def heads_forward(qkv, fix, scale, put):
    first = lane_masks(qkv(0, 0).shape)
    scores = []
    for pair in range(3):
        k = qkv(1, pair)
        scores.append([dot_nt(q, k) for q in sides(qkv(0, pair), first)])
    shares = [[softmax_rows(fix(item * scale)).astype(BF) for item in both] for both in scores]
    for pair in range(3):
        v = qkv(2, pair)
        outs = [dot_nn(item, v) for item in shares[pair]]
        put(pair, jnp.where(first, outs[0], outs[1]).astype(BF))


def heads_backward(qkv, back, fix, scale, put):
    first = lane_masks(qkv(0, 0).shape)
    scores, backs = [], []
    for pair in range(3):
        k, v = qkv(1, pair), qkv(2, pair)
        scores.append([dot_nt(q, k) for q in sides(qkv(0, pair), first)])
        backs.append([dot_nt(b, v) for b in sides(back(pair), first)])
    low_shares, low_scores = [], []
    for pair in range(3):
        low_shares.append([])
        low_scores.append([])
        for side in range(2):
            shares = softmax_rows(fix(scores[pair][side] * scale))
            back_shares = backs[pair][side]
            inner = jnp.sum(back_shares * shares, axis=-1, keepdims=True)
            low_scores[pair].append((shares * (back_shares - inner)).astype(BF))
            low_shares[pair].append(shares.astype(BF))
    for pair in range(3):
        q, k, bm = qkv(0, pair), qkv(1, pair), back(pair)
        gq = [dot_nn(item, k) for item in low_scores[pair]]
        gk = [dot_tn(item, q) for item in low_scores[pair]]
        gv = [dot_tn(item, bm) for item in low_shares[pair]]
        put(0, pair, (jnp.where(first, gq[0], gq[1]) * scale).astype(BF))
        put(1, pair, (jnp.where(first, gk[0], gk[1]) * scale).astype(BF))
        put(2, pair, jnp.where(first, gv[0], gv[1]).astype(BF))


def column(part, pair):
    start = part * 384 + pair * 128
    return slice(start, start + 128)


def spatial_fix(count_ref, padded, places):
    col = lax.broadcasted_iota(jnp.int32, (padded, padded), 1)
    floor = jnp.where(col < places, far_below, 3.0 * far_below)
    allowed = col < jnp.minimum(count_ref[0], places)
    return lambda scores: jnp.where(allowed, scores, floor)


def temporal_fix(tile):
    size = FRAMES * tile
    row = lax.broadcasted_iota(jnp.int32, (size, size), 0)
    col = lax.broadcasted_iota(jnp.int32, (size, size), 1)
    same = (row & (tile - 1)) == (col & (tile - 1))
    return lambda scores: jnp.where(same, scores, 3.0 * far_below)


class Grid:
    def __init__(self):
        self.shards = lax.axis_size("shard")
        self.depth = self.shards // 2
        shard = lax.axis_index("shard")
        self.z = shard // 2
        self.x = shard % 2
        self.y = lax.axis_index("ctx")
        self.t = lax.axis_index("tp")
        self.direct = self.depth == 4

    def perm(self, move):
        pairs = []
        for z in range(self.depth):
            for x in range(2):
                for y in range(2):
                    for t in range(2):
                        tz, tx, ty, tt = move(z, x, y, t)
                        pairs.append(
                            (((z * 2 + x) * 2 + y) * 2 + t, ((tz * 2 + tx) * 2 + ty) * 2 + tt)
                        )
        return pairs

    def send(self, value, pairs):
        return lax.ppermute(value, AXES, pairs)

    def over_x(self, value):
        return self.send(value, self.perm(lambda z, x, y, t: (z, 1 - x, y, t)))

    def over_y(self, value):
        return self.send(value, self.perm(lambda z, x, y, t: (z, x, 1 - y, t)))

    def over_t(self, value):
        return self.send(value, self.perm(lambda z, x, y, t: (z, x, y, 1 - t)))

    def over_z(self, value, step):
        depth = self.depth
        return self.send(value, self.perm(lambda z, x, y, t: ((z + step) % depth, x, y, t)))

    def over_bit(self, value, bit):
        pairs = []
        for s in range(self.shards):
            for y in range(2):
                for t in range(2):
                    pairs.append(((s * 2 + y) * 2 + t, ((s ^ bit) * 2 + y) * 2 + t))
        return self.send(value, pairs)

    def total(self, value, across):
        if across:
            value = value + self.over_t(value)
        value = value + self.over_y(value)
        bit = 1
        while bit < self.shards:
            value = value + self.over_bit(value, bit)
            bit *= 2
        return value


class Sums:
    def __init__(self, place, source, part, own, ra, rb, sx, sy, rx, ry, low, gz, send, recv):
        self.place, self.source, self.part, self.own = place, source, part, own
        self.ra, self.rb, self.sx, self.sy = ra, rb, sx, sy
        self.rx, self.ry, self.low, self.gz = rx, ry, low, gz
        self.send, self.recv = send, recv
        self.depth = part.shape[0]
        self.half = part.shape[0] // 2

    def copy(self, number, src, dst, target):
        return remote(src, dst, self.send.at[number], self.recv.at[number], target)

    def far(self):
        x, y = self.place.x, self.place.y
        low, high = pl.ds(0, self.half), pl.ds(self.half, self.half)
        return [
            self.copy(0, self.source.at[low, 1 - x, 1 - y], self.ra, self.place.over_y()),
            self.copy(1, self.source.at[high, 1 - x, 1 - y], self.rb, self.place.over_x()),
        ]

    def near(self):
        return [
            self.copy(2, self.sx, self.rx, self.place.over_x()),
            self.copy(3, self.sy, self.ry, self.place.over_y()),
        ]

    def deep(self):
        return [
            self.copy(
                3 + k,
                self.low.at[lax.rem(self.place.z + k, self.depth)],
                self.gz.at[k - 1],
                self.place.over_z(k),
            )
            for k in range(1, self.depth)
        ]

    def first(self):
        for item in self.far():
            item.start()

    def second(self):
        x, y, half = self.place.x, self.place.y, self.half
        for item in self.far():
            item.wait()
        for k in range(2 * half):
            toward_x, toward_y = self.part[k, 1 - x, y], self.part[k, x, 1 - y]
            if k < half:
                toward_x = toward_x + self.ra[k]
            else:
                toward_y = toward_y + self.rb[k - half]
            self.sx[k] = toward_x
            self.sy[k] = toward_y
        for item in self.near():
            item.start()

    def kept(self, k):
        mine = self.part[k, self.place.x, self.place.y].astype(F32)
        return mine + self.rx[k].astype(F32) + self.ry[k].astype(F32)

    def third(self):
        for item in self.near():
            item.wait()
        for k in range(self.depth):
            mine = self.part[k, self.place.x, self.place.y]
            self.low[k] = mine + (self.rx[k] + self.ry[k])
        for item in self.deep():
            item.start()

    def last(self):
        for item in self.deep():
            item.wait()
        total = self.kept(self.place.z)
        for k in range(self.depth - 1):
            total = total + self.gz[k].astype(F32)
        self.own[...] = total


def remote(src, dst, send, recv, target):
    return pltpu.make_async_remote_copy(
        src_ref=src,
        dst_ref=dst,
        send_sem=send,
        recv_sem=recv,
        device_id=target,
        device_id_type=pl.DeviceIdType.MESH,
    )


class Place:
    def __init__(self, depth):
        self.depth = depth
        shard = lax.axis_index("shard")
        self.z = shard // 2
        self.x = lax.rem(shard, 2)
        self.y = lax.axis_index("ctx")
        self.t = lax.axis_index("tp")

    def over_x(self):
        return {"shard": self.z * 2 + 1 - self.x}

    def over_y(self):
        return {"ctx": 1 - self.y}

    def over_t(self):
        return {"tp": 1 - self.t}

    def over_z(self, step):
        return {"shard": lax.rem(self.z + step, self.depth) * 2 + self.x}

    def meet(self, chips, cores):
        barrier = pltpu.get_barrier_semaphore()
        targets = [self.over_t()] if cores else []
        if chips:
            targets += [self.over_x(), self.over_y()]
            targets += [self.over_z(k) for k in range(1, self.depth)]
        for target in targets:
            pl.semaphore_signal(
                barrier, inc=1, device_id=target, device_id_type=pl.DeviceIdType.MESH
            )
        pl.semaphore_wait(barrier, len(targets))


class Carrier:
    def __init__(self, place, cores, sources, parts, owns, scratch):
        self.place, self.cores = place, cores
        self.sums = [
            Sums(place, source, part, own, *scratch[10 * i : 10 * i + 10])
            for i, (source, part, own) in enumerate(zip(sources, parts, owns))
        ]

    def step(self, number):
        lead, rest = self.sums[:1], self.sums[1:]
        if number == 0:
            self.place.meet(bool(self.sums), self.cores)
            for item in lead + rest:
                item.first()
        elif number == 1:
            for item in lead:
                item.second()
        elif number == 2:
            for item in lead:
                item.third()
            for item in rest:
                item.second()
        elif number == 3:
            for item in rest:
                item.third()
        else:
            for item in lead + rest:
                item.last()


def carried(grid, parts):
    depth = grid.depth
    cubes, shapes, scratch = [], [], []
    for part in parts:
        step_rows, lanes = part.shape[0] // (depth * 4), part.shape[1]
        block = lambda count: pltpu.VMEM((count, step_rows, lanes), BF)
        cubes.append(part.reshape(depth, 2, 2, step_rows, lanes))
        shapes.append(jax.ShapeDtypeStruct((step_rows, lanes), F32))
        scratch += [block(depth // 2)] * 2 + [block(depth)] * 5 + [block(depth - 1)]
        scratch += [pltpu.SemaphoreType.DMA((3 + depth,))] * 2
    return cubes, shapes, scratch


def stage_params(number, vmem=58, sends=True):
    if not sends:
        return pltpu.CompilerParams(vmem_limit_bytes=vmem << 20)
    return pltpu.CompilerParams(
        collective_id=number, has_side_effects=True, vmem_limit_bytes=vmem << 20
    )


def stage_cost(flops):
    return pl.CostEstimate(flops=flops, bytes_accessed=30000000, transcendentals=0)


VMEM_SPEC = pl.BlockSpec(memory_space=pltpu.VMEM)
SMEM_SPEC = pl.BlockSpec(memory_space=pltpu.SMEM)


ANY_SPEC = pl.BlockSpec(memory_space=pl.ANY)


def is_big(item):
    return item.shape[-1] >= 128 and math.prod(item.shape) >= 65536


class Staging:
    def __init__(self, smem, ins, outs):
        self.smem = smem
        self.ins = [i >= smem and is_big(item) for i, item in enumerate(ins)]
        self.outs = [is_big(item) for item in outs]
        self.in_shapes = [item for item, big in zip(ins, self.ins) if big]
        self.out_shapes = [item for item, big in zip(outs, self.outs) if big]

    def in_specs(self):
        specs = [ANY_SPEC if big else VMEM_SPEC for big in self.ins]
        return [SMEM_SPEC] * self.smem + specs[self.smem :]

    def out_specs(self):
        return [ANY_SPEC if big else VMEM_SPEC for big in self.outs]

    def scratch(self):
        held = self.in_shapes + self.out_shapes
        blocks = [pltpu.VMEM(item.shape, item.dtype) for item in held]
        return blocks + [pltpu.SemaphoreType.DMA((len(held),))]

    def count(self):
        return len(self.in_shapes) + len(self.out_shapes) + 1

    def open(self, in_refs, out_refs, refs):
        refs = list(refs)
        sems = refs.pop()
        number = 0
        pairs = []
        for group, flags in ((in_refs, self.ins), (out_refs, self.outs)):
            view, moves = [], []
            for ref, big in zip(group, flags):
                if big:
                    moves.append((ref, refs[number], sems.at[number]))
                    ref = refs[number]
                    number += 1
                view.append(ref)
            pairs.append((view, moves))
        (self.in_view, self.in_moves), (self.out_view, self.out_moves) = pairs
        return self.in_view, self.out_view

    def fetch(self):
        copies = [pltpu.make_async_copy(src, dst, sem) for src, dst, sem in self.in_moves]
        for item in copies:
            item.start()
        for item in copies:
            item.wait()

    def flush(self):
        copies = [pltpu.make_async_copy(src, dst, sem) for dst, src, sem in self.out_moves]
        for item in copies:
            item.start()
        for item in copies:
            item.wait()


def row_of(ref, index):
    return ref.at[pl.ds(index, 1)]


def splitter(refs):
    refs = list(refs)
    return lambda count: [refs.pop(0) for _ in range(count)]


class Hops:
    def __init__(self, place, pieces, refs, total, held, came, send, recv):
        z = place.z
        targets = [place.over_t(), place.over_y(), place.over_x()]
        targets.append({"shard": (z + 1 - 2 * lax.rem(z, 2)) * 2 + place.x})
        targets.append({"shard": (z + 2 - 4 * (z // 2)) * 2 + place.x})
        self.pieces, self.refs = pieces, refs
        self.total, self.held, self.came = total, held, came
        self.copies = [
            remote(held.at[k], came.at[k], send.at[k], recv.at[k], target)
            for k, target in enumerate(targets)
        ]

    def begin(self):
        self.held[0] = jnp.zeros(self.held.shape[1:], F32)
        for ref, (start, count, row, lane) in zip(self.refs, self.pieces):
            lanes = ref.shape[1]
            self.held[0, row : row + count, lane : lane + lanes] = ref[start : start + count]
        self.copies[0].start()

    def hop(self, number):
        self.copies[number - 1].wait()
        value = self.held[number - 1] + self.came[number - 1]
        if number < len(self.copies):
            self.held[number] = value
            self.copies[number].start()
        else:
            self.total[...] = value


class Small:
    def __init__(self, width):
        self.arrays, self.pieces, self.rows, self.width = [], [], 0, width

    def add(self, array, start, count, lane=0, stay=False):
        self.arrays.append(array)
        self.pieces.append((start, count, self.rows, lane))
        if not stay:
            self.rows += count

    def shape(self):
        return jax.ShapeDtypeStruct((-(-self.rows // 8) * 8, self.width), F32)

    def plain(self):
        whole = jnp.zeros(self.shape().shape, F32)
        for array, (start, count, row, lane) in zip(self.arrays, self.pieces):
            whole = whole.at[row : row + count, lane : lane + array.shape[1]].set(
                array[start : start + count]
            )
        return lax.psum(whole, AXES)


def hop_scratch(small):
    block = pltpu.VMEM((5,) + small.shape().shape, F32)
    return [block, block] + [pltpu.SemaphoreType.DMA((5,))] * 2


def tail_body(depth, count, pieces, *refs):
    take = splitter(refs)
    parts, small, (away,) = take(count), take(len(pieces)), take(1)
    owns, (total, back) = take(count), take(2)
    hop_refs, (send, recv) = take(4), take(2)
    place = Place(depth)
    carrier = Carrier(place, True, parts, parts, owns, take(10 * count))
    hops = Hops(place, pieces, small, total, *hop_refs)
    across = remote(away, back, send.at[0], recv.at[0], place.over_y())
    carrier.step(0)
    hops.begin()
    for number in range(1, 5):
        hops.hop(number)
        if number < 4:
            carrier.step(number)
    across.start()
    hops.hop(5)
    carrier.step(4)
    across.wait()


def tail_sums(grid, number, parts, small, away):
    cubes, shapes, scratch = carried(grid, parts)
    count = len(small.arrays)
    result = pl.pallas_call(
        functools.partial(tail_body, grid.depth, len(parts), small.pieces),
        in_specs=[VMEM_SPEC] * (len(parts) + count + 1),
        out_specs=[VMEM_SPEC] * (len(parts) + 2),
        out_shape=shapes + [small.shape(), jax.ShapeDtypeStruct(away.shape, away.dtype)],
        scratch_shapes=hop_scratch(small) + [pltpu.SemaphoreType.DMA((1,))] * 2 + scratch,
        compiler_params=stage_params(number),
        cost_estimate=stage_cost(20000000000),
        name="sum_rows",
    )(*cubes, *small.arrays, away)
    return result[:-2], result[-2], result[-1]


def norm_back_rows(e, unit, scale, gain):
    along = e * gain
    lanes = e.shape[-1]
    mean_along = jnp.sum(along, axis=-1, keepdims=True) * (1.0 / lanes)
    mean_unit = jnp.sum(along * unit, axis=-1, keepdims=True) * (1.0 / lanes)
    return scale * (along - mean_along - unit * mean_unit)


def column_sum(value):
    return jnp.sum(value, axis=0, keepdims=True)


def tie(value, *others):
    return lax.optimization_barrier((value, *others))[0]


class Near:
    def __init__(self, place, line, whole, other, send, recv):
        self.place, self.line, self.whole, self.other = place, line, whole, other
        self.send, self.recv = send, recv
        self.depth = line.shape[0]

    def pair(self, number, src, dst, target):
        return remote(src, dst, self.send.at[number], self.recv.at[number], target)

    def at(self, ref, dx, dy, low=0, size=None):
        x = 1 - self.place.x if dx else self.place.x
        y = 1 - self.place.y if dy else self.place.y
        return ref.at[pl.ds(low, size or self.depth), x, y]

    def sides(self):
        dst = self.at(self.whole, 0, 0)
        return [
            self.pair(0, self.line, dst, self.place.over_x()),
            self.pair(1, self.line, dst, self.place.over_y()),
        ]

    def corners(self):
        half = self.depth // 2
        first = self.at(self.whole, 1, 0, 0, half)
        second = self.at(self.whole, 0, 1, half, half)
        return [
            self.pair(2, first, first, self.place.over_y()),
            self.pair(3, second, second, self.place.over_x()),
        ]

    def swap(self, number):
        if self.other is None:
            return []
        if number == 0:
            src, dst = self.line, self.at(self.other, 0, 0)
        else:
            dx, dy = number & 1, number >> 1
            src, dst = self.at(self.whole, dx, dy), self.at(self.other, dx, dy)
        return [self.pair(4 + number, src, dst, self.place.over_t())]

    def begin(self):
        for item in self.sides() + self.swap(0) + [self.keep()]:
            item.start()

    def keep(self):
        return pltpu.make_async_copy(self.line, self.at(self.whole, 0, 0), self.send.at[8])

    def middle(self):
        for item in self.sides():
            item.wait()
        for item in self.corners() + self.swap(1) + self.swap(2):
            item.start()

    def corner_in(self):
        for item in self.corners():
            item.wait()
        for item in self.swap(3):
            item.start()

    def end(self):
        for number in range(4):
            for item in self.swap(number):
                item.wait()
        self.keep().wait()


class Deep:
    def __init__(self, place, block, line, send, recv):
        self.place, self.block, self.line, self.send, self.recv = place, block, line, send, recv

    def copies(self):
        return [
            remote(
                self.block,
                self.line.at[self.place.z],
                self.send.at[k - 1],
                self.recv.at[k - 1],
                self.place.over_z(k),
            )
            for k in range(1, self.line.shape[0])
        ]

    def begin(self):
        for item in self.copies():
            item.start()
        self.line[self.place.z] = self.block[...]

    def end(self):
        for item in self.copies():
            item.wait()


class Load:
    def __init__(self, grid, near=(), swapped=(), deep=(), across=()):
        self.depth = grid.depth
        self.swapped = list(swapped)
        self.near_count, self.deep_count = len(near), len(deep)
        self.inputs = list(near) + list(deep) + list(across)
        self.across_count = len(across)
        self.shapes, self.scratch, self.specs = [], [], []
        for line, both in zip(near, swapped):
            depth, step_rows, lanes = line.shape
            shape = jax.ShapeDtypeStruct((depth, 2, 2, step_rows, lanes), BF)
            self.shapes += [shape] * (2 if both else 1)
            self.specs += [ANY_SPEC] * (2 if both else 1)
            self.scratch += [pltpu.SemaphoreType.DMA((9,)), pltpu.SemaphoreType.DMA((8,))]
        for block in deep:
            self.shapes.append(jax.ShapeDtypeStruct((self.depth,) + block.shape, BF))
            self.specs.append(VMEM_SPEC)
            self.scratch += [pltpu.SemaphoreType.DMA((self.depth - 1,))] * 2

        for item in across:
            self.shapes.append(jax.ShapeDtypeStruct(item.shape, item.dtype))
            self.specs.append(VMEM_SPEC)
            self.scratch += [pltpu.SemaphoreType.DMA((1,))] * 2

    def results(self, arrays):
        arrays = list(arrays)
        flat = lambda item: item.reshape(-1, item.shape[-1])
        near = []
        for both in self.swapped:
            own = flat(arrays.pop(0))
            near.append((own, flat(arrays.pop(0)) if both else None))
        return near, arrays


class Loader:
    def __init__(self, place, cores, load, ins, outs, sems):
        self.place, self.cores, self.load = place, cores, load
        ins, outs, sems = list(ins), list(outs), list(sems)
        self.near = []
        for both in load.swapped:
            whole = outs.pop(0)
            other = outs.pop(0) if both else None
            self.near.append(Near(place, ins.pop(0), whole, other, sems.pop(0), sems.pop(0)))
        self.deep = [
            Deep(place, ins.pop(0), outs.pop(0), sems.pop(0), sems.pop(0))
            for _ in range(load.deep_count)
        ]
        self.across = []
        for _ in range(load.across_count):
            send, recv = sems.pop(0), sems.pop(0)
            self.across.append(
                remote(ins.pop(0), outs.pop(0), send.at[0], recv.at[0], place.over_y())
            )

    def begin(self):
        chips = bool(self.near or self.deep or self.across)
        if chips or self.cores:
            self.place.meet(chips, self.cores or bool(self.near))
        for item in self.near + self.deep:
            item.begin()
        for item in self.across:
            item.start()

    def middle(self):
        for item in self.near:
            item.middle()

    def end(self):
        for item in self.near:
            item.corner_in()
        for item in self.near:
            item.end()
        for item in self.deep:
            item.end()
        for item in self.across:
            item.wait()


def open_kernel(load, staging, refs, scratch):
    take = splitter(refs)
    in_refs = take(len(staging.ins))
    load_ins = take(len(load.inputs))
    out_refs = take(len(staging.outs))
    load_outs = take(len(load.shapes))
    scratch_refs = take(scratch)
    in_refs, out_refs = staging.open(in_refs, out_refs, take(staging.count()))
    return in_refs, out_refs, scratch_refs, (load_ins, load_outs, take(len(load.scratch)))


def kernel_call(body, number, ins, shapes, scratch, load, name, smem=0, cores=False):
    staging = Staging(smem, ins, shapes)
    result = pl.pallas_call(
        functools.partial(body, staging),
        in_specs=staging.in_specs() + [VMEM_SPEC] * len(load.inputs),
        out_specs=staging.out_specs() + load.specs,
        out_shape=list(shapes) + load.shapes,
        scratch_shapes=list(scratch) + staging.scratch() + load.scratch,
        compiler_params=stage_params(number, sends=cores or bool(load.inputs)),
        cost_estimate=stage_cost(20000000000),
        name=name,
    )(*ins, *load.inputs)
    return result[: len(shapes)], load.results(result[len(shapes) :])


def first_body(count, depth, next_count, *refs):
    take = splitter(refs)
    blocks, next_blocks = take(count), take(next_count)
    swapped = [False] + [True] * (count - 1)
    wholes = [take(2) if both else take(1) + [None] for both in swapped]
    next_lines = take(next_count)
    lines = take(count)
    place = Place(depth)
    deep = [Deep(place, blocks[i], lines[i], *take(2)) for i in range(count)]
    near = [Near(place, lines[i], *wholes[i], *take(2)) for i in range(count)]
    after = [Deep(place, next_blocks[i], next_lines[i], *take(2)) for i in range(next_count)]
    place.meet(True, True)
    for item in deep:
        item.begin()
    for one, two in zip(deep, near):
        one.end()
        two.begin()
    for item in after:
        item.begin()
    for item in near:
        item.middle()
    for item in near:
        item.corner_in()
    for item in near:
        item.end()
    for item in after:
        item.end()


def first_gather(grid, number, blocks, next_blocks):
    depth = grid.depth
    whole = lambda item: jax.ShapeDtypeStruct((depth, 2, 2) + item.shape, BF)
    line = lambda item: (depth,) + item.shape
    shapes = [whole(blocks[0])]
    for item in blocks[1:]:
        shapes += [whole(item)] * 2
    shapes += [jax.ShapeDtypeStruct(line(item), BF) for item in next_blocks]
    sems = lambda size: [pltpu.SemaphoreType.DMA((size,))] * 2
    scratch = [pltpu.VMEM(line(item), BF) for item in blocks]
    for _ in blocks:
        scratch += sems(depth - 1)
    for _ in blocks:
        scratch += [pltpu.SemaphoreType.DMA((9,)), pltpu.SemaphoreType.DMA((8,))]
    for _ in next_blocks:
        scratch += sems(depth - 1)
    arrays = list(
        pl.pallas_call(
            functools.partial(first_body, len(blocks), depth, len(next_blocks)),
            in_specs=[VMEM_SPEC] * (len(blocks) + len(next_blocks)),
            out_specs=[ANY_SPEC] * (2 * len(blocks) - 1) + [VMEM_SPEC] * len(next_blocks),
            out_shape=shapes,
            scratch_shapes=scratch,
            compiler_params=stage_params(number),
            cost_estimate=stage_cost(20000000000),
            name="first_gather",
        )(*blocks, *next_blocks)
    )
    flat = lambda item: item.reshape(-1, item.shape[-1])
    near = [(flat(arrays.pop(0)), None)]
    for _ in blocks[1:]:
        near.append((flat(arrays.pop(0)), flat(arrays.pop(0))))
    return near, arrays


def norm_rows(state, gain, shift):
    lanes = state.shape[-1]
    center = state - jnp.sum(state, axis=-1, keepdims=True) * (1.0 / lanes)
    spread = jnp.sum(center * center, axis=-1, keepdims=True) * (1.0 / lanes)
    scale = lax.rsqrt(spread + epsilon)
    unit = center * scale
    return (unit * gain + shift).astype(BF), unit, scale


def square_sum(value, valid):
    return jnp.sum(jnp.sum(value * value, axis=-1, keepdims=True) * valid, axis=0, keepdims=True)


def temporal_body(load, att_scale, layer, staging, *refs):
    ins, outs, scratch, loads = open_kernel(load, staging, refs, 3)
    state, valid, gain, shift, tri, tri_bias, merge0, merge1, merge_bias, mixing, mix_bias = ins
    out, unit, scale, normed, qkv, mine, swap, joined, sq = outs
    away, send, recv = scratch
    gain, shift = row_of(gain, 3 * layer), row_of(shift, 3 * layer)
    tri_bias = row_of(tri_bias, layer)
    merge_bias, mix_bias = row_of(merge_bias, 4 * layer), row_of(mix_bias, 4 * layer + 1)
    place = Place(load.depth)
    loader = Loader(place, True, load, *loads)
    frames, padded, width = state.shape
    loader.begin()
    staging.fetch()

    def norm_one(f, carry):
        low, u, s = norm_rows(state[f], gain[...], shift[...])
        normed[f] = low
        unit[f] = u
        scale[f] = s
        return carry

    lax.fori_loop(0, frames, norm_one, 0)
    own = normed.at[pl.ds(0, frames)]
    swap_normed = remote(
        own, normed.at[pl.ds(frames, frames)], send.at[0], recv.at[0], place.over_t()
    )
    swap_normed.start()

    def project(f, carry):
        qkv[f] = (dot_nn(normed[f], tri[...]) + tri_bias[...]).astype(BF)
        return carry

    lax.fori_loop(0, frames, project, 0)
    swap_normed.wait()
    lax.fori_loop(frames, 2 * frames, project, 0)
    tile = 16
    fix = temporal_fix(tile)

    def one(i, carry):
        at = pl.ds(pl.multiple_of(i * tile, tile), tile)

        def put(pair, value):
            cols = slice(pair * 128, pair * 128 + 128)
            both = value.reshape(2 * frames, tile, 128)
            mine[:, at, cols] = both[:frames]
            away[:, at, cols] = both[frames:]

        heads_forward(
            lambda part, pair: qkv[:, at, column(part, pair)].reshape(2 * frames * tile, 128),
            fix,
            att_scale,
            put,
        )
        return carry

    lax.fori_loop(0, padded // tile, one, 0)
    swap_mixed = remote(away, swap, send.at[1], recv.at[1], place.over_t())
    swap_mixed.start()
    loader.middle()
    swap_mixed.wait()

    def finish(f, carry):
        low = (
            dot_nt(mine[f], merge0[...]) + dot_nt(swap[f], merge1[...]) + merge_bias[...]
        ).astype(BF)
        joined[f] = low
        branch = dot_nn(low, mixing[...]) + mix_bias[...]
        out[f] = state[f] + branch
        return carry + square_sum(branch, valid[...])

    total = lax.fori_loop(0, frames, finish, jnp.zeros((1, 1), F32))
    sq[...] = jnp.broadcast_to(total, sq.shape)
    staging.flush()
    loader.end()


def temporal_stage(number, layer, state, valid, gain, shift, w, biases, load, att_scale):
    frames, padded, width = state.shape
    split = w["merge_t"][0].shape[1]
    shape = lambda dims, kind=BF: jax.ShapeDtypeStruct(dims, kind)
    ins = [state, valid, gain, shift, w["triple_t"], biases[0], *w["merge_t"], biases[1]]
    ins += [w["mixing"], biases[2]]
    return kernel_call(
        functools.partial(temporal_body, load, att_scale, layer),
        number,
        ins,
        [
            shape((frames, padded, width), F32),
            shape((frames, padded, width), F32),
            shape((frames, padded, 1), F32),
            shape((2 * frames, padded, width)),
            shape((2 * frames, padded, 3 * split)),
            shape((frames, padded, split)),
            shape((frames, padded, split)),
            shape((frames, padded, width)),
            shape((8, 128), F32),
        ],
        [pltpu.VMEM((frames, padded, split), BF)] + [pltpu.SemaphoreType.DMA((2,))] * 2,
        load,
        "temporal_forward",
        cores=True,
    )


def spatial_body(load, places, att_scale, layer, staging, *refs):
    ins, outs, scratch, loads = open_kernel(load, staging, refs, 0)
    count_ref, state, valid, gain, shift, tri0, tri1, bias0, bias1, merge0, merge1, out_bias = ins
    out, unit, scale, normed, qkv0, qkv1, mixed0, mixed1, sq = outs
    gain, shift = row_of(gain, 3 * layer + 1), row_of(shift, 3 * layer + 1)
    bias0, bias1 = row_of(bias0, layer), row_of(bias1, layer)
    out_bias = row_of(out_bias, 4 * layer + 2)
    place = Place(load.depth)
    loader = Loader(place, False, load, *loads)
    frames, padded, width = state.shape
    fix = spatial_fix(count_ref, padded, places)
    loader.begin()
    staging.fetch()

    def one(f, carry):
        low, u, s = norm_rows(state[f], gain[...], shift[...])
        normed[f] = low
        unit[f] = u
        scale[f] = s
        for tri, bias, qkv, mixed in (
            (tri0, bias0, qkv0, mixed0),
            (tri1, bias1, qkv1, mixed1),
        ):
            qkv[f] = (dot_nn(low, tri[...]) + bias[...]).astype(BF)

            def put(pair, value, mixed=mixed):
                mixed[f, :, pair * 128 : pair * 128 + 128] = value

            heads_forward(
                lambda part, pair, qkv=qkv: qkv[f, :, column(part, pair)], fix, att_scale, put
            )
        branch = dot_nt(mixed0[f], merge0[...]) + dot_nt(mixed1[f], merge1[...]) + out_bias[...]
        out[f] = state[f] + branch
        return carry + square_sum(branch, valid[...])

    cut = frames - 1
    total = lax.fori_loop(0, cut, one, jnp.zeros((1, 1), F32))
    loader.middle()
    total = lax.fori_loop(cut, frames, one, total)
    sq[...] = jnp.broadcast_to(total, sq.shape)
    staging.flush()
    loader.end()


def spatial_stage(number, layer, count_ref, state, valid, gain, shift, w, biases, load, places, att_scale):
    frames, padded, width = state.shape
    split = w["merge_s"][0].shape[1]
    shape = lambda dims, kind=BF: jax.ShapeDtypeStruct(dims, kind)
    ins = [count_ref, state, valid, gain, shift, *w["triple_s"], biases[0], biases[1]]
    ins += [*w["merge_s"], biases[2]]
    return kernel_call(
        functools.partial(spatial_body, load, places, att_scale, layer),
        number,
        ins,
        [
            shape((frames, padded, width), F32),
            shape((frames, padded, width), F32),
            shape((frames, padded, 1), F32),
            shape((frames, padded, width)),
            shape((frames, padded, 3 * split)),
            shape((frames, padded, 3 * split)),
            shape((frames, padded, split)),
            shape((frames, padded, split)),
            shape((8, 128), F32),
        ],
        [],
        load,
        "spatial_forward",
        1,
    )


def feed_body(load, layer, staging, *refs):
    ins, outs, scratch, loads = open_kernel(load, staging, refs, 0)
    state, valid, gain, shift, up0, up1, bias0, bias1, down0, down1, out_bias = ins
    out, unit, scale, normed, act0, act1, slope0, slope1, sq = outs
    gain, shift = row_of(gain, 3 * layer + 2), row_of(shift, 3 * layer + 2)
    bias0, bias1 = row_of(bias0, layer), row_of(bias1, layer)
    out_bias = row_of(out_bias, 4 * layer + 3)
    place = Place(load.depth)
    loader = Loader(place, False, load, *loads)
    frames, padded, width = state.shape
    loader.begin()
    staging.fetch()

    def one(f, carry):
        low, u, s = norm_rows(state[f], gain[...], shift[...])
        normed[f] = low
        unit[f] = u
        scale[f] = s
        branch = jnp.broadcast_to(out_bias[...], (padded, width))
        for up, bias, down, act, slope in (
            (up0, bias0, down0, act0, slope0),
            (up1, bias1, down1, act1, slope1),
        ):
            lanes = up.shape[1]
            piece = lanes // 3
            for number in range(3):
                cols = slice(number * piece, (number + 1) * piece)
                hidden = dot_nn(low, up[:, cols]) + bias[:, cols]
                below = 0.5 * (1.0 + lax.erf(hidden * root_half))
                act[f, :, cols] = (hidden * below).astype(BF)
                slope[f, :, cols] = (
                    below + hidden * gauss_scale * jnp.exp(-0.5 * hidden * hidden)
                ).astype(BF)
            branch = branch + dot_nt(act[f], down[...])
        value = state[f] + branch
        out[f] = value
        return (
            carry[0] + square_sum(branch, valid[...]),
            carry[1] + square_sum(value, valid[...]),
        )

    zero = jnp.zeros((1, 1), F32)
    cut = frames - 1
    total = lax.fori_loop(0, cut, one, (zero, zero))
    loader.middle()
    total = lax.fori_loop(cut, frames, one, total)
    sq[...] = jnp.broadcast_to(total[0], sq.shape)
    sq[0:1] = jnp.broadcast_to(total[1], (1, sq.shape[1]))
    staging.flush()
    loader.end()


def feed_stage(number, layer, state, valid, gain, shift, w, biases, load):
    frames, padded, width = state.shape
    hid = w["up"][0].shape[1]
    shape = lambda dims, kind=BF: jax.ShapeDtypeStruct(dims, kind)
    ins = [state, valid, gain, shift, *w["up"], biases[0], biases[1], *w["down"], biases[2]]
    return kernel_call(
        functools.partial(feed_body, load, layer),
        number,
        ins,
        [
            shape((frames, padded, width), F32),
            shape((frames, padded, width), F32),
            shape((frames, padded, 1), F32),
            shape((frames, padded, width)),
        ]
        + [shape((frames, padded, hid))] * 4
        + [shape((8, 128), F32)],
        [],
        load,
        "feed_forward",
    )


def feed_back_body(depth, count, steps, layer, *refs):
    take = splitter(refs)
    state, normed, unit, scale, gain = take(5)
    gain = row_of(gain, 3 * layer + 2)
    oth, own = take(4), take(4)
    parts = take(count)
    out, sums, g_up, g_down, h_own, h_oth = take(6)
    owns = take(count)
    r, rt, nt, bh, s_up, s_down, r_up, r_down, send, recv = take(10)
    place = Place(depth)
    carrier = Carrier(place, True, parts, parts, owns, take(10 * count))
    frames, padded, width = state.shape
    rows_all = frames * padded
    i = pl.program_id(0)

    @pl.when(i == 0)
    def _():
        carrier.step(0)
        sums[...] = jnp.zeros_like(sums)

        def begin(f, carry):
            low = state[f].astype(BF)
            r[f] = low
            out[f] = jnp.zeros((padded, width), F32)
            return carry + column_sum(low.astype(F32))

        sums[2:3] = lax.fori_loop(0, frames, begin, jnp.zeros((1, width), F32))
        rt[...] = r[...].reshape(rows_all, width).T
        nt[...] = normed[...].reshape(rows_all, width).T

    def work(down, up, active, slope, h_sum):
        lanes = down.shape[1]

        def one(f, carry):
            value = (dot_nn(r[f], down[...]) * slope[f].astype(F32)).astype(BF)
            bh[f] = value
            out[f] += dot_nt(value, up[...])
            return carry + column_sum(value.astype(F32))

        h_sum[...] = lax.fori_loop(0, frames, one, jnp.zeros((1, lanes), F32))
        return (
            dot_nn(nt[...], bh[...].reshape(rows_all, lanes)),
            dot_nn(rt[...], active[...].reshape(rows_all, lanes)),
        )

    def swaps(j):
        return [
            remote(s_up.at[j], r_up.at[j], send.at[0, j], recv.at[0, j], place.over_t()),
            remote(s_down.at[j], r_down.at[j], send.at[1, j], recv.at[1, j], place.over_t()),
        ]

    @pl.when(i < steps)
    def _():
        up_part, down_part = work(*oth, h_oth)
        s_up[i] = up_part.astype(BF)
        s_down[i] = down_part.astype(BF)
        for item in swaps(i):
            item.start()

    for number, at in ((1, 1), (2, 3), (3, 4)):
        if count:

            @pl.when(i == at)
            def _(number=number):
                carrier.step(number)

    @pl.when(i >= steps)
    def _():
        j = i - steps
        up_part, down_part = work(*own, h_own)
        for item in swaps(j):
            item.wait()
        g_up[...] = (up_part + r_up[j].astype(F32)).astype(BF)
        g_down[...] = (down_part + r_down[j].astype(F32)).astype(BF)

    @pl.when(i == 2 * steps - 1)
    def _():
        def finish(f, carry):
            e, u = out[f], unit[f]
            out[f] = state[f] + norm_back_rows(e, u, scale[f], gain[...])
            return (carry[0] + column_sum(e * u), carry[1] + column_sum(e))

        zero = jnp.zeros((1, width), F32)
        sums[0:1], sums[1:2] = lax.fori_loop(0, frames, finish, (zero, zero))
        carrier.step(4)


def feed_back(grid, number, layer, state, kept, gain, w, parts):
    frames, padded, width = state.shape
    hid = w["up"][0].shape[1]
    steps = 3
    lanes = hid // steps
    cubes, shapes, scratch = carried(grid, parts)
    whole = lambda item: pl.BlockSpec(
        item.shape, lambda i: (0,) * item.ndim, pipeline_mode=pl.Buffered(1)
    )
    first = lambda i: jnp.minimum(i, steps - 1)
    later = lambda i: jnp.maximum(i - steps, 0)

    def side(at):
        weight = pl.BlockSpec((width, lanes), lambda i: (0, at(i)))
        token = pl.BlockSpec((frames, padded, lanes), lambda i: (0, 0, at(i)))
        return [weight, weight, token, token]

    tokens = lambda item: item.reshape(frames, padded, hid)
    sides = [
        [w["down"][k], w["up"][k], tokens(kept["active"][k]), tokens(kept["slope"][k])]
        for k in (1, 0)
    ]
    fixed = [state, kept["normed_m"], kept["unit_m"], kept["scale_m"], gain]
    vec = lambda at: pl.BlockSpec((1, lanes), lambda i: (0, at(i)))
    result = pl.pallas_call(
        functools.partial(feed_back_body, grid.depth, len(parts), steps, layer),
        grid=(2 * steps,),
        in_specs=[whole(item) for item in fixed]
        + side(first)
        + side(later)
        + [whole(item) for item in cubes],
        out_specs=[
            pl.BlockSpec((frames, padded, width), lambda i: (0, 0, 0)),
            pl.BlockSpec((8, width), lambda i: (0, 0)),
            pl.BlockSpec((width, lanes), lambda i: (0, later(i))),
            pl.BlockSpec((width, lanes), lambda i: (0, later(i))),
            vec(later),
            vec(first),
        ]
        + [pl.BlockSpec(item.shape, lambda i: (0, 0)) for item in shapes],
        out_shape=[
            jax.ShapeDtypeStruct((frames, padded, width), F32),
            jax.ShapeDtypeStruct((8, width), F32),
            jax.ShapeDtypeStruct((width, hid), BF),
            jax.ShapeDtypeStruct((width, hid), BF),
            jax.ShapeDtypeStruct((1, hid), F32),
            jax.ShapeDtypeStruct((1, hid), F32),
        ]
        + shapes,
        scratch_shapes=[
            pltpu.VMEM((frames, padded, width), BF),
            pltpu.VMEM((width, frames * padded), BF),
            pltpu.VMEM((width, frames * padded), BF),
            pltpu.VMEM((frames, padded, lanes), BF),
        ]
        + [pltpu.VMEM((steps, width, lanes), BF)] * 4
        + [pltpu.SemaphoreType.DMA((2, steps))] * 2
        + scratch,
        compiler_params=stage_params(number),
        cost_estimate=stage_cost(24000000000),
        name="feed_back",
    )(*fixed, *sides[0], *sides[1], *cubes)
    return result[0], result[1], result[2:4], (result[4], result[5]), result[6:]


def spatial_back_body(depth, count, places, att_scale, layer, staging, *refs):
    take = splitter(refs)
    in_refs, out_refs = take(14 + count), take(5 + count)
    own_scratch, sum_scratch = take(13), take(10 * count)
    sources = in_refs[14:]
    in_refs, out_refs = staging.open(in_refs, out_refs, take(staging.count()))
    take = splitter(in_refs + out_refs + own_scratch + sum_scratch)
    (count_ref, state, merge0, merge1, mixed0, mixed1, qkv0, qkv1) = take(8)
    tri0, tri1, normed, unit, scale, gain = take(6)
    gain = row_of(gain, 3 * layer + 1)
    parts = take(count)
    out, sums, q_sums, g_tri, g_merge = take(5)
    owns = take(count)
    r, bm0, bm1, b0, b1, rt, nt, s_tri, r_tri, s_merge, r_merge, send, recv = take(13)
    place = Place(depth)
    carrier = Carrier(place, True, sources, parts, owns, take(10 * count))
    frames, padded, width = state.shape
    rows_all = frames * padded
    split = merge0.shape[1]
    fix = spatial_fix(count_ref, padded, places)
    carrier.step(0)
    staging.fetch()

    def one(f, carry):
        low = state[f].astype(BF)
        r[f] = low
        for merge, bm, src, dst in ((merge0, bm0, qkv0, b0), (merge1, bm1, qkv1, b1)):
            bm[...] = dot_nn(low, merge[...]).astype(BF)

            def put(part, pair, value, dst=dst):
                dst[f, :, column(part, pair)] = value

            heads_backward(
                lambda part, pair, src=src: src[f, :, column(part, pair)],
                lambda pair, bm=bm: bm[:, pair * 128 : pair * 128 + 128],
                fix,
                att_scale,
                put,
            )
        return carry + column_sum(low.astype(F32))

    sums[...] = jnp.zeros_like(sums)
    q_sums[...] = jnp.zeros_like(q_sums)
    half = frames // 2
    total = lax.fori_loop(0, half, one, jnp.zeros((1, width), F32))
    carrier.step(1)
    sums[2:3] = lax.fori_loop(half, frames, one, total)
    carrier.step(2)
    rt[...] = r[...].reshape(rows_all, width).T
    nt[...] = normed[...].reshape(rows_all, width).T
    flat = lambda ref, part: ref[:, :, part * split : (part + 1) * split].reshape(rows_all, split)
    swap_tri = remote(s_tri, r_tri, send.at[0], recv.at[0], place.over_t())
    swap_merge = remote(s_merge, r_merge, send.at[1], recv.at[1], place.over_t())
    s_merge[...] = dot_nn(rt[...], mixed1[...]).astype(BF)
    swap_merge.start()
    for part in range(3):
        cols = slice(part * split, (part + 1) * split)
        s_tri[:, cols] = dot_nn(nt[...], flat(b1, part)).astype(BF)
    swap_tri.start()
    carrier.step(3)

    def finish(f, carry):
        e = dot_nt(b0[f], tri0[...]) + dot_nt(b1[f], tri1[...])
        u = unit[f]
        out[f] = state[f] + norm_back_rows(e, u, scale[f], gain[...])
        return (
            carry[0] + column_sum(e * u),
            carry[1] + column_sum(e),
            carry[2] + column_sum(b0[f].astype(F32)),
            carry[3] + column_sum(b1[f].astype(F32)),
        )

    zero, wide = jnp.zeros((1, width), F32), jnp.zeros((1, 3 * split), F32)
    sums[0:1], sums[1:2], mine, theirs = lax.fori_loop(
        0, frames, finish, (zero, zero, wide, wide)
    )
    for number, value in ((0, mine), (1, theirs)):
        q_sums[number : number + 1, :split] = value[:, :split]
        q_sums[number : number + 1, split:] = value[:, 2 * split :]
    swap_merge.wait()
    g_merge[...] = (dot_nn(rt[...], mixed0[...]) + r_merge[...].astype(F32)).astype(BF)
    swap_tri.wait()
    for part in range(3):
        cols = slice(part * split, (part + 1) * split)
        mine = dot_nn(nt[...], flat(b0, part))
        g_tri[:, cols] = (mine + r_tri[:, cols].astype(F32)).astype(BF)
    carrier.step(4)
    staging.flush()


def spatial_back(grid, number, layer, count_ref, state, kept, gain, w, parts, places, att_scale):
    frames, padded, width = state.shape
    split = w["merge_s"][0].shape[1]
    cubes, shapes, scratch = carried(grid, parts)
    flat = [item.reshape(frames * padded, split) for item in kept["mixed_s"]]
    fixed = [count_ref, state, *w["merge_s"], *flat, *kept["qkv_s"], *w["triple_s"]]
    fixed += [kept["normed_s"], kept["unit_s"], kept["scale_s"], gain]
    ins = fixed + cubes
    outs = [
        jax.ShapeDtypeStruct((frames, padded, width), F32),
        jax.ShapeDtypeStruct((8, width), F32),
        jax.ShapeDtypeStruct((8, 2 * split), F32),
        jax.ShapeDtypeStruct((width, 3 * split), BF),
        jax.ShapeDtypeStruct((width, split), BF),
    ] + shapes
    staging = Staging(1, ins, outs)
    result = pl.pallas_call(
        functools.partial(
            spatial_back_body, grid.depth, len(parts), places, att_scale, layer, staging
        ),
        in_specs=staging.in_specs(),
        out_specs=staging.out_specs(),
        out_shape=outs,
        scratch_shapes=[pltpu.VMEM((frames, padded, width), BF)]
        + [pltpu.VMEM((padded, split), BF)] * 2
        + [pltpu.VMEM((frames, padded, 3 * split), BF)] * 2
        + [pltpu.VMEM((width, frames * padded), BF)] * 2
        + [pltpu.VMEM((width, 3 * split), BF)] * 2
        + [pltpu.VMEM((width, split), BF)] * 2
        + [pltpu.SemaphoreType.DMA((2,))] * 2
        + scratch
        + staging.scratch(),
        compiler_params=stage_params(number),
        cost_estimate=stage_cost(24000000000),
        name="spatial_stage",
    )(*ins)
    return result[0], result[1], result[2], result[3:5], result[5:]


def temporal_back_body(depth, count, att_scale, layer, staging, pieces, *refs):
    take = splitter(refs)
    chained = 1 if pieces else 0
    in_refs, small = take(13 + count), take(len(pieces))
    out_refs, total = take(6 + count), take(chained)
    own_scratch, sum_scratch, hop_refs = take(13), take(10 * count), take(4 * chained)
    sources = in_refs[13:]
    in_refs, out_refs = staging.open(in_refs, out_refs, take(staging.count()))
    take = splitter(in_refs + out_refs + own_scratch + sum_scratch)
    state, mixing, joined, merge0, merge1, mine, swap, qkv, tri = take(9)
    normed, unit, scale, gain = take(4)
    gain = row_of(gain, 3 * layer)
    parts = take(count)
    out, sums, q_sums, g_tri, g_merge, g_mix = take(6)
    owns = take(count)
    r, bj, away, bm, b, nt, rt, s_merge, r_merge, s_back, r_back, send, recv = take(13)
    place = Place(depth)
    carrier = Carrier(place, True, sources, parts, owns, take(10 * count))
    frames, padded, width = state.shape
    rows_all = frames * padded
    split = merge0.shape[1]
    carrier.step(0)
    hops = Hops(place, pieces, small, *total, *hop_refs) if chained else None
    if chained:
        hops.begin()
    staging.fetch()

    def begin(f, carry):
        low = state[f].astype(BF)
        r[f] = low
        value = dot_nt(low, mixing[...]).astype(BF)
        bj[f] = value
        bm[f] = dot_nn(value, merge0[...]).astype(BF)
        away[f] = dot_nn(value, merge1[...]).astype(BF)
        return (carry[0] + column_sum(low.astype(F32)), carry[1] + column_sum(value.astype(F32)))

    sums[...] = jnp.zeros_like(sums)
    q_sums[...] = jnp.zeros_like(q_sums)
    zero = jnp.zeros((1, width), F32)
    sums[3:4], sums[2:3] = lax.fori_loop(0, frames, begin, (zero, zero))
    swap_bm = remote(
        away, bm.at[pl.ds(frames, frames)], send.at[0], recv.at[0], place.over_t()
    )
    swap_bm.start()
    rt[...] = bj[...].reshape(rows_all, width).T
    s_merge[...] = dot_nn(rt[...], swap[...].reshape(rows_all, split)).astype(BF)
    swap_merge = remote(s_merge, r_merge, send.at[1], recv.at[1], place.over_t())
    swap_merge.start()
    carrier.step(1)
    if chained:
        hops.hop(1)
    rt[...] = joined[...].reshape(rows_all, width).T
    for half in range(2):
        cols = slice(half * split, (half + 1) * split)
        g_mix[:, cols] = dot_nn(rt[...], r[:, :, cols].reshape(rows_all, split))
    rt[...] = bj[...].reshape(rows_all, width).T
    swap_merge.wait()
    g_merge[...] = (dot_nn(rt[...], mine[...].reshape(rows_all, split)) + r_merge[...].astype(F32)).astype(BF)
    swap_bm.wait()
    tile = 16
    fix = temporal_fix(tile)

    def one(i, carry):
        at = pl.ds(pl.multiple_of(i * tile, tile), tile)

        def put(part, pair, value):
            b[:, at, column(part, pair)] = value.reshape(FRAMES, tile, 128)

        heads_backward(
            lambda part, pair: qkv[:, at, column(part, pair)].reshape(FRAMES * tile, 128),
            lambda pair: bm[:, at, pair * 128 : pair * 128 + 128].reshape(FRAMES * tile, 128),
            fix,
            att_scale,
            put,
        )
        return carry

    tiles = padded // tile
    lax.fori_loop(0, tiles // 3, one, 0)
    if chained:
        hops.hop(2)
    lax.fori_loop(tiles // 3, 2 * tiles // 3, one, 0)
    carrier.step(2)
    if chained:
        hops.hop(3)
    lax.fori_loop(2 * tiles // 3, tiles, one, 0)
    if chained:
        hops.hop(4)
    carrier.step(3)

    def toward(f, carry):
        s_back[f] = dot_nt(b[f + frames], tri[...]).astype(BF)
        return carry

    lax.fori_loop(0, frames, toward, 0)
    swap_back = remote(s_back, r_back, send.at[2], recv.at[2], place.over_t())
    swap_back.start()
    nt[...] = normed[...].reshape(2 * rows_all, width).T
    for part in range(3):
        cols = slice(part * split, (part + 1) * split)
        g_tri[:, cols] = dot_nn(
            nt[...], b[:, :, cols].reshape(2 * rows_all, split)
        ).astype(BF)
    swap_back.wait()

    def finish(f, carry):
        e = dot_nt(b[f], tri[...]) + r_back[f].astype(F32)
        u = unit[f]
        out[f] = state[f] + norm_back_rows(e, u, scale[f], gain[...])
        both = column_sum(b[f].astype(F32)) + column_sum(b[f + frames].astype(F32))
        return (carry[0] + column_sum(e * u), carry[1] + column_sum(e), carry[2] + both)

    sums[0:1], sums[1:2], wide = lax.fori_loop(
        0, frames, finish, (zero, zero, jnp.zeros((1, 3 * split), F32))
    )
    q_sums[0:1, :split] = wide[:, :split]
    q_sums[0:1, split:] = wide[:, 2 * split :]
    if chained:
        hops.hop(5)
    carrier.step(4)
    staging.flush()


def temporal_back(grid, number, layer, state, kept, gain, w, parts, att_scale, small=None):
    frames, padded, width = state.shape
    split = w["merge_t"][0].shape[1]
    cubes, shapes, scratch = carried(grid, parts)
    fixed = [state, w["mixing"], kept["joined"], *w["merge_t"], *kept["mixed_t"], kept["qkv_t"]]
    fixed += [w["triple_t"], kept["normed_t"], kept["unit_t"], kept["scale_t"], gain]
    ins = fixed + cubes
    outs = [
        jax.ShapeDtypeStruct((frames, padded, width), F32),
        jax.ShapeDtypeStruct((8, width), F32),
        jax.ShapeDtypeStruct((8, 2 * split), F32),
        jax.ShapeDtypeStruct((width, 3 * split), BF),
        jax.ShapeDtypeStruct((width, split), BF),
        jax.ShapeDtypeStruct((width, width), F32),
    ] + shapes
    staging = Staging(0, ins, outs)
    pieces = small.pieces if small else []
    chained = 1 if small else 0
    result = pl.pallas_call(
        functools.partial(
            temporal_back_body, grid.depth, len(parts), att_scale, layer, staging, pieces
        ),
        in_specs=staging.in_specs() + [VMEM_SPEC] * len(pieces),
        out_specs=staging.out_specs() + [VMEM_SPEC] * chained,
        out_shape=outs + ([small.shape()] if small else []),
        scratch_shapes=[pltpu.VMEM((frames, padded, width), BF)] * 2
        + [pltpu.VMEM((frames, padded, split), BF)]
        + [pltpu.VMEM((2 * frames, padded, split), BF)]
        + [pltpu.VMEM((2 * frames, padded, 3 * split), BF)]
        + [pltpu.VMEM((width, 2 * frames * padded), BF)]
        + [pltpu.VMEM((width, frames * padded), BF)]
        + [pltpu.VMEM((width, split), BF)] * 2
        + [pltpu.VMEM((frames, padded, width), BF)] * 2
        + [pltpu.SemaphoreType.DMA((3,))] * 2
        + scratch
        + (hop_scratch(small) if chained else [])
        + staging.scratch(),
        compiler_params=stage_params(number, 60),
        cost_estimate=stage_cost(24000000000),
        name="temporal_stage",
    )(*ins, *(small.arrays if small else []))
    end = 6 + len(parts)
    return result[0], result[1], result[2], result[3:6], result[6:end], result[end:]


def plain_sums(parts):
    return [
        lax.psum_scatter(part.astype(F32), ("shard", "ctx"), scatter_dimension=0, tiled=True)
        for part in parts
    ]


def split_columns(value, widths):
    outs, start = [], 0
    for width in widths:
        outs.append(value[..., start : start + width])
        start += width
    return outs


def per_device(
    video_clips,
    cotangent,
    slot_clip,
    valid_places,
    norm_gain,
    norm_bias,
    triple_weight,
    entry_bias,
    merge_weight,
    branch_bias,
    mixing_weight,
    up_weight,
    up_bias,
    down_weight,
):
    grid = Grid()
    slots, frames_here, places_here, width = video_clips.shape
    places = places_here * 2
    padded = -(-places // 16) * 16
    scale = HEAD_DIM ** (-0.5)
    step_rows = triple_weight.shape[2]
    half_rows = step_rows // 2
    own_first = grid.t == 0
    straight = grid.t == grid.y

    clip_ids = jnp.arange(valid_places.shape[0], dtype=jnp.int32)
    my_clip = lax.dynamic_index_in_dim(slot_clip, grid.y, 0, keepdims=False)
    count = jnp.sum(jnp.where(my_clip == clip_ids, valid_places, 0)).astype(jnp.int32)
    valid_here = (jnp.arange(padded, dtype=jnp.int32) < count).astype(F32)[None, :, None]
    count_ref = count.reshape(1)

    def spread_in(value):
        mine = lax.dynamic_index_in_dim(value, grid.y, 0, keepdims=False)
        theirs = lax.dynamic_index_in_dim(value, 1 - grid.y, 0, keepdims=False)
        return spread_in_last(mine, grid.over_y(theirs))

    def spread_in_last(mine, got):
        keep = jnp.where(straight, mine, got)
        send = jnp.where(straight, got, mine)
        swap = grid.over_t(send)
        low = jnp.where(own_first, keep, swap)
        high = jnp.where(own_first, swap, keep)
        gap = jnp.zeros((frames_here, padded - places, width), mine.dtype)
        return jnp.concatenate([low, high, gap], axis=1)

    def spread_first(value):
        low = value[:, :places_here]
        high = value[:, places_here:places]
        keep = jnp.where(own_first, low, high)
        send = jnp.where(own_first, high, low)
        swap = grid.over_t(send)
        return jnp.where(straight, swap, keep), jnp.where(straight, keep, swap)

    def spread_last(got, mine):
        first = jnp.where(grid.y == 0, mine, got)
        second = jnp.where(grid.y == 0, got, mine)
        return jnp.stack([first, second])

    def spread_out(value):
        away, mine = spread_first(value)
        return spread_last(grid.over_y(away), mine)

    def pack_mix(item):
        return jnp.concatenate([item[..., : width // 2], item[..., width // 2 :]], axis=-2)

    def block_triple(layer, part):
        return [triple_weight[layer, part, :, i] for i in range(3)]

    def block_out(layer):
        return [merge_weight[layer, 0].T, pack_mix(mixing_weight[layer])]

    def block_s(layer):
        return block_triple(layer, 1) + [merge_weight[layer, 1].T]

    def block_m(layer):
        return [up_weight[layer], down_weight[layer].T]

    split = triple_weight.shape[-1]
    hid = up_weight.shape[-1]
    wide_t = (3 * split, split, width // 2)
    wide_s = (3 * split, split)
    wide_m = (hid, hid)

    def unpack_mix(item):
        cube = item.reshape(-1, 2, half_rows, width // 2)
        return jnp.concatenate([cube[:, 0], cube[:, 1]], axis=-1)

    def with_other(item):
        return (item, grid.over_t(item))

    def mixing_of(both):
        mix_own, mix_oth = [unpack_mix(item) for item in both]
        return jnp.stack(
            [jnp.where(own_first, mix_own, mix_oth), jnp.where(own_first, mix_oth, mix_own)],
            axis=1,
        ).reshape(width, width)

    def blocks_of(layer, stage):
        if stage == "t":
            triple = jnp.concatenate(block_triple(layer, 0), axis=1)
            return [triple] + block_out(layer)
        if stage == "s":
            return [jnp.concatenate(block_triple(layer, 1), axis=1), merge_weight[layer, 1].T]
        return block_m(layer)

    order = [(layer, stage) for layer in range(LAYERS) for stage in "tsm"]
    gathered = [dict() for _ in range(LAYERS)]

    def settle(key, near):
        w = gathered[key[0]]
        if key[1] == "t":
            w.update(triple_t=near[0][0], merge_t=near[1], mixing=mixing_of(near[2]))
        elif key[1] == "s":
            w.update(triple_s=near[0], merge_s=near[1])
        else:
            w.update(up=near[0], down=near[1])

    def direct_gather(block):
        return lax.all_gather(block, ("shard", "ctx"), axis=0, tiled=True)

    lines = {}
    if grid.direct:
        near, lines[order[1]] = first_gather(
            grid, 7, blocks_of(*order[0]), blocks_of(*order[1])
        )
        settle(order[0], near)
    else:
        for key in order:
            settle(key, [with_other(direct_gather(item)) for item in blocks_of(*key)])

    def load_at(index):
        if not grid.direct:
            return Load(grid)
        near, swapped, deep, across = (), (), (), ()
        if index + 1 < len(order):
            near = lines[order[index + 1]]
            swapped = [not (order[index + 1][1] == "t" and i == 0) for i in range(len(near))]
        if index + 2 < len(order):
            deep = blocks_of(*order[index + 2])
        if index + 1 == len(order):
            across = [far_cotangent]
        return Load(grid, near, swapped, deep, across)

    def loaded(index, got):
        near, new_lines = got
        if index + 1 == len(order):
            lines["across"] = new_lines[0] if grid.direct else grid.over_y(far_cotangent)
            new_lines = ()
        if grid.direct and index + 1 < len(order):
            settle(order[index + 1], near)
        if grid.direct and index + 2 < len(order):
            lines[order[index + 2]] = new_lines

    small = jnp.concatenate([entry_bias[:, 1].reshape(LAYERS, -1), up_bias], axis=1)
    small_oth = grid.over_t(small)
    middle = jnp.zeros((LAYERS, split), F32)

    def query_value(both):
        return jnp.concatenate([both[:, :split], middle, both[:, split : 2 * split]], axis=1)

    gains, shifts = [item.reshape(3 * LAYERS, width) for item in (norm_gain, norm_bias)]
    biases = branch_bias.reshape(4 * LAYERS, width)
    bias_t = query_value(entry_bias[:, 0].reshape(LAYERS, -1))
    bias_s = [query_value(item) for item in (small, small_oth)]
    bias_m = [up_bias, small_oth[:, 2 * split :]]

    state = spread_in(video_clips).astype(F32)
    valid_rows = valid_here[0]
    low_cotangent = cotangent.astype(BF)
    near_cotangent = lax.dynamic_index_in_dim(low_cotangent, grid.y, 0, keepdims=False)
    far_cotangent = lax.dynamic_index_in_dim(low_cotangent, 1 - grid.y, 0, keepdims=False)
    stored = []
    squares = []
    for layer in range(LAYERS):
        w = gathered[layer]
        first = 3 * layer
        (state, unit_t, scale_t, normed_t, qkv_t, mine, swap, joined, sq_t), got = temporal_stage(
            8 + first,
            layer,
            state,
            valid_rows,
            gains,
            shifts,
            w,
            [bias_t, biases, biases],
            load_at(first),
            scale,
        )
        loaded(first, got)
        (state, unit_s, scale_s, normed_s, qkv0, qkv1, mixed0, mixed1, sq_s), got = spatial_stage(
            9 + first,
            layer,
            count_ref,
            state,
            valid_rows,
            gains,
            shifts,
            w,
            bias_s + [biases],
            load_at(first + 1),
            places,
            scale,
        )
        loaded(first + 1, got)
        (state, unit_m, scale_m, normed_m, act0, act1, slope0, slope1, sq_m), got = feed_stage(
            10 + first,
            layer,
            state,
            valid_rows,
            gains,
            shifts,
            w,
            bias_m + [biases],
            load_at(first + 2),
        )
        loaded(first + 2, got)
        squares.append((sq_t, sq_s, sq_m))
        stored.append(
            dict(
                unit_t=unit_t,
                scale_t=scale_t,
                normed_t=normed_t,
                qkv_t=qkv_t,
                mixed_t=(mine, swap),
                joined=joined,
                unit_s=unit_s,
                scale_s=scale_s,
                normed_s=normed_s,
                qkv_s=[qkv0, qkv1],
                mixed_s=[mixed0, mixed1],
                unit_m=unit_m,
                scale_m=scale_m,
                normed_m=normed_m,
                active=[act0, act1],
                slope=[slope0, slope1],
            )
        )
    upstream = spread_in_last(near_cotangent, lines["across"]).astype(F32) * valid_here
    block_output = spread_out(state.astype(BF))

    shards = [None] * LAYERS
    sums = {}
    vectors, half_rows_of = [None] * LAYERS, [None] * LAYERS
    waiting = None

    def both_cores(mine, theirs):
        return [jnp.where(own_first, mine, theirs), jnp.where(own_first, theirs, mine)]

    def carry_sums(names, parts):
        nonlocal waiting
        if not grid.direct:
            sums.update(zip(names, plain_sums(parts)))
            return
        waiting = (names, parts)

    def carried_parts():
        return waiting[1] if waiting else []

    def arrived_sums(result):
        nonlocal waiting
        if waiting:
            sums.update(zip(waiting[0], result))
        waiting = None

    for layer in range(LAYERS - 1, -1, -1):
        w, kept = gathered[layer], stored[layer]
        upstream, vec_m, parts_m, hidden_part, got = feed_back(
            grid, layer, layer, upstream, kept, gains, w, carried_parts()
        )
        arrived_sums(got)
        carry_sums([("up", layer)], parts_m[:1])
        upstream, vec_s, entry_s, parts_s, got = spatial_back(
            grid,
            2 + layer,
            layer,
            count_ref,
            upstream,
            kept,
            gains,
            w,
            carried_parts(),
            places,
            scale,
        )
        arrived_sums(got)
        carry_sums(
            [("down", layer), ("triple_s", layer), ("merge_s", layer)], [parts_m[1]] + list(parts_s)
        )
        per_row = hid // width
        hidden_rows = [item.reshape(per_row, width) for item in hidden_part]
        half_rows_of[layer] = both_cores(
            jnp.concatenate([entry_s[:1], hidden_rows[0]]),
            jnp.concatenate([entry_s[1:2], hidden_rows[1]]),
        )
        vectors[layer] = [vec_s, vec_m]
        early = None
        if layer == 0:
            early = Small(width)
            for vec_pair in vectors:
                early.add(vec_pair[0], 0, 3)
                early.add(vec_pair[1], 0, 3)
            early.add(last_vec, 0, 4)
            for item in half_rows_of:
                early.add(item[0], 0, 3)
                early.add(item[1], 0, 3)
            for item in last_half:
                early.add(item, 0, 1)
            for sq_t, sq_s, sq_m in squares:
                for place_at, (item, start) in enumerate(
                    ((sq_t, 0), (sq_s, 0), (sq_m, 1), (sq_m, 0))
                ):
                    early.add(item, start, 1, 128 * place_at, place_at < 3)
        early_rows = early
        upstream, vec_t, entry_t, parts_t, got, early = temporal_back(
            grid,
            4 + layer,
            layer,
            upstream,
            kept,
            gains,
            w,
            carried_parts(),
            scale,
            early if grid.direct else None,
        )
        arrived_sums(got)
        mix_part = parts_t[2].reshape(-1, 2, half_rows, width)
        mix_mine = lax.dynamic_index_in_dim(mix_part, grid.t, 1, keepdims=False)
        mix_theirs = lax.dynamic_index_in_dim(mix_part, 1 - grid.t, 1, keepdims=False)
        mix_got = grid.over_t(mix_theirs.astype(BF)).astype(F32)
        mix_sum = pack_mix((mix_mine + mix_got).astype(BF)).reshape(width, width // 2)
        carry_sums(
            [("triple_t", layer), ("merge_t", layer), ("mix", layer)],
            [parts_t[0], parts_t[1], mix_sum],
        )
        last_vec = vec_t
        last_half = both_cores(entry_t[:1], jnp.zeros_like(entry_t[:1]))

    small = Small(width)
    small.add(last_vec, 0, 4)
    for item in last_half:
        small.add(item, 0, 1)
    out_low, out_ready = spread_first(upstream.astype(BF))
    if waiting:
        got, small, out_got = tail_sums(grid, 6, carried_parts(), small, out_low)
        arrived_sums(got)
        (early,) = early
    else:
        small, early = small.plain(), early_rows.plain()
        out_got = grid.over_y(out_low)
    input_grad = spread_last(out_got, out_ready).astype(F32)
    names = ("triple_t", "merge_t", "mix", "triple_s", "merge_s", "up", "down")
    for layer in range(LAYERS):
        shards[layer] = [sums[name, layer] for name in names]
    block = 6 * LAYERS
    pairs = early[:block].reshape(LAYERS, 2, 3, width)
    ends = jnp.stack([small[:4], early[block : block + 4]])
    gain_sum, shift_sum = [
        jnp.concatenate([ends[:, k : k + 1], pairs[:, :, k]], axis=1) for k in range(2)
    ]
    bias_sum = jnp.concatenate([ends[:, 2:4], pairs[:, :, 2]], axis=1)
    start = block + 4
    half_sums = early[start : start + 6 * LAYERS].reshape(LAYERS, 2, 3, width)
    end_sums = jnp.stack([small[4:6], early[start + 6 * LAYERS : start + 6 * LAYERS + 2]])
    half_sums = lax.dynamic_index_in_dim(half_sums, grid.t, 1, keepdims=False)
    end_sums = lax.dynamic_index_in_dim(end_sums, grid.t, 1, keepdims=False)
    entry_sum = jnp.stack([end_sums, half_sums[:, 0]], axis=1).reshape(LAYERS, 2, 2, split)
    hidden_sum = half_sums[:, 1:].reshape(LAYERS, hid)
    start = start + 6 * LAYERS + 2
    square_sums = early[start : start + LAYERS, : 4 * 128].reshape(LAYERS, 4, 128)[:, :, 0]
    tokens = FRAMES * width * jnp.sum(valid_places).astype(F32)
    root_squares = jnp.sqrt(square_sums / tokens)

    def unpack_rows(item):
        return jnp.concatenate([item[:half_rows], item[half_rows:]], axis=-1)

    def triple_shape(item):
        return item.reshape(step_rows, 3, split)

    return (
        block_output,
        input_grad,
        gain_sum,
        shift_sum,
        jnp.stack([jnp.stack([triple_shape(s[0]), triple_shape(s[3])]) for s in shards]),
        entry_sum,
        jnp.stack([jnp.stack([s[1].T, s[4].T]) for s in shards]),
        bias_sum,
        jnp.stack([unpack_rows(s[2]) for s in shards]),
        jnp.stack([s[5] for s in shards]),
        hidden_sum,
        jnp.stack([s[6].T for s in shards]),
        root_squares,
    )


def solution(mesh):
    return jax.shard_map(
        per_device,
        mesh=mesh,
        in_specs=(
            P("shard", "ctx", "tp", None),
            P("shard", "ctx", "tp", None),
            P("shard"),
            P(),
            P(),
            P(),
            P(None, None, ("shard", "ctx"), None, "tp"),
            P(None, None, None, "tp"),
            P(None, None, "tp", ("shard", "ctx")),
            P(),
            P(None, ("shard", "ctx", "tp"), None),
            P(None, ("shard", "ctx"), "tp"),
            P(None, "tp"),
            P(None, "tp", ("shard", "ctx")),
        ),
        out_specs=(
            P("shard", "ctx", "tp", None),
            P("shard", "ctx", "tp", None),
            P(),
            P(),
            P(None, None, ("shard", "ctx"), None, "tp"),
            P(None, None, None, "tp"),
            P(None, None, "tp", ("shard", "ctx")),
            P(),
            P(None, ("shard", "ctx", "tp"), None),
            P(None, ("shard", "ctx"), "tp"),
            P(None, "tp"),
            P(None, "tp", ("shard", "ctx")),
            P(),
        ),
        check_vma=False,
    )
```

```python
import functools
import math

import jax
import jax.numpy as jnp
from jax import lax
from jax.experimental import pallas as pl
from jax.experimental.pallas import tpu as pltpu
from jax.sharding import PartitionSpec as P

HEAD_DIM = 64
FRAMES = 8
LAYERS = 2
AXES = ("shard", "ctx", "tp")
BF = jnp.bfloat16
F32 = jnp.float32

far_below = -1000000000.0
epsilon = 1e-06
root_half = 0.7071067811865476
gauss_scale = 0.3989422804014327


def dot_nn(left, right):
    return lax.dot_general(left, right, (((1,), (0,)), ((), ())), preferred_element_type=F32)


def dot_nt(left, right):
    return lax.dot_general(left, right, (((1,), (1,)), ((), ())), preferred_element_type=F32)


def dot_tn(left, right):
    return lax.dot_general(left, right, (((0,), (0,)), ((), ())), preferred_element_type=F32)


def rows(value):
    return value.reshape(-1, value.shape[-1])


def row_total(value):
    return jnp.sum(rows(value).astype(F32), axis=0)


def lane_masks(shape):
    lane = lax.broadcasted_iota(jnp.int32, shape, 1)
    return lane < HEAD_DIM


def softmax_rows(scores):
    top = jnp.max(scores, axis=-1, keepdims=True)
    raised = jnp.exp(scores - top)
    total = jnp.sum(raised, axis=-1, keepdims=True)
    return raised * (1.0 / total)


def sides(value, first):
    zero = jnp.zeros_like(value)
    return [jnp.where(first, value, zero), jnp.where(first, zero, value)]


def heads_forward(qkv, fix, scale, put):
    first = lane_masks(qkv(0, 0).shape)
    scores = []
    for pair in range(3):
        k = qkv(1, pair)
        scores.append([dot_nt(q, k) for q in sides(qkv(0, pair), first)])
    shares = [[softmax_rows(fix(item * scale)).astype(BF) for item in both] for both in scores]
    for pair in range(3):
        v = qkv(2, pair)
        outs = [dot_nn(item, v) for item in shares[pair]]
        put(pair, jnp.where(first, outs[0], outs[1]).astype(BF))


def heads_backward(qkv, back, fix, scale, put):
    first = lane_masks(qkv(0, 0).shape)
    scores, backs = [], []
    for pair in range(3):
        k, v = qkv(1, pair), qkv(2, pair)
        scores.append([dot_nt(q, k) for q in sides(qkv(0, pair), first)])
        backs.append([dot_nt(b, v) for b in sides(back(pair), first)])
    low_shares, low_scores = [], []
    for pair in range(3):
        low_shares.append([])
        low_scores.append([])
        for side in range(2):
            shares = softmax_rows(fix(scores[pair][side] * scale))
            back_shares = backs[pair][side]
            inner = jnp.sum(back_shares * shares, axis=-1, keepdims=True)
            low_scores[pair].append((shares * (back_shares - inner)).astype(BF))
            low_shares[pair].append(shares.astype(BF))
    for pair in range(3):
        q, k, bm = qkv(0, pair), qkv(1, pair), back(pair)
        gq = [dot_nn(item, k) for item in low_scores[pair]]
        gk = [dot_tn(item, q) for item in low_scores[pair]]
        gv = [dot_tn(item, bm) for item in low_shares[pair]]
        put(0, pair, (jnp.where(first, gq[0], gq[1]) * scale).astype(BF))
        put(1, pair, (jnp.where(first, gk[0], gk[1]) * scale).astype(BF))
        put(2, pair, jnp.where(first, gv[0], gv[1]).astype(BF))


def column(part, pair):
    start = part * 384 + pair * 128
    return slice(start, start + 128)


def spatial_fix(count_ref, padded, places):
    col = lax.broadcasted_iota(jnp.int32, (padded, padded), 1)
    floor = jnp.where(col < places, far_below, 3.0 * far_below)
    allowed = col < jnp.minimum(count_ref[0], places)
    return lambda scores: jnp.where(allowed, scores, floor)


def temporal_fix(tile):
    size = FRAMES * tile
    row = lax.broadcasted_iota(jnp.int32, (size, size), 0)
    col = lax.broadcasted_iota(jnp.int32, (size, size), 1)
    same = (row & (tile - 1)) == (col & (tile - 1))
    return lambda scores: jnp.where(same, scores, 3.0 * far_below)


class Grid:
    def __init__(self):
        self.shards = lax.axis_size("shard")
        self.depth = self.shards // 2
        shard = lax.axis_index("shard")
        self.z = shard // 2
        self.x = shard % 2
        self.y = lax.axis_index("ctx")
        self.t = lax.axis_index("tp")
        self.direct = self.depth == 4

    def perm(self, move):
        pairs = []
        for z in range(self.depth):
            for x in range(2):
                for y in range(2):
                    for t in range(2):
                        tz, tx, ty, tt = move(z, x, y, t)
                        pairs.append(
                            (((z * 2 + x) * 2 + y) * 2 + t, ((tz * 2 + tx) * 2 + ty) * 2 + tt)
                        )
        return pairs

    def send(self, value, pairs):
        return lax.ppermute(value, AXES, pairs)

    def over_x(self, value):
        return self.send(value, self.perm(lambda z, x, y, t: (z, 1 - x, y, t)))

    def over_y(self, value):
        return self.send(value, self.perm(lambda z, x, y, t: (z, x, 1 - y, t)))

    def over_t(self, value):
        return self.send(value, self.perm(lambda z, x, y, t: (z, x, y, 1 - t)))

    def over_z(self, value, step):
        depth = self.depth
        return self.send(value, self.perm(lambda z, x, y, t: ((z + step) % depth, x, y, t)))

    def over_bit(self, value, bit):
        pairs = []
        for s in range(self.shards):
            for y in range(2):
                for t in range(2):
                    pairs.append(((s * 2 + y) * 2 + t, ((s ^ bit) * 2 + y) * 2 + t))
        return self.send(value, pairs)

    def total(self, value, across):
        if across:
            value = value + self.over_t(value)
        value = value + self.over_y(value)
        bit = 1
        while bit < self.shards:
            value = value + self.over_bit(value, bit)
            bit *= 2
        return value


class Sums:
    def __init__(self, place, source, part, own, ra, rb, sx, sy, rx, ry, low, gz, send, recv):
        self.place, self.source, self.part, self.own = place, source, part, own
        self.ra, self.rb, self.sx, self.sy = ra, rb, sx, sy
        self.rx, self.ry, self.low, self.gz = rx, ry, low, gz
        self.send, self.recv = send, recv
        self.depth = part.shape[0]
        self.half = part.shape[0] // 2

    def copy(self, number, src, dst, target):
        return remote(src, dst, self.send.at[number], self.recv.at[number], target)

    def far(self):
        x, y = self.place.x, self.place.y
        low, high = pl.ds(0, self.half), pl.ds(self.half, self.half)
        return [
            self.copy(0, self.source.at[low, 1 - x, 1 - y], self.ra, self.place.over_y()),
            self.copy(1, self.source.at[high, 1 - x, 1 - y], self.rb, self.place.over_x()),
        ]

    def near(self):
        return [
            self.copy(2, self.sx, self.rx, self.place.over_x()),
            self.copy(3, self.sy, self.ry, self.place.over_y()),
        ]

    def deep(self):
        return [
            self.copy(
                3 + k,
                self.low.at[lax.rem(self.place.z + k, self.depth)],
                self.gz.at[k - 1],
                self.place.over_z(k),
            )
            for k in range(1, self.depth)
        ]

    def first(self):
        for item in self.far():
            item.start()

    def second(self):
        x, y, half = self.place.x, self.place.y, self.half
        for item in self.far():
            item.wait()
        for k in range(2 * half):
            toward_x, toward_y = self.part[k, 1 - x, y], self.part[k, x, 1 - y]
            if k < half:
                toward_x = toward_x + self.ra[k]
            else:
                toward_y = toward_y + self.rb[k - half]
            self.sx[k] = toward_x
            self.sy[k] = toward_y
        for item in self.near():
            item.start()

    def kept(self, k):
        mine = self.part[k, self.place.x, self.place.y].astype(F32)
        return mine + self.rx[k].astype(F32) + self.ry[k].astype(F32)

    def third(self):
        for item in self.near():
            item.wait()
        for k in range(self.depth):
            mine = self.part[k, self.place.x, self.place.y]
            self.low[k] = mine + (self.rx[k] + self.ry[k])
        for item in self.deep():
            item.start()

    def last(self):
        for item in self.deep():
            item.wait()
        total = self.kept(self.place.z)
        for k in range(self.depth - 1):
            total = total + self.gz[k].astype(F32)
        self.own[...] = total


def remote(src, dst, send, recv, target):
    return pltpu.make_async_remote_copy(
        src_ref=src,
        dst_ref=dst,
        send_sem=send,
        recv_sem=recv,
        device_id=target,
        device_id_type=pl.DeviceIdType.MESH,
    )


class Place:
    def __init__(self, depth):
        self.depth = depth
        shard = lax.axis_index("shard")
        self.z = shard // 2
        self.x = lax.rem(shard, 2)
        self.y = lax.axis_index("ctx")
        self.t = lax.axis_index("tp")

    def over_x(self):
        return {"shard": self.z * 2 + 1 - self.x}

    def over_y(self):
        return {"ctx": 1 - self.y}

    def over_t(self):
        return {"tp": 1 - self.t}

    def over_z(self, step):
        return {"shard": lax.rem(self.z + step, self.depth) * 2 + self.x}

    def meet(self, chips, cores):
        barrier = pltpu.get_barrier_semaphore()
        targets = [self.over_t()] if cores else []
        if chips:
            targets += [self.over_x(), self.over_y()]
            targets += [self.over_z(k) for k in range(1, self.depth)]
        for target in targets:
            pl.semaphore_signal(
                barrier, inc=1, device_id=target, device_id_type=pl.DeviceIdType.MESH
            )
        pl.semaphore_wait(barrier, len(targets))


class Carrier:
    def __init__(self, place, cores, starts, sources, parts, owns, scratch):
        self.place, self.cores = place, cores
        lanes = [pl.ds(start, own.shape[1]) for start, own in zip(starts, owns)]
        sources = [ref.at[:, :, :, :, cols] for ref, cols in zip(sources, lanes)]
        parts = [ref.at[:, :, :, :, cols] for ref, cols in zip(parts, lanes)]
        self.sums = [
            Sums(place, source, part, own, *scratch[10 * i : 10 * i + 10])
            for i, (source, part, own) in enumerate(zip(sources, parts, owns))
        ]

    def step(self, number):
        lead, rest = self.sums[:1], self.sums[1:]
        if number == 0:
            self.place.meet(bool(self.sums), self.cores)
            for item in lead + rest:
                item.first()
        elif number == 1:
            for item in lead:
                item.second()
        elif number == 2:
            for item in lead:
                item.third()
            for item in rest:
                item.second()
        elif number == 3:
            for item in rest:
                item.third()
        else:
            for item in lead + rest:
                item.last()


def carried(grid, parts):
    depth = grid.depth
    cubes, shapes, scratch = [], [], []
    for part, start, lanes in parts:
        step_rows = part.shape[0] // (depth * 4)
        block = lambda count: pltpu.VMEM((count, step_rows, lanes), BF)
        cubes.append(part.reshape(depth, 2, 2, step_rows, part.shape[1]))
        shapes.append(jax.ShapeDtypeStruct((step_rows, lanes), F32))
        scratch += [block(depth // 2)] * 2 + [block(depth)] * 5 + [block(depth - 1)]
        scratch += [pltpu.SemaphoreType.DMA((3 + depth,))] * 2
    return cubes, shapes, scratch


def stage_params(number, vmem=58, sends=True):
    if not sends:
        return pltpu.CompilerParams(vmem_limit_bytes=vmem << 20)
    return pltpu.CompilerParams(
        collective_id=number, has_side_effects=True, vmem_limit_bytes=vmem << 20
    )


def stage_cost(flops):
    return pl.CostEstimate(flops=flops, bytes_accessed=30000000, transcendentals=0)


VMEM_SPEC = pl.BlockSpec(memory_space=pltpu.VMEM)
SMEM_SPEC = pl.BlockSpec(memory_space=pltpu.SMEM)


ANY_SPEC = pl.BlockSpec(memory_space=pl.ANY)


def is_big(item):
    return item.shape[-1] >= 128 and math.prod(item.shape) >= 65536


class Staging:
    def __init__(self, smem, ins, outs):
        self.smem = smem
        self.ins = [i >= smem and is_big(item) for i, item in enumerate(ins)]
        self.outs = [is_big(item) for item in outs]
        self.in_shapes = [item for item, big in zip(ins, self.ins) if big]
        self.out_shapes = [item for item, big in zip(outs, self.outs) if big]

    def in_specs(self):
        specs = [ANY_SPEC if big else VMEM_SPEC for big in self.ins]
        return [SMEM_SPEC] * self.smem + specs[self.smem :]

    def out_specs(self):
        return [ANY_SPEC if big else VMEM_SPEC for big in self.outs]

    def scratch(self):
        held = self.in_shapes + self.out_shapes
        blocks = [pltpu.VMEM(item.shape, item.dtype) for item in held]
        return blocks + [pltpu.SemaphoreType.DMA((len(held),))]

    def count(self):
        return len(self.in_shapes) + len(self.out_shapes) + 1

    def open(self, in_refs, out_refs, refs):
        refs = list(refs)
        sems = refs.pop()
        number = 0
        pairs = []
        for group, flags in ((in_refs, self.ins), (out_refs, self.outs)):
            view, moves = [], []
            for ref, big in zip(group, flags):
                if big:
                    moves.append((ref, refs[number], sems.at[number]))
                    ref = refs[number]
                    number += 1
                view.append(ref)
            pairs.append((view, moves))
        (self.in_view, self.in_moves), (self.out_view, self.out_moves) = pairs
        return self.in_view, self.out_view

    def fetch(self):
        copies = [pltpu.make_async_copy(src, dst, sem) for src, dst, sem in self.in_moves]
        for item in copies:
            item.start()
        for item in copies:
            item.wait()

    def flush(self):
        copies = [pltpu.make_async_copy(src, dst, sem) for dst, src, sem in self.out_moves]
        for item in copies:
            item.start()
        for item in copies:
            item.wait()


def row_of(ref, index):
    return ref.at[pl.ds(index, 1)]


def splitter(refs):
    refs = list(refs)
    return lambda count: [refs.pop(0) for _ in range(count)]


class Hops:
    def __init__(self, place, pieces, refs, total, held, came, send, recv):
        z = place.z
        targets = [place.over_t(), place.over_y(), place.over_x()]
        targets.append({"shard": (z + 1 - 2 * lax.rem(z, 2)) * 2 + place.x})
        targets.append({"shard": (z + 2 - 4 * (z // 2)) * 2 + place.x})
        self.pieces, self.refs = pieces, refs
        self.total, self.held, self.came = total, held, came
        self.copies = [
            remote(held.at[k], came.at[k], send.at[k], recv.at[k], target)
            for k, target in enumerate(targets)
        ]

    def begin(self):
        self.held[0] = jnp.zeros(self.held.shape[1:], F32)
        for ref, (start, count, row, lane) in zip(self.refs, self.pieces):
            lanes = ref.shape[1]
            self.held[0, row : row + count, lane : lane + lanes] = ref[start : start + count]
        self.copies[0].start()

    def hop(self, number):
        self.copies[number - 1].wait()
        value = self.held[number - 1] + self.came[number - 1]
        if number < len(self.copies):
            self.held[number] = value
            self.copies[number].start()
        else:
            self.total[...] = value


class Small:
    def __init__(self, width):
        self.arrays, self.pieces, self.rows, self.width = [], [], 0, width

    def add(self, array, start, count, lane=0, stay=False):
        self.arrays.append(array)
        self.pieces.append((start, count, self.rows, lane))
        if not stay:
            self.rows += count

    def shape(self):
        return jax.ShapeDtypeStruct((-(-self.rows // 8) * 8, self.width), F32)

    def plain(self):
        whole = jnp.zeros(self.shape().shape, F32)
        for array, (start, count, row, lane) in zip(self.arrays, self.pieces):
            whole = whole.at[row : row + count, lane : lane + array.shape[1]].set(
                array[start : start + count]
            )
        return lax.psum(whole, AXES)


def hop_scratch(small):
    block = pltpu.VMEM((5,) + small.shape().shape, F32)
    return [block, block] + [pltpu.SemaphoreType.DMA((5,))] * 2


def tail_body(depth, starts, pieces, *refs):
    take = splitter(refs)
    count = len(starts)
    parts, small, (away,) = take(count), take(len(pieces)), take(1)
    owns, (total, back) = take(count), take(2)
    hop_refs, (send, recv) = take(4), take(2)
    place = Place(depth)
    carrier = Carrier(place, True, starts, parts, parts, owns, take(10 * count))
    hops = Hops(place, pieces, small, total, *hop_refs)
    across = remote(away, back, send.at[0], recv.at[0], place.over_y())
    carrier.step(0)
    hops.begin()
    for number in range(1, 5):
        hops.hop(number)
        if number < 4:
            carrier.step(number)
    across.start()
    hops.hop(5)
    carrier.step(4)
    across.wait()


def starts_of(parts):
    return [start for _, start, _ in parts]


def tail_sums(grid, number, parts, small, away):
    cubes, shapes, scratch = carried(grid, parts)
    count = len(small.arrays)
    result = pl.pallas_call(
        functools.partial(tail_body, grid.depth, starts_of(parts), small.pieces),
        in_specs=[VMEM_SPEC] * (len(parts) + count + 1),
        out_specs=[VMEM_SPEC] * (len(parts) + 2),
        out_shape=shapes + [small.shape(), jax.ShapeDtypeStruct(away.shape, away.dtype)],
        scratch_shapes=hop_scratch(small) + [pltpu.SemaphoreType.DMA((1,))] * 2 + scratch,
        compiler_params=stage_params(number),
        cost_estimate=stage_cost(20000000000),
        name="sum_rows",
    )(*cubes, *small.arrays, away)
    return result[:-2], result[-2], result[-1]


def norm_back_rows(e, unit, scale, gain):
    along = e * gain
    lanes = e.shape[-1]
    mean_along = jnp.sum(along, axis=-1, keepdims=True) * (1.0 / lanes)
    mean_unit = jnp.sum(along * unit, axis=-1, keepdims=True) * (1.0 / lanes)
    return scale * (along - mean_along - unit * mean_unit)


def column_sum(value):
    return jnp.sum(value, axis=0, keepdims=True)


def tie(value, *others):
    return lax.optimization_barrier((value, *others))[0]


class Near:
    def __init__(self, place, line, whole, other, send, recv):
        self.place, self.line, self.whole, self.other = place, line, whole, other
        self.send, self.recv = send, recv
        self.depth = line.shape[0]

    def pair(self, number, src, dst, target):
        return remote(src, dst, self.send.at[number], self.recv.at[number], target)

    def at(self, ref, dx, dy, low=0, size=None):
        x = 1 - self.place.x if dx else self.place.x
        y = 1 - self.place.y if dy else self.place.y
        view = ref.at[pl.ds(low, size or self.depth), x, y]
        return view.at[:, self.place.t] if len(ref.shape) == 6 else view

    def sides(self):
        dst = self.at(self.whole, 0, 0)
        return [
            self.pair(0, self.line, dst, self.place.over_x()),
            self.pair(1, self.line, dst, self.place.over_y()),
        ]

    def corners(self):
        half = self.depth // 2
        first = self.at(self.whole, 1, 0, 0, half)
        second = self.at(self.whole, 0, 1, half, half)
        return [
            self.pair(2, first, first, self.place.over_y()),
            self.pair(3, second, second, self.place.over_x()),
        ]

    def swap(self, number):
        if self.other is None:
            return []
        if number == 0:
            src, dst = self.line, self.at(self.other, 0, 0)
        else:
            dx, dy = number & 1, number >> 1
            src, dst = self.at(self.whole, dx, dy), self.at(self.other, dx, dy)
        return [self.pair(4 + number, src, dst, self.place.over_t())]

    def begin(self):
        for item in self.sides() + self.swap(0) + [self.keep()]:
            item.start()

    def keep(self):
        return pltpu.make_async_copy(self.line, self.at(self.whole, 0, 0), self.send.at[8])

    def middle(self):
        for item in self.sides():
            item.wait()
        for item in self.corners() + self.swap(1) + self.swap(2):
            item.start()

    def corner_in(self):
        for item in self.corners():
            item.wait()
        for item in self.swap(3):
            item.start()

    def end(self):
        for number in range(4):
            for item in self.swap(number):
                item.wait()
        self.keep().wait()


class Deep:
    def __init__(self, place, block, line, send, recv):
        self.place, self.block, self.line, self.send, self.recv = place, block, line, send, recv

    def copies(self):
        return [
            remote(
                self.block,
                self.line.at[self.place.z],
                self.send.at[k - 1],
                self.recv.at[k - 1],
                self.place.over_z(k),
            )
            for k in range(1, self.line.shape[0])
        ]

    def begin(self):
        for item in self.copies():
            item.start()
        self.line[self.place.z] = self.block[...]

    def end(self):
        for item in self.copies():
            item.wait()


def landing(line, both):
    depth, step_rows, lanes = line
    if both == "one":
        return [jax.ShapeDtypeStruct((depth, 2, 2, 2, step_rows, lanes), BF)]
    return [jax.ShapeDtypeStruct((depth, 2, 2, step_rows, lanes), BF)] * (2 if both else 1)


def landed(outs, both):
    whole = outs.pop(0)
    if both == "one":
        return whole, whole
    return whole, outs.pop(0) if both else None


class Load:
    def __init__(self, grid, near=(), swapped=(), deep=(), across=()):
        self.depth = grid.depth
        self.swapped = list(swapped)
        self.near_count, self.deep_count = len(near), len(deep)
        self.inputs = list(near) + list(deep) + list(across)
        self.across_count = len(across)
        self.shapes, self.scratch, self.specs = [], [], []
        for line, both in zip(near, swapped):
            shapes = landing(line.shape, both)
            self.shapes += shapes
            self.specs += [ANY_SPEC] * len(shapes)
            self.scratch += [pltpu.SemaphoreType.DMA((9,)), pltpu.SemaphoreType.DMA((8,))]
        for block in deep:
            self.shapes.append(jax.ShapeDtypeStruct((self.depth,) + block.shape, BF))
            self.specs.append(VMEM_SPEC)
            self.scratch += [pltpu.SemaphoreType.DMA((self.depth - 1,))] * 2

        for item in across:
            self.shapes.append(jax.ShapeDtypeStruct(item.shape, item.dtype))
            self.specs.append(VMEM_SPEC)
            self.scratch += [pltpu.SemaphoreType.DMA((1,))] * 2

    def results(self, arrays):
        arrays = list(arrays)
        flat = lambda item: item.reshape(-1, item.shape[-1])
        near = []
        for both in self.swapped:
            near.append([None if item is None else flat(item) for item in landed(arrays, both)])
        return near, arrays


class Loader:
    def __init__(self, place, cores, load, ins, outs, sems):
        self.place, self.cores, self.load = place, cores, load
        ins, outs, sems = list(ins), list(outs), list(sems)
        self.near = []
        for both in load.swapped:
            whole, other = landed(outs, both)
            self.near.append(Near(place, ins.pop(0), whole, other, sems.pop(0), sems.pop(0)))
        self.deep = [
            Deep(place, ins.pop(0), outs.pop(0), sems.pop(0), sems.pop(0))
            for _ in range(load.deep_count)
        ]
        self.across = []
        for _ in range(load.across_count):
            send, recv = sems.pop(0), sems.pop(0)
            self.across.append(
                remote(ins.pop(0), outs.pop(0), send.at[0], recv.at[0], place.over_y())
            )

    def begin(self):
        chips = bool(self.near or self.deep or self.across)
        if chips or self.cores:
            self.place.meet(chips, self.cores or bool(self.near))
        for item in self.near + self.deep:
            item.begin()
        for item in self.across:
            item.start()

    def middle(self):
        for item in self.near:
            item.middle()

    def end(self):
        for item in self.near:
            item.corner_in()
        for item in self.near:
            item.end()
        for item in self.deep:
            item.end()
        for item in self.across:
            item.wait()


def open_kernel(load, staging, refs, scratch):
    take = splitter(refs)
    in_refs = take(len(staging.ins))
    load_ins = take(len(load.inputs))
    out_refs = take(len(staging.outs))
    load_outs = take(len(load.shapes))
    scratch_refs = take(scratch)
    in_refs, out_refs = staging.open(in_refs, out_refs, take(staging.count()))
    return in_refs, out_refs, scratch_refs, (load_ins, load_outs, take(len(load.scratch)))


def kernel_call(body, number, ins, shapes, scratch, load, name, smem=0, cores=False):
    staging = Staging(smem, ins, shapes)
    result = pl.pallas_call(
        functools.partial(body, staging),
        in_specs=staging.in_specs() + [VMEM_SPEC] * len(load.inputs),
        out_specs=staging.out_specs() + load.specs,
        out_shape=list(shapes) + load.shapes,
        scratch_shapes=list(scratch) + staging.scratch() + load.scratch,
        compiler_params=stage_params(number, sends=cores or bool(load.inputs)),
        cost_estimate=stage_cost(20000000000),
        name=name,
    )(*ins, *load.inputs)
    return result[: len(shapes)], load.results(result[len(shapes) :])


def first_body(swapped, depth, next_count, *refs):
    take = splitter(refs)
    count = len(swapped)
    blocks, next_blocks = take(count), take(next_count)
    wholes = [landed(take(2 if both is True else 1), both) for both in swapped]
    next_lines = take(next_count)
    lines = take(count)
    place = Place(depth)
    deep = [Deep(place, blocks[i], lines[i], *take(2)) for i in range(count)]
    near = [Near(place, lines[i], *wholes[i], *take(2)) for i in range(count)]
    after = [Deep(place, next_blocks[i], next_lines[i], *take(2)) for i in range(next_count)]
    place.meet(True, True)
    for item in deep:
        item.begin()
    for one, two in zip(deep, near):
        one.end()
        two.begin()
    for item in after:
        item.begin()
    for item in near:
        item.middle()
    for item in near:
        item.corner_in()
    for item in near:
        item.end()
    for item in after:
        item.end()


def first_gather(grid, number, blocks, swapped, next_blocks):
    depth = grid.depth
    line = lambda item: (depth,) + item.shape
    shapes = []
    for item, both in zip(blocks, swapped):
        shapes += landing(line(item), both)
    specs = [ANY_SPEC] * len(shapes) + [VMEM_SPEC] * len(next_blocks)
    shapes += [jax.ShapeDtypeStruct(line(item), BF) for item in next_blocks]
    sems = lambda size: [pltpu.SemaphoreType.DMA((size,))] * 2
    scratch = [pltpu.VMEM(line(item), BF) for item in blocks]
    for _ in blocks:
        scratch += sems(depth - 1)
    for _ in blocks:
        scratch += [pltpu.SemaphoreType.DMA((9,)), pltpu.SemaphoreType.DMA((8,))]
    for _ in next_blocks:
        scratch += sems(depth - 1)
    arrays = list(
        pl.pallas_call(
            functools.partial(first_body, tuple(swapped), depth, len(next_blocks)),
            in_specs=[VMEM_SPEC] * (len(blocks) + len(next_blocks)),
            out_specs=specs,
            out_shape=shapes,
            scratch_shapes=scratch,
            compiler_params=stage_params(number),
            cost_estimate=stage_cost(20000000000),
            name="first_gather",
        )(*blocks, *next_blocks)
    )
    flat = lambda item: None if item is None else item.reshape(-1, item.shape[-1])
    near = [[flat(item) for item in landed(arrays, both)] for both in swapped]
    return near, arrays


def norm_rows(state, gain, shift):
    lanes = state.shape[-1]
    center = state - jnp.sum(state, axis=-1, keepdims=True) * (1.0 / lanes)
    spread = jnp.sum(center * center, axis=-1, keepdims=True) * (1.0 / lanes)
    scale = lax.rsqrt(spread + epsilon)
    unit = center * scale
    return (unit * gain + shift).astype(BF), unit, scale


def square_sum(value, valid):
    return jnp.sum(jnp.sum(value * value, axis=-1, keepdims=True) * valid, axis=0, keepdims=True)


def temporal_body(load, att_scale, layer, staging, *refs):
    ins, outs, scratch, loads = open_kernel(load, staging, refs, 3)
    state, valid, gain, shift, tri, tri_bias, merge0, merge1, merge_bias, mixing, mix_bias = ins
    out, unit, scale, normed, qkv, mine, swap, joined, sq = outs
    away, send, recv = scratch
    gain, shift = row_of(gain, 3 * layer), row_of(shift, 3 * layer)
    tri_bias = row_of(tri_bias, layer)
    merge_bias, mix_bias = row_of(merge_bias, 4 * layer), row_of(mix_bias, 4 * layer + 1)
    place = Place(load.depth)
    loader = Loader(place, True, load, *loads)
    frames, padded, width = state.shape
    loader.begin()
    staging.fetch()

    def norm_one(f, carry):
        low, u, s = norm_rows(state[f], gain[...], shift[...])
        normed[f] = low
        unit[f] = u
        scale[f] = s
        return carry

    lax.fori_loop(0, frames, norm_one, 0)
    own = normed.at[pl.ds(0, frames)]
    swap_normed = remote(
        own, normed.at[pl.ds(frames, frames)], send.at[0], recv.at[0], place.over_t()
    )
    swap_normed.start()

    def project(f, carry):
        qkv[f] = (dot_nn(normed[f], tri[...]) + tri_bias[...]).astype(BF)
        return carry

    lax.fori_loop(0, frames, project, 0)
    swap_normed.wait()
    lax.fori_loop(frames, 2 * frames, project, 0)
    tile = 16
    fix = temporal_fix(tile)

    def one(i, carry):
        at = pl.ds(pl.multiple_of(i * tile, tile), tile)

        def put(pair, value):
            cols = slice(pair * 128, pair * 128 + 128)
            both = value.reshape(2 * frames, tile, 128)
            mine[:, at, cols] = both[:frames]
            away[:, at, cols] = both[frames:]

        heads_forward(
            lambda part, pair: qkv[:, at, column(part, pair)].reshape(2 * frames * tile, 128),
            fix,
            att_scale,
            put,
        )
        return carry

    lax.fori_loop(0, padded // tile, one, 0)
    swap_mixed = remote(away, swap, send.at[1], recv.at[1], place.over_t())
    swap_mixed.start()
    loader.middle()
    swap_mixed.wait()

    def finish(f, carry):
        low = (
            dot_nt(mine[f], merge0[...]) + dot_nt(swap[f], merge1[...]) + merge_bias[...]
        ).astype(BF)
        joined[f] = low
        branch = dot_nn(low, mixing[...]) + mix_bias[...]
        out[f] = state[f] + branch
        return carry + square_sum(branch, valid[...])

    total = lax.fori_loop(0, frames, finish, jnp.zeros((1, 1), F32))
    sq[...] = jnp.broadcast_to(total, sq.shape)
    staging.flush()
    loader.end()


def temporal_stage(number, layer, state, valid, gain, shift, w, biases, load, att_scale):
    frames, padded, width = state.shape
    split = w["merge_t"][0].shape[1]
    shape = lambda dims, kind=BF: jax.ShapeDtypeStruct(dims, kind)
    ins = [state, valid, gain, shift, w["triple_t"], biases[0], *w["merge_t"], biases[1]]
    ins += [w["mixing"], biases[2]]
    return kernel_call(
        functools.partial(temporal_body, load, att_scale, layer),
        number,
        ins,
        [
            shape((frames, padded, width), F32),
            shape((frames, padded, width), F32),
            shape((frames, padded, 1), F32),
            shape((2 * frames, padded, width)),
            shape((2 * frames, padded, 3 * split)),
            shape((frames, padded, split)),
            shape((frames, padded, split)),
            shape((frames, padded, width)),
            shape((8, 128), F32),
        ],
        [pltpu.VMEM((frames, padded, split), BF)] + [pltpu.SemaphoreType.DMA((2,))] * 2,
        load,
        "temporal_forward",
        cores=True,
    )


def spatial_body(load, places, att_scale, layer, staging, *refs):
    ins, outs, scratch, loads = open_kernel(load, staging, refs, 0)
    count_ref, state, valid, gain, shift, tri0, tri1, bias0, bias1, merge0, merge1, out_bias = ins
    out, unit, scale, normed, qkv0, qkv1, mixed0, mixed1, sq = outs
    gain, shift = row_of(gain, 3 * layer + 1), row_of(shift, 3 * layer + 1)
    bias0, bias1 = row_of(bias0, layer), row_of(bias1, layer)
    out_bias = row_of(out_bias, 4 * layer + 2)
    place = Place(load.depth)
    loader = Loader(place, False, load, *loads)
    frames, padded, width = state.shape
    fix = spatial_fix(count_ref, padded, places)
    loader.begin()
    staging.fetch()

    def one(f, carry):
        low, u, s = norm_rows(state[f], gain[...], shift[...])
        normed[f] = low
        unit[f] = u
        scale[f] = s
        for tri, bias, qkv, mixed in (
            (tri0, bias0, qkv0, mixed0),
            (tri1, bias1, qkv1, mixed1),
        ):
            qkv[f] = (dot_nn(low, tri[...]) + bias[...]).astype(BF)

            def put(pair, value, mixed=mixed):
                mixed[f, :, pair * 128 : pair * 128 + 128] = value

            heads_forward(
                lambda part, pair, qkv=qkv: qkv[f, :, column(part, pair)], fix, att_scale, put
            )
        branch = dot_nt(mixed0[f], merge0[...]) + dot_nt(mixed1[f], merge1[...]) + out_bias[...]
        out[f] = state[f] + branch
        return carry + square_sum(branch, valid[...])

    cut = frames - 1
    total = lax.fori_loop(0, cut, one, jnp.zeros((1, 1), F32))
    loader.middle()
    total = lax.fori_loop(cut, frames, one, total)
    sq[...] = jnp.broadcast_to(total, sq.shape)
    staging.flush()
    loader.end()


def spatial_stage(number, layer, count_ref, state, valid, gain, shift, w, biases, load, places, att_scale):
    frames, padded, width = state.shape
    split = w["merge_s"][0].shape[1]
    shape = lambda dims, kind=BF: jax.ShapeDtypeStruct(dims, kind)
    ins = [count_ref, state, valid, gain, shift, *w["triple_s"], biases[0], biases[1]]
    ins += [*w["merge_s"], biases[2]]
    return kernel_call(
        functools.partial(spatial_body, load, places, att_scale, layer),
        number,
        ins,
        [
            shape((frames, padded, width), F32),
            shape((frames, padded, width), F32),
            shape((frames, padded, 1), F32),
            shape((frames, padded, width)),
            shape((frames, padded, 3 * split)),
            shape((frames, padded, 3 * split)),
            shape((frames, padded, split)),
            shape((frames, padded, split)),
            shape((8, 128), F32),
        ],
        [],
        load,
        "spatial_forward",
        1,
    )


def feed_body(load, layer, staging, *refs):
    ins, outs, scratch, loads = open_kernel(load, staging, refs, 0)
    state, valid, gain, shift, up0, up1, bias0, bias1, down0, down1, out_bias = ins
    out, unit, scale, normed, act0, act1, slope0, slope1, sq = outs
    gain, shift = row_of(gain, 3 * layer + 2), row_of(shift, 3 * layer + 2)
    bias0, bias1 = row_of(bias0, layer), row_of(bias1, layer)
    out_bias = row_of(out_bias, 4 * layer + 3)
    place = Place(load.depth)
    loader = Loader(place, False, load, *loads)
    frames, padded, width = state.shape
    loader.begin()
    staging.fetch()

    def one(f, carry):
        low, u, s = norm_rows(state[f], gain[...], shift[...])
        normed[f] = low
        unit[f] = u
        scale[f] = s
        branch = jnp.broadcast_to(out_bias[...], (padded, width))
        for up, bias, down, act, slope in (
            (up0, bias0, down0, act0, slope0),
            (up1, bias1, down1, act1, slope1),
        ):
            lanes = up.shape[1]
            piece = lanes // 3
            for number in range(3):
                cols = slice(number * piece, (number + 1) * piece)
                hidden = dot_nn(low, up[:, cols]) + bias[:, cols]
                below = 0.5 * (1.0 + lax.erf(hidden * root_half))
                act[f, :, cols] = (hidden * below).astype(BF)
                slope[f, :, cols] = (
                    below + hidden * gauss_scale * jnp.exp(-0.5 * hidden * hidden)
                ).astype(BF)
            branch = branch + dot_nt(act[f], down[...])
        value = state[f] + branch
        out[f] = value
        return (
            carry[0] + square_sum(branch, valid[...]),
            carry[1] + square_sum(value, valid[...]),
        )

    zero = jnp.zeros((1, 1), F32)
    cut = frames - 1
    total = lax.fori_loop(0, cut, one, (zero, zero))
    loader.middle()
    total = lax.fori_loop(cut, frames, one, total)
    sq[...] = jnp.broadcast_to(total[0], sq.shape)
    sq[0:1] = jnp.broadcast_to(total[1], (1, sq.shape[1]))
    staging.flush()
    loader.end()


def feed_stage(number, layer, state, valid, gain, shift, w, biases, load):
    frames, padded, width = state.shape
    hid = w["up"][0].shape[1]
    shape = lambda dims, kind=BF: jax.ShapeDtypeStruct(dims, kind)
    ins = [state, valid, gain, shift, *w["up"], biases[0], biases[1], *w["down"], biases[2]]
    return kernel_call(
        functools.partial(feed_body, load, layer),
        number,
        ins,
        [
            shape((frames, padded, width), F32),
            shape((frames, padded, width), F32),
            shape((frames, padded, 1), F32),
            shape((frames, padded, width)),
        ]
        + [shape((frames, padded, hid))] * 4
        + [shape((8, 128), F32)],
        [],
        load,
        "feed_forward",
    )


def feed_back_body(depth, starts, steps, layer, *refs):
    take = splitter(refs)
    count = len(starts)
    state, normed, unit, scale, gain = take(5)
    gain = row_of(gain, 3 * layer + 2)
    oth, own = take(4), take(4)
    parts = take(count)
    out, sums, g_up, g_down, h_own, h_oth = take(6)
    owns = take(count)
    r, rt, nt, bh, s_up, s_down, r_up, r_down, send, recv = take(10)
    place = Place(depth)
    carrier = Carrier(place, True, starts, parts, parts, owns, take(10 * count))
    frames, padded, width = state.shape
    rows_all = frames * padded
    i = pl.program_id(0)

    @pl.when(i == 0)
    def _():
        carrier.step(0)
        sums[...] = jnp.zeros_like(sums)

        def begin(f, carry):
            low = state[f].astype(BF)
            r[f] = low
            out[f] = jnp.zeros((padded, width), F32)
            return carry + column_sum(low.astype(F32))

        sums[2:3] = lax.fori_loop(0, frames, begin, jnp.zeros((1, width), F32))
        rt[...] = r[...].reshape(rows_all, width).T
        nt[...] = normed[...].reshape(rows_all, width).T

    def work(down, up, active, slope, h_sum):
        lanes = down.shape[1]

        def one(f, carry):
            value = (dot_nn(r[f], down[...]) * slope[f].astype(F32)).astype(BF)
            bh[f] = value
            out[f] += dot_nt(value, up[...])
            return carry + column_sum(value.astype(F32))

        h_sum[...] = lax.fori_loop(0, frames, one, jnp.zeros((1, lanes), F32))
        return (
            dot_nn(nt[...], bh[...].reshape(rows_all, lanes)),
            dot_nn(rt[...], active[...].reshape(rows_all, lanes)),
        )

    def swaps(j):
        return [
            remote(s_up.at[j], r_up.at[j], send.at[0, j], recv.at[0, j], place.over_t()),
            remote(s_down.at[j], r_down.at[j], send.at[1, j], recv.at[1, j], place.over_t()),
        ]

    @pl.when(i < steps)
    def _():
        up_part, down_part = work(*oth, h_oth)
        s_up[i] = up_part.astype(BF)
        s_down[i] = down_part.astype(BF)
        for item in swaps(i):
            item.start()

    for number, at in ((1, 1), (2, 3), (3, 4)):
        if count:

            @pl.when(i == at)
            def _(number=number):
                carrier.step(number)

    @pl.when(i >= steps)
    def _():
        j = i - steps
        up_part, down_part = work(*own, h_own)
        for item in swaps(j):
            item.wait()
        g_up[...] = (up_part + r_up[j].astype(F32)).astype(BF)
        g_down[...] = (down_part + r_down[j].astype(F32)).astype(BF)

    @pl.when(i == 2 * steps - 1)
    def _():
        def finish(f, carry):
            e, u = out[f], unit[f]
            out[f] = state[f] + norm_back_rows(e, u, scale[f], gain[...])
            return (carry[0] + column_sum(e * u), carry[1] + column_sum(e))

        zero = jnp.zeros((1, width), F32)
        sums[0:1], sums[1:2] = lax.fori_loop(0, frames, finish, (zero, zero))
        carrier.step(4)


def feed_back(grid, number, layer, state, kept, gain, w, parts):
    frames, padded, width = state.shape
    hid = w["up"][0].shape[1]
    steps = 3
    lanes = hid // steps
    cubes, shapes, scratch = carried(grid, parts)
    whole = lambda item: pl.BlockSpec(
        item.shape, lambda i: (0,) * item.ndim, pipeline_mode=pl.Buffered(1)
    )
    first = lambda i: jnp.minimum(i, steps - 1)
    later = lambda i: jnp.maximum(i - steps, 0)

    def side(at):
        weight = pl.BlockSpec((width, lanes), lambda i: (0, at(i)))
        token = pl.BlockSpec((frames, padded, lanes), lambda i: (0, 0, at(i)))
        return [weight, weight, token, token]

    tokens = lambda item: item.reshape(frames, padded, hid)
    sides = [
        [w["down"][k], w["up"][k], tokens(kept["active"][k]), tokens(kept["slope"][k])]
        for k in (1, 0)
    ]
    fixed = [state, kept["normed_m"], kept["unit_m"], kept["scale_m"], gain]
    vec = lambda at: pl.BlockSpec((1, lanes), lambda i: (0, at(i)))
    result = pl.pallas_call(
        functools.partial(feed_back_body, grid.depth, starts_of(parts), steps, layer),
        grid=(2 * steps,),
        in_specs=[whole(item) for item in fixed]
        + side(first)
        + side(later)
        + [whole(item) for item in cubes],
        out_specs=[
            pl.BlockSpec((frames, padded, width), lambda i: (0, 0, 0)),
            pl.BlockSpec((8, width), lambda i: (0, 0)),
            pl.BlockSpec((width, lanes), lambda i: (0, later(i))),
            pl.BlockSpec((width, lanes), lambda i: (0, later(i))),
            vec(later),
            vec(first),
        ]
        + [pl.BlockSpec(item.shape, lambda i: (0, 0)) for item in shapes],
        out_shape=[
            jax.ShapeDtypeStruct((frames, padded, width), F32),
            jax.ShapeDtypeStruct((8, width), F32),
            jax.ShapeDtypeStruct((width, hid), BF),
            jax.ShapeDtypeStruct((width, hid), BF),
            jax.ShapeDtypeStruct((1, hid), F32),
            jax.ShapeDtypeStruct((1, hid), F32),
        ]
        + shapes,
        scratch_shapes=[
            pltpu.VMEM((frames, padded, width), BF),
            pltpu.VMEM((width, frames * padded), BF),
            pltpu.VMEM((width, frames * padded), BF),
            pltpu.VMEM((frames, padded, lanes), BF),
        ]
        + [pltpu.VMEM((steps, width, lanes), BF)] * 4
        + [pltpu.SemaphoreType.DMA((2, steps))] * 2
        + scratch,
        compiler_params=stage_params(number),
        cost_estimate=stage_cost(24000000000),
        name="feed_back",
    )(*fixed, *sides[0], *sides[1], *cubes)
    return result[0], result[1], result[2:4], (result[4], result[5]), result[6:]


def spatial_back_body(depth, starts, places, att_scale, layer, staging, *refs):
    take = splitter(refs)
    count = len(starts)
    in_refs, out_refs = take(14 + count), take(5 + count)
    own_scratch, sum_scratch = take(13), take(10 * count)
    sources = in_refs[14:]
    in_refs, out_refs = staging.open(in_refs, out_refs, take(staging.count()))
    take = splitter(in_refs + out_refs + own_scratch + sum_scratch)
    (count_ref, state, merge0, merge1, mixed0, mixed1, qkv0, qkv1) = take(8)
    tri0, tri1, normed, unit, scale, gain = take(6)
    gain = row_of(gain, 3 * layer + 1)
    parts = take(count)
    out, sums, q_sums, g_tri, g_merge = take(5)
    owns = take(count)
    r, bm0, bm1, b0, b1, rt, nt, s_tri, r_tri, s_merge, r_merge, send, recv = take(13)
    place = Place(depth)
    carrier = Carrier(place, True, starts, sources, parts, owns, take(10 * count))
    frames, padded, width = state.shape
    rows_all = frames * padded
    split = merge0.shape[1]
    fix = spatial_fix(count_ref, padded, places)
    carrier.step(0)
    staging.fetch()

    def one(f, carry):
        low = state[f].astype(BF)
        r[f] = low
        for merge, bm, src, dst in ((merge0, bm0, qkv0, b0), (merge1, bm1, qkv1, b1)):
            bm[...] = dot_nn(low, merge[...]).astype(BF)

            def put(part, pair, value, dst=dst):
                dst[f, :, column(part, pair)] = value

            heads_backward(
                lambda part, pair, src=src: src[f, :, column(part, pair)],
                lambda pair, bm=bm: bm[:, pair * 128 : pair * 128 + 128],
                fix,
                att_scale,
                put,
            )
        return carry + column_sum(low.astype(F32))

    sums[...] = jnp.zeros_like(sums)
    q_sums[...] = jnp.zeros_like(q_sums)
    half = frames // 2
    total = lax.fori_loop(0, half, one, jnp.zeros((1, width), F32))
    carrier.step(1)
    sums[2:3] = lax.fori_loop(half, frames, one, total)
    carrier.step(2)
    rt[...] = r[...].reshape(rows_all, width).T
    nt[...] = normed[...].reshape(rows_all, width).T
    flat = lambda ref, part: ref[:, :, part * split : (part + 1) * split].reshape(rows_all, split)
    swap_tri = remote(s_tri, r_tri, send.at[0], recv.at[0], place.over_t())
    swap_merge = remote(s_merge, r_merge, send.at[1], recv.at[1], place.over_t())
    s_merge[...] = dot_nn(rt[...], mixed1[...]).astype(BF)
    swap_merge.start()
    for part in range(3):
        cols = slice(part * split, (part + 1) * split)
        s_tri[:, cols] = dot_nn(nt[...], flat(b1, part)).astype(BF)
    swap_tri.start()
    carrier.step(3)

    def finish(f, carry):
        e = dot_nt(b0[f], tri0[...]) + dot_nt(b1[f], tri1[...])
        u = unit[f]
        out[f] = state[f] + norm_back_rows(e, u, scale[f], gain[...])
        return (
            carry[0] + column_sum(e * u),
            carry[1] + column_sum(e),
            carry[2] + column_sum(b0[f].astype(F32)),
            carry[3] + column_sum(b1[f].astype(F32)),
        )

    zero, wide = jnp.zeros((1, width), F32), jnp.zeros((1, 3 * split), F32)
    sums[0:1], sums[1:2], mine, theirs = lax.fori_loop(
        0, frames, finish, (zero, zero, wide, wide)
    )
    for number, value in ((0, mine), (1, theirs)):
        q_sums[number : number + 1, :split] = value[:, :split]
        q_sums[number : number + 1, split:] = value[:, 2 * split :]
    swap_merge.wait()
    g_merge[...] = (dot_nn(rt[...], mixed0[...]) + r_merge[...].astype(F32)).astype(BF)
    swap_tri.wait()
    for part in range(3):
        cols = slice(part * split, (part + 1) * split)
        mine = dot_nn(nt[...], flat(b0, part))
        g_tri[:, cols] = (mine + r_tri[:, cols].astype(F32)).astype(BF)
    carrier.step(4)
    staging.flush()


def spatial_back(grid, number, layer, count_ref, state, kept, gain, w, parts, places, att_scale):
    frames, padded, width = state.shape
    split = w["merge_s"][0].shape[1]
    cubes, shapes, scratch = carried(grid, parts)
    flat = [item.reshape(frames * padded, split) for item in kept["mixed_s"]]
    fixed = [count_ref, state, *w["merge_s"], *flat, *kept["qkv_s"], *w["triple_s"]]
    fixed += [kept["normed_s"], kept["unit_s"], kept["scale_s"], gain]
    ins = fixed + cubes
    outs = [
        jax.ShapeDtypeStruct((frames, padded, width), F32),
        jax.ShapeDtypeStruct((8, width), F32),
        jax.ShapeDtypeStruct((8, 2 * split), F32),
        jax.ShapeDtypeStruct((width, 3 * split), BF),
        jax.ShapeDtypeStruct((width, split), BF),
    ] + shapes
    staging = Staging(1, ins, outs)
    result = pl.pallas_call(
        functools.partial(
            spatial_back_body, grid.depth, starts_of(parts), places, att_scale, layer, staging
        ),
        in_specs=staging.in_specs(),
        out_specs=staging.out_specs(),
        out_shape=outs,
        scratch_shapes=[pltpu.VMEM((frames, padded, width), BF)]
        + [pltpu.VMEM((padded, split), BF)] * 2
        + [pltpu.VMEM((frames, padded, 3 * split), BF)] * 2
        + [pltpu.VMEM((width, frames * padded), BF)] * 2
        + [pltpu.VMEM((width, 3 * split), BF)] * 2
        + [pltpu.VMEM((width, split), BF)] * 2
        + [pltpu.SemaphoreType.DMA((2,))] * 2
        + scratch
        + staging.scratch(),
        compiler_params=stage_params(number),
        cost_estimate=stage_cost(24000000000),
        name="spatial_stage",
    )(*ins)
    return result[0], result[1], result[2], result[3:5], result[5:]


def temporal_back_body(depth, starts, att_scale, layer, staging, pieces, joined_mix, *refs):
    take = splitter(refs)
    count = len(starts)
    chained = 1 if pieces else 0
    in_refs, small = take(13 + count), take(len(pieces))
    out_refs, total = take(6 + count), take(chained)
    own_scratch, sum_scratch, hop_refs = take(13), take(10 * count), take(4 * chained)
    mix_refs = take(3) if joined_mix else None
    sources = in_refs[13:]
    in_refs, out_refs = staging.open(in_refs, out_refs, take(staging.count()))
    take = splitter(in_refs + out_refs + own_scratch + sum_scratch)
    state, mixing, joined, merge0, merge1, mine, swap, qkv, tri = take(9)
    normed, unit, scale, gain = take(4)
    gain = row_of(gain, 3 * layer)
    parts = take(count)
    out, sums, q_sums, g_tri, g_merge, g_mix = take(6)
    owns = take(count)
    r, bj, away, bm, b, nt, rt, s_merge, r_merge, s_back, r_back, send, recv = take(13)
    joins = len(g_mix.shape) == 3
    if joins:
        (whole_mix, s_mix, r_mix), shard_mix = mix_refs, g_mix
    place = Place(depth)
    carrier = Carrier(place, True, starts, sources, parts, owns, take(10 * count))
    frames, padded, width = state.shape
    rows_all = frames * padded
    split = merge0.shape[1]
    carrier.step(0)
    hops = Hops(place, pieces, small, *total, *hop_refs) if chained else None
    if chained:
        hops.begin()
    staging.fetch()

    def begin(f, carry):
        low = state[f].astype(BF)
        r[f] = low
        value = dot_nt(low, mixing[...]).astype(BF)
        bj[f] = value
        bm[f] = dot_nn(value, merge0[...]).astype(BF)
        away[f] = dot_nn(value, merge1[...]).astype(BF)
        return (carry[0] + column_sum(low.astype(F32)), carry[1] + column_sum(value.astype(F32)))

    sums[...] = jnp.zeros_like(sums)
    q_sums[...] = jnp.zeros_like(q_sums)
    zero = jnp.zeros((1, width), F32)
    sums[3:4], sums[2:3] = lax.fori_loop(0, frames, begin, (zero, zero))
    swap_bm = remote(
        away, bm.at[pl.ds(frames, frames)], send.at[0], recv.at[0], place.over_t()
    )
    swap_bm.start()
    rt[...] = bj[...].reshape(rows_all, width).T
    s_merge[...] = dot_nn(rt[...], swap[...].reshape(rows_all, split)).astype(BF)
    swap_merge = remote(s_merge, r_merge, send.at[1], recv.at[1], place.over_t())
    swap_merge.start()
    carrier.step(1)
    if chained:
        hops.hop(1)
    rt[...] = joined[...].reshape(rows_all, width).T
    for half in range(2):
        cols = slice(half * split, (half + 1) * split)
        mix_part = dot_nn(rt[...], r[:, :, cols].reshape(rows_all, split))
        (whole_mix if joins else g_mix)[:, cols] = mix_part
    if joins:
        blocks, step = shard_mix.shape[0], shard_mix.shape[1]

        def mix_rows(k, core):
            at = pl.multiple_of((2 * k + core) * step, 8)
            return whole_mix[pl.ds(at, step), :]

        for k in range(blocks):
            s_mix[k] = mix_rows(k, 1 - place.t).astype(BF)
        swap_mix = remote(s_mix, r_mix, send.at[3], recv.at[3], place.over_t())
        swap_mix.start()
    rt[...] = bj[...].reshape(rows_all, width).T
    swap_merge.wait()
    g_merge[...] = (dot_nn(rt[...], mine[...].reshape(rows_all, split)) + r_merge[...].astype(F32)).astype(BF)
    swap_bm.wait()
    tile = 16
    fix = temporal_fix(tile)

    def one(i, carry):
        at = pl.ds(pl.multiple_of(i * tile, tile), tile)

        def put(part, pair, value):
            b[:, at, column(part, pair)] = value.reshape(FRAMES, tile, 128)

        heads_backward(
            lambda part, pair: qkv[:, at, column(part, pair)].reshape(FRAMES * tile, 128),
            lambda pair: bm[:, at, pair * 128 : pair * 128 + 128].reshape(FRAMES * tile, 128),
            fix,
            att_scale,
            put,
        )
        return carry

    tiles = padded // tile
    lax.fori_loop(0, tiles // 3, one, 0)
    if joins:
        swap_mix.wait()
        for k in range(blocks):
            shard_mix[k] = (mix_rows(k, place.t) + r_mix[k].astype(F32)).astype(BF)
    if chained:
        hops.hop(2)
    lax.fori_loop(tiles // 3, 2 * tiles // 3, one, 0)
    carrier.step(2)
    if chained:
        hops.hop(3)
    lax.fori_loop(2 * tiles // 3, tiles, one, 0)
    if chained:
        hops.hop(4)
    carrier.step(3)

    def toward(f, carry):
        s_back[f] = dot_nt(b[f + frames], tri[...]).astype(BF)
        return carry

    lax.fori_loop(0, frames, toward, 0)
    swap_back = remote(s_back, r_back, send.at[2], recv.at[2], place.over_t())
    swap_back.start()
    nt[...] = normed[...].reshape(2 * rows_all, width).T
    for part in range(3):
        cols = slice(part * split, (part + 1) * split)
        g_tri[:, cols] = dot_nn(
            nt[...], b[:, :, cols].reshape(2 * rows_all, split)
        ).astype(BF)
    swap_back.wait()

    def finish(f, carry):
        e = dot_nt(b[f], tri[...]) + r_back[f].astype(F32)
        u = unit[f]
        out[f] = state[f] + norm_back_rows(e, u, scale[f], gain[...])
        both = column_sum(b[f].astype(F32)) + column_sum(b[f + frames].astype(F32))
        return (carry[0] + column_sum(e * u), carry[1] + column_sum(e), carry[2] + both)

    sums[0:1], sums[1:2], wide = lax.fori_loop(
        0, frames, finish, (zero, zero, jnp.zeros((1, 3 * split), F32))
    )
    q_sums[0:1, :split] = wide[:, :split]
    q_sums[0:1, split:] = wide[:, 2 * split :]
    if chained:
        hops.hop(5)
    carrier.step(4)
    staging.flush()


def temporal_back(grid, number, layer, state, kept, gain, w, parts, att_scale, small=None):
    frames, padded, width = state.shape
    split = w["merge_t"][0].shape[1]
    cubes, shapes, scratch = carried(grid, parts)
    fixed = [state, w["mixing"], kept["joined"], *w["merge_t"], *kept["mixed_t"], kept["qkv_t"]]
    fixed += [w["triple_t"], kept["normed_t"], kept["unit_t"], kept["scale_t"], gain]
    ins = fixed + cubes
    outs = [
        jax.ShapeDtypeStruct((frames, padded, width), F32),
        jax.ShapeDtypeStruct((8, width), F32),
        jax.ShapeDtypeStruct((8, 2 * split), F32),
        jax.ShapeDtypeStruct((width, 3 * split), BF),
        jax.ShapeDtypeStruct((width, split), BF),
        jax.ShapeDtypeStruct((width, width), F32),
    ] + shapes
    mix_scratch = []
    if grid.direct:
        step = width // (4 * grid.depth) // 2
        outs[5] = jax.ShapeDtypeStruct((4 * grid.depth, step, width), BF)
        mix_scratch = [pltpu.VMEM((width, width), F32)]
        mix_scratch += [pltpu.VMEM((4 * grid.depth, step, width), BF)] * 2
    staging = Staging(0, ins, outs)
    pieces = small.pieces if small else []
    chained = 1 if small else 0
    result = pl.pallas_call(
        functools.partial(
            temporal_back_body, grid.depth, starts_of(parts), att_scale, layer, staging, pieces, grid.direct
        ),
        in_specs=staging.in_specs() + [VMEM_SPEC] * len(pieces),
        out_specs=staging.out_specs() + [VMEM_SPEC] * chained,
        out_shape=outs + ([small.shape()] if small else []),
        scratch_shapes=[pltpu.VMEM((frames, padded, width), BF)] * 2
        + [pltpu.VMEM((frames, padded, split), BF)]
        + [pltpu.VMEM((2 * frames, padded, split), BF)]
        + [pltpu.VMEM((2 * frames, padded, 3 * split), BF)]
        + [pltpu.VMEM((width, 2 * frames * padded), BF)]
        + [pltpu.VMEM((width, frames * padded), BF)]
        + [pltpu.VMEM((width, split), BF)] * 2
        + [pltpu.VMEM((frames, padded, width), BF)] * 2
        + [pltpu.SemaphoreType.DMA((4,))] * 2
        + scratch
        + (hop_scratch(small) if chained else [])
        + mix_scratch
        + staging.scratch(),
        compiler_params=stage_params(number, 60),
        cost_estimate=stage_cost(24000000000),
        name="temporal_stage",
    )(*ins, *(small.arrays if small else []))
    end = 6 + len(parts)
    return result[0], result[1], result[2], result[3:6], result[6:end], result[end:]


def plain_sums(parts):
    return [
        lax.psum_scatter(part.astype(F32), ("shard", "ctx"), scatter_dimension=0, tiled=True)
        for part in parts
    ]


def split_columns(value, widths):
    outs, start = [], 0
    for width in widths:
        outs.append(value[..., start : start + width])
        start += width
    return outs


def per_device(
    video_clips,
    cotangent,
    slot_clip,
    valid_places,
    norm_gain,
    norm_bias,
    triple_weight,
    entry_bias,
    merge_weight,
    branch_bias,
    mixing_weight,
    up_weight,
    up_bias,
    down_weight,
):
    grid = Grid()
    slots, frames_here, places_here, width = video_clips.shape
    places = places_here * 2
    padded = -(-places // 16) * 16
    scale = HEAD_DIM ** (-0.5)
    step_rows = triple_weight.shape[2]
    half_rows = step_rows // 2
    own_first = grid.t == 0
    straight = grid.t == grid.y

    clip_ids = jnp.arange(valid_places.shape[0], dtype=jnp.int32)
    my_clip = lax.dynamic_index_in_dim(slot_clip, grid.y, 0, keepdims=False)
    count = jnp.sum(jnp.where(my_clip == clip_ids, valid_places, 0)).astype(jnp.int32)
    valid_here = (jnp.arange(padded, dtype=jnp.int32) < count).astype(F32)[None, :, None]
    count_ref = count.reshape(1)

    def spread_in(value):
        mine = lax.dynamic_index_in_dim(value, grid.y, 0, keepdims=False)
        theirs = lax.dynamic_index_in_dim(value, 1 - grid.y, 0, keepdims=False)
        return spread_in_last(mine, grid.over_y(theirs))

    def spread_in_last(mine, got):
        keep = jnp.where(straight, mine, got)
        send = jnp.where(straight, got, mine)
        swap = grid.over_t(send)
        low = jnp.where(own_first, keep, swap)
        high = jnp.where(own_first, swap, keep)
        gap = jnp.zeros((frames_here, padded - places, width), mine.dtype)
        return jnp.concatenate([low, high, gap], axis=1)

    def spread_first(value):
        low = value[:, :places_here]
        high = value[:, places_here:places]
        keep = jnp.where(own_first, low, high)
        send = jnp.where(own_first, high, low)
        swap = grid.over_t(send)
        return jnp.where(straight, swap, keep), jnp.where(straight, keep, swap)

    def spread_last(got, mine):
        first = jnp.where(grid.y == 0, mine, got)
        second = jnp.where(grid.y == 0, got, mine)
        return jnp.stack([first, second])

    def spread_out(value):
        away, mine = spread_first(value)
        return spread_last(grid.over_y(away), mine)

    def pack_mix(item):
        return jnp.concatenate([item[..., : width // 2], item[..., width // 2 :]], axis=-2)

    def block_triple(layer, part):
        return [triple_weight[layer, part, :, i] for i in range(3)]

    def block_out(layer):
        return [merge_weight[layer, 0].T, pack_mix(mixing_weight[layer])]

    def block_s(layer):
        return block_triple(layer, 1) + [merge_weight[layer, 1].T]

    def block_m(layer):
        return [up_weight[layer], down_weight[layer].T]

    split = triple_weight.shape[-1]
    hid = up_weight.shape[-1]
    wide_t = (3 * split, split, width // 2)
    wide_s = (3 * split, split)
    wide_m = (hid, hid)

    def unpack_mix(item):
        cube = item.reshape(-1, 2, half_rows, width // 2)
        return jnp.concatenate([cube[:, 0], cube[:, 1]], axis=-1)

    def with_other(item):
        return (item, grid.over_t(item))

    def mixing_of(both):
        mix_own, mix_oth = [unpack_mix(item) for item in both]
        return jnp.stack(
            [jnp.where(own_first, mix_own, mix_oth), jnp.where(own_first, mix_oth, mix_own)],
            axis=1,
        ).reshape(width, width)

    def block_named(layer, name):
        if name == "triple_t":
            return jnp.concatenate(block_triple(layer, 0), axis=1)
        if name == "triple_s":
            return jnp.concatenate(block_triple(layer, 1), axis=1)
        if name == "merge_t":
            return merge_weight[layer, 0].T
        if name == "mix":
            return mixing_weight[layer] if grid.direct else pack_mix(mixing_weight[layer])
        if name == "merge_s":
            return merge_weight[layer, 1].T
        return block_m(layer)[0 if name == "up" else 1]

    gathered = [dict() for _ in range(LAYERS)]

    def settle(keys, near):
        for (layer, name), both in zip(keys, near):
            w = gathered[layer]
            if name == "triple_t":
                w[name] = both[0]
            elif name == "mix":
                w["mixing"] = both[0] if grid.direct else mixing_of(both)
            else:
                w[name] = both

    ahead = [
        [(0, "triple_t"), (0, "merge_t"), (0, "mix")],
        [(0, "triple_s"), (0, "merge_s"), (0, "up")],
        [(0, "down")],
        [(1, "triple_t"), (1, "merge_t"), (1, "mix")],
        [(1, "triple_s"), (1, "merge_s"), (1, "up")],
        [(1, "down")],
        [],
        [],
    ]
    named = lambda keys: [block_named(*key) for key in keys]
    modes = {"triple_t": False, "mix": "one"}
    modes_of = lambda keys: [modes.get(name, True) for _, name in keys]
    lines = {}
    if grid.direct:
        near, lines[1] = first_gather(
            grid, 7, named(ahead[0]), modes_of(ahead[0]), named(ahead[1])
        )
        settle(ahead[0], near)
    else:
        for keys in ahead:
            settle(
                keys,
                [
                    with_other(lax.all_gather(item, ("shard", "ctx"), axis=0, tiled=True))
                    for item in named(keys)
                ],
            )

    def load_at(index):
        across = [far_cotangent] if index == 3 * LAYERS - 1 and grid.direct else []
        if not grid.direct:
            return Load(grid)
        keys = ahead[index + 1]
        swapped = modes_of(keys)
        near = lines[index + 1] if keys else []
        return Load(grid, near, swapped, named(ahead[index + 2]), across)

    def loaded(index, got):
        near, new_lines = got
        if index == 3 * LAYERS - 1:
            lines["across"] = new_lines[0] if grid.direct else grid.over_y(far_cotangent)
        elif grid.direct:
            settle(ahead[index + 1], near)
            lines[index + 2] = new_lines

    small = jnp.concatenate([entry_bias[:, 1].reshape(LAYERS, -1), up_bias], axis=1)
    small_oth = grid.over_t(small)
    middle = jnp.zeros((LAYERS, split), F32)

    def query_value(both):
        return jnp.concatenate([both[:, :split], middle, both[:, split : 2 * split]], axis=1)

    gains, shifts = [item.reshape(3 * LAYERS, width) for item in (norm_gain, norm_bias)]
    biases = branch_bias.reshape(4 * LAYERS, width)
    bias_t = query_value(entry_bias[:, 0].reshape(LAYERS, -1))
    bias_s = [query_value(item) for item in (small, small_oth)]
    bias_m = [up_bias, small_oth[:, 2 * split :]]

    state = spread_in(video_clips).astype(F32)
    valid_rows = valid_here[0]
    low_cotangent = cotangent.astype(BF)
    near_cotangent = lax.dynamic_index_in_dim(low_cotangent, grid.y, 0, keepdims=False)
    far_cotangent = lax.dynamic_index_in_dim(low_cotangent, 1 - grid.y, 0, keepdims=False)
    stored = []
    squares = []
    for layer in range(LAYERS):
        w = gathered[layer]
        first = 3 * layer
        (state, unit_t, scale_t, normed_t, qkv_t, mine, swap, joined, sq_t), got = temporal_stage(
            8 + first,
            layer,
            state,
            valid_rows,
            gains,
            shifts,
            w,
            [bias_t, biases, biases],
            load_at(first),
            scale,
        )
        loaded(first, got)
        (state, unit_s, scale_s, normed_s, qkv0, qkv1, mixed0, mixed1, sq_s), got = spatial_stage(
            9 + first,
            layer,
            count_ref,
            state,
            valid_rows,
            gains,
            shifts,
            w,
            bias_s + [biases],
            load_at(first + 1),
            places,
            scale,
        )
        loaded(first + 1, got)
        (state, unit_m, scale_m, normed_m, act0, act1, slope0, slope1, sq_m), got = feed_stage(
            10 + first,
            layer,
            state,
            valid_rows,
            gains,
            shifts,
            w,
            bias_m + [biases],
            load_at(first + 2),
        )
        loaded(first + 2, got)
        squares.append((sq_t, sq_s, sq_m))
        stored.append(
            dict(
                unit_t=unit_t,
                scale_t=scale_t,
                normed_t=normed_t,
                qkv_t=qkv_t,
                mixed_t=(mine, swap),
                joined=joined,
                unit_s=unit_s,
                scale_s=scale_s,
                normed_s=normed_s,
                qkv_s=[qkv0, qkv1],
                mixed_s=[mixed0, mixed1],
                unit_m=unit_m,
                scale_m=scale_m,
                normed_m=normed_m,
                active=[act0, act1],
                slope=[slope0, slope1],
            )
        )
    upstream = spread_in_last(near_cotangent, lines["across"]).astype(F32) * valid_here
    block_output = spread_out(state.astype(BF))

    shards = [None] * LAYERS
    sums = {}
    vectors, half_rows_of = [None] * LAYERS, [None] * LAYERS
    waiting = None

    def both_cores(mine, theirs):
        return [jnp.where(own_first, mine, theirs), jnp.where(own_first, theirs, mine)]

    def carry_sums(names, parts):
        nonlocal waiting
        if not grid.direct:
            sums.update(
                zip(names, plain_sums([item[:, start : start + size] for item, start, size in parts]))
            )
            return
        waiting = (names, parts)

    def carried_parts():
        return waiting[1] if waiting else []

    def arrived_sums(result):
        nonlocal waiting
        if waiting:
            sums.update(zip(waiting[0], result))
        waiting = None

    for layer in range(LAYERS - 1, -1, -1):
        w, kept = gathered[layer], stored[layer]
        upstream, vec_m, parts_m, hidden_part, got = feed_back(
            grid, layer, layer, upstream, kept, gains, w, carried_parts()
        )
        arrived_sums(got)
        cut = hid // 2
        carry_sums(
            [("up", layer), ("down_a", layer)], [(parts_m[0], 0, hid), (parts_m[1], 0, cut)]
        )
        upstream, vec_s, entry_s, parts_s, got = spatial_back(
            grid,
            2 + layer,
            layer,
            count_ref,
            upstream,
            kept,
            gains,
            w,
            carried_parts(),
            places,
            scale,
        )
        arrived_sums(got)
        carry_sums(
            [("triple_s", layer), ("down_b", layer), ("merge_s", layer)],
            [(parts_s[0], 0, 3 * split), (parts_m[1], cut, cut), (parts_s[1], 0, split)],
        )
        per_row = hid // width
        hidden_rows = [item.reshape(per_row, width) for item in hidden_part]
        half_rows_of[layer] = both_cores(
            jnp.concatenate([entry_s[:1], hidden_rows[0]]),
            jnp.concatenate([entry_s[1:2], hidden_rows[1]]),
        )
        vectors[layer] = [vec_s, vec_m]
        early = None
        if layer == 0:
            early = Small(width)
            for vec_pair in vectors:
                early.add(vec_pair[0], 0, 3)
                early.add(vec_pair[1], 0, 3)
            early.add(last_vec, 0, 4)
            for item in half_rows_of:
                early.add(item[0], 0, 3)
                early.add(item[1], 0, 3)
            for item in last_half:
                early.add(item, 0, 1)
            for sq_t, sq_s, sq_m in squares:
                for place_at, (item, start) in enumerate(
                    ((sq_t, 0), (sq_s, 0), (sq_m, 1), (sq_m, 0))
                ):
                    early.add(item, start, 1, 128 * place_at, place_at < 3)
        early_rows = early
        upstream, vec_t, entry_t, parts_t, got, early = temporal_back(
            grid,
            4 + layer,
            layer,
            upstream,
            kept,
            gains,
            w,
            carried_parts(),
            scale,
            early if grid.direct else None,
        )
        arrived_sums(got)
        if grid.direct:
            mix_sum = parts_t[2].reshape(width // 2, width)
        else:
            mix_part = parts_t[2].reshape(-1, 2, half_rows, width)
            mix_mine = lax.dynamic_index_in_dim(mix_part, grid.t, 1, keepdims=False)
            mix_theirs = lax.dynamic_index_in_dim(mix_part, 1 - grid.t, 1, keepdims=False)
            mix_got = grid.over_t(mix_theirs.astype(BF)).astype(F32)
            mix_sum = (mix_mine + mix_got).astype(BF).reshape(width // 2, width)
        carry_sums(
            [("triple_t", layer), ("merge_t", layer), ("mix", layer)],
            [(parts_t[0], 0, 3 * split), (parts_t[1], 0, split), (mix_sum, 0, width)],
        )
        last_vec = vec_t
        last_half = both_cores(entry_t[:1], jnp.zeros_like(entry_t[:1]))

    small = Small(width)
    small.add(last_vec, 0, 4)
    for item in last_half:
        small.add(item, 0, 1)
    out_low, out_ready = spread_first(upstream.astype(BF))
    if waiting:
        got, small, out_got = tail_sums(grid, 6, carried_parts(), small, out_low)
        arrived_sums(got)
        (early,) = early
    else:
        small, early = small.plain(), early_rows.plain()
        out_got = grid.over_y(out_low)
    input_grad = spread_last(out_got, out_ready).astype(F32)
    names = ("triple_t", "merge_t", "mix", "triple_s", "merge_s", "up")
    for layer in range(LAYERS):
        down = jnp.concatenate([sums["down_a", layer], sums["down_b", layer]], axis=1)
        shards[layer] = [sums[name, layer] for name in names] + [down]
    block = 6 * LAYERS
    pairs = early[:block].reshape(LAYERS, 2, 3, width)
    ends = jnp.stack([small[:4], early[block : block + 4]])
    gain_sum, shift_sum = [
        jnp.concatenate([ends[:, k : k + 1], pairs[:, :, k]], axis=1) for k in range(2)
    ]
    bias_sum = jnp.concatenate([ends[:, 2:4], pairs[:, :, 2]], axis=1)
    start = block + 4
    half_sums = early[start : start + 6 * LAYERS].reshape(LAYERS, 2, 3, width)
    end_sums = jnp.stack([small[4:6], early[start + 6 * LAYERS : start + 6 * LAYERS + 2]])
    half_sums = lax.dynamic_index_in_dim(half_sums, grid.t, 1, keepdims=False)
    end_sums = lax.dynamic_index_in_dim(end_sums, grid.t, 1, keepdims=False)
    entry_sum = jnp.stack([end_sums, half_sums[:, 0]], axis=1).reshape(LAYERS, 2, 2, split)
    hidden_sum = half_sums[:, 1:].reshape(LAYERS, hid)
    start = start + 6 * LAYERS + 2
    square_sums = early[start : start + LAYERS, : 4 * 128].reshape(LAYERS, 4, 128)[:, :, 0]
    tokens = FRAMES * width * jnp.sum(valid_places).astype(F32)
    root_squares = jnp.sqrt(square_sums / tokens)

    def triple_shape(item):
        return item.reshape(step_rows, 3, split)

    return (
        block_output,
        input_grad,
        gain_sum,
        shift_sum,
        jnp.stack([jnp.stack([triple_shape(s[0]), triple_shape(s[3])]) for s in shards]),
        entry_sum,
        jnp.stack([jnp.stack([s[1].T, s[4].T]) for s in shards]),
        bias_sum,
        jnp.stack([s[2] for s in shards]),
        jnp.stack([s[5] for s in shards]),
        hidden_sum,
        jnp.stack([s[6].T for s in shards]),
        root_squares,
    )


def solution(mesh):
    return jax.shard_map(
        per_device,
        mesh=mesh,
        in_specs=(
            P("shard", "ctx", "tp", None),
            P("shard", "ctx", "tp", None),
            P("shard"),
            P(),
            P(),
            P(),
            P(None, None, ("shard", "ctx"), None, "tp"),
            P(None, None, None, "tp"),
            P(None, None, "tp", ("shard", "ctx")),
            P(),
            P(None, ("shard", "ctx", "tp"), None),
            P(None, ("shard", "ctx"), "tp"),
            P(None, "tp"),
            P(None, "tp", ("shard", "ctx")),
        ),
        out_specs=(
            P("shard", "ctx", "tp", None),
            P("shard", "ctx", "tp", None),
            P(),
            P(),
            P(None, None, ("shard", "ctx"), None, "tp"),
            P(None, None, None, "tp"),
            P(None, None, "tp", ("shard", "ctx")),
            P(),
            P(None, ("shard", "ctx", "tp"), None),
            P(None, ("shard", "ctx"), "tp"),
            P(None, "tp"),
            P(None, "tp", ("shard", "ctx")),
            P(),
        ),
        check_vma=False,
    )
```

```python
import functools
import math

import jax
import jax.numpy as jnp
from jax import lax
from jax.experimental import pallas as pl
from jax.experimental.pallas import tpu as pltpu
from jax.sharding import PartitionSpec as P

HEAD_DIM = 64
FRAMES = 8
LAYERS = 2
AXES = ("shard", "ctx", "tp")
BF = jnp.bfloat16
F32 = jnp.float32

far_below = -1000000000.0
epsilon = 1e-06
root_half = 0.7071067811865476
gauss_scale = 0.3989422804014327


def dot_nn(left, right):
    return lax.dot_general(left, right, (((1,), (0,)), ((), ())), preferred_element_type=F32)


def dot_nt(left, right):
    return lax.dot_general(left, right, (((1,), (1,)), ((), ())), preferred_element_type=F32)


def dot_tn(left, right):
    return lax.dot_general(left, right, (((0,), (0,)), ((), ())), preferred_element_type=F32)


def rows(value):
    return value.reshape(-1, value.shape[-1])


def row_total(value):
    return jnp.sum(rows(value).astype(F32), axis=0)


def lane_masks(shape):
    lane = lax.broadcasted_iota(jnp.int32, shape, 1)
    return lane < HEAD_DIM


def softmax_rows(scores):
    top = jnp.max(scores, axis=-1, keepdims=True)
    raised = jnp.exp(scores - top)
    total = jnp.sum(raised, axis=-1, keepdims=True)
    return raised * (1.0 / total)


def sides(value, first):
    zero = jnp.zeros_like(value)
    return [jnp.where(first, value, zero), jnp.where(first, zero, value)]


def heads_forward(qkv, fix, scale, put):
    first = lane_masks(qkv(0, 0).shape)
    scores = []
    for pair in range(3):
        k = qkv(1, pair)
        scores.append([dot_nt(q, k) for q in sides(qkv(0, pair), first)])
    shares = [[softmax_rows(fix(item * scale)).astype(BF) for item in both] for both in scores]
    for pair in range(3):
        v = qkv(2, pair)
        outs = [dot_nn(item, v) for item in shares[pair]]
        put(pair, jnp.where(first, outs[0], outs[1]).astype(BF))


def heads_backward(qkv, back, fix, scale, put):
    first = lane_masks(qkv(0, 0).shape)
    scores, backs = [], []
    for pair in range(3):
        k, v = qkv(1, pair), qkv(2, pair)
        scores.append([dot_nt(q, k) for q in sides(qkv(0, pair), first)])
        backs.append([dot_nt(b, v) for b in sides(back(pair), first)])
    low_shares, low_scores = [], []
    for pair in range(3):
        low_shares.append([])
        low_scores.append([])
        for side in range(2):
            shares = softmax_rows(fix(scores[pair][side] * scale))
            back_shares = backs[pair][side]
            inner = jnp.sum(back_shares * shares, axis=-1, keepdims=True)
            low_scores[pair].append((shares * (back_shares - inner)).astype(BF))
            low_shares[pair].append(shares.astype(BF))
    for pair in range(3):
        q, k, bm = qkv(0, pair), qkv(1, pair), back(pair)
        gq = [dot_nn(item, k) for item in low_scores[pair]]
        gk = [dot_tn(item, q) for item in low_scores[pair]]
        gv = [dot_tn(item, bm) for item in low_shares[pair]]
        put(0, pair, (jnp.where(first, gq[0], gq[1]) * scale).astype(BF))
        put(1, pair, (jnp.where(first, gk[0], gk[1]) * scale).astype(BF))
        put(2, pair, jnp.where(first, gv[0], gv[1]).astype(BF))


def column(part, pair):
    start = part * 384 + pair * 128
    return slice(start, start + 128)


def spatial_fix(count_ref, padded, places):
    col = lax.broadcasted_iota(jnp.int32, (padded, padded), 1)
    floor = jnp.where(col < places, far_below, 3.0 * far_below)
    allowed = col < jnp.minimum(count_ref[0], places)
    return lambda scores: jnp.where(allowed, scores, floor)


def temporal_fix(tile):
    size = FRAMES * tile
    row = lax.broadcasted_iota(jnp.int32, (size, size), 0)
    col = lax.broadcasted_iota(jnp.int32, (size, size), 1)
    same = (row & (tile - 1)) == (col & (tile - 1))
    return lambda scores: jnp.where(same, scores, 3.0 * far_below)


class Grid:
    def __init__(self):
        self.shards = lax.axis_size("shard")
        self.depth = self.shards // 2
        shard = lax.axis_index("shard")
        self.z = shard // 2
        self.x = shard % 2
        self.y = lax.axis_index("ctx")
        self.t = lax.axis_index("tp")
        self.direct = self.depth == 4

    def perm(self, move):
        pairs = []
        for z in range(self.depth):
            for x in range(2):
                for y in range(2):
                    for t in range(2):
                        tz, tx, ty, tt = move(z, x, y, t)
                        pairs.append(
                            (((z * 2 + x) * 2 + y) * 2 + t, ((tz * 2 + tx) * 2 + ty) * 2 + tt)
                        )
        return pairs

    def send(self, value, pairs):
        return lax.ppermute(value, AXES, pairs)

    def over_x(self, value):
        return self.send(value, self.perm(lambda z, x, y, t: (z, 1 - x, y, t)))

    def over_y(self, value):
        return self.send(value, self.perm(lambda z, x, y, t: (z, x, 1 - y, t)))

    def over_t(self, value):
        return self.send(value, self.perm(lambda z, x, y, t: (z, x, y, 1 - t)))

    def over_z(self, value, step):
        depth = self.depth
        return self.send(value, self.perm(lambda z, x, y, t: ((z + step) % depth, x, y, t)))

    def over_bit(self, value, bit):
        pairs = []
        for s in range(self.shards):
            for y in range(2):
                for t in range(2):
                    pairs.append(((s * 2 + y) * 2 + t, ((s ^ bit) * 2 + y) * 2 + t))
        return self.send(value, pairs)

    def total(self, value, across):
        if across:
            value = value + self.over_t(value)
        value = value + self.over_y(value)
        bit = 1
        while bit < self.shards:
            value = value + self.over_bit(value, bit)
            bit *= 2
        return value


class Sums:
    def __init__(self, place, source, part, own, ra, rb, sx, sy, rx, ry, low, gz, send, recv):
        self.place, self.source, self.part, self.own = place, source, part, own
        self.ra, self.rb, self.sx, self.sy = ra, rb, sx, sy
        self.rx, self.ry, self.low, self.gz = rx, ry, low, gz
        self.send, self.recv = send, recv
        self.depth = part.shape[0]
        self.half = part.shape[0] // 2

    def copy(self, number, src, dst, target):
        return remote(src, dst, self.send.at[number], self.recv.at[number], target)

    def far(self):
        x, y = self.place.x, self.place.y
        low, high = pl.ds(0, self.half), pl.ds(self.half, self.half)
        return [
            self.copy(0, self.source.at[low, 1 - x, 1 - y], self.ra, self.place.over_y()),
            self.copy(1, self.source.at[high, 1 - x, 1 - y], self.rb, self.place.over_x()),
        ]

    def near(self):
        return [
            self.copy(2, self.sx, self.rx, self.place.over_x()),
            self.copy(3, self.sy, self.ry, self.place.over_y()),
        ]

    def deep(self):
        return [
            self.copy(
                3 + k,
                self.low.at[lax.rem(self.place.z + k, self.depth)],
                self.gz.at[k - 1],
                self.place.over_z(k),
            )
            for k in range(1, self.depth)
        ]

    def first(self):
        for item in self.far():
            item.start()

    def second(self):
        x, y, half = self.place.x, self.place.y, self.half
        for item in self.far():
            item.wait()
        for k in range(2 * half):
            toward_x, toward_y = self.part[k, 1 - x, y], self.part[k, x, 1 - y]
            if k < half:
                toward_x = toward_x + self.ra[k]
            else:
                toward_y = toward_y + self.rb[k - half]
            self.sx[k] = toward_x
            self.sy[k] = toward_y
        for item in self.near():
            item.start()

    def kept(self, k):
        mine = self.part[k, self.place.x, self.place.y].astype(F32)
        return mine + self.rx[k].astype(F32) + self.ry[k].astype(F32)

    def third(self):
        for item in self.near():
            item.wait()
        for k in range(self.depth):
            mine = self.part[k, self.place.x, self.place.y]
            self.low[k] = mine + (self.rx[k] + self.ry[k])
        for item in self.deep():
            item.start()

    def last(self):
        for item in self.deep():
            item.wait()
        total = self.kept(self.place.z)
        for k in range(self.depth - 1):
            total = total + self.gz[k].astype(F32)
        self.own[...] = total


def remote(src, dst, send, recv, target):
    return pltpu.make_async_remote_copy(
        src_ref=src,
        dst_ref=dst,
        send_sem=send,
        recv_sem=recv,
        device_id=target,
        device_id_type=pl.DeviceIdType.MESH,
    )


class Place:
    def __init__(self, depth):
        self.depth = depth
        shard = lax.axis_index("shard")
        self.z = shard // 2
        self.x = lax.rem(shard, 2)
        self.y = lax.axis_index("ctx")
        self.t = lax.axis_index("tp")

    def over_x(self):
        return {"shard": self.z * 2 + 1 - self.x}

    def over_y(self):
        return {"ctx": 1 - self.y}

    def over_t(self):
        return {"tp": 1 - self.t}

    def over_z(self, step):
        return {"shard": lax.rem(self.z + step, self.depth) * 2 + self.x}

    def meet(self, chips, cores):
        barrier = pltpu.get_barrier_semaphore()
        targets = [self.over_t()] if cores else []
        if chips:
            targets += [self.over_x(), self.over_y()]
            targets += [self.over_z(k) for k in range(1, self.depth)]
        for target in targets:
            pl.semaphore_signal(
                barrier, inc=1, device_id=target, device_id_type=pl.DeviceIdType.MESH
            )
        pl.semaphore_wait(barrier, len(targets))


class Carrier:
    def __init__(self, place, cores, starts, sources, parts, owns, scratch, most=2):
        self.place, self.cores = place, cores
        lanes = [pl.ds(start, own.shape[1]) for start, own in zip(starts, owns)]
        sources = [ref.at[:, :, :, :, cols] for ref, cols in zip(sources, lanes)]
        parts = [ref.at[:, :, :, :, cols] for ref, cols in zip(parts, lanes)]
        self.sums = [
            Sums(place, source, part, own, *scratch[10 * i : 10 * i + 10])
            for i, (source, part, own) in enumerate(zip(sources, parts, owns))
        ]
        self.groups = [[item] for item in self.sums[: most - 1]]
        if self.sums[most - 1 :]:
            self.groups.append(self.sums[most - 1 :])

    def begin(self):
        self.place.meet(bool(self.sums), self.cores)
        for item in self.sums:
            item.first()

    def step(self, number):
        if number == 0:
            self.begin()
            return
        last = len(self.groups)
        if 2 <= number <= last + 1:
            for item in self.groups[number - 2]:
                item.third()
        if number <= last:
            for item in self.groups[number - 1]:
                item.second()

    def end(self):
        for item in self.sums:
            item.last()


def carried(grid, parts):
    depth = grid.depth
    cubes, shapes, scratch = [], [], []
    for part, start, lanes in parts:
        step_rows = part.shape[0] // (depth * 4)
        block = lambda count: pltpu.VMEM((count, step_rows, lanes), BF)
        cubes.append(part.reshape(depth, 2, 2, step_rows, part.shape[1]))
        shapes.append(jax.ShapeDtypeStruct((step_rows, lanes), F32))
        scratch += [block(depth // 2)] * 2 + [block(depth)] * 5 + [block(depth - 1)]
        scratch += [pltpu.SemaphoreType.DMA((3 + depth,))] * 2
    return cubes, shapes, scratch


def stage_params(number, vmem=58, sends=True):
    if not sends:
        return pltpu.CompilerParams(vmem_limit_bytes=vmem << 20)
    return pltpu.CompilerParams(
        collective_id=number, has_side_effects=True, vmem_limit_bytes=vmem << 20
    )


def stage_cost(flops):
    return pl.CostEstimate(flops=flops, bytes_accessed=30000000, transcendentals=0)


VMEM_SPEC = pl.BlockSpec(memory_space=pltpu.VMEM)
SMEM_SPEC = pl.BlockSpec(memory_space=pltpu.SMEM)


ANY_SPEC = pl.BlockSpec(memory_space=pl.ANY)


def is_big(item):
    return item.shape[-1] >= 128 and math.prod(item.shape) >= 65536


class Staging:
    def __init__(self, smem, ins, outs):
        self.smem = smem
        self.ins = [i >= smem and is_big(item) for i, item in enumerate(ins)]
        self.outs = [is_big(item) for item in outs]
        self.in_shapes = [item for item, big in zip(ins, self.ins) if big]
        self.out_shapes = [item for item, big in zip(outs, self.outs) if big]

    def in_specs(self):
        specs = [ANY_SPEC if big else VMEM_SPEC for big in self.ins]
        return [SMEM_SPEC] * self.smem + specs[self.smem :]

    def out_specs(self):
        return [ANY_SPEC if big else VMEM_SPEC for big in self.outs]

    def scratch(self):
        held = self.in_shapes + self.out_shapes
        blocks = [pltpu.VMEM(item.shape, item.dtype) for item in held]
        return blocks + [pltpu.SemaphoreType.DMA((len(held),))]

    def count(self):
        return len(self.in_shapes) + len(self.out_shapes) + 1

    def open(self, in_refs, out_refs, refs):
        refs = list(refs)
        sems = refs.pop()
        number = 0
        pairs = []
        for group, flags in ((in_refs, self.ins), (out_refs, self.outs)):
            view, moves = [], []
            for ref, big in zip(group, flags):
                if big:
                    moves.append((ref, refs[number], sems.at[number]))
                    ref = refs[number]
                    number += 1
                view.append(ref)
            pairs.append((view, moves))
        (self.in_view, self.in_moves), (self.out_view, self.out_moves) = pairs
        return self.in_view, self.out_view

    def fetch(self):
        copies = [pltpu.make_async_copy(src, dst, sem) for src, dst, sem in self.in_moves]
        for item in copies:
            item.start()
        for item in copies:
            item.wait()

    def move_out(self, moves):
        copies = [pltpu.make_async_copy(src, dst, sem) for dst, src, sem in moves]
        for item in copies:
            item.start()
        for item in copies:
            item.wait()

    def flush(self, count=None):
        self.moved = len(self.out_moves) if count is None else sum(self.outs[:count])
        self.move_out(self.out_moves[: self.moved])

    def flush_rest(self):
        self.move_out(self.out_moves[self.moved :])


def row_of(ref, index):
    return ref.at[pl.ds(index, 1)]


def splitter(refs):
    refs = list(refs)
    return lambda count: [refs.pop(0) for _ in range(count)]


class Hops:
    def __init__(self, place, pieces, refs, total, held, came, send, recv):
        z = place.z
        targets = [place.over_t()]
        targets.append({"shard": (z + 1 - 2 * lax.rem(z, 2)) * 2 + place.x})
        targets.append({"shard": (z + 2 - 4 * (z // 2)) * 2 + place.x})
        targets += [place.over_x(), place.over_y()]
        self.pieces, self.refs = pieces, refs
        self.total, self.held, self.came = total, held, came
        self.copies = [
            remote(held.at[k], came.at[k], send.at[k], recv.at[k], target)
            for k, target in enumerate(targets)
        ]

    def begin(self):
        self.held[0] = jnp.zeros(self.held.shape[1:], F32)
        for ref, (start, count, row, lane) in zip(self.refs, self.pieces):
            lanes = ref.shape[1]
            self.held[0, row : row + count, lane : lane + lanes] = ref[start : start + count]
        self.copies[0].start()

    def hop(self, number):
        self.copies[number - 1].wait()
        value = self.held[number - 1] + self.came[number - 1]
        if number < len(self.copies):
            self.held[number] = value
            self.copies[number].start()
        else:
            self.total[...] = value


class Small:
    def __init__(self, width):
        self.arrays, self.pieces, self.rows, self.width = [], [], 0, width

    def add(self, array, start, count, lane=0, stay=False):
        self.arrays.append(array)
        self.pieces.append((start, count, self.rows, lane))
        if not stay:
            self.rows += count

    def shape(self):
        return jax.ShapeDtypeStruct((-(-self.rows // 8) * 8, self.width), F32)

    def plain(self):
        whole = jnp.zeros(self.shape().shape, F32)
        for array, (start, count, row, lane) in zip(self.arrays, self.pieces):
            whole = whole.at[row : row + count, lane : lane + array.shape[1]].set(
                array[start : start + count]
            )
        return lax.psum(whole, AXES)


def hop_scratch(small):
    block = pltpu.VMEM((5,) + small.shape().shape, F32)
    return [block, block] + [pltpu.SemaphoreType.DMA((5,))] * 2


def tail_body(depth, starts, pieces, *refs):
    take = splitter(refs)
    count = len(starts)
    parts, small, (away,) = take(count), take(len(pieces)), take(1)
    owns, (total, back) = take(count), take(2)
    hop_refs, (send, recv) = take(4), take(2)
    place = Place(depth)
    carrier = Carrier(place, True, starts, parts, parts, owns, take(10 * count))
    hops = Hops(place, pieces, small, total, *hop_refs)
    across = remote(away, back, send.at[0], recv.at[0], place.over_y())
    carrier.step(0)
    hops.begin()
    for number in range(1, 4):
        hops.hop(number)
        carrier.step(number)
    hops.hop(4)
    across.start()
    hops.hop(5)
    carrier.end()
    across.wait()


def starts_of(parts):
    return [start for _, start, _ in parts]


def tail_sums(grid, number, parts, small, away):
    cubes, shapes, scratch = carried(grid, parts)
    count = len(small.arrays)
    result = pl.pallas_call(
        functools.partial(tail_body, grid.depth, starts_of(parts), small.pieces),
        in_specs=[VMEM_SPEC] * (len(parts) + count + 1),
        out_specs=[VMEM_SPEC] * (len(parts) + 2),
        out_shape=shapes + [small.shape(), jax.ShapeDtypeStruct(away.shape, away.dtype)],
        scratch_shapes=hop_scratch(small) + [pltpu.SemaphoreType.DMA((1,))] * 2 + scratch,
        compiler_params=stage_params(number),
        cost_estimate=stage_cost(20000000000),
        name="sum_rows",
    )(*cubes, *small.arrays, away)
    return result[:-2], result[-2], result[-1]


def norm_back_rows(e, unit, scale, gain):
    along = e * gain
    lanes = e.shape[-1]
    mean_along = jnp.sum(along, axis=-1, keepdims=True) * (1.0 / lanes)
    mean_unit = jnp.sum(along * unit, axis=-1, keepdims=True) * (1.0 / lanes)
    return scale * (along - mean_along - unit * mean_unit)


def column_sum(value):
    return jnp.sum(value, axis=0, keepdims=True)


def tie(value, *others):
    return lax.optimization_barrier((value, *others))[0]


class Near:
    def __init__(self, place, line, whole, other, send, recv):
        self.place, self.line, self.whole, self.other = place, line, whole, other
        self.send, self.recv = send, recv
        self.depth = line.shape[0]

    def pair(self, number, src, dst, target):
        return remote(src, dst, self.send.at[number], self.recv.at[number], target)

    def at(self, ref, dx, dy, low=0, size=None):
        x = 1 - self.place.x if dx else self.place.x
        y = 1 - self.place.y if dy else self.place.y
        view = ref.at[pl.ds(low, size or self.depth), x, y]
        return view.at[:, self.place.t] if len(ref.shape) == 6 else view

    def sides(self):
        dst = self.at(self.whole, 0, 0)
        return [
            self.pair(0, self.line, dst, self.place.over_x()),
            self.pair(1, self.line, dst, self.place.over_y()),
        ]

    def corners(self):
        half = self.depth // 2
        first = self.at(self.whole, 1, 0, 0, half)
        second = self.at(self.whole, 0, 1, half, half)
        return [
            self.pair(2, first, first, self.place.over_y()),
            self.pair(3, second, second, self.place.over_x()),
        ]

    def swap(self, number):
        if self.other is None:
            return []
        if number == 0:
            src, dst = self.line, self.at(self.other, 0, 0)
        else:
            dx, dy = number & 1, number >> 1
            src, dst = self.at(self.whole, dx, dy), self.at(self.other, dx, dy)
        return [self.pair(4 + number, src, dst, self.place.over_t())]

    def begin(self):
        for item in self.sides() + self.swap(0) + [self.keep()]:
            item.start()

    def keep(self):
        return pltpu.make_async_copy(self.line, self.at(self.whole, 0, 0), self.send.at[8])

    def middle(self):
        for item in self.sides():
            item.wait()
        for item in self.corners() + self.swap(1) + self.swap(2):
            item.start()

    def corner_in(self):
        for item in self.corners():
            item.wait()
        for item in self.swap(3):
            item.start()

    def end(self):
        for number in range(4):
            for item in self.swap(number):
                item.wait()
        self.keep().wait()


class Deep:
    def __init__(self, place, block, line, send, recv):
        self.place, self.block, self.line, self.send, self.recv = place, block, line, send, recv

    def copies(self):
        return [
            remote(
                self.block,
                self.line.at[self.place.z],
                self.send.at[k - 1],
                self.recv.at[k - 1],
                self.place.over_z(k),
            )
            for k in range(1, self.line.shape[0])
        ]

    def begin(self):
        for item in self.copies():
            item.start()
        self.line[self.place.z] = self.block[...]

    def end(self):
        for item in self.copies():
            item.wait()


def landing(line, both):
    depth, step_rows, lanes = line
    if both == "one":
        return [jax.ShapeDtypeStruct((depth, 2, 2, 2, step_rows, lanes), BF)]
    return [jax.ShapeDtypeStruct((depth, 2, 2, step_rows, lanes), BF)] * (2 if both else 1)


def landed(outs, both):
    whole = outs.pop(0)
    if both == "one":
        return whole, whole
    return whole, outs.pop(0) if both else None


class Load:
    def __init__(self, grid, near=(), swapped=(), deep=(), across=()):
        self.depth = grid.depth
        self.swapped = list(swapped)
        self.near_count, self.deep_count = len(near), len(deep)
        self.inputs = list(near) + list(deep) + list(across)
        self.across_count = len(across)
        self.shapes, self.scratch, self.specs = [], [], []
        for line, both in zip(near, swapped):
            shapes = landing(line.shape, both)
            self.shapes += shapes
            self.specs += [ANY_SPEC] * len(shapes)
            self.scratch += [pltpu.SemaphoreType.DMA((9,)), pltpu.SemaphoreType.DMA((8,))]
        for block in deep:
            self.shapes.append(jax.ShapeDtypeStruct((self.depth,) + block.shape, BF))
            self.specs.append(VMEM_SPEC)
            self.scratch += [pltpu.SemaphoreType.DMA((self.depth - 1,))] * 2

        for item in across:
            self.shapes.append(jax.ShapeDtypeStruct(item.shape, item.dtype))
            self.specs.append(VMEM_SPEC)
            self.scratch += [pltpu.SemaphoreType.DMA((1,))] * 2

    def results(self, arrays):
        arrays = list(arrays)
        flat = lambda item: item.reshape(-1, item.shape[-1])
        near = []
        for both in self.swapped:
            near.append([None if item is None else flat(item) for item in landed(arrays, both)])
        return near, arrays


class Loader:
    def __init__(self, place, cores, load, ins, outs, sems):
        self.place, self.cores, self.load = place, cores, load
        ins, outs, sems = list(ins), list(outs), list(sems)
        self.near = []
        for both in load.swapped:
            whole, other = landed(outs, both)
            self.near.append(Near(place, ins.pop(0), whole, other, sems.pop(0), sems.pop(0)))
        self.deep = [
            Deep(place, ins.pop(0), outs.pop(0), sems.pop(0), sems.pop(0))
            for _ in range(load.deep_count)
        ]
        self.across = []
        for _ in range(load.across_count):
            send, recv = sems.pop(0), sems.pop(0)
            self.across.append(
                remote(ins.pop(0), outs.pop(0), send.at[0], recv.at[0], place.over_y())
            )

    def begin(self):
        chips = bool(self.near or self.deep or self.across)
        if chips or self.cores:
            self.place.meet(chips, self.cores or bool(self.near))
        for item in self.near + self.deep:
            item.begin()
        for item in self.across:
            item.start()

    def middle(self):
        for item in self.near:
            item.middle()

    def end(self):
        for item in self.near:
            item.corner_in()
        for item in self.near:
            item.end()
        for item in self.deep:
            item.end()
        for item in self.across:
            item.wait()


def open_kernel(load, staging, refs, scratch):
    take = splitter(refs)
    in_refs = take(len(staging.ins))
    load_ins = take(len(load.inputs))
    out_refs = take(len(staging.outs))
    load_outs = take(len(load.shapes))
    scratch_refs = take(scratch)
    in_refs, out_refs = staging.open(in_refs, out_refs, take(staging.count()))
    return in_refs, out_refs, scratch_refs, (load_ins, load_outs, take(len(load.scratch)))


def kernel_call(body, number, ins, shapes, scratch, load, name, smem=0, cores=False):
    staging = Staging(smem, ins, shapes)
    result = pl.pallas_call(
        functools.partial(body, staging),
        in_specs=staging.in_specs() + [VMEM_SPEC] * len(load.inputs),
        out_specs=staging.out_specs() + load.specs,
        out_shape=list(shapes) + load.shapes,
        scratch_shapes=list(scratch) + staging.scratch() + load.scratch,
        compiler_params=stage_params(number, sends=cores or bool(load.inputs)),
        cost_estimate=stage_cost(20000000000),
        name=name,
    )(*ins, *load.inputs)
    return result[: len(shapes)], load.results(result[len(shapes) :])


def first_body(swapped, depth, next_count, *refs):
    take = splitter(refs)
    count = len(swapped)
    blocks, next_blocks = take(count), take(next_count)
    wholes = [landed(take(2 if both is True else 1), both) for both in swapped]
    next_lines = take(next_count)
    lines = take(count)
    place = Place(depth)
    deep = [Deep(place, blocks[i], lines[i], *take(2)) for i in range(count)]
    near = [Near(place, lines[i], *wholes[i], *take(2)) for i in range(count)]
    after = [Deep(place, next_blocks[i], next_lines[i], *take(2)) for i in range(next_count)]
    place.meet(True, True)
    for item in deep:
        item.begin()
    for one, two in zip(deep, near):
        one.end()
        two.begin()
    for item in after:
        item.begin()
    for item in near:
        item.middle()
    for item in near:
        item.corner_in()
    for item in near:
        item.end()
    for item in after:
        item.end()


def first_gather(grid, number, blocks, swapped, next_blocks):
    depth = grid.depth
    line = lambda item: (depth,) + item.shape
    shapes = []
    for item, both in zip(blocks, swapped):
        shapes += landing(line(item), both)
    specs = [ANY_SPEC] * len(shapes) + [VMEM_SPEC] * len(next_blocks)
    shapes += [jax.ShapeDtypeStruct(line(item), BF) for item in next_blocks]
    sems = lambda size: [pltpu.SemaphoreType.DMA((size,))] * 2
    scratch = [pltpu.VMEM(line(item), BF) for item in blocks]
    for _ in blocks:
        scratch += sems(depth - 1)
    for _ in blocks:
        scratch += [pltpu.SemaphoreType.DMA((9,)), pltpu.SemaphoreType.DMA((8,))]
    for _ in next_blocks:
        scratch += sems(depth - 1)
    arrays = list(
        pl.pallas_call(
            functools.partial(first_body, tuple(swapped), depth, len(next_blocks)),
            in_specs=[VMEM_SPEC] * (len(blocks) + len(next_blocks)),
            out_specs=specs,
            out_shape=shapes,
            scratch_shapes=scratch,
            compiler_params=stage_params(number),
            cost_estimate=stage_cost(20000000000),
            name="first_gather",
        )(*blocks, *next_blocks)
    )
    flat = lambda item: None if item is None else item.reshape(-1, item.shape[-1])
    near = [[flat(item) for item in landed(arrays, both)] for both in swapped]
    return near, arrays


def norm_rows(state, gain, shift):
    lanes = state.shape[-1]
    center = state - jnp.sum(state, axis=-1, keepdims=True) * (1.0 / lanes)
    spread = jnp.sum(center * center, axis=-1, keepdims=True) * (1.0 / lanes)
    scale = lax.rsqrt(spread + epsilon)
    unit = center * scale
    return (unit * gain + shift).astype(BF), unit, scale


def square_sum(value, valid):
    return jnp.sum(jnp.sum(value * value, axis=-1, keepdims=True) * valid, axis=0, keepdims=True)


def temporal_body(load, att_scale, layer, staging, *refs):
    ins, outs, scratch, loads = open_kernel(load, staging, refs, 3)
    state, valid, gain, shift, tri, tri_bias, merge0, merge1, merge_bias, mixing, mix_bias = ins
    out, unit, scale, normed, qkv, mine, swap, joined, sq = outs
    away, send, recv = scratch
    gain, shift = row_of(gain, 3 * layer), row_of(shift, 3 * layer)
    tri_bias = row_of(tri_bias, layer)
    merge_bias, mix_bias = row_of(merge_bias, 4 * layer), row_of(mix_bias, 4 * layer + 1)
    place = Place(load.depth)
    loader = Loader(place, True, load, *loads)
    frames, padded, width = state.shape
    loader.begin()
    staging.fetch()

    def norm_one(f, carry):
        low, u, s = norm_rows(state[f], gain[...], shift[...])
        normed[f] = low
        unit[f] = u
        scale[f] = s
        return carry

    lax.fori_loop(0, frames, norm_one, 0)
    own = normed.at[pl.ds(0, frames)]
    swap_normed = remote(
        own, normed.at[pl.ds(frames, frames)], send.at[0], recv.at[0], place.over_t()
    )
    swap_normed.start()

    def project(f, carry):
        qkv[f] = (dot_nn(normed[f], tri[...]) + tri_bias[...]).astype(BF)
        return carry

    lax.fori_loop(0, frames, project, 0)
    swap_normed.wait()
    lax.fori_loop(frames, 2 * frames, project, 0)
    tile = 16
    fix = temporal_fix(tile)

    def one(i, carry):
        at = pl.ds(pl.multiple_of(i * tile, tile), tile)

        def put(pair, value):
            cols = slice(pair * 128, pair * 128 + 128)
            both = value.reshape(2 * frames, tile, 128)
            mine[:, at, cols] = both[:frames]
            away[:, at, cols] = both[frames:]

        heads_forward(
            lambda part, pair: qkv[:, at, column(part, pair)].reshape(2 * frames * tile, 128),
            fix,
            att_scale,
            put,
        )
        return carry

    lax.fori_loop(0, padded // tile, one, 0)
    swap_mixed = remote(away, swap, send.at[1], recv.at[1], place.over_t())
    swap_mixed.start()
    loader.middle()
    swap_mixed.wait()

    def finish(f, carry):
        low = (
            dot_nt(mine[f], merge0[...]) + dot_nt(swap[f], merge1[...]) + merge_bias[...]
        ).astype(BF)
        joined[f] = low
        branch = dot_nn(low, mixing[...]) + mix_bias[...]
        out[f] = state[f] + branch
        return carry + square_sum(branch, valid[...])

    total = lax.fori_loop(0, frames, finish, jnp.zeros((1, 1), F32))
    sq[...] = jnp.broadcast_to(total, sq.shape)
    staging.flush()
    loader.end()


def temporal_stage(number, layer, state, valid, gain, shift, w, biases, load, att_scale):
    frames, padded, width = state.shape
    split = w["merge_t"][0].shape[1]
    shape = lambda dims, kind=BF: jax.ShapeDtypeStruct(dims, kind)
    ins = [state, valid, gain, shift, w["triple_t"], biases[0], *w["merge_t"], biases[1]]
    ins += [w["mixing"], biases[2]]
    return kernel_call(
        functools.partial(temporal_body, load, att_scale, layer),
        number,
        ins,
        [
            shape((frames, padded, width), F32),
            shape((frames, padded, width), F32),
            shape((frames, padded, 1), F32),
            shape((2 * frames, padded, width)),
            shape((2 * frames, padded, 3 * split)),
            shape((frames, padded, split)),
            shape((frames, padded, split)),
            shape((frames, padded, width)),
            shape((8, 128), F32),
        ],
        [pltpu.VMEM((frames, padded, split), BF)] + [pltpu.SemaphoreType.DMA((2,))] * 2,
        load,
        "temporal_forward",
        cores=True,
    )


def spatial_body(load, places, att_scale, layer, staging, *refs):
    ins, outs, scratch, loads = open_kernel(load, staging, refs, 0)
    count_ref, state, valid, gain, shift, tri0, tri1, bias0, bias1, merge0, merge1, out_bias = ins
    out, unit, scale, normed, qkv0, qkv1, mixed0, mixed1, sq = outs
    gain, shift = row_of(gain, 3 * layer + 1), row_of(shift, 3 * layer + 1)
    bias0, bias1 = row_of(bias0, layer), row_of(bias1, layer)
    out_bias = row_of(out_bias, 4 * layer + 2)
    place = Place(load.depth)
    loader = Loader(place, False, load, *loads)
    frames, padded, width = state.shape
    fix = spatial_fix(count_ref, padded, places)
    loader.begin()
    staging.fetch()

    def one(f, carry):
        low, u, s = norm_rows(state[f], gain[...], shift[...])
        normed[f] = low
        unit[f] = u
        scale[f] = s
        for tri, bias, qkv, mixed in (
            (tri0, bias0, qkv0, mixed0),
            (tri1, bias1, qkv1, mixed1),
        ):
            qkv[f] = (dot_nn(low, tri[...]) + bias[...]).astype(BF)

            def put(pair, value, mixed=mixed):
                mixed[f, :, pair * 128 : pair * 128 + 128] = value

            heads_forward(
                lambda part, pair, qkv=qkv: qkv[f, :, column(part, pair)], fix, att_scale, put
            )
        branch = dot_nt(mixed0[f], merge0[...]) + dot_nt(mixed1[f], merge1[...]) + out_bias[...]
        out[f] = state[f] + branch
        return carry + square_sum(branch, valid[...])

    cut = frames - 1
    total = lax.fori_loop(0, cut, one, jnp.zeros((1, 1), F32))
    loader.middle()
    total = lax.fori_loop(cut, frames, one, total)
    sq[...] = jnp.broadcast_to(total, sq.shape)
    staging.flush()
    loader.end()


def spatial_stage(number, layer, count_ref, state, valid, gain, shift, w, biases, load, places, att_scale):
    frames, padded, width = state.shape
    split = w["merge_s"][0].shape[1]
    shape = lambda dims, kind=BF: jax.ShapeDtypeStruct(dims, kind)
    ins = [count_ref, state, valid, gain, shift, *w["triple_s"], biases[0], biases[1]]
    ins += [*w["merge_s"], biases[2]]
    return kernel_call(
        functools.partial(spatial_body, load, places, att_scale, layer),
        number,
        ins,
        [
            shape((frames, padded, width), F32),
            shape((frames, padded, width), F32),
            shape((frames, padded, 1), F32),
            shape((frames, padded, width)),
            shape((frames, padded, 3 * split)),
            shape((frames, padded, 3 * split)),
            shape((frames, padded, split)),
            shape((frames, padded, split)),
            shape((8, 128), F32),
        ],
        [],
        load,
        "spatial_forward",
        1,
    )


def feed_body(load, layer, staging, *refs):
    ins, outs, scratch, loads = open_kernel(load, staging, refs, 0)
    state, valid, gain, shift, up0, up1, bias0, bias1, down0, down1, out_bias = ins
    out, unit, scale, normed, act0, act1, slope0, slope1, sq = outs
    gain, shift = row_of(gain, 3 * layer + 2), row_of(shift, 3 * layer + 2)
    bias0, bias1 = row_of(bias0, layer), row_of(bias1, layer)
    out_bias = row_of(out_bias, 4 * layer + 3)
    place = Place(load.depth)
    loader = Loader(place, False, load, *loads)
    frames, padded, width = state.shape
    loader.begin()
    staging.fetch()

    def one(f, carry):
        low, u, s = norm_rows(state[f], gain[...], shift[...])
        normed[f] = low
        unit[f] = u
        scale[f] = s
        branch = jnp.broadcast_to(out_bias[...], (padded, width))
        for up, bias, down, act, slope in (
            (up0, bias0, down0, act0, slope0),
            (up1, bias1, down1, act1, slope1),
        ):
            lanes = up.shape[1]
            piece = lanes // 3
            for number in range(3):
                cols = slice(number * piece, (number + 1) * piece)
                hidden = dot_nn(low, up[:, cols]) + bias[:, cols]
                below = 0.5 * (1.0 + lax.erf(hidden * root_half))
                act[f, :, cols] = (hidden * below).astype(BF)
                slope[f, :, cols] = (
                    below + hidden * gauss_scale * jnp.exp(-0.5 * hidden * hidden)
                ).astype(BF)
            branch = branch + dot_nt(act[f], down[...])
        value = state[f] + branch
        out[f] = value
        return (
            carry[0] + square_sum(branch, valid[...]),
            carry[1] + square_sum(value, valid[...]),
        )

    zero = jnp.zeros((1, 1), F32)
    cut = frames - 1
    total = lax.fori_loop(0, cut, one, (zero, zero))
    loader.middle()
    total = lax.fori_loop(cut, frames, one, total)
    sq[...] = jnp.broadcast_to(total[0], sq.shape)
    sq[0:1] = jnp.broadcast_to(total[1], (1, sq.shape[1]))
    staging.flush()
    loader.end()


def feed_stage(number, layer, state, valid, gain, shift, w, biases, load):
    frames, padded, width = state.shape
    hid = w["up"][0].shape[1]
    shape = lambda dims, kind=BF: jax.ShapeDtypeStruct(dims, kind)
    ins = [state, valid, gain, shift, *w["up"], biases[0], biases[1], *w["down"], biases[2]]
    return kernel_call(
        functools.partial(feed_body, load, layer),
        number,
        ins,
        [
            shape((frames, padded, width), F32),
            shape((frames, padded, width), F32),
            shape((frames, padded, 1), F32),
            shape((frames, padded, width)),
        ]
        + [shape((frames, padded, hid))] * 4
        + [shape((8, 128), F32)],
        [],
        load,
        "feed_forward",
    )


def feed_back_body(depth, starts, steps, layer, *refs):
    take = splitter(refs)
    count = len(starts)
    state, normed, unit, scale, gain = take(5)
    gain = row_of(gain, 3 * layer + 2)
    oth, own = take(4), take(4)
    parts = take(count)
    out, sums, g_up, g_down, h_own, h_oth = take(6)
    owns = take(count)
    r, rt, nt, bh, s_up, s_down, r_up, r_down, send, recv = take(10)
    place = Place(depth)
    carrier = Carrier(place, True, starts, parts, parts, owns, take(10 * count))
    frames, padded, width = state.shape
    rows_all = frames * padded
    i = pl.program_id(0)

    @pl.when(i == 0)
    def _():
        carrier.step(0)
        sums[...] = jnp.zeros_like(sums)

        def begin(f, carry):
            low = state[f].astype(BF)
            r[f] = low
            out[f] = jnp.zeros((padded, width), F32)
            return carry + column_sum(low.astype(F32))

        sums[2:3] = lax.fori_loop(0, frames, begin, jnp.zeros((1, width), F32))
        rt[...] = r[...].reshape(rows_all, width).T
        nt[...] = normed[...].reshape(rows_all, width).T

    def work(down, up, active, slope, h_sum):
        lanes = down.shape[1]

        value = dot_nn(r[...].reshape(rows_all, width), down[...])
        value = (value * slope[...].reshape(rows_all, lanes).astype(F32)).astype(BF)
        bh[...] = value.reshape(frames, padded, lanes)
        h_sum[...] = column_sum(value.astype(F32))
        out[...] += dot_nt(value, up[...]).reshape(frames, padded, width)
        return (
            dot_nn(nt[...], bh[...].reshape(rows_all, lanes)),
            dot_nn(rt[...], active[...].reshape(rows_all, lanes)),
        )

    def swaps(j):
        return [
            remote(s_up.at[j], r_up.at[j], send.at[0, j], recv.at[0, j], place.over_t()),
            remote(s_down.at[j], r_down.at[j], send.at[1, j], recv.at[1, j], place.over_t()),
        ]

    @pl.when(i < steps)
    def _():
        up_part, down_part = work(*oth, h_oth)
        s_up[i] = up_part.astype(BF)
        s_down[i] = down_part.astype(BF)
        for item in swaps(i):
            item.start()

    for number, at in ((1, 1), (2, 3), (3, 4)):
        if count:

            @pl.when(i == at)
            def _(number=number):
                carrier.step(number)

    @pl.when(i >= steps)
    def _():
        j = i - steps
        up_part, down_part = work(*own, h_own)
        for item in swaps(j):
            item.wait()
        g_up[...] = (up_part + r_up[j].astype(F32)).astype(BF)
        g_down[...] = (down_part + r_down[j].astype(F32)).astype(BF)

    @pl.when(i == 2 * steps - 1)
    def _():
        def finish(f, carry):
            e, u = out[f], unit[f]
            out[f] = state[f] + norm_back_rows(e, u, scale[f], gain[...])
            return (carry[0] + column_sum(e * u), carry[1] + column_sum(e))

        zero = jnp.zeros((1, width), F32)
        sums[0:1], sums[1:2] = lax.fori_loop(0, frames, finish, (zero, zero))
        carrier.end()


def feed_back(grid, number, layer, state, kept, gain, w, parts):
    frames, padded, width = state.shape
    hid = w["up"][0].shape[1]
    steps = 3
    lanes = hid // steps
    cubes, shapes, scratch = carried(grid, parts)
    whole = lambda item: pl.BlockSpec(
        item.shape, lambda i: (0,) * item.ndim, pipeline_mode=pl.Buffered(1)
    )
    first = lambda i: jnp.minimum(i, steps - 1)
    later = lambda i: jnp.maximum(i - steps, 0)

    def side(at):
        weight = pl.BlockSpec((width, lanes), lambda i: (0, at(i)))
        token = pl.BlockSpec((frames, padded, lanes), lambda i: (0, 0, at(i)))
        return [weight, weight, token, token]

    tokens = lambda item: item.reshape(frames, padded, hid)
    sides = [
        [w["down"][k], w["up"][k], tokens(kept["active"][k]), tokens(kept["slope"][k])]
        for k in (1, 0)
    ]
    fixed = [state, kept["normed_m"], kept["unit_m"], kept["scale_m"], gain]
    vec = lambda at: pl.BlockSpec((1, lanes), lambda i: (0, at(i)))
    result = pl.pallas_call(
        functools.partial(feed_back_body, grid.depth, starts_of(parts), steps, layer),
        grid=(2 * steps,),
        in_specs=[whole(item) for item in fixed]
        + side(first)
        + side(later)
        + [whole(item) for item in cubes],
        out_specs=[
            pl.BlockSpec((frames, padded, width), lambda i: (0, 0, 0)),
            pl.BlockSpec((8, width), lambda i: (0, 0)),
            pl.BlockSpec((width, lanes), lambda i: (0, later(i))),
            pl.BlockSpec((width, lanes), lambda i: (0, later(i))),
            vec(later),
            vec(first),
        ]
        + [pl.BlockSpec(item.shape, lambda i: (0, 0)) for item in shapes],
        out_shape=[
            jax.ShapeDtypeStruct((frames, padded, width), F32),
            jax.ShapeDtypeStruct((8, width), F32),
            jax.ShapeDtypeStruct((width, hid), BF),
            jax.ShapeDtypeStruct((width, hid), BF),
            jax.ShapeDtypeStruct((1, hid), F32),
            jax.ShapeDtypeStruct((1, hid), F32),
        ]
        + shapes,
        scratch_shapes=[
            pltpu.VMEM((frames, padded, width), BF),
            pltpu.VMEM((width, frames * padded), BF),
            pltpu.VMEM((width, frames * padded), BF),
            pltpu.VMEM((frames, padded, lanes), BF),
        ]
        + [pltpu.VMEM((steps, width, lanes), BF)] * 4
        + [pltpu.SemaphoreType.DMA((2, steps))] * 2
        + scratch,
        compiler_params=stage_params(number),
        cost_estimate=stage_cost(24000000000),
        name="feed_back",
    )(*fixed, *sides[0], *sides[1], *cubes)
    return result[0], result[1], result[2:4], (result[4], result[5]), result[6:]


def spatial_back_body(depth, starts, places, att_scale, layer, staging, *refs):
    take = splitter(refs)
    count = len(starts)
    in_refs, out_refs = take(14 + count), take(5 + count)
    own_scratch, sum_scratch = take(13), take(10 * count)
    sources = in_refs[14:]
    in_refs, out_refs = staging.open(in_refs, out_refs, take(staging.count()))
    take = splitter(in_refs + out_refs + own_scratch + sum_scratch)
    (count_ref, state, merge0, merge1, mixed0, mixed1, qkv0, qkv1) = take(8)
    tri0, tri1, normed, unit, scale, gain = take(6)
    gain = row_of(gain, 3 * layer + 1)
    parts = take(count)
    out, sums, q_sums, g_tri, g_merge = take(5)
    owns = take(count)
    r, bm0, bm1, b0, b1, rt, nt, s_tri, r_tri, s_merge, r_merge, send, recv = take(13)
    place = Place(depth)
    carrier = Carrier(place, True, starts, sources, parts, owns, take(10 * count), 3)
    frames, padded, width = state.shape
    rows_all = frames * padded
    split = merge0.shape[1]
    fix = spatial_fix(count_ref, padded, places)
    carrier.step(0)
    staging.fetch()

    def one(f, carry):
        low = state[f].astype(BF)
        r[f] = low
        for merge, bm, src, dst in ((merge0, bm0, qkv0, b0), (merge1, bm1, qkv1, b1)):
            bm[...] = dot_nn(low, merge[...]).astype(BF)

            def put(part, pair, value, dst=dst):
                dst[f, :, column(part, pair)] = value

            heads_backward(
                lambda part, pair, src=src: src[f, :, column(part, pair)],
                lambda pair, bm=bm: bm[:, pair * 128 : pair * 128 + 128],
                fix,
                att_scale,
                put,
            )
        return carry + column_sum(low.astype(F32))

    sums[...] = jnp.zeros_like(sums)
    q_sums[...] = jnp.zeros_like(q_sums)
    total = jnp.zeros((1, width), F32)
    for number in range(3):
        total = lax.fori_loop(number, number + 1, one, total)
        carrier.step(number + 1)
    sums[2:3] = lax.fori_loop(3, frames, one, total)
    carrier.step(4)
    rt[...] = r[...].reshape(rows_all, width).T
    nt[...] = normed[...].reshape(rows_all, width).T
    flat = lambda ref, part: ref[:, :, part * split : (part + 1) * split].reshape(rows_all, split)
    swap_tri = remote(s_tri, r_tri, send.at[0], recv.at[0], place.over_t())
    swap_merge = remote(s_merge, r_merge, send.at[1], recv.at[1], place.over_t())
    s_merge[...] = dot_nn(rt[...], mixed1[...]).astype(BF)
    swap_merge.start()
    for part in range(3):
        cols = slice(part * split, (part + 1) * split)
        s_tri[:, cols] = dot_nn(nt[...], flat(b1, part)).astype(BF)
    swap_tri.start()

    def finish(f, carry):
        e = dot_nt(b0[f], tri0[...]) + dot_nt(b1[f], tri1[...])
        u = unit[f]
        out[f] = state[f] + norm_back_rows(e, u, scale[f], gain[...])
        return (
            carry[0] + column_sum(e * u),
            carry[1] + column_sum(e),
            carry[2] + column_sum(b0[f].astype(F32)),
            carry[3] + column_sum(b1[f].astype(F32)),
        )

    zero, wide = jnp.zeros((1, width), F32), jnp.zeros((1, 3 * split), F32)
    sums[0:1], sums[1:2], mine, theirs = lax.fori_loop(
        0, frames, finish, (zero, zero, wide, wide)
    )
    for number, value in ((0, mine), (1, theirs)):
        q_sums[number : number + 1, :split] = value[:, :split]
        q_sums[number : number + 1, split:] = value[:, 2 * split :]
    swap_merge.wait()
    g_merge[...] = (dot_nn(rt[...], mixed0[...]) + r_merge[...].astype(F32)).astype(BF)
    swap_tri.wait()
    for part in range(3):
        cols = slice(part * split, (part + 1) * split)
        mine = dot_nn(nt[...], flat(b0, part))
        g_tri[:, cols] = (mine + r_tri[:, cols].astype(F32)).astype(BF)
    staging.flush(5)
    carrier.end()
    staging.flush_rest()


def spatial_back(grid, number, layer, count_ref, state, kept, gain, w, parts, places, att_scale):
    frames, padded, width = state.shape
    split = w["merge_s"][0].shape[1]
    cubes, shapes, scratch = carried(grid, parts)
    flat = [item.reshape(frames * padded, split) for item in kept["mixed_s"]]
    fixed = [count_ref, state, *w["merge_s"], *flat, *kept["qkv_s"], *w["triple_s"]]
    fixed += [kept["normed_s"], kept["unit_s"], kept["scale_s"], gain]
    ins = fixed + cubes
    outs = [
        jax.ShapeDtypeStruct((frames, padded, width), F32),
        jax.ShapeDtypeStruct((8, width), F32),
        jax.ShapeDtypeStruct((8, 2 * split), F32),
        jax.ShapeDtypeStruct((width, 3 * split), BF),
        jax.ShapeDtypeStruct((width, split), BF),
    ] + shapes
    staging = Staging(1, ins, outs)
    result = pl.pallas_call(
        functools.partial(
            spatial_back_body, grid.depth, starts_of(parts), places, att_scale, layer, staging
        ),
        in_specs=staging.in_specs(),
        out_specs=staging.out_specs(),
        out_shape=outs,
        scratch_shapes=[pltpu.VMEM((frames, padded, width), BF)]
        + [pltpu.VMEM((padded, split), BF)] * 2
        + [pltpu.VMEM((frames, padded, 3 * split), BF)] * 2
        + [pltpu.VMEM((width, frames * padded), BF)] * 2
        + [pltpu.VMEM((width, 3 * split), BF)] * 2
        + [pltpu.VMEM((width, split), BF)] * 2
        + [pltpu.SemaphoreType.DMA((2,))] * 2
        + scratch
        + staging.scratch(),
        compiler_params=stage_params(number),
        cost_estimate=stage_cost(24000000000),
        name="spatial_stage",
    )(*ins)
    return result[0], result[1], result[2], result[3:5], result[5:]


def temporal_back_body(depth, starts, att_scale, layer, staging, pieces, joined_mix, *refs):
    take = splitter(refs)
    count = len(starts)
    chained = 1 if pieces else 0
    in_refs, small = take(13 + count), take(len(pieces))
    out_refs, total = take(6 + count), take(chained)
    own_scratch, sum_scratch, hop_refs = take(13), take(10 * count), take(4 * chained)
    mix_refs = take(3) if joined_mix else None
    sources = in_refs[13:]
    in_refs, out_refs = staging.open(in_refs, out_refs, take(staging.count()))
    take = splitter(in_refs + out_refs + own_scratch + sum_scratch)
    state, mixing, joined, merge0, merge1, mine, swap, qkv, tri = take(9)
    normed, unit, scale, gain = take(4)
    gain = row_of(gain, 3 * layer)
    parts = take(count)
    out, sums, q_sums, g_tri, g_merge, g_mix = take(6)
    owns = take(count)
    r, bj, away, bm, b, nt, rt, s_merge, r_merge, s_back, r_back, send, recv = take(13)
    joins = len(g_mix.shape) == 3
    if joins:
        (whole_mix, s_mix, r_mix), shard_mix = mix_refs, g_mix
    place = Place(depth)
    carrier = Carrier(place, True, starts, sources, parts, owns, take(10 * count))
    frames, padded, width = state.shape
    rows_all = frames * padded
    split = merge0.shape[1]
    carrier.step(0)
    hops = Hops(place, pieces, small, *total, *hop_refs) if chained else None
    if chained:
        hops.begin()
    staging.fetch()

    def begin(f, carry):
        low = state[f].astype(BF)
        r[f] = low
        value = dot_nt(low, mixing[...]).astype(BF)
        bj[f] = value
        bm[f] = dot_nn(value, merge0[...]).astype(BF)
        away[f] = dot_nn(value, merge1[...]).astype(BF)
        return (carry[0] + column_sum(low.astype(F32)), carry[1] + column_sum(value.astype(F32)))

    sums[...] = jnp.zeros_like(sums)
    q_sums[...] = jnp.zeros_like(q_sums)
    zero = jnp.zeros((1, width), F32)
    sums[3:4], sums[2:3] = lax.fori_loop(0, frames, begin, (zero, zero))
    swap_bm = remote(
        away, bm.at[pl.ds(frames, frames)], send.at[0], recv.at[0], place.over_t()
    )
    swap_bm.start()
    rt[...] = bj[...].reshape(rows_all, width).T
    s_merge[...] = dot_nn(rt[...], swap[...].reshape(rows_all, split)).astype(BF)
    swap_merge = remote(s_merge, r_merge, send.at[1], recv.at[1], place.over_t())
    swap_merge.start()
    carrier.step(1)
    if chained:
        hops.hop(1)
    rt[...] = joined[...].reshape(rows_all, width).T
    for half in range(2):
        cols = slice(half * split, (half + 1) * split)
        mix_part = dot_nn(rt[...], r[:, :, cols].reshape(rows_all, split))
        (whole_mix if joins else g_mix)[:, cols] = mix_part
    if joins:
        blocks, step = shard_mix.shape[0], shard_mix.shape[1]

        def mix_rows(k, core):
            at = pl.multiple_of((2 * k + core) * step, 8)
            return whole_mix[pl.ds(at, step), :]

        for k in range(blocks):
            s_mix[k] = mix_rows(k, 1 - place.t).astype(BF)
        swap_mix = remote(s_mix, r_mix, send.at[3], recv.at[3], place.over_t())
        swap_mix.start()
    rt[...] = bj[...].reshape(rows_all, width).T
    swap_merge.wait()
    g_merge[...] = (dot_nn(rt[...], mine[...].reshape(rows_all, split)) + r_merge[...].astype(F32)).astype(BF)
    swap_bm.wait()
    tile = 16
    fix = temporal_fix(tile)

    def one(i, carry):
        at = pl.ds(pl.multiple_of(i * tile, tile), tile)

        def put(part, pair, value):
            b[:, at, column(part, pair)] = value.reshape(FRAMES, tile, 128)

        heads_backward(
            lambda part, pair: qkv[:, at, column(part, pair)].reshape(FRAMES * tile, 128),
            lambda pair: bm[:, at, pair * 128 : pair * 128 + 128].reshape(FRAMES * tile, 128),
            fix,
            att_scale,
            put,
        )
        return carry

    tiles = padded // tile
    lax.fori_loop(0, tiles // 3, one, 0)
    if joins:
        swap_mix.wait()
        for k in range(blocks):
            shard_mix[k] = (mix_rows(k, place.t) + r_mix[k].astype(F32)).astype(BF)
    if chained:
        hops.hop(2)
    lax.fori_loop(tiles // 3, 2 * tiles // 3, one, 0)
    carrier.step(2)
    if chained:
        hops.hop(3)
    lax.fori_loop(2 * tiles // 3, tiles, one, 0)
    if chained:
        hops.hop(4)
    carrier.step(3)

    def toward(f, carry):
        s_back[f] = dot_nt(b[f + frames], tri[...]).astype(BF)
        return carry

    lax.fori_loop(0, frames, toward, 0)
    swap_back = remote(s_back, r_back, send.at[2], recv.at[2], place.over_t())
    swap_back.start()
    nt[...] = normed[...].reshape(2 * rows_all, width).T
    for part in range(3):
        cols = slice(part * split, (part + 1) * split)
        g_tri[:, cols] = dot_nn(
            nt[...], b[:, :, cols].reshape(2 * rows_all, split)
        ).astype(BF)
    swap_back.wait()

    def finish(f, carry):
        e = dot_nt(b[f], tri[...]) + r_back[f].astype(F32)
        u = unit[f]
        out[f] = state[f] + norm_back_rows(e, u, scale[f], gain[...])
        both = column_sum(b[f].astype(F32)) + column_sum(b[f + frames].astype(F32))
        return (carry[0] + column_sum(e * u), carry[1] + column_sum(e), carry[2] + both)

    sums[0:1], sums[1:2], wide = lax.fori_loop(
        0, frames, finish, (zero, zero, jnp.zeros((1, 3 * split), F32))
    )
    q_sums[0:1, :split] = wide[:, :split]
    q_sums[0:1, split:] = wide[:, 2 * split :]
    if chained:
        hops.hop(5)
    staging.flush(6)
    carrier.end()
    staging.flush_rest()


def temporal_back(grid, number, layer, state, kept, gain, w, parts, att_scale, small=None):
    frames, padded, width = state.shape
    split = w["merge_t"][0].shape[1]
    cubes, shapes, scratch = carried(grid, parts)
    fixed = [state, w["mixing"], kept["joined"], *w["merge_t"], *kept["mixed_t"], kept["qkv_t"]]
    fixed += [w["triple_t"], kept["normed_t"], kept["unit_t"], kept["scale_t"], gain]
    ins = fixed + cubes
    outs = [
        jax.ShapeDtypeStruct((frames, padded, width), F32),
        jax.ShapeDtypeStruct((8, width), F32),
        jax.ShapeDtypeStruct((8, 2 * split), F32),
        jax.ShapeDtypeStruct((width, 3 * split), BF),
        jax.ShapeDtypeStruct((width, split), BF),
        jax.ShapeDtypeStruct((width, width), F32),
    ] + shapes
    mix_scratch = []
    if grid.direct:
        step = width // (4 * grid.depth) // 2
        outs[5] = jax.ShapeDtypeStruct((4 * grid.depth, step, width), BF)
        mix_scratch = [pltpu.VMEM((width, width), F32)]
        mix_scratch += [pltpu.VMEM((4 * grid.depth, step, width), BF)] * 2
    staging = Staging(0, ins, outs)
    pieces = small.pieces if small else []
    chained = 1 if small else 0
    result = pl.pallas_call(
        functools.partial(
            temporal_back_body, grid.depth, starts_of(parts), att_scale, layer, staging, pieces, grid.direct
        ),
        in_specs=staging.in_specs() + [VMEM_SPEC] * len(pieces),
        out_specs=staging.out_specs() + [VMEM_SPEC] * chained,
        out_shape=outs + ([small.shape()] if small else []),
        scratch_shapes=[pltpu.VMEM((frames, padded, width), BF)] * 2
        + [pltpu.VMEM((frames, padded, split), BF)]
        + [pltpu.VMEM((2 * frames, padded, split), BF)]
        + [pltpu.VMEM((2 * frames, padded, 3 * split), BF)]
        + [pltpu.VMEM((width, 2 * frames * padded), BF)]
        + [pltpu.VMEM((width, frames * padded), BF)]
        + [pltpu.VMEM((width, split), BF)] * 2
        + [pltpu.VMEM((frames, padded, width), BF)] * 2
        + [pltpu.SemaphoreType.DMA((4,))] * 2
        + scratch
        + (hop_scratch(small) if chained else [])
        + mix_scratch
        + staging.scratch(),
        compiler_params=stage_params(number, 60),
        cost_estimate=stage_cost(24000000000),
        name="temporal_stage",
    )(*ins, *(small.arrays if small else []))
    end = 6 + len(parts)
    return result[0], result[1], result[2], result[3:6], result[6:end], result[end:]


def plain_sums(parts):
    return [
        lax.psum_scatter(part.astype(F32), ("shard", "ctx"), scatter_dimension=0, tiled=True)
        for part in parts
    ]


def split_columns(value, widths):
    outs, start = [], 0
    for width in widths:
        outs.append(value[..., start : start + width])
        start += width
    return outs


def per_device(
    video_clips,
    cotangent,
    slot_clip,
    valid_places,
    norm_gain,
    norm_bias,
    triple_weight,
    entry_bias,
    merge_weight,
    branch_bias,
    mixing_weight,
    up_weight,
    up_bias,
    down_weight,
):
    grid = Grid()
    slots, frames_here, places_here, width = video_clips.shape
    places = places_here * 2
    padded = -(-places // 16) * 16
    scale = HEAD_DIM ** (-0.5)
    step_rows = triple_weight.shape[2]
    half_rows = step_rows // 2
    own_first = grid.t == 0
    straight = grid.t == grid.y

    clip_ids = jnp.arange(valid_places.shape[0], dtype=jnp.int32)
    my_clip = lax.dynamic_index_in_dim(slot_clip, grid.y, 0, keepdims=False)
    count = jnp.sum(jnp.where(my_clip == clip_ids, valid_places, 0)).astype(jnp.int32)
    valid_here = (jnp.arange(padded, dtype=jnp.int32) < count).astype(F32)[None, :, None]
    count_ref = count.reshape(1)

    def spread_in(value):
        mine = lax.dynamic_index_in_dim(value, grid.y, 0, keepdims=False)
        theirs = lax.dynamic_index_in_dim(value, 1 - grid.y, 0, keepdims=False)
        return spread_in_last(mine, grid.over_y(theirs))

    def spread_in_last(mine, got):
        keep = jnp.where(straight, mine, got)
        send = jnp.where(straight, got, mine)
        swap = grid.over_t(send)
        low = jnp.where(own_first, keep, swap)
        high = jnp.where(own_first, swap, keep)
        gap = jnp.zeros((frames_here, padded - places, width), mine.dtype)
        return jnp.concatenate([low, high, gap], axis=1)

    def spread_first(value):
        low = value[:, :places_here]
        high = value[:, places_here:places]
        keep = jnp.where(own_first, low, high)
        send = jnp.where(own_first, high, low)
        swap = grid.over_t(send)
        return jnp.where(straight, swap, keep), jnp.where(straight, keep, swap)

    def spread_last(got, mine):
        first = jnp.where(grid.y == 0, mine, got)
        second = jnp.where(grid.y == 0, got, mine)
        return jnp.stack([first, second])

    def spread_out(value):
        away, mine = spread_first(value)
        return spread_last(grid.over_y(away), mine)

    def pack_mix(item):
        return jnp.concatenate([item[..., : width // 2], item[..., width // 2 :]], axis=-2)

    def block_triple(layer, part):
        return [triple_weight[layer, part, :, i] for i in range(3)]

    def block_out(layer):
        return [merge_weight[layer, 0].T, pack_mix(mixing_weight[layer])]

    def block_s(layer):
        return block_triple(layer, 1) + [merge_weight[layer, 1].T]

    def block_m(layer):
        return [up_weight[layer], down_weight[layer].T]

    split = triple_weight.shape[-1]
    hid = up_weight.shape[-1]
    wide_t = (3 * split, split, width // 2)
    wide_s = (3 * split, split)
    wide_m = (hid, hid)

    def unpack_mix(item):
        cube = item.reshape(-1, 2, half_rows, width // 2)
        return jnp.concatenate([cube[:, 0], cube[:, 1]], axis=-1)

    def with_other(item):
        return (item, grid.over_t(item))

    def mixing_of(both):
        mix_own, mix_oth = [unpack_mix(item) for item in both]
        return jnp.stack(
            [jnp.where(own_first, mix_own, mix_oth), jnp.where(own_first, mix_oth, mix_own)],
            axis=1,
        ).reshape(width, width)

    def block_named(layer, name):
        if name == "triple_t":
            return jnp.concatenate(block_triple(layer, 0), axis=1)
        if name == "triple_s":
            return jnp.concatenate(block_triple(layer, 1), axis=1)
        if name == "merge_t":
            return merge_weight[layer, 0].T
        if name == "mix":
            return mixing_weight[layer] if grid.direct else pack_mix(mixing_weight[layer])
        if name == "merge_s":
            return merge_weight[layer, 1].T
        return block_m(layer)[0 if name == "up" else 1]

    gathered = [dict() for _ in range(LAYERS)]

    def settle(keys, near):
        for (layer, name), both in zip(keys, near):
            w = gathered[layer]
            if name == "triple_t":
                w[name] = both[0]
            elif name == "mix":
                w["mixing"] = both[0] if grid.direct else mixing_of(both)
            else:
                w[name] = both

    ahead = [
        [(0, "triple_t"), (0, "merge_t"), (0, "mix")],
        [(0, "triple_s"), (0, "merge_s"), (0, "up")],
        [(0, "down")],
        [(1, "triple_t"), (1, "merge_t"), (1, "mix")],
        [(1, "triple_s"), (1, "merge_s"), (1, "up")],
        [(1, "down")],
        [],
        [],
    ]
    named = lambda keys: [block_named(*key) for key in keys]
    modes = {"triple_t": False, "mix": "one"}
    modes_of = lambda keys: [modes.get(name, True) for _, name in keys]
    lines = {}
    if grid.direct:
        near, lines[1] = first_gather(
            grid, 7, named(ahead[0]), modes_of(ahead[0]), named(ahead[1])
        )
        settle(ahead[0], near)
    else:
        for keys in ahead:
            settle(
                keys,
                [
                    with_other(lax.all_gather(item, ("shard", "ctx"), axis=0, tiled=True))
                    for item in named(keys)
                ],
            )

    def load_at(index):
        across = [far_cotangent] if index == 3 * LAYERS - 1 and grid.direct else []
        if not grid.direct:
            return Load(grid)
        keys = ahead[index + 1]
        swapped = modes_of(keys)
        near = lines[index + 1] if keys else []
        return Load(grid, near, swapped, named(ahead[index + 2]), across)

    def loaded(index, got):
        near, new_lines = got
        if index == 3 * LAYERS - 1:
            lines["across"] = new_lines[0] if grid.direct else grid.over_y(far_cotangent)
        elif grid.direct:
            settle(ahead[index + 1], near)
            lines[index + 2] = new_lines

    small = jnp.concatenate([entry_bias[:, 1].reshape(LAYERS, -1), up_bias], axis=1)
    small_oth = grid.over_t(small)
    middle = jnp.zeros((LAYERS, split), F32)

    def query_value(both):
        return jnp.concatenate([both[:, :split], middle, both[:, split : 2 * split]], axis=1)

    gains, shifts = [item.reshape(3 * LAYERS, width) for item in (norm_gain, norm_bias)]
    biases = branch_bias.reshape(4 * LAYERS, width)
    bias_t = query_value(entry_bias[:, 0].reshape(LAYERS, -1))
    bias_s = [query_value(item) for item in (small, small_oth)]
    bias_m = [up_bias, small_oth[:, 2 * split :]]

    state = spread_in(video_clips).astype(F32)
    valid_rows = valid_here[0]
    low_cotangent = cotangent.astype(BF)
    near_cotangent = lax.dynamic_index_in_dim(low_cotangent, grid.y, 0, keepdims=False)
    far_cotangent = lax.dynamic_index_in_dim(low_cotangent, 1 - grid.y, 0, keepdims=False)
    stored = []
    squares = []
    for layer in range(LAYERS):
        w = gathered[layer]
        first = 3 * layer
        (state, unit_t, scale_t, normed_t, qkv_t, mine, swap, joined, sq_t), got = temporal_stage(
            8 + first,
            layer,
            state,
            valid_rows,
            gains,
            shifts,
            w,
            [bias_t, biases, biases],
            load_at(first),
            scale,
        )
        loaded(first, got)
        (state, unit_s, scale_s, normed_s, qkv0, qkv1, mixed0, mixed1, sq_s), got = spatial_stage(
            9 + first,
            layer,
            count_ref,
            state,
            valid_rows,
            gains,
            shifts,
            w,
            bias_s + [biases],
            load_at(first + 1),
            places,
            scale,
        )
        loaded(first + 1, got)
        (state, unit_m, scale_m, normed_m, act0, act1, slope0, slope1, sq_m), got = feed_stage(
            10 + first,
            layer,
            state,
            valid_rows,
            gains,
            shifts,
            w,
            bias_m + [biases],
            load_at(first + 2),
        )
        loaded(first + 2, got)
        squares.append((sq_t, sq_s, sq_m))
        stored.append(
            dict(
                unit_t=unit_t,
                scale_t=scale_t,
                normed_t=normed_t,
                qkv_t=qkv_t,
                mixed_t=(mine, swap),
                joined=joined,
                unit_s=unit_s,
                scale_s=scale_s,
                normed_s=normed_s,
                qkv_s=[qkv0, qkv1],
                mixed_s=[mixed0, mixed1],
                unit_m=unit_m,
                scale_m=scale_m,
                normed_m=normed_m,
                active=[act0, act1],
                slope=[slope0, slope1],
            )
        )
    upstream = spread_in_last(near_cotangent, lines["across"]).astype(F32) * valid_here
    block_output = spread_out(state.astype(BF))

    shards = [None] * LAYERS
    sums = {}
    vectors, half_rows_of = [None] * LAYERS, [None] * LAYERS
    waiting = None

    def both_cores(mine, theirs):
        return [jnp.where(own_first, mine, theirs), jnp.where(own_first, theirs, mine)]

    def carry_sums(names, parts):
        nonlocal waiting
        if not grid.direct:
            sums.update(
                zip(names, plain_sums([item[:, start : start + size] for item, start, size in parts]))
            )
            return
        waiting = (names, parts)

    def carried_parts():
        return waiting[1] if waiting else []

    def arrived_sums(result):
        nonlocal waiting
        if waiting:
            sums.update(zip(waiting[0], result))
        waiting = None

    for layer in range(LAYERS - 1, -1, -1):
        w, kept = gathered[layer], stored[layer]
        upstream, vec_m, parts_m, hidden_part, got = feed_back(
            grid, layer, layer, upstream, kept, gains, w, carried_parts()
        )
        arrived_sums(got)
        cut = hid // 2
        carry_sums(
            [("up_a", layer), ("up_b", layer), ("down_a", layer)],
            [(parts_m[0], 0, cut), (parts_m[0], cut, cut), (parts_m[1], 0, cut)],
        )
        upstream, vec_s, entry_s, parts_s, got = spatial_back(
            grid,
            2 + layer,
            layer,
            count_ref,
            upstream,
            kept,
            gains,
            w,
            carried_parts(),
            places,
            scale,
        )
        arrived_sums(got)
        carry_sums(
            [("triple_s", layer), ("down_b", layer), ("merge_s", layer)],
            [(parts_s[0], 0, 3 * split), (parts_m[1], cut, cut), (parts_s[1], 0, split)],
        )
        per_row = hid // width
        hidden_rows = [item.reshape(per_row, width) for item in hidden_part]
        half_rows_of[layer] = both_cores(
            jnp.concatenate([entry_s[:1], hidden_rows[0]]),
            jnp.concatenate([entry_s[1:2], hidden_rows[1]]),
        )
        vectors[layer] = [vec_s, vec_m]
        early = None
        if layer == 0:
            early = Small(width)
            for vec_pair in vectors:
                early.add(vec_pair[0], 0, 3)
                early.add(vec_pair[1], 0, 3)
            early.add(last_vec, 0, 4)
            for item in half_rows_of:
                early.add(item[0], 0, 3)
                early.add(item[1], 0, 3)
            for item in last_half:
                early.add(item, 0, 1)
            for sq_t, sq_s, sq_m in squares:
                for place_at, (item, start) in enumerate(
                    ((sq_t, 0), (sq_s, 0), (sq_m, 1), (sq_m, 0))
                ):
                    early.add(item, start, 1, 128 * place_at, place_at < 3)
        early_rows = early
        upstream, vec_t, entry_t, parts_t, got, early = temporal_back(
            grid,
            4 + layer,
            layer,
            upstream,
            kept,
            gains,
            w,
            carried_parts(),
            scale,
            early if grid.direct else None,
        )
        arrived_sums(got)
        if grid.direct:
            mix_sum = parts_t[2].reshape(width // 2, width)
        else:
            mix_part = parts_t[2].reshape(-1, 2, half_rows, width)
            mix_mine = lax.dynamic_index_in_dim(mix_part, grid.t, 1, keepdims=False)
            mix_theirs = lax.dynamic_index_in_dim(mix_part, 1 - grid.t, 1, keepdims=False)
            mix_got = grid.over_t(mix_theirs.astype(BF)).astype(F32)
            mix_sum = (mix_mine + mix_got).astype(BF).reshape(width // 2, width)
        carry_sums(
            [("triple_t", layer), ("merge_t", layer), ("mix", layer)],
            [(parts_t[0], 0, 3 * split), (parts_t[1], 0, split), (mix_sum, 0, width)],
        )
        last_vec = vec_t
        last_half = both_cores(entry_t[:1], jnp.zeros_like(entry_t[:1]))

    small = Small(width)
    small.add(last_vec, 0, 4)
    for item in last_half:
        small.add(item, 0, 1)
    out_low, out_ready = spread_first(upstream.astype(BF))
    if waiting:
        got, small, out_got = tail_sums(grid, 6, carried_parts(), small, out_low)
        arrived_sums(got)
        (early,) = early
    else:
        small, early = small.plain(), early_rows.plain()
        out_got = grid.over_y(out_low)
    input_grad = spread_last(out_got, out_ready).astype(F32)
    names = ("triple_t", "merge_t", "mix", "triple_s", "merge_s")
    for layer in range(LAYERS):
        up, down = [
            jnp.concatenate([sums[name + "_a", layer], sums[name + "_b", layer]], axis=1)
            for name in ("up", "down")
        ]
        shards[layer] = [sums[name, layer] for name in names] + [up, down]
    block = 6 * LAYERS
    pairs = early[:block].reshape(LAYERS, 2, 3, width)
    ends = jnp.stack([small[:4], early[block : block + 4]])
    gain_sum, shift_sum = [
        jnp.concatenate([ends[:, k : k + 1], pairs[:, :, k]], axis=1) for k in range(2)
    ]
    bias_sum = jnp.concatenate([ends[:, 2:4], pairs[:, :, 2]], axis=1)
    start = block + 4
    half_sums = early[start : start + 6 * LAYERS].reshape(LAYERS, 2, 3, width)
    end_sums = jnp.stack([small[4:6], early[start + 6 * LAYERS : start + 6 * LAYERS + 2]])
    half_sums = lax.dynamic_index_in_dim(half_sums, grid.t, 1, keepdims=False)
    end_sums = lax.dynamic_index_in_dim(end_sums, grid.t, 1, keepdims=False)
    entry_sum = jnp.stack([end_sums, half_sums[:, 0]], axis=1).reshape(LAYERS, 2, 2, split)
    hidden_sum = half_sums[:, 1:].reshape(LAYERS, hid)
    start = start + 6 * LAYERS + 2
    square_sums = early[start : start + LAYERS, : 4 * 128].reshape(LAYERS, 4, 128)[:, :, 0]
    tokens = FRAMES * width * jnp.sum(valid_places).astype(F32)
    root_squares = jnp.sqrt(square_sums / tokens)

    def triple_shape(item):
        return item.reshape(step_rows, 3, split)

    return (
        block_output,
        input_grad,
        gain_sum,
        shift_sum,
        jnp.stack([jnp.stack([triple_shape(s[0]), triple_shape(s[3])]) for s in shards]),
        entry_sum,
        jnp.stack([jnp.stack([s[1].T, s[4].T]) for s in shards]),
        bias_sum,
        jnp.stack([s[2] for s in shards]),
        jnp.stack([s[5] for s in shards]),
        hidden_sum,
        jnp.stack([s[6].T for s in shards]),
        root_squares,
    )


def solution(mesh):
    return jax.shard_map(
        per_device,
        mesh=mesh,
        in_specs=(
            P("shard", "ctx", "tp", None),
            P("shard", "ctx", "tp", None),
            P("shard"),
            P(),
            P(),
            P(),
            P(None, None, ("shard", "ctx"), None, "tp"),
            P(None, None, None, "tp"),
            P(None, None, "tp", ("shard", "ctx")),
            P(),
            P(None, ("shard", "ctx", "tp"), None),
            P(None, ("shard", "ctx"), "tp"),
            P(None, "tp"),
            P(None, "tp", ("shard", "ctx")),
        ),
        out_specs=(
            P("shard", "ctx", "tp", None),
            P("shard", "ctx", "tp", None),
            P(),
            P(),
            P(None, None, ("shard", "ctx"), None, "tp"),
            P(None, None, None, "tp"),
            P(None, None, "tp", ("shard", "ctx")),
            P(),
            P(None, ("shard", "ctx", "tp"), None),
            P(None, ("shard", "ctx"), "tp"),
            P(None, "tp"),
            P(None, "tp", ("shard", "ctx")),
            P(),
        ),
        check_vma=False,
    )
```

```python
import functools
import math

import jax
import jax.numpy as jnp
from jax import lax
from jax.experimental import pallas as pl
from jax.experimental.pallas import tpu as pltpu
from jax.sharding import PartitionSpec as P

HEAD_DIM = 64
FRAMES = 8
LAYERS = 2
AXES = ("shard", "ctx", "tp")
BF = jnp.bfloat16
F32 = jnp.float32

far_below = -1000000000.0
epsilon = 1e-06
root_half = 0.7071067811865476
gauss_scale = 0.3989422804014327


def dot_nn(left, right):
    return lax.dot_general(left, right, (((1,), (0,)), ((), ())), preferred_element_type=F32)


def dot_nt(left, right):
    return lax.dot_general(left, right, (((1,), (1,)), ((), ())), preferred_element_type=F32)


def dot_tn(left, right):
    return lax.dot_general(left, right, (((0,), (0,)), ((), ())), preferred_element_type=F32)


def rows(value):
    return value.reshape(-1, value.shape[-1])


def row_total(value):
    return jnp.sum(rows(value).astype(F32), axis=0)


def lane_masks(shape):
    lane = lax.broadcasted_iota(jnp.int32, shape, 1)
    return lane < HEAD_DIM


def softmax_rows(scores):
    top = jnp.max(scores, axis=-1, keepdims=True)
    raised = jnp.exp(scores - top)
    total = jnp.sum(raised, axis=-1, keepdims=True)
    return raised * (1.0 / total)


def sides(value, first):
    zero = jnp.zeros_like(value)
    return [jnp.where(first, value, zero), jnp.where(first, zero, value)]


def heads_forward(qkv, fix, scale, put):
    first = lane_masks(qkv(0, 0).shape)
    scores = []
    for pair in range(3):
        k = qkv(1, pair)
        scores.append([dot_nt(q, k) for q in sides(qkv(0, pair), first)])
    shares = [[softmax_rows(fix(item * scale)).astype(BF) for item in both] for both in scores]
    for pair in range(3):
        v = qkv(2, pair)
        outs = [dot_nn(item, v) for item in shares[pair]]
        put(pair, jnp.where(first, outs[0], outs[1]).astype(BF))


def heads_backward(qkv, back, fix, scale, put):
    first = lane_masks(qkv(0, 0).shape)
    scores, backs = [], []
    for pair in range(3):
        k, v = qkv(1, pair), qkv(2, pair)
        scores.append([dot_nt(q, k) for q in sides(qkv(0, pair), first)])
        backs.append([dot_nt(b, v) for b in sides(back(pair), first)])
    low_shares, low_scores = [], []
    for pair in range(3):
        low_shares.append([])
        low_scores.append([])
        for side in range(2):
            shares = softmax_rows(fix(scores[pair][side] * scale))
            back_shares = backs[pair][side]
            inner = jnp.sum(back_shares * shares, axis=-1, keepdims=True)
            low_scores[pair].append((shares * (back_shares - inner)).astype(BF))
            low_shares[pair].append(shares.astype(BF))
    for pair in range(3):
        q, k, bm = qkv(0, pair), qkv(1, pair), back(pair)
        gq = [dot_nn(item, k) for item in low_scores[pair]]
        gk = [dot_tn(item, q) for item in low_scores[pair]]
        gv = [dot_tn(item, bm) for item in low_shares[pair]]
        put(0, pair, (jnp.where(first, gq[0], gq[1]) * scale).astype(BF))
        put(1, pair, (jnp.where(first, gk[0], gk[1]) * scale).astype(BF))
        put(2, pair, jnp.where(first, gv[0], gv[1]).astype(BF))


def column(part, pair):
    start = part * 384 + pair * 128
    return slice(start, start + 128)


def spatial_fix(count_ref, padded, places):
    col = lax.broadcasted_iota(jnp.int32, (padded, padded), 1)
    floor = jnp.where(col < places, far_below, 3.0 * far_below)
    allowed = col < jnp.minimum(count_ref[0], places)
    return lambda scores: jnp.where(allowed, scores, floor)


def temporal_fix(tile):
    size = FRAMES * tile
    row = lax.broadcasted_iota(jnp.int32, (size, size), 0)
    col = lax.broadcasted_iota(jnp.int32, (size, size), 1)
    same = (row & (tile - 1)) == (col & (tile - 1))
    return lambda scores: jnp.where(same, scores, 3.0 * far_below)


class Grid:
    def __init__(self):
        self.shards = lax.axis_size("shard")
        self.depth = self.shards // 2
        shard = lax.axis_index("shard")
        self.z = shard // 2
        self.x = shard % 2
        self.y = lax.axis_index("ctx")
        self.t = lax.axis_index("tp")
        self.direct = self.depth == 4

    def perm(self, move):
        pairs = []
        for z in range(self.depth):
            for x in range(2):
                for y in range(2):
                    for t in range(2):
                        tz, tx, ty, tt = move(z, x, y, t)
                        pairs.append(
                            (((z * 2 + x) * 2 + y) * 2 + t, ((tz * 2 + tx) * 2 + ty) * 2 + tt)
                        )
        return pairs

    def send(self, value, pairs):
        return lax.ppermute(value, AXES, pairs)

    def over_x(self, value):
        return self.send(value, self.perm(lambda z, x, y, t: (z, 1 - x, y, t)))

    def over_y(self, value):
        return self.send(value, self.perm(lambda z, x, y, t: (z, x, 1 - y, t)))

    def over_t(self, value):
        return self.send(value, self.perm(lambda z, x, y, t: (z, x, y, 1 - t)))

    def over_z(self, value, step):
        depth = self.depth
        return self.send(value, self.perm(lambda z, x, y, t: ((z + step) % depth, x, y, t)))

    def over_bit(self, value, bit):
        pairs = []
        for s in range(self.shards):
            for y in range(2):
                for t in range(2):
                    pairs.append(((s * 2 + y) * 2 + t, ((s ^ bit) * 2 + y) * 2 + t))
        return self.send(value, pairs)

    def total(self, value, across):
        if across:
            value = value + self.over_t(value)
        value = value + self.over_y(value)
        bit = 1
        while bit < self.shards:
            value = value + self.over_bit(value, bit)
            bit *= 2
        return value


class Sums:
    def __init__(self, place, source, part, own, ra, rb, sx, sy, rx, ry, low, gz, send, recv):
        self.place, self.source, self.part, self.own = place, source, part, own
        self.ra, self.rb, self.sx, self.sy = ra, rb, sx, sy
        self.rx, self.ry, self.low, self.gz = rx, ry, low, gz
        self.send, self.recv = send, recv
        self.depth = part.shape[0]
        self.half = part.shape[0] // 2

    def copy(self, number, src, dst, target):
        return remote(src, dst, self.send.at[number], self.recv.at[number], target)

    def far(self):
        x, y = self.place.x, self.place.y
        low, high = pl.ds(0, self.half), pl.ds(self.half, self.half)
        return [
            self.copy(0, self.source.at[low, 1 - x, 1 - y], self.ra, self.place.over_y()),
            self.copy(1, self.source.at[high, 1 - x, 1 - y], self.rb, self.place.over_x()),
        ]

    def near(self):
        return [
            self.copy(2, self.sx, self.rx, self.place.over_x()),
            self.copy(3, self.sy, self.ry, self.place.over_y()),
        ]

    def deep(self):
        return [
            self.copy(
                3 + k,
                self.low.at[lax.rem(self.place.z + k, self.depth)],
                self.gz.at[k - 1],
                self.place.over_z(k),
            )
            for k in range(1, self.depth)
        ]

    def first(self):
        for item in self.far():
            item.start()

    def second(self):
        x, y, half = self.place.x, self.place.y, self.half
        for item in self.far():
            item.wait()
        for k in range(2 * half):
            toward_x, toward_y = self.part[k, 1 - x, y], self.part[k, x, 1 - y]
            if k < half:
                toward_x = toward_x + self.ra[k]
            else:
                toward_y = toward_y + self.rb[k - half]
            self.sx[k] = toward_x
            self.sy[k] = toward_y
        for item in self.near():
            item.start()

    def kept(self, k):
        mine = self.part[k, self.place.x, self.place.y].astype(F32)
        return mine + self.rx[k].astype(F32) + self.ry[k].astype(F32)

    def third(self):
        for item in self.near():
            item.wait()
        for k in range(self.depth):
            mine = self.part[k, self.place.x, self.place.y]
            self.low[k] = mine + (self.rx[k] + self.ry[k])
        for item in self.deep():
            item.start()

    def last(self):
        for item in self.deep():
            item.wait()
        total = self.kept(self.place.z)
        for k in range(self.depth - 1):
            total = total + self.gz[k].astype(F32)
        self.own[...] = total


def remote(src, dst, send, recv, target):
    return pltpu.make_async_remote_copy(
        src_ref=src,
        dst_ref=dst,
        send_sem=send,
        recv_sem=recv,
        device_id=target,
        device_id_type=pl.DeviceIdType.MESH,
    )


class Place:
    def __init__(self, depth):
        self.depth = depth
        shard = lax.axis_index("shard")
        self.z = shard // 2
        self.x = lax.rem(shard, 2)
        self.y = lax.axis_index("ctx")
        self.t = lax.axis_index("tp")

    def over_x(self):
        return {"shard": self.z * 2 + 1 - self.x}

    def over_y(self):
        return {"ctx": 1 - self.y}

    def over_t(self):
        return {"tp": 1 - self.t}

    def over_z(self, step):
        return {"shard": lax.rem(self.z + step, self.depth) * 2 + self.x}

    def meet(self, chips, cores):
        barrier = pltpu.get_barrier_semaphore()
        targets = [self.over_t()] if cores else []
        if chips:
            targets += [self.over_x(), self.over_y()]
            targets += [self.over_z(k) for k in range(1, self.depth)]
        for target in targets:
            pl.semaphore_signal(
                barrier, inc=1, device_id=target, device_id_type=pl.DeviceIdType.MESH
            )
        pl.semaphore_wait(barrier, len(targets))


class Carrier:
    def __init__(self, place, cores, starts, sources, parts, owns, scratch, most=2):
        self.place, self.cores = place, cores
        lanes = [pl.ds(start, own.shape[1]) for start, own in zip(starts, owns)]
        sources = [ref.at[:, :, :, :, cols] for ref, cols in zip(sources, lanes)]
        parts = [ref.at[:, :, :, :, cols] for ref, cols in zip(parts, lanes)]
        self.sums = [
            Sums(place, source, part, own, *scratch[10 * i : 10 * i + 10])
            for i, (source, part, own) in enumerate(zip(sources, parts, owns))
        ]
        self.groups = [[item] for item in self.sums[: most - 1]]
        if self.sums[most - 1 :]:
            self.groups.append(self.sums[most - 1 :])

    def begin(self):
        self.place.meet(bool(self.sums), self.cores)
        for item in self.sums:
            item.first()

    def step(self, number):
        if number == 0:
            self.begin()
            return
        last = len(self.groups)
        if 2 <= number <= last + 1:
            for item in self.groups[number - 2]:
                item.third()
        if number <= last:
            for item in self.groups[number - 1]:
                item.second()

    def end(self):
        for item in self.sums:
            item.last()


def carried(grid, parts):
    depth = grid.depth
    cubes, shapes, scratch = [], [], []
    for part, start, lanes in parts:
        step_rows = part.shape[0] // (depth * 4)
        block = lambda count: pltpu.VMEM((count, step_rows, lanes), BF)
        cubes.append(part.reshape(depth, 2, 2, step_rows, part.shape[1]))
        shapes.append(jax.ShapeDtypeStruct((step_rows, lanes), F32))
        scratch += [block(depth // 2)] * 2 + [block(depth)] * 5 + [block(depth - 1)]
        scratch += [pltpu.SemaphoreType.DMA((3 + depth,))] * 2
    return cubes, shapes, scratch


def stage_params(number, vmem=58, sends=True):
    if not sends:
        return pltpu.CompilerParams(vmem_limit_bytes=vmem << 20)
    return pltpu.CompilerParams(
        collective_id=number, has_side_effects=True, vmem_limit_bytes=vmem << 20
    )


def stage_cost(flops):
    return pl.CostEstimate(flops=flops, bytes_accessed=30000000, transcendentals=0)


VMEM_SPEC = pl.BlockSpec(memory_space=pltpu.VMEM)
SMEM_SPEC = pl.BlockSpec(memory_space=pltpu.SMEM)


ANY_SPEC = pl.BlockSpec(memory_space=pl.ANY)


def is_big(item):
    return item.shape[-1] >= 128 and math.prod(item.shape) >= 65536


class Staging:
    def __init__(self, smem, ins, outs):
        self.smem = smem
        self.ins = [i >= smem and is_big(item) for i, item in enumerate(ins)]
        self.outs = [is_big(item) for item in outs]
        self.in_shapes = [item for item, big in zip(ins, self.ins) if big]
        self.out_shapes = [item for item, big in zip(outs, self.outs) if big]

    def in_specs(self):
        specs = [ANY_SPEC if big else VMEM_SPEC for big in self.ins]
        return [SMEM_SPEC] * self.smem + specs[self.smem :]

    def out_specs(self):
        return [ANY_SPEC if big else VMEM_SPEC for big in self.outs]

    def scratch(self):
        held = self.in_shapes + self.out_shapes
        blocks = [pltpu.VMEM(item.shape, item.dtype) for item in held]
        return blocks + [pltpu.SemaphoreType.DMA((len(held),))]

    def count(self):
        return len(self.in_shapes) + len(self.out_shapes) + 1

    def open(self, in_refs, out_refs, refs):
        refs = list(refs)
        sems = refs.pop()
        number = 0
        pairs = []
        for group, flags in ((in_refs, self.ins), (out_refs, self.outs)):
            view, moves = [], []
            for ref, big in zip(group, flags):
                if big:
                    moves.append((ref, refs[number], sems.at[number]))
                    ref = refs[number]
                    number += 1
                view.append(ref)
            pairs.append((view, moves))
        (self.in_view, self.in_moves), (self.out_view, self.out_moves) = pairs
        return self.in_view, self.out_view

    def fetch(self):
        copies = [pltpu.make_async_copy(src, dst, sem) for src, dst, sem in self.in_moves]
        for item in copies:
            item.start()
        for item in copies:
            item.wait()

    def move_out(self, moves):
        copies = [pltpu.make_async_copy(src, dst, sem) for dst, src, sem in moves]
        for item in copies:
            item.start()
        for item in copies:
            item.wait()

    def flush(self, count=None):
        self.moved = len(self.out_moves) if count is None else sum(self.outs[:count])
        self.move_out(self.out_moves[: self.moved])

    def flush_rest(self):
        self.move_out(self.out_moves[self.moved :])


def row_of(ref, index):
    return ref.at[pl.ds(index, 1)]


def splitter(refs):
    refs = list(refs)
    return lambda count: [refs.pop(0) for _ in range(count)]


class Hops:
    def __init__(self, place, pieces, refs, total, held, came, send, recv):
        z = place.z
        targets = [place.over_t()]
        targets.append({"shard": (z + 1 - 2 * lax.rem(z, 2)) * 2 + place.x})
        targets.append({"shard": (z + 2 - 4 * (z // 2)) * 2 + place.x})
        targets += [place.over_x(), place.over_y()]
        self.pieces, self.refs = pieces, refs
        self.total, self.held, self.came = total, held, came
        self.copies = [
            remote(held.at[k], came.at[k], send.at[k], recv.at[k], target)
            for k, target in enumerate(targets)
        ]

    def begin(self):
        self.held[0] = jnp.zeros(self.held.shape[1:], F32)
        for ref, (start, count, row, lane) in zip(self.refs, self.pieces):
            lanes = ref.shape[1]
            self.held[0, row : row + count, lane : lane + lanes] = ref[start : start + count]
        self.copies[0].start()

    def hop(self, number):
        self.copies[number - 1].wait()
        value = self.held[number - 1] + self.came[number - 1]
        if number < len(self.copies):
            self.held[number] = value
            self.copies[number].start()
        else:
            self.total[...] = value


class Small:
    def __init__(self, width):
        self.arrays, self.pieces, self.rows, self.width = [], [], 0, width

    def add(self, array, start, count, lane=0, stay=False):
        self.arrays.append(array)
        self.pieces.append((start, count, self.rows, lane))
        if not stay:
            self.rows += count

    def shape(self):
        return jax.ShapeDtypeStruct((-(-self.rows // 8) * 8, self.width), F32)

    def plain(self):
        whole = jnp.zeros(self.shape().shape, F32)
        for array, (start, count, row, lane) in zip(self.arrays, self.pieces):
            whole = whole.at[row : row + count, lane : lane + array.shape[1]].set(
                array[start : start + count]
            )
        return lax.psum(whole, AXES)


def hop_scratch(small):
    block = pltpu.VMEM((5,) + small.shape().shape, F32)
    return [block, block] + [pltpu.SemaphoreType.DMA((5,))] * 2


def tail_body(depth, starts, pieces, *refs):
    take = splitter(refs)
    count = len(starts)
    parts, small, (away,) = take(count), take(len(pieces)), take(1)
    owns, (total, back) = take(count), take(2)
    hop_refs, (send, recv) = take(4), take(2)
    place = Place(depth)
    carrier = Carrier(place, True, starts, parts, parts, owns, take(10 * count))
    hops = Hops(place, pieces, small, total, *hop_refs)
    across = remote(away, back, send.at[0], recv.at[0], place.over_y())
    carrier.step(0)
    hops.begin()
    for number in range(1, 4):
        hops.hop(number)
        carrier.step(number)
    hops.hop(4)
    across.start()
    hops.hop(5)
    carrier.end()
    across.wait()


def starts_of(parts):
    return [start for _, start, _ in parts]


def tail_sums(grid, number, parts, small, away):
    cubes, shapes, scratch = carried(grid, parts)
    count = len(small.arrays)
    result = pl.pallas_call(
        functools.partial(tail_body, grid.depth, starts_of(parts), small.pieces),
        in_specs=[VMEM_SPEC] * (len(parts) + count + 1),
        out_specs=[VMEM_SPEC] * (len(parts) + 2),
        out_shape=shapes + [small.shape(), jax.ShapeDtypeStruct(away.shape, away.dtype)],
        scratch_shapes=hop_scratch(small) + [pltpu.SemaphoreType.DMA((1,))] * 2 + scratch,
        compiler_params=stage_params(number),
        cost_estimate=stage_cost(20000000000),
        name="sum_rows",
    )(*cubes, *small.arrays, away)
    return result[:-2], result[-2], result[-1]


def norm_back_rows(e, unit, scale, gain):
    along = e * gain
    lanes = e.shape[-1]
    mean_along = jnp.sum(along, axis=-1, keepdims=True) * (1.0 / lanes)
    mean_unit = jnp.sum(along * unit, axis=-1, keepdims=True) * (1.0 / lanes)
    return scale * (along - mean_along - unit * mean_unit)


def column_sum(value):
    return jnp.sum(value, axis=0, keepdims=True)


def tie(value, *others):
    return lax.optimization_barrier((value, *others))[0]


class Near:
    def __init__(self, place, line, whole, other, send, recv):
        self.place, self.line, self.whole, self.other = place, line, whole, other
        self.send, self.recv = send, recv
        self.depth = line.shape[0]

    def pair(self, number, src, dst, target):
        return remote(src, dst, self.send.at[number], self.recv.at[number], target)

    def at(self, ref, dx, dy, low=0, size=None):
        x = 1 - self.place.x if dx else self.place.x
        y = 1 - self.place.y if dy else self.place.y
        view = ref.at[pl.ds(low, size or self.depth), x, y]
        return view.at[:, self.place.t] if len(ref.shape) == 6 else view

    def sides(self):
        dst = self.at(self.whole, 0, 0)
        return [
            self.pair(0, self.line, dst, self.place.over_x()),
            self.pair(1, self.line, dst, self.place.over_y()),
        ]

    def corners(self):
        half = self.depth // 2
        first = self.at(self.whole, 1, 0, 0, half)
        second = self.at(self.whole, 0, 1, half, half)
        return [
            self.pair(2, first, first, self.place.over_y()),
            self.pair(3, second, second, self.place.over_x()),
        ]

    def swap(self, number):
        if self.other is None:
            return []
        if number == 0:
            src, dst = self.line, self.at(self.other, 0, 0)
        else:
            dx, dy = number & 1, number >> 1
            src, dst = self.at(self.whole, dx, dy), self.at(self.other, dx, dy)
        return [self.pair(4 + number, src, dst, self.place.over_t())]

    def begin(self):
        for item in self.sides() + self.swap(0) + [self.keep()]:
            item.start()

    def keep(self):
        return pltpu.make_async_copy(self.line, self.at(self.whole, 0, 0), self.send.at[8])

    def middle(self):
        for item in self.sides():
            item.wait()
        for item in self.corners() + self.swap(1) + self.swap(2):
            item.start()

    def corner_in(self):
        for item in self.corners():
            item.wait()
        for item in self.swap(3):
            item.start()

    def end(self):
        for number in range(4):
            for item in self.swap(number):
                item.wait()
        self.keep().wait()


class Deep:
    def __init__(self, place, block, line, send, recv):
        self.place, self.block, self.line, self.send, self.recv = place, block, line, send, recv

    def copies(self):
        return [
            remote(
                self.block,
                self.line.at[self.place.z],
                self.send.at[k - 1],
                self.recv.at[k - 1],
                self.place.over_z(k),
            )
            for k in range(1, self.line.shape[0])
        ]

    def begin(self):
        for item in self.copies():
            item.start()
        self.line[self.place.z] = self.block[...]

    def end(self):
        for item in self.copies():
            item.wait()


def landing(line, both):
    depth, step_rows, lanes = line
    if both == "one":
        return [jax.ShapeDtypeStruct((depth, 2, 2, 2, step_rows, lanes), BF)]
    return [jax.ShapeDtypeStruct((depth, 2, 2, step_rows, lanes), BF)] * (2 if both else 1)


def landed(outs, both):
    whole = outs.pop(0)
    if both == "one":
        return whole, whole
    return whole, outs.pop(0) if both else None


class Load:
    def __init__(self, grid, near=(), swapped=(), deep=(), across=()):
        self.depth = grid.depth
        self.swapped = list(swapped)
        self.near_count, self.deep_count = len(near), len(deep)
        self.inputs = list(near) + list(deep) + list(across)
        self.across_count = len(across)
        self.shapes, self.scratch, self.specs = [], [], []
        for line, both in zip(near, swapped):
            shapes = landing(line.shape, both)
            self.shapes += shapes
            self.specs += [ANY_SPEC] * len(shapes)
            self.scratch += [pltpu.SemaphoreType.DMA((9,)), pltpu.SemaphoreType.DMA((8,))]
        for block in deep:
            self.shapes.append(jax.ShapeDtypeStruct((self.depth,) + block.shape, BF))
            self.specs.append(VMEM_SPEC)
            self.scratch += [pltpu.SemaphoreType.DMA((self.depth - 1,))] * 2

        for item in across:
            self.shapes.append(jax.ShapeDtypeStruct(item.shape, item.dtype))
            self.specs.append(VMEM_SPEC)
            self.scratch += [pltpu.SemaphoreType.DMA((1,))] * 2

    def results(self, arrays):
        arrays = list(arrays)
        flat = lambda item: item.reshape(-1, item.shape[-1])
        near = []
        for both in self.swapped:
            near.append([None if item is None else flat(item) for item in landed(arrays, both)])
        return near, arrays


class Loader:
    def __init__(self, place, cores, load, ins, outs, sems):
        self.place, self.cores, self.load = place, cores, load
        ins, outs, sems = list(ins), list(outs), list(sems)
        self.near = []
        for both in load.swapped:
            whole, other = landed(outs, both)
            self.near.append(Near(place, ins.pop(0), whole, other, sems.pop(0), sems.pop(0)))
        self.deep = [
            Deep(place, ins.pop(0), outs.pop(0), sems.pop(0), sems.pop(0))
            for _ in range(load.deep_count)
        ]
        self.across = []
        for _ in range(load.across_count):
            send, recv = sems.pop(0), sems.pop(0)
            self.across.append(
                remote(ins.pop(0), outs.pop(0), send.at[0], recv.at[0], place.over_y())
            )

    def begin(self):
        chips = bool(self.near or self.deep or self.across)
        if chips or self.cores:
            self.place.meet(chips, self.cores or bool(self.near))
        for item in self.near + self.deep:
            item.begin()
        for item in self.across:
            item.start()

    def middle(self):
        for item in self.near:
            item.middle()

    def end(self):
        for item in self.near:
            item.corner_in()
        for item in self.near:
            item.end()
        for item in self.deep:
            item.end()
        for item in self.across:
            item.wait()


def open_kernel(load, staging, refs, scratch):
    take = splitter(refs)
    in_refs = take(len(staging.ins))
    load_ins = take(len(load.inputs))
    out_refs = take(len(staging.outs))
    load_outs = take(len(load.shapes))
    scratch_refs = take(scratch)
    in_refs, out_refs = staging.open(in_refs, out_refs, take(staging.count()))
    return in_refs, out_refs, scratch_refs, (load_ins, load_outs, take(len(load.scratch)))


def kernel_call(body, number, ins, shapes, scratch, load, name, smem=0, cores=False):
    staging = Staging(smem, ins, shapes)
    result = pl.pallas_call(
        functools.partial(body, staging),
        in_specs=staging.in_specs() + [VMEM_SPEC] * len(load.inputs),
        out_specs=staging.out_specs() + load.specs,
        out_shape=list(shapes) + load.shapes,
        scratch_shapes=list(scratch) + staging.scratch() + load.scratch,
        compiler_params=stage_params(number, sends=cores or bool(load.inputs)),
        cost_estimate=stage_cost(20000000000),
        name=name,
    )(*ins, *load.inputs)
    return result[: len(shapes)], load.results(result[len(shapes) :])


def first_body(swapped, depth, next_count, *refs):
    take = splitter(refs)
    count = len(swapped)
    blocks, next_blocks = take(count), take(next_count)
    wholes = [landed(take(2 if both is True else 1), both) for both in swapped]
    next_lines = take(next_count)
    lines = take(count)
    place = Place(depth)
    deep = [Deep(place, blocks[i], lines[i], *take(2)) for i in range(count)]
    near = [Near(place, lines[i], *wholes[i], *take(2)) for i in range(count)]
    after = [Deep(place, next_blocks[i], next_lines[i], *take(2)) for i in range(next_count)]
    place.meet(True, True)
    for item in deep:
        item.begin()
    for one, two in zip(deep, near):
        one.end()
        two.begin()
    for item in after:
        item.begin()
    for item in near:
        item.middle()
    for item in near:
        item.corner_in()
    for item in near:
        item.end()
    for item in after:
        item.end()


def first_gather(grid, number, blocks, swapped, next_blocks):
    depth = grid.depth
    line = lambda item: (depth,) + item.shape
    shapes = []
    for item, both in zip(blocks, swapped):
        shapes += landing(line(item), both)
    specs = [ANY_SPEC] * len(shapes) + [VMEM_SPEC] * len(next_blocks)
    shapes += [jax.ShapeDtypeStruct(line(item), BF) for item in next_blocks]
    sems = lambda size: [pltpu.SemaphoreType.DMA((size,))] * 2
    scratch = [pltpu.VMEM(line(item), BF) for item in blocks]
    for _ in blocks:
        scratch += sems(depth - 1)
    for _ in blocks:
        scratch += [pltpu.SemaphoreType.DMA((9,)), pltpu.SemaphoreType.DMA((8,))]
    for _ in next_blocks:
        scratch += sems(depth - 1)
    arrays = list(
        pl.pallas_call(
            functools.partial(first_body, tuple(swapped), depth, len(next_blocks)),
            in_specs=[VMEM_SPEC] * (len(blocks) + len(next_blocks)),
            out_specs=specs,
            out_shape=shapes,
            scratch_shapes=scratch,
            compiler_params=stage_params(number),
            cost_estimate=stage_cost(20000000000),
            name="first_gather",
        )(*blocks, *next_blocks)
    )
    flat = lambda item: None if item is None else item.reshape(-1, item.shape[-1])
    near = [[flat(item) for item in landed(arrays, both)] for both in swapped]
    return near, arrays


def norm_rows(state, gain, shift):
    lanes = state.shape[-1]
    center = state - jnp.sum(state, axis=-1, keepdims=True) * (1.0 / lanes)
    spread = jnp.sum(center * center, axis=-1, keepdims=True) * (1.0 / lanes)
    scale = lax.rsqrt(spread + epsilon)
    unit = center * scale
    return (unit * gain + shift).astype(BF), unit, scale


def square_sum(value, valid):
    return jnp.sum(jnp.sum(value * value, axis=-1, keepdims=True) * valid, axis=0, keepdims=True)


def temporal_body(load, att_scale, layer, staging, *refs):
    ins, outs, scratch, loads = open_kernel(load, staging, refs, 3)
    state, valid, gain, shift, tri, tri_bias, merge0, merge1, merge_bias, mixing, mix_bias = ins
    out, unit, scale, normed, qkv, mine, swap, joined, sq = outs
    away, send, recv = scratch
    gain, shift = row_of(gain, 3 * layer), row_of(shift, 3 * layer)
    tri_bias = row_of(tri_bias, layer)
    merge_bias, mix_bias = row_of(merge_bias, 4 * layer), row_of(mix_bias, 4 * layer + 1)
    place = Place(load.depth)
    loader = Loader(place, True, load, *loads)
    frames, padded, width = state.shape
    loader.begin()
    staging.fetch()

    def norm_one(f, carry):
        low, u, s = norm_rows(state[f], gain[...], shift[...])
        normed[f] = low
        unit[f] = u
        scale[f] = s
        return carry

    lax.fori_loop(0, frames, norm_one, 0)
    own = normed.at[pl.ds(0, frames)]
    swap_normed = remote(
        own, normed.at[pl.ds(frames, frames)], send.at[0], recv.at[0], place.over_t()
    )
    swap_normed.start()

    def project(f, carry):
        qkv[f] = (dot_nn(normed[f], tri[...]) + tri_bias[...]).astype(BF)
        return carry

    lax.fori_loop(0, frames, project, 0)
    swap_normed.wait()
    lax.fori_loop(frames, 2 * frames, project, 0)
    tile = 16
    fix = temporal_fix(tile)

    def one(i, carry):
        at = pl.ds(pl.multiple_of(i * tile, tile), tile)

        def put(pair, value):
            cols = slice(pair * 128, pair * 128 + 128)
            both = value.reshape(2 * frames, tile, 128)
            mine[:, at, cols] = both[:frames]
            away[:, at, cols] = both[frames:]

        heads_forward(
            lambda part, pair: qkv[:, at, column(part, pair)].reshape(2 * frames * tile, 128),
            fix,
            att_scale,
            put,
        )
        return carry

    lax.fori_loop(0, padded // tile, one, 0)
    swap_mixed = remote(away, swap, send.at[1], recv.at[1], place.over_t())
    swap_mixed.start()
    loader.middle()
    swap_mixed.wait()

    def finish(f, carry):
        low = (
            dot_nt(mine[f], merge0[...]) + dot_nt(swap[f], merge1[...]) + merge_bias[...]
        ).astype(BF)
        joined[f] = low
        branch = dot_nn(low, mixing[...]) + mix_bias[...]
        out[f] = state[f] + branch
        return carry + square_sum(branch, valid[...])

    total = lax.fori_loop(0, frames, finish, jnp.zeros((1, 1), F32))
    sq[...] = jnp.broadcast_to(total, sq.shape)
    staging.flush()
    loader.end()


def temporal_stage(number, layer, state, valid, gain, shift, w, biases, load, att_scale):
    frames, padded, width = state.shape
    split = w["merge_t"][0].shape[1]
    shape = lambda dims, kind=BF: jax.ShapeDtypeStruct(dims, kind)
    ins = [state, valid, gain, shift, w["triple_t"], biases[0], *w["merge_t"], biases[1]]
    ins += [w["mixing"], biases[2]]
    return kernel_call(
        functools.partial(temporal_body, load, att_scale, layer),
        number,
        ins,
        [
            shape((frames, padded, width), F32),
            shape((frames, padded, width), F32),
            shape((frames, padded, 1), F32),
            shape((2 * frames, padded, width)),
            shape((2 * frames, padded, 3 * split)),
            shape((frames, padded, split)),
            shape((frames, padded, split)),
            shape((frames, padded, width)),
            shape((8, 128), F32),
        ],
        [pltpu.VMEM((frames, padded, split), BF)] + [pltpu.SemaphoreType.DMA((2,))] * 2,
        load,
        "temporal_forward",
        cores=True,
    )


def spatial_body(load, places, att_scale, layer, staging, *refs):
    ins, outs, scratch, loads = open_kernel(load, staging, refs, 0)
    count_ref, state, valid, gain, shift, tri0, tri1, bias0, bias1, merge0, merge1, out_bias = ins
    out, unit, scale, normed, qkv0, qkv1, mixed0, mixed1, sq = outs
    gain, shift = row_of(gain, 3 * layer + 1), row_of(shift, 3 * layer + 1)
    bias0, bias1 = row_of(bias0, layer), row_of(bias1, layer)
    out_bias = row_of(out_bias, 4 * layer + 2)
    place = Place(load.depth)
    loader = Loader(place, False, load, *loads)
    frames, padded, width = state.shape
    fix = spatial_fix(count_ref, padded, places)
    loader.begin()
    staging.fetch()

    def one(f, carry):
        low, u, s = norm_rows(state[f], gain[...], shift[...])
        normed[f] = low
        unit[f] = u
        scale[f] = s
        for tri, bias, qkv, mixed in (
            (tri0, bias0, qkv0, mixed0),
            (tri1, bias1, qkv1, mixed1),
        ):
            qkv[f] = (dot_nn(low, tri[...]) + bias[...]).astype(BF)

            def put(pair, value, mixed=mixed):
                mixed[f, :, pair * 128 : pair * 128 + 128] = value

            heads_forward(
                lambda part, pair, qkv=qkv: qkv[f, :, column(part, pair)], fix, att_scale, put
            )
        branch = dot_nt(mixed0[f], merge0[...]) + dot_nt(mixed1[f], merge1[...]) + out_bias[...]
        out[f] = state[f] + branch
        return carry + square_sum(branch, valid[...])

    cut = frames - 1
    total = lax.fori_loop(0, cut, one, jnp.zeros((1, 1), F32))
    loader.middle()
    total = lax.fori_loop(cut, frames, one, total)
    sq[...] = jnp.broadcast_to(total, sq.shape)
    staging.flush()
    loader.end()


def spatial_stage(number, layer, count_ref, state, valid, gain, shift, w, biases, load, places, att_scale):
    frames, padded, width = state.shape
    split = w["merge_s"][0].shape[1]
    shape = lambda dims, kind=BF: jax.ShapeDtypeStruct(dims, kind)
    ins = [count_ref, state, valid, gain, shift, *w["triple_s"], biases[0], biases[1]]
    ins += [*w["merge_s"], biases[2]]
    return kernel_call(
        functools.partial(spatial_body, load, places, att_scale, layer),
        number,
        ins,
        [
            shape((frames, padded, width), F32),
            shape((frames, padded, width), F32),
            shape((frames, padded, 1), F32),
            shape((frames, padded, width)),
            shape((frames, padded, 3 * split)),
            shape((frames, padded, 3 * split)),
            shape((frames, padded, split)),
            shape((frames, padded, split)),
            shape((8, 128), F32),
        ],
        [],
        load,
        "spatial_forward",
        1,
    )


def feed_body(load, layer, staging, *refs):
    ins, outs, scratch, loads = open_kernel(load, staging, refs, 0)
    state, valid, gain, shift, up0, up1, bias0, bias1, down0, down1, out_bias = ins
    out, unit, scale, normed, act0, act1, slope0, slope1, sq = outs
    gain, shift = row_of(gain, 3 * layer + 2), row_of(shift, 3 * layer + 2)
    bias0, bias1 = row_of(bias0, layer), row_of(bias1, layer)
    out_bias = row_of(out_bias, 4 * layer + 3)
    place = Place(load.depth)
    loader = Loader(place, False, load, *loads)
    frames, padded, width = state.shape
    loader.begin()
    staging.fetch()

    def one(f, carry):
        low, u, s = norm_rows(state[f], gain[...], shift[...])
        normed[f] = low
        unit[f] = u
        scale[f] = s
        branch = jnp.broadcast_to(out_bias[...], (padded, width))
        for up, bias, down, act, slope in (
            (up0, bias0, down0, act0, slope0),
            (up1, bias1, down1, act1, slope1),
        ):
            lanes = up.shape[1]
            piece = lanes // 3
            for number in range(3):
                cols = slice(number * piece, (number + 1) * piece)
                hidden = dot_nn(low, up[:, cols]) + bias[:, cols]
                below = 0.5 * (1.0 + lax.erf(hidden * root_half))
                act[f, :, cols] = (hidden * below).astype(BF)
                slope[f, :, cols] = (
                    below + hidden * gauss_scale * jnp.exp(-0.5 * hidden * hidden)
                ).astype(BF)
            branch = branch + dot_nt(act[f], down[...])
        value = state[f] + branch
        out[f] = value
        return (
            carry[0] + square_sum(branch, valid[...]),
            carry[1] + square_sum(value, valid[...]),
        )

    zero = jnp.zeros((1, 1), F32)
    cut = frames - 1
    total = lax.fori_loop(0, cut, one, (zero, zero))
    loader.middle()
    total = lax.fori_loop(cut, frames, one, total)
    sq[...] = jnp.broadcast_to(total[0], sq.shape)
    sq[0:1] = jnp.broadcast_to(total[1], (1, sq.shape[1]))
    staging.flush()
    loader.end()


def feed_stage(number, layer, state, valid, gain, shift, w, biases, load):
    frames, padded, width = state.shape
    hid = w["up"][0].shape[1]
    shape = lambda dims, kind=BF: jax.ShapeDtypeStruct(dims, kind)
    ins = [state, valid, gain, shift, *w["up"], biases[0], biases[1], *w["down"], biases[2]]
    return kernel_call(
        functools.partial(feed_body, load, layer),
        number,
        ins,
        [
            shape((frames, padded, width), F32),
            shape((frames, padded, width), F32),
            shape((frames, padded, 1), F32),
            shape((frames, padded, width)),
        ]
        + [shape((frames, padded, hid))] * 4
        + [shape((8, 128), F32)],
        [],
        load,
        "feed_forward",
    )


def feed_back_body(depth, starts, steps, layer, *refs):
    take = splitter(refs)
    count = len(starts)
    state, normed, unit, scale, gain = take(5)
    gain = row_of(gain, 3 * layer + 2)
    oth, own = take(4), take(4)
    parts = take(count)
    out, sums, g_up, g_down, h_own, h_oth = take(6)
    owns = take(count)
    r, rt, nt, bh, s_up, s_down, r_up, r_down, send, recv = take(10)
    place = Place(depth)
    carrier = Carrier(place, True, starts, parts, parts, owns, take(10 * count))
    frames, padded, width = state.shape
    rows_all = frames * padded
    i = pl.program_id(0)

    @pl.when(i == 0)
    def _():
        carrier.step(0)
        sums[...] = jnp.zeros_like(sums)

        def begin(f, carry):
            low = state[f].astype(BF)
            r[f] = low
            out[f] = jnp.zeros((padded, width), F32)
            return carry + column_sum(low.astype(F32))

        sums[2:3] = lax.fori_loop(0, frames, begin, jnp.zeros((1, width), F32))
        rt[...] = r[...].reshape(rows_all, width).T
        nt[...] = normed[...].reshape(rows_all, width).T

    def work(down, up, active, slope, h_sum):
        lanes = down.shape[1]

        value = dot_nn(r[...].reshape(rows_all, width), down[...])
        value = (value * slope[...].reshape(rows_all, lanes).astype(F32)).astype(BF)
        bh[...] = value.reshape(frames, padded, lanes)
        h_sum[...] = column_sum(value.astype(F32))
        out[...] += dot_nt(value, up[...]).reshape(frames, padded, width)
        return (
            dot_nn(nt[...], bh[...].reshape(rows_all, lanes)),
            dot_nn(rt[...], active[...].reshape(rows_all, lanes)),
        )

    def swaps(j):
        return [
            remote(s_up.at[j], r_up.at[j], send.at[0, j], recv.at[0, j], place.over_t()),
            remote(s_down.at[j], r_down.at[j], send.at[1, j], recv.at[1, j], place.over_t()),
        ]

    for number, at in ((1, 1), (2, 3), (3, 4)):
        if count:

            @pl.when(i == at)
            def _(number=number):
                carrier.step(number)

    @pl.when(i < steps)
    def _():
        up_part, down_part = work(*oth, h_oth)
        s_up[i] = up_part.astype(BF)
        s_down[i] = down_part.astype(BF)
        for item in swaps(i):
            item.start()

    @pl.when(i >= steps)
    def _():
        j = i - steps
        up_part, down_part = work(*own, h_own)
        for item in swaps(j):
            item.wait()
        g_up[...] = (up_part + r_up[j].astype(F32)).astype(BF)
        g_down[...] = (down_part + r_down[j].astype(F32)).astype(BF)

    @pl.when(i == 2 * steps - 1)
    def _():
        def finish(f, carry):
            e, u = out[f], unit[f]
            out[f] = state[f] + norm_back_rows(e, u, scale[f], gain[...])
            return (carry[0] + column_sum(e * u), carry[1] + column_sum(e))

        zero = jnp.zeros((1, width), F32)
        sums[0:1], sums[1:2] = lax.fori_loop(0, frames, finish, (zero, zero))
        carrier.end()


def feed_back(grid, number, layer, state, kept, gain, w, parts):
    frames, padded, width = state.shape
    hid = w["up"][0].shape[1]
    steps = 3
    lanes = hid // steps
    cubes, shapes, scratch = carried(grid, parts)
    whole = lambda item: pl.BlockSpec(
        item.shape, lambda i: (0,) * item.ndim, pipeline_mode=pl.Buffered(1)
    )
    first = lambda i: jnp.minimum(i, steps - 1)
    later = lambda i: jnp.maximum(i - steps, 0)

    def side(at):
        weight = pl.BlockSpec((width, lanes), lambda i: (0, at(i)))
        token = pl.BlockSpec((frames, padded, lanes), lambda i: (0, 0, at(i)))
        return [weight, weight, token, token]

    tokens = lambda item: item.reshape(frames, padded, hid)
    sides = [
        [w["down"][k], w["up"][k], tokens(kept["active"][k]), tokens(kept["slope"][k])]
        for k in (1, 0)
    ]
    fixed = [state, kept["normed_m"], kept["unit_m"], kept["scale_m"], gain]
    vec = lambda at: pl.BlockSpec((1, lanes), lambda i: (0, at(i)))
    result = pl.pallas_call(
        functools.partial(feed_back_body, grid.depth, starts_of(parts), steps, layer),
        grid=(2 * steps,),
        in_specs=[whole(item) for item in fixed]
        + side(first)
        + side(later)
        + [whole(item) for item in cubes],
        out_specs=[
            pl.BlockSpec((frames, padded, width), lambda i: (0, 0, 0)),
            pl.BlockSpec((8, width), lambda i: (0, 0)),
            pl.BlockSpec((width, lanes), lambda i: (0, later(i))),
            pl.BlockSpec((width, lanes), lambda i: (0, later(i))),
            vec(later),
            vec(first),
        ]
        + [pl.BlockSpec(item.shape, lambda i: (0, 0)) for item in shapes],
        out_shape=[
            jax.ShapeDtypeStruct((frames, padded, width), F32),
            jax.ShapeDtypeStruct((8, width), F32),
            jax.ShapeDtypeStruct((width, hid), BF),
            jax.ShapeDtypeStruct((width, hid), BF),
            jax.ShapeDtypeStruct((1, hid), F32),
            jax.ShapeDtypeStruct((1, hid), F32),
        ]
        + shapes,
        scratch_shapes=[
            pltpu.VMEM((frames, padded, width), BF),
            pltpu.VMEM((width, frames * padded), BF),
            pltpu.VMEM((width, frames * padded), BF),
            pltpu.VMEM((frames, padded, lanes), BF),
        ]
        + [pltpu.VMEM((steps, width, lanes), BF)] * 4
        + [pltpu.SemaphoreType.DMA((2, steps))] * 2
        + scratch,
        compiler_params=stage_params(number),
        cost_estimate=stage_cost(24000000000),
        name="feed_back",
    )(*fixed, *sides[0], *sides[1], *cubes)
    return result[0], result[1], result[2:4], (result[4], result[5]), result[6:]


def spatial_back_body(depth, starts, places, att_scale, layer, staging, *refs):
    take = splitter(refs)
    count = len(starts)
    in_refs, out_refs = take(14 + count), take(5 + count)
    own_scratch, sum_scratch = take(13), take(10 * count)
    sources = in_refs[14:]
    in_refs, out_refs = staging.open(in_refs, out_refs, take(staging.count()))
    take = splitter(in_refs + out_refs + own_scratch + sum_scratch)
    (count_ref, state, merge0, merge1, mixed0, mixed1, qkv0, qkv1) = take(8)
    tri0, tri1, normed, unit, scale, gain = take(6)
    gain = row_of(gain, 3 * layer + 1)
    parts = take(count)
    out, sums, q_sums, g_tri, g_merge = take(5)
    owns = take(count)
    r, bm0, bm1, b0, b1, rt, nt, s_tri, r_tri, s_merge, r_merge, send, recv = take(13)
    place = Place(depth)
    carrier = Carrier(place, True, starts, sources, parts, owns, take(10 * count), 3)
    frames, padded, width = state.shape
    rows_all = frames * padded
    split = merge0.shape[1]
    fix = spatial_fix(count_ref, padded, places)
    carrier.step(0)
    staging.fetch()

    def one(f, carry):
        low = state[f].astype(BF)
        r[f] = low
        for merge, bm, src, dst in ((merge0, bm0, qkv0, b0), (merge1, bm1, qkv1, b1)):
            bm[...] = dot_nn(low, merge[...]).astype(BF)

            def put(part, pair, value, dst=dst):
                dst[f, :, column(part, pair)] = value

            heads_backward(
                lambda part, pair, src=src: src[f, :, column(part, pair)],
                lambda pair, bm=bm: bm[:, pair * 128 : pair * 128 + 128],
                fix,
                att_scale,
                put,
            )
        return carry + column_sum(low.astype(F32))

    sums[...] = jnp.zeros_like(sums)
    q_sums[...] = jnp.zeros_like(q_sums)
    total = jnp.zeros((1, width), F32)
    total = lax.fori_loop(0, 2, one, total)
    carrier.step(1)
    total = lax.fori_loop(2, 3, one, total)
    carrier.step(2)
    sums[2:3] = lax.fori_loop(3, frames, one, total)
    rt[...] = r[...].reshape(rows_all, width).T
    nt[...] = normed[...].reshape(rows_all, width).T
    flat = lambda ref, part: ref[:, :, part * split : (part + 1) * split].reshape(rows_all, split)
    swap_tri = remote(s_tri, r_tri, send.at[0], recv.at[0], place.over_t())
    swap_merge = remote(s_merge, r_merge, send.at[1], recv.at[1], place.over_t())
    s_merge[...] = dot_nn(rt[...], mixed1[...]).astype(BF)
    swap_merge.start()
    for part in range(3):
        cols = slice(part * split, (part + 1) * split)
        s_tri[:, cols] = dot_nn(nt[...], flat(b1, part)).astype(BF)
    swap_tri.start()
    carrier.step(3)

    def finish(f, carry):
        e = dot_nt(b0[f], tri0[...]) + dot_nt(b1[f], tri1[...])
        u = unit[f]
        out[f] = state[f] + norm_back_rows(e, u, scale[f], gain[...])
        return (
            carry[0] + column_sum(e * u),
            carry[1] + column_sum(e),
            carry[2] + column_sum(b0[f].astype(F32)),
            carry[3] + column_sum(b1[f].astype(F32)),
        )

    zero, wide = jnp.zeros((1, width), F32), jnp.zeros((1, 3 * split), F32)
    sums[0:1], sums[1:2], mine, theirs = lax.fori_loop(
        0, frames, finish, (zero, zero, wide, wide)
    )
    carrier.step(4)
    for number, value in ((0, mine), (1, theirs)):
        q_sums[number : number + 1, :split] = value[:, :split]
        q_sums[number : number + 1, split:] = value[:, 2 * split :]
    swap_merge.wait()
    g_merge[...] = (dot_nn(rt[...], mixed0[...]) + r_merge[...].astype(F32)).astype(BF)
    swap_tri.wait()
    for part in range(3):
        cols = slice(part * split, (part + 1) * split)
        mine = dot_nn(nt[...], flat(b0, part))
        g_tri[:, cols] = (mine + r_tri[:, cols].astype(F32)).astype(BF)
    staging.flush(5)
    carrier.end()
    staging.flush_rest()


def spatial_back(grid, number, layer, count_ref, state, kept, gain, w, parts, places, att_scale):
    frames, padded, width = state.shape
    split = w["merge_s"][0].shape[1]
    cubes, shapes, scratch = carried(grid, parts)
    flat = [item.reshape(frames * padded, split) for item in kept["mixed_s"]]
    fixed = [count_ref, state, *w["merge_s"], *flat, *kept["qkv_s"], *w["triple_s"]]
    fixed += [kept["normed_s"], kept["unit_s"], kept["scale_s"], gain]
    ins = fixed + cubes
    outs = [
        jax.ShapeDtypeStruct((frames, padded, width), F32),
        jax.ShapeDtypeStruct((8, width), F32),
        jax.ShapeDtypeStruct((8, 2 * split), F32),
        jax.ShapeDtypeStruct((width, 3 * split), BF),
        jax.ShapeDtypeStruct((width, split), BF),
    ] + shapes
    staging = Staging(1, ins, outs)
    result = pl.pallas_call(
        functools.partial(
            spatial_back_body, grid.depth, starts_of(parts), places, att_scale, layer, staging
        ),
        in_specs=staging.in_specs(),
        out_specs=staging.out_specs(),
        out_shape=outs,
        scratch_shapes=[pltpu.VMEM((frames, padded, width), BF)]
        + [pltpu.VMEM((padded, split), BF)] * 2
        + [pltpu.VMEM((frames, padded, 3 * split), BF)] * 2
        + [pltpu.VMEM((width, frames * padded), BF)] * 2
        + [pltpu.VMEM((width, 3 * split), BF)] * 2
        + [pltpu.VMEM((width, split), BF)] * 2
        + [pltpu.SemaphoreType.DMA((2,))] * 2
        + scratch
        + staging.scratch(),
        compiler_params=stage_params(number),
        cost_estimate=stage_cost(24000000000),
        name="spatial_stage",
    )(*ins)
    return result[0], result[1], result[2], result[3:5], result[5:]


def temporal_back_body(depth, starts, att_scale, layer, staging, pieces, joined_mix, *refs):
    take = splitter(refs)
    count = len(starts)
    chained = 1 if pieces else 0
    in_refs, small = take(13 + count), take(len(pieces))
    out_refs, total = take(6 + count), take(chained)
    own_scratch, sum_scratch, hop_refs = take(13), take(10 * count), take(4 * chained)
    mix_refs = take(3) if joined_mix else None
    sources = in_refs[13:]
    in_refs, out_refs = staging.open(in_refs, out_refs, take(staging.count()))
    take = splitter(in_refs + out_refs + own_scratch + sum_scratch)
    state, mixing, joined, merge0, merge1, mine, swap, qkv, tri = take(9)
    normed, unit, scale, gain = take(4)
    gain = row_of(gain, 3 * layer)
    parts = take(count)
    out, sums, q_sums, g_tri, g_merge, g_mix = take(6)
    owns = take(count)
    r, bj, away, bm, b, nt, rt, s_merge, r_merge, s_back, r_back, send, recv = take(13)
    joins = len(g_mix.shape) == 3
    if joins:
        (whole_mix, s_mix, r_mix), shard_mix = mix_refs, g_mix
    place = Place(depth)
    carrier = Carrier(place, True, starts, sources, parts, owns, take(10 * count))
    frames, padded, width = state.shape
    rows_all = frames * padded
    split = merge0.shape[1]
    carrier.step(0)
    hops = Hops(place, pieces, small, *total, *hop_refs) if chained else None
    if chained:
        hops.begin()
    staging.fetch()

    def begin(f, carry):
        low = state[f].astype(BF)
        r[f] = low
        value = dot_nt(low, mixing[...]).astype(BF)
        bj[f] = value
        bm[f] = dot_nn(value, merge0[...]).astype(BF)
        away[f] = dot_nn(value, merge1[...]).astype(BF)
        return (carry[0] + column_sum(low.astype(F32)), carry[1] + column_sum(value.astype(F32)))

    sums[...] = jnp.zeros_like(sums)
    q_sums[...] = jnp.zeros_like(q_sums)
    zero = jnp.zeros((1, width), F32)
    sums[3:4], sums[2:3] = lax.fori_loop(0, frames, begin, (zero, zero))
    swap_bm = remote(
        away, bm.at[pl.ds(frames, frames)], send.at[0], recv.at[0], place.over_t()
    )
    swap_bm.start()
    carrier.step(1)
    rt[...] = bj[...].reshape(rows_all, width).T
    s_merge[...] = dot_nn(rt[...], swap[...].reshape(rows_all, split)).astype(BF)
    swap_merge = remote(s_merge, r_merge, send.at[1], recv.at[1], place.over_t())
    swap_merge.start()
    if chained:
        hops.hop(1)
    rt[...] = joined[...].reshape(rows_all, width).T
    for half in range(2):
        cols = slice(half * split, (half + 1) * split)
        mix_part = dot_nn(rt[...], r[:, :, cols].reshape(rows_all, split))
        (whole_mix if joins else g_mix)[:, cols] = mix_part
    if joins:
        blocks, step = shard_mix.shape[0], shard_mix.shape[1]

        def mix_rows(k, core):
            at = pl.multiple_of((2 * k + core) * step, 8)
            return whole_mix[pl.ds(at, step), :]

        for k in range(blocks):
            s_mix[k] = mix_rows(k, 1 - place.t).astype(BF)
        swap_mix = remote(s_mix, r_mix, send.at[3], recv.at[3], place.over_t())
        swap_mix.start()
    rt[...] = bj[...].reshape(rows_all, width).T
    swap_merge.wait()
    g_merge[...] = (dot_nn(rt[...], mine[...].reshape(rows_all, split)) + r_merge[...].astype(F32)).astype(BF)
    swap_bm.wait()
    tile = 16
    fix = temporal_fix(tile)

    def one(i, carry):
        at = pl.ds(pl.multiple_of(i * tile, tile), tile)

        def put(part, pair, value):
            b[:, at, column(part, pair)] = value.reshape(FRAMES, tile, 128)

        heads_backward(
            lambda part, pair: qkv[:, at, column(part, pair)].reshape(FRAMES * tile, 128),
            lambda pair: bm[:, at, pair * 128 : pair * 128 + 128].reshape(FRAMES * tile, 128),
            fix,
            att_scale,
            put,
        )
        return carry

    tiles = padded // tile
    lax.fori_loop(0, tiles // 3, one, 0)
    if joins:
        swap_mix.wait()
        for k in range(blocks):
            shard_mix[k] = (mix_rows(k, place.t) + r_mix[k].astype(F32)).astype(BF)
    carrier.step(2)
    if chained:
        hops.hop(2)
    lax.fori_loop(tiles // 3, 2 * tiles // 3, one, 0)
    if chained:
        hops.hop(3)
    lax.fori_loop(2 * tiles // 3, tiles, one, 0)
    if chained:
        hops.hop(4)
    carrier.step(3)

    def toward(f, carry):
        s_back[f] = dot_nt(b[f + frames], tri[...]).astype(BF)
        return carry

    lax.fori_loop(0, frames, toward, 0)
    swap_back = remote(s_back, r_back, send.at[2], recv.at[2], place.over_t())
    swap_back.start()
    nt[...] = normed[...].reshape(2 * rows_all, width).T
    for part in range(3):
        cols = slice(part * split, (part + 1) * split)
        g_tri[:, cols] = dot_nn(
            nt[...], b[:, :, cols].reshape(2 * rows_all, split)
        ).astype(BF)
    swap_back.wait()

    def finish(f, carry):
        e = dot_nt(b[f], tri[...]) + r_back[f].astype(F32)
        u = unit[f]
        out[f] = state[f] + norm_back_rows(e, u, scale[f], gain[...])
        both = column_sum(b[f].astype(F32)) + column_sum(b[f + frames].astype(F32))
        return (carry[0] + column_sum(e * u), carry[1] + column_sum(e), carry[2] + both)

    sums[0:1], sums[1:2], wide = lax.fori_loop(
        0, frames, finish, (zero, zero, jnp.zeros((1, 3 * split), F32))
    )
    q_sums[0:1, :split] = wide[:, :split]
    q_sums[0:1, split:] = wide[:, 2 * split :]
    if chained:
        hops.hop(5)
    staging.flush(6)
    carrier.end()
    staging.flush_rest()


def temporal_back(grid, number, layer, state, kept, gain, w, parts, att_scale, small=None):
    frames, padded, width = state.shape
    split = w["merge_t"][0].shape[1]
    cubes, shapes, scratch = carried(grid, parts)
    fixed = [state, w["mixing"], kept["joined"], *w["merge_t"], *kept["mixed_t"], kept["qkv_t"]]
    fixed += [w["triple_t"], kept["normed_t"], kept["unit_t"], kept["scale_t"], gain]
    ins = fixed + cubes
    outs = [
        jax.ShapeDtypeStruct((frames, padded, width), F32),
        jax.ShapeDtypeStruct((8, width), F32),
        jax.ShapeDtypeStruct((8, 2 * split), F32),
        jax.ShapeDtypeStruct((width, 3 * split), BF),
        jax.ShapeDtypeStruct((width, split), BF),
        jax.ShapeDtypeStruct((width, width), F32),
    ] + shapes
    mix_scratch = []
    if grid.direct:
        step = width // (4 * grid.depth) // 2
        outs[5] = jax.ShapeDtypeStruct((4 * grid.depth, step, width), BF)
        mix_scratch = [pltpu.VMEM((width, width), F32)]
        mix_scratch += [pltpu.VMEM((4 * grid.depth, step, width), BF)] * 2
    staging = Staging(0, ins, outs)
    pieces = small.pieces if small else []
    chained = 1 if small else 0
    result = pl.pallas_call(
        functools.partial(
            temporal_back_body, grid.depth, starts_of(parts), att_scale, layer, staging, pieces, grid.direct
        ),
        in_specs=staging.in_specs() + [VMEM_SPEC] * len(pieces),
        out_specs=staging.out_specs() + [VMEM_SPEC] * chained,
        out_shape=outs + ([small.shape()] if small else []),
        scratch_shapes=[pltpu.VMEM((frames, padded, width), BF)] * 2
        + [pltpu.VMEM((frames, padded, split), BF)]
        + [pltpu.VMEM((2 * frames, padded, split), BF)]
        + [pltpu.VMEM((2 * frames, padded, 3 * split), BF)]
        + [pltpu.VMEM((width, 2 * frames * padded), BF)]
        + [pltpu.VMEM((width, frames * padded), BF)]
        + [pltpu.VMEM((width, split), BF)] * 2
        + [pltpu.VMEM((frames, padded, width), BF)] * 2
        + [pltpu.SemaphoreType.DMA((4,))] * 2
        + scratch
        + (hop_scratch(small) if chained else [])
        + mix_scratch
        + staging.scratch(),
        compiler_params=stage_params(number, 60),
        cost_estimate=stage_cost(24000000000),
        name="temporal_stage",
    )(*ins, *(small.arrays if small else []))
    end = 6 + len(parts)
    return result[0], result[1], result[2], result[3:6], result[6:end], result[end:]


def plain_sums(parts):
    return [
        lax.psum_scatter(part.astype(F32), ("shard", "ctx"), scatter_dimension=0, tiled=True)
        for part in parts
    ]


def split_columns(value, widths):
    outs, start = [], 0
    for width in widths:
        outs.append(value[..., start : start + width])
        start += width
    return outs


def per_device(
    video_clips,
    cotangent,
    slot_clip,
    valid_places,
    norm_gain,
    norm_bias,
    triple_weight,
    entry_bias,
    merge_weight,
    branch_bias,
    mixing_weight,
    up_weight,
    up_bias,
    down_weight,
):
    grid = Grid()
    slots, frames_here, places_here, width = video_clips.shape
    places = places_here * 2
    padded = -(-places // 16) * 16
    scale = HEAD_DIM ** (-0.5)
    step_rows = triple_weight.shape[2]
    half_rows = step_rows // 2
    own_first = grid.t == 0
    straight = grid.t == grid.y

    clip_ids = jnp.arange(valid_places.shape[0], dtype=jnp.int32)
    my_clip = lax.dynamic_index_in_dim(slot_clip, grid.y, 0, keepdims=False)
    count = jnp.sum(jnp.where(my_clip == clip_ids, valid_places, 0)).astype(jnp.int32)
    valid_here = (jnp.arange(padded, dtype=jnp.int32) < count).astype(F32)[None, :, None]
    count_ref = count.reshape(1)

    def spread_in(value):
        mine = lax.dynamic_index_in_dim(value, grid.y, 0, keepdims=False)
        theirs = lax.dynamic_index_in_dim(value, 1 - grid.y, 0, keepdims=False)
        return spread_in_last(mine, grid.over_y(theirs))

    def spread_in_last(mine, got):
        keep = jnp.where(straight, mine, got)
        send = jnp.where(straight, got, mine)
        swap = grid.over_t(send)
        low = jnp.where(own_first, keep, swap)
        high = jnp.where(own_first, swap, keep)
        gap = jnp.zeros((frames_here, padded - places, width), mine.dtype)
        return jnp.concatenate([low, high, gap], axis=1)

    def spread_first(value):
        low = value[:, :places_here]
        high = value[:, places_here:places]
        keep = jnp.where(own_first, low, high)
        send = jnp.where(own_first, high, low)
        swap = grid.over_t(send)
        return jnp.where(straight, swap, keep), jnp.where(straight, keep, swap)

    def spread_last(got, mine):
        first = jnp.where(grid.y == 0, mine, got)
        second = jnp.where(grid.y == 0, got, mine)
        return jnp.stack([first, second])

    def spread_out(value):
        away, mine = spread_first(value)
        return spread_last(grid.over_y(away), mine)

    def pack_mix(item):
        return jnp.concatenate([item[..., : width // 2], item[..., width // 2 :]], axis=-2)

    def block_triple(layer, part):
        return [triple_weight[layer, part, :, i] for i in range(3)]

    def block_out(layer):
        return [merge_weight[layer, 0].T, pack_mix(mixing_weight[layer])]

    def block_s(layer):
        return block_triple(layer, 1) + [merge_weight[layer, 1].T]

    def block_m(layer):
        return [up_weight[layer], down_weight[layer].T]

    split = triple_weight.shape[-1]
    hid = up_weight.shape[-1]
    wide_t = (3 * split, split, width // 2)
    wide_s = (3 * split, split)
    wide_m = (hid, hid)

    def unpack_mix(item):
        cube = item.reshape(-1, 2, half_rows, width // 2)
        return jnp.concatenate([cube[:, 0], cube[:, 1]], axis=-1)

    def with_other(item):
        return (item, grid.over_t(item))

    def mixing_of(both):
        mix_own, mix_oth = [unpack_mix(item) for item in both]
        return jnp.stack(
            [jnp.where(own_first, mix_own, mix_oth), jnp.where(own_first, mix_oth, mix_own)],
            axis=1,
        ).reshape(width, width)

    def block_named(layer, name):
        if name == "triple_t":
            return jnp.concatenate(block_triple(layer, 0), axis=1)
        if name == "triple_s":
            return jnp.concatenate(block_triple(layer, 1), axis=1)
        if name == "merge_t":
            return merge_weight[layer, 0].T
        if name == "mix":
            return mixing_weight[layer] if grid.direct else pack_mix(mixing_weight[layer])
        if name == "merge_s":
            return merge_weight[layer, 1].T
        return block_m(layer)[0 if name == "up" else 1]

    gathered = [dict() for _ in range(LAYERS)]

    def settle(keys, near):
        for (layer, name), both in zip(keys, near):
            w = gathered[layer]
            if name == "triple_t":
                w[name] = both[0]
            elif name == "mix":
                w["mixing"] = both[0] if grid.direct else mixing_of(both)
            else:
                w[name] = both

    ahead = [
        [(0, "triple_t"), (0, "merge_t"), (0, "mix")],
        [(0, "triple_s"), (0, "merge_s"), (0, "up")],
        [(0, "down")],
        [(1, "triple_t"), (1, "merge_t"), (1, "mix")],
        [(1, "triple_s"), (1, "merge_s"), (1, "up")],
        [(1, "down")],
        [],
        [],
    ]
    named = lambda keys: [block_named(*key) for key in keys]
    modes = {"triple_t": False, "mix": "one"}
    modes_of = lambda keys: [modes.get(name, True) for _, name in keys]
    lines = {}
    if grid.direct:
        near, lines[1] = first_gather(
            grid, 7, named(ahead[0]), modes_of(ahead[0]), named(ahead[1])
        )
        settle(ahead[0], near)
    else:
        for keys in ahead:
            settle(
                keys,
                [
                    with_other(lax.all_gather(item, ("shard", "ctx"), axis=0, tiled=True))
                    for item in named(keys)
                ],
            )

    def load_at(index):
        across = [far_cotangent] if index == 3 * LAYERS - 1 and grid.direct else []
        if not grid.direct:
            return Load(grid)
        keys = ahead[index + 1]
        swapped = modes_of(keys)
        near = lines[index + 1] if keys else []
        return Load(grid, near, swapped, named(ahead[index + 2]), across)

    def loaded(index, got):
        near, new_lines = got
        if index == 3 * LAYERS - 1:
            lines["across"] = new_lines[0] if grid.direct else grid.over_y(far_cotangent)
        elif grid.direct:
            settle(ahead[index + 1], near)
            lines[index + 2] = new_lines

    small = jnp.concatenate([entry_bias[:, 1].reshape(LAYERS, -1), up_bias], axis=1)
    small_oth = grid.over_t(small)
    middle = jnp.zeros((LAYERS, split), F32)

    def query_value(both):
        return jnp.concatenate([both[:, :split], middle, both[:, split : 2 * split]], axis=1)

    gains, shifts = [item.reshape(3 * LAYERS, width) for item in (norm_gain, norm_bias)]
    biases = branch_bias.reshape(4 * LAYERS, width)
    bias_t = query_value(entry_bias[:, 0].reshape(LAYERS, -1))
    bias_s = [query_value(item) for item in (small, small_oth)]
    bias_m = [up_bias, small_oth[:, 2 * split :]]

    state = spread_in(video_clips).astype(F32)
    valid_rows = valid_here[0]
    low_cotangent = cotangent.astype(BF)
    near_cotangent = lax.dynamic_index_in_dim(low_cotangent, grid.y, 0, keepdims=False)
    far_cotangent = lax.dynamic_index_in_dim(low_cotangent, 1 - grid.y, 0, keepdims=False)
    stored = []
    squares = []
    for layer in range(LAYERS):
        w = gathered[layer]
        first = 3 * layer
        (state, unit_t, scale_t, normed_t, qkv_t, mine, swap, joined, sq_t), got = temporal_stage(
            8 + first,
            layer,
            state,
            valid_rows,
            gains,
            shifts,
            w,
            [bias_t, biases, biases],
            load_at(first),
            scale,
        )
        loaded(first, got)
        (state, unit_s, scale_s, normed_s, qkv0, qkv1, mixed0, mixed1, sq_s), got = spatial_stage(
            9 + first,
            layer,
            count_ref,
            state,
            valid_rows,
            gains,
            shifts,
            w,
            bias_s + [biases],
            load_at(first + 1),
            places,
            scale,
        )
        loaded(first + 1, got)
        (state, unit_m, scale_m, normed_m, act0, act1, slope0, slope1, sq_m), got = feed_stage(
            10 + first,
            layer,
            state,
            valid_rows,
            gains,
            shifts,
            w,
            bias_m + [biases],
            load_at(first + 2),
        )
        loaded(first + 2, got)
        squares.append((sq_t, sq_s, sq_m))
        stored.append(
            dict(
                unit_t=unit_t,
                scale_t=scale_t,
                normed_t=normed_t,
                qkv_t=qkv_t,
                mixed_t=(mine, swap),
                joined=joined,
                unit_s=unit_s,
                scale_s=scale_s,
                normed_s=normed_s,
                qkv_s=[qkv0, qkv1],
                mixed_s=[mixed0, mixed1],
                unit_m=unit_m,
                scale_m=scale_m,
                normed_m=normed_m,
                active=[act0, act1],
                slope=[slope0, slope1],
            )
        )
    upstream = spread_in_last(near_cotangent, lines["across"]).astype(F32) * valid_here
    block_output = spread_out(state.astype(BF))

    shards = [None] * LAYERS
    sums = {}
    vectors, half_rows_of = [None] * LAYERS, [None] * LAYERS
    waiting = None

    def both_cores(mine, theirs):
        return [jnp.where(own_first, mine, theirs), jnp.where(own_first, theirs, mine)]

    def carry_sums(names, parts):
        nonlocal waiting
        if not grid.direct:
            sums.update(
                zip(names, plain_sums([item[:, start : start + size] for item, start, size in parts]))
            )
            return
        waiting = (names, parts)

    def carried_parts():
        return waiting[1] if waiting else []

    def arrived_sums(result):
        nonlocal waiting
        if waiting:
            sums.update(zip(waiting[0], result))
        waiting = None

    for layer in range(LAYERS - 1, -1, -1):
        w, kept = gathered[layer], stored[layer]
        upstream, vec_m, parts_m, hidden_part, got = feed_back(
            grid, layer, layer, upstream, kept, gains, w, carried_parts()
        )
        arrived_sums(got)
        cut = hid // 2
        carry_sums(
            [("up_a", layer), ("up_b", layer), ("down_a", layer)],
            [(parts_m[0], 0, cut), (parts_m[0], cut, cut), (parts_m[1], 0, cut)],
        )
        upstream, vec_s, entry_s, parts_s, got = spatial_back(
            grid,
            2 + layer,
            layer,
            count_ref,
            upstream,
            kept,
            gains,
            w,
            carried_parts(),
            places,
            scale,
        )
        arrived_sums(got)
        carry_sums(
            [("triple_s", layer), ("down_b", layer), ("merge_s", layer)],
            [(parts_s[0], 0, 3 * split), (parts_m[1], cut, cut), (parts_s[1], 0, split)],
        )
        per_row = hid // width
        hidden_rows = [item.reshape(per_row, width) for item in hidden_part]
        half_rows_of[layer] = both_cores(
            jnp.concatenate([entry_s[:1], hidden_rows[0]]),
            jnp.concatenate([entry_s[1:2], hidden_rows[1]]),
        )
        vectors[layer] = [vec_s, vec_m]
        early = None
        if layer == 0:
            early = Small(width)
            for vec_pair in vectors:
                early.add(vec_pair[0], 0, 3)
                early.add(vec_pair[1], 0, 3)
            early.add(last_vec, 0, 4)
            for item in half_rows_of:
                early.add(item[0], 0, 3)
                early.add(item[1], 0, 3)
            for item in last_half:
                early.add(item, 0, 1)
            for sq_t, sq_s, sq_m in squares:
                for place_at, (item, start) in enumerate(
                    ((sq_t, 0), (sq_s, 0), (sq_m, 1), (sq_m, 0))
                ):
                    early.add(item, start, 1, 128 * place_at, place_at < 3)
        early_rows = early
        upstream, vec_t, entry_t, parts_t, got, early = temporal_back(
            grid,
            4 + layer,
            layer,
            upstream,
            kept,
            gains,
            w,
            carried_parts(),
            scale,
            early if grid.direct else None,
        )
        arrived_sums(got)
        if grid.direct:
            mix_sum = parts_t[2].reshape(width // 2, width)
        else:
            mix_part = parts_t[2].reshape(-1, 2, half_rows, width)
            mix_mine = lax.dynamic_index_in_dim(mix_part, grid.t, 1, keepdims=False)
            mix_theirs = lax.dynamic_index_in_dim(mix_part, 1 - grid.t, 1, keepdims=False)
            mix_got = grid.over_t(mix_theirs.astype(BF)).astype(F32)
            mix_sum = (mix_mine + mix_got).astype(BF).reshape(width // 2, width)
        carry_sums(
            [("triple_t", layer), ("merge_t", layer), ("mix", layer)],
            [(parts_t[0], 0, 3 * split), (parts_t[1], 0, split), (mix_sum, 0, width)],
        )
        last_vec = vec_t
        last_half = both_cores(entry_t[:1], jnp.zeros_like(entry_t[:1]))

    small = Small(width)
    small.add(last_vec, 0, 4)
    for item in last_half:
        small.add(item, 0, 1)
    out_low, out_ready = spread_first(upstream.astype(BF))
    if waiting:
        got, small, out_got = tail_sums(grid, 6, carried_parts(), small, out_low)
        arrived_sums(got)
        (early,) = early
    else:
        small, early = small.plain(), early_rows.plain()
        out_got = grid.over_y(out_low)
    input_grad = spread_last(out_got, out_ready).astype(F32)
    names = ("triple_t", "merge_t", "mix", "triple_s", "merge_s")
    for layer in range(LAYERS):
        up, down = [
            jnp.concatenate([sums[name + "_a", layer], sums[name + "_b", layer]], axis=1)
            for name in ("up", "down")
        ]
        shards[layer] = [sums[name, layer] for name in names] + [up, down]
    block = 6 * LAYERS
    pairs = early[:block].reshape(LAYERS, 2, 3, width)
    ends = jnp.stack([small[:4], early[block : block + 4]])
    gain_sum, shift_sum = [
        jnp.concatenate([ends[:, k : k + 1], pairs[:, :, k]], axis=1) for k in range(2)
    ]
    bias_sum = jnp.concatenate([ends[:, 2:4], pairs[:, :, 2]], axis=1)
    start = block + 4
    half_sums = early[start : start + 6 * LAYERS].reshape(LAYERS, 2, 3, width)
    end_sums = jnp.stack([small[4:6], early[start + 6 * LAYERS : start + 6 * LAYERS + 2]])
    half_sums = lax.dynamic_index_in_dim(half_sums, grid.t, 1, keepdims=False)
    end_sums = lax.dynamic_index_in_dim(end_sums, grid.t, 1, keepdims=False)
    entry_sum = jnp.stack([end_sums, half_sums[:, 0]], axis=1).reshape(LAYERS, 2, 2, split)
    hidden_sum = half_sums[:, 1:].reshape(LAYERS, hid)
    start = start + 6 * LAYERS + 2
    square_sums = early[start : start + LAYERS, : 4 * 128].reshape(LAYERS, 4, 128)[:, :, 0]
    tokens = FRAMES * width * jnp.sum(valid_places).astype(F32)
    root_squares = jnp.sqrt(square_sums / tokens)

    def triple_shape(item):
        return item.reshape(step_rows, 3, split)

    return (
        block_output,
        input_grad,
        gain_sum,
        shift_sum,
        jnp.stack([jnp.stack([triple_shape(s[0]), triple_shape(s[3])]) for s in shards]),
        entry_sum,
        jnp.stack([jnp.stack([s[1].T, s[4].T]) for s in shards]),
        bias_sum,
        jnp.stack([s[2] for s in shards]),
        jnp.stack([s[5] for s in shards]),
        hidden_sum,
        jnp.stack([s[6].T for s in shards]),
        root_squares,
    )


def solution(mesh):
    return jax.shard_map(
        per_device,
        mesh=mesh,
        in_specs=(
            P("shard", "ctx", "tp", None),
            P("shard", "ctx", "tp", None),
            P("shard"),
            P(),
            P(),
            P(),
            P(None, None, ("shard", "ctx"), None, "tp"),
            P(None, None, None, "tp"),
            P(None, None, "tp", ("shard", "ctx")),
            P(),
            P(None, ("shard", "ctx", "tp"), None),
            P(None, ("shard", "ctx"), "tp"),
            P(None, "tp"),
            P(None, "tp", ("shard", "ctx")),
        ),
        out_specs=(
            P("shard", "ctx", "tp", None),
            P("shard", "ctx", "tp", None),
            P(),
            P(),
            P(None, None, ("shard", "ctx"), None, "tp"),
            P(None, None, None, "tp"),
            P(None, None, "tp", ("shard", "ctx")),
            P(),
            P(None, ("shard", "ctx", "tp"), None),
            P(None, ("shard", "ctx"), "tp"),
            P(None, "tp"),
            P(None, "tp", ("shard", "ctx")),
            P(),
        ),
        check_vma=False,
    )
```

```python
import functools
import math

import jax
import jax.numpy as jnp
from jax import lax
from jax.experimental import pallas as pl
from jax.experimental.pallas import tpu as pltpu
from jax.sharding import PartitionSpec as P

HEAD_DIM = 64
FRAMES = 8
LAYERS = 2
AXES = ("shard", "ctx", "tp")
BF = jnp.bfloat16
F32 = jnp.float32

far_below = -1000000000.0
epsilon = 1e-06
root_half = 0.7071067811865476
gauss_scale = 0.3989422804014327


def dot_nn(left, right):
    return lax.dot_general(left, right, (((1,), (0,)), ((), ())), preferred_element_type=F32)


def dot_nt(left, right):
    return lax.dot_general(left, right, (((1,), (1,)), ((), ())), preferred_element_type=F32)


def dot_tn(left, right):
    return lax.dot_general(left, right, (((0,), (0,)), ((), ())), preferred_element_type=F32)


def rows(value):
    return value.reshape(-1, value.shape[-1])


def row_total(value):
    return jnp.sum(rows(value).astype(F32), axis=0)


def lane_masks(shape):
    lane = lax.broadcasted_iota(jnp.int32, shape, 1)
    return lane < HEAD_DIM


def softmax_rows(scores):
    top = jnp.max(scores, axis=-1, keepdims=True)
    raised = jnp.exp(scores - top)
    total = jnp.sum(raised, axis=-1, keepdims=True)
    return raised * (1.0 / total)


def sides(value, first):
    zero = jnp.zeros_like(value)
    return [jnp.where(first, value, zero), jnp.where(first, zero, value)]


def heads_forward(qkv, fix, scale, put):
    first = lane_masks(qkv(0, 0).shape)
    scores = []
    for pair in range(3):
        k = qkv(1, pair)
        scores.append([dot_nt(q, k) for q in sides(qkv(0, pair), first)])
    shares = [[softmax_rows(fix(item * scale)).astype(BF) for item in both] for both in scores]
    for pair in range(3):
        v = qkv(2, pair)
        outs = [dot_nn(item, v) for item in shares[pair]]
        put(pair, jnp.where(first, outs[0], outs[1]).astype(BF))


def heads_backward(qkv, back, fix, scale, put):
    first = lane_masks(qkv(0, 0).shape)
    scores, backs = [], []
    for pair in range(3):
        k, v = qkv(1, pair), qkv(2, pair)
        scores.append([dot_nt(q, k) for q in sides(qkv(0, pair), first)])
        backs.append([dot_nt(b, v) for b in sides(back(pair), first)])
    low_shares, low_scores = [], []
    for pair in range(3):
        low_shares.append([])
        low_scores.append([])
        for side in range(2):
            shares = softmax_rows(fix(scores[pair][side] * scale))
            back_shares = backs[pair][side]
            inner = jnp.sum(back_shares * shares, axis=-1, keepdims=True)
            low_scores[pair].append((shares * (back_shares - inner)).astype(BF))
            low_shares[pair].append(shares.astype(BF))
    for pair in range(3):
        q, k, bm = qkv(0, pair), qkv(1, pair), back(pair)
        gq = [dot_nn(item, k) for item in low_scores[pair]]
        gk = [dot_tn(item, q) for item in low_scores[pair]]
        gv = [dot_tn(item, bm) for item in low_shares[pair]]
        put(0, pair, (jnp.where(first, gq[0], gq[1]) * scale).astype(BF))
        put(1, pair, (jnp.where(first, gk[0], gk[1]) * scale).astype(BF))
        put(2, pair, jnp.where(first, gv[0], gv[1]).astype(BF))


def column(part, pair):
    start = part * 384 + pair * 128
    return slice(start, start + 128)


def spatial_fix(count_ref, padded, places):
    col = lax.broadcasted_iota(jnp.int32, (padded, padded), 1)
    floor = jnp.where(col < places, far_below, 3.0 * far_below)
    allowed = col < jnp.minimum(count_ref[0], places)
    return lambda scores: jnp.where(allowed, scores, floor)


def temporal_fix(tile):
    size = FRAMES * tile
    row = lax.broadcasted_iota(jnp.int32, (size, size), 0)
    col = lax.broadcasted_iota(jnp.int32, (size, size), 1)
    same = (row & (tile - 1)) == (col & (tile - 1))
    return lambda scores: jnp.where(same, scores, 3.0 * far_below)


class Grid:
    def __init__(self):
        self.shards = lax.axis_size("shard")
        self.depth = self.shards // 2
        shard = lax.axis_index("shard")
        self.z = shard // 2
        self.x = shard % 2
        self.y = lax.axis_index("ctx")
        self.t = lax.axis_index("tp")
        self.direct = self.depth == 4

    def perm(self, move):
        pairs = []
        for z in range(self.depth):
            for x in range(2):
                for y in range(2):
                    for t in range(2):
                        tz, tx, ty, tt = move(z, x, y, t)
                        pairs.append(
                            (((z * 2 + x) * 2 + y) * 2 + t, ((tz * 2 + tx) * 2 + ty) * 2 + tt)
                        )
        return pairs

    def send(self, value, pairs):
        return lax.ppermute(value, AXES, pairs)

    def over_x(self, value):
        return self.send(value, self.perm(lambda z, x, y, t: (z, 1 - x, y, t)))

    def over_y(self, value):
        return self.send(value, self.perm(lambda z, x, y, t: (z, x, 1 - y, t)))

    def over_t(self, value):
        return self.send(value, self.perm(lambda z, x, y, t: (z, x, y, 1 - t)))

    def over_z(self, value, step):
        depth = self.depth
        return self.send(value, self.perm(lambda z, x, y, t: ((z + step) % depth, x, y, t)))

    def over_bit(self, value, bit):
        pairs = []
        for s in range(self.shards):
            for y in range(2):
                for t in range(2):
                    pairs.append(((s * 2 + y) * 2 + t, ((s ^ bit) * 2 + y) * 2 + t))
        return self.send(value, pairs)

    def total(self, value, across):
        if across:
            value = value + self.over_t(value)
        value = value + self.over_y(value)
        bit = 1
        while bit < self.shards:
            value = value + self.over_bit(value, bit)
            bit *= 2
        return value


class Sums:
    def __init__(self, place, source, part, own, ra, rb, sx, sy, rx, ry, low, gz, send, recv):
        self.place, self.source, self.part, self.own = place, source, part, own
        self.ra, self.rb, self.sx, self.sy = ra, rb, sx, sy
        self.rx, self.ry, self.low, self.gz = rx, ry, low, gz
        self.send, self.recv = send, recv
        self.depth = part.shape[0]
        self.half = part.shape[0] // 2

    def copy(self, number, src, dst, target):
        return remote(src, dst, self.send.at[number], self.recv.at[number], target)

    def far(self):
        x, y = self.place.x, self.place.y
        low, high = pl.ds(0, self.half), pl.ds(self.half, self.half)
        return [
            self.copy(0, self.source.at[low, 1 - x, 1 - y], self.ra, self.place.over_y()),
            self.copy(1, self.source.at[high, 1 - x, 1 - y], self.rb, self.place.over_x()),
        ]

    def near(self):
        return [
            self.copy(2, self.sx, self.rx, self.place.over_x()),
            self.copy(3, self.sy, self.ry, self.place.over_y()),
        ]

    def deep(self):
        return [
            self.copy(
                3 + k,
                self.low.at[lax.rem(self.place.z + k, self.depth)],
                self.gz.at[k - 1],
                self.place.over_z(k),
            )
            for k in range(1, self.depth)
        ]

    def first(self):
        for item in self.far():
            item.start()

    def second(self):
        x, y, half = self.place.x, self.place.y, self.half
        for item in self.far():
            item.wait()
        for k in range(2 * half):
            toward_x, toward_y = self.part[k, 1 - x, y], self.part[k, x, 1 - y]
            if k < half:
                toward_x = toward_x + self.ra[k]
            else:
                toward_y = toward_y + self.rb[k - half]
            self.sx[k] = toward_x
            self.sy[k] = toward_y
        for item in self.near():
            item.start()

    def kept(self, k):
        mine = self.part[k, self.place.x, self.place.y].astype(F32)
        return mine + self.rx[k].astype(F32) + self.ry[k].astype(F32)

    def third(self):
        for item in self.near():
            item.wait()
        for k in range(self.depth):
            mine = self.part[k, self.place.x, self.place.y]
            self.low[k] = mine + (self.rx[k] + self.ry[k])
        for item in self.deep():
            item.start()

    def last(self):
        for item in self.deep():
            item.wait()
        total = self.kept(self.place.z)
        for k in range(self.depth - 1):
            total = total + self.gz[k].astype(F32)
        self.own[...] = total


def remote(src, dst, send, recv, target):
    return pltpu.make_async_remote_copy(
        src_ref=src,
        dst_ref=dst,
        send_sem=send,
        recv_sem=recv,
        device_id=target,
        device_id_type=pl.DeviceIdType.MESH,
    )


class Place:
    def __init__(self, depth):
        self.depth = depth
        shard = lax.axis_index("shard")
        self.z = shard // 2
        self.x = lax.rem(shard, 2)
        self.y = lax.axis_index("ctx")
        self.t = lax.axis_index("tp")

    def over_x(self):
        return {"shard": self.z * 2 + 1 - self.x}

    def over_y(self):
        return {"ctx": 1 - self.y}

    def over_t(self):
        return {"tp": 1 - self.t}

    def over_z(self, step):
        return {"shard": lax.rem(self.z + step, self.depth) * 2 + self.x}

    def meet(self, chips, cores):
        barrier = pltpu.get_barrier_semaphore()
        targets = [self.over_t()] if cores else []
        if chips:
            targets += [self.over_x(), self.over_y()]
            targets += [self.over_z(k) for k in range(1, self.depth)]
        for target in targets:
            pl.semaphore_signal(
                barrier, inc=1, device_id=target, device_id_type=pl.DeviceIdType.MESH
            )
        pl.semaphore_wait(barrier, len(targets))


class Carrier:
    def __init__(self, place, cores, starts, sources, parts, owns, scratch, most=2):
        self.place, self.cores = place, cores
        lanes = [pl.ds(start, own.shape[1]) for start, own in zip(starts, owns)]
        sources = [ref.at[:, :, :, :, cols] for ref, cols in zip(sources, lanes)]
        parts = [ref.at[:, :, :, :, cols] for ref, cols in zip(parts, lanes)]
        self.sums = [
            Sums(place, source, part, own, *scratch[10 * i : 10 * i + 10])
            for i, (source, part, own) in enumerate(zip(sources, parts, owns))
        ]
        self.groups = [[item] for item in self.sums[: most - 1]]
        if self.sums[most - 1 :]:
            self.groups.append(self.sums[most - 1 :])

    def begin(self):
        self.place.meet(bool(self.sums), self.cores)
        for item in self.sums:
            item.first()

    def step(self, number):
        if number == 0:
            self.begin()
            return
        last = len(self.groups)
        if 2 <= number <= last + 1:
            for item in self.groups[number - 2]:
                item.third()
        if number <= last:
            for item in self.groups[number - 1]:
                item.second()

    def end(self):
        for item in self.sums:
            item.last()


def carried(grid, parts):
    depth = grid.depth
    cubes, shapes, scratch = [], [], []
    for part, start, lanes in parts:
        step_rows = part.shape[0] // (depth * 4)
        block = lambda count: pltpu.VMEM((count, step_rows, lanes), BF)
        cubes.append(part.reshape(depth, 2, 2, step_rows, part.shape[1]))
        shapes.append(jax.ShapeDtypeStruct((step_rows, lanes), F32))
        scratch += [block(depth // 2)] * 2 + [block(depth)] * 5 + [block(depth - 1)]
        scratch += [pltpu.SemaphoreType.DMA((3 + depth,))] * 2
    return cubes, shapes, scratch


def stage_params(number, vmem=58, sends=True):
    if not sends:
        return pltpu.CompilerParams(vmem_limit_bytes=vmem << 20)
    return pltpu.CompilerParams(
        collective_id=number, has_side_effects=True, vmem_limit_bytes=vmem << 20
    )


def stage_cost(flops):
    return pl.CostEstimate(flops=flops, bytes_accessed=30000000, transcendentals=0)


VMEM_SPEC = pl.BlockSpec(memory_space=pltpu.VMEM)
SMEM_SPEC = pl.BlockSpec(memory_space=pltpu.SMEM)


ANY_SPEC = pl.BlockSpec(memory_space=pl.ANY)


def is_big(item):
    return item.shape[-1] >= 128 and math.prod(item.shape) >= 65536


class Staging:
    def __init__(self, smem, ins, outs):
        self.smem = smem
        self.ins = [i >= smem and is_big(item) for i, item in enumerate(ins)]
        self.outs = [is_big(item) for item in outs]
        self.in_shapes = [item for item, big in zip(ins, self.ins) if big]
        self.out_shapes = [item for item, big in zip(outs, self.outs) if big]

    def in_specs(self):
        specs = [ANY_SPEC if big else VMEM_SPEC for big in self.ins]
        return [SMEM_SPEC] * self.smem + specs[self.smem :]

    def out_specs(self):
        return [ANY_SPEC if big else VMEM_SPEC for big in self.outs]

    def scratch(self):
        held = self.in_shapes + self.out_shapes
        blocks = [pltpu.VMEM(item.shape, item.dtype) for item in held]
        return blocks + [pltpu.SemaphoreType.DMA((len(held),))]

    def count(self):
        return len(self.in_shapes) + len(self.out_shapes) + 1

    def open(self, in_refs, out_refs, refs):
        refs = list(refs)
        sems = refs.pop()
        number = 0
        pairs = []
        for group, flags in ((in_refs, self.ins), (out_refs, self.outs)):
            view, moves = [], []
            for ref, big in zip(group, flags):
                if big:
                    moves.append((ref, refs[number], sems.at[number]))
                    ref = refs[number]
                    number += 1
                view.append(ref)
            pairs.append((view, moves))
        (self.in_view, self.in_moves), (self.out_view, self.out_moves) = pairs
        return self.in_view, self.out_view

    def fetch(self):
        copies = [pltpu.make_async_copy(src, dst, sem) for src, dst, sem in self.in_moves]
        for item in copies:
            item.start()
        for item in copies:
            item.wait()

    def move_out(self, moves):
        copies = [pltpu.make_async_copy(src, dst, sem) for dst, src, sem in moves]
        for item in copies:
            item.start()
        for item in copies:
            item.wait()

    def flush(self, count=None):
        self.moved = len(self.out_moves) if count is None else sum(self.outs[:count])
        self.move_out(self.out_moves[: self.moved])

    def flush_rest(self):
        self.move_out(self.out_moves[self.moved :])


def row_of(ref, index):
    return ref.at[pl.ds(index, 1)]


def splitter(refs):
    refs = list(refs)
    return lambda count: [refs.pop(0) for _ in range(count)]


class Hops:
    def __init__(self, place, pieces, refs, total, held, came, send, recv):
        z = place.z
        targets = [place.over_t()]
        targets.append({"shard": (z + 1 - 2 * lax.rem(z, 2)) * 2 + place.x})
        targets.append({"shard": (z + 2 - 4 * (z // 2)) * 2 + place.x})
        targets += [place.over_x(), place.over_y()]
        self.pieces, self.refs = pieces, refs
        self.total, self.held, self.came = total, held, came
        self.copies = [
            remote(held.at[k], came.at[k], send.at[k], recv.at[k], target)
            for k, target in enumerate(targets)
        ]

    def begin(self):
        self.held[0] = jnp.zeros(self.held.shape[1:], F32)
        for ref, (start, count, row, lane) in zip(self.refs, self.pieces):
            lanes = ref.shape[1]
            self.held[0, row : row + count, lane : lane + lanes] = ref[start : start + count]
        self.copies[0].start()

    def hop(self, number):
        self.copies[number - 1].wait()
        value = self.held[number - 1] + self.came[number - 1]
        if number < len(self.copies):
            self.held[number] = value
            self.copies[number].start()
        else:
            self.total[...] = value


class Small:
    def __init__(self, width):
        self.arrays, self.pieces, self.rows, self.width = [], [], 0, width

    def add(self, array, start, count, lane=0, stay=False):
        self.arrays.append(array)
        self.pieces.append((start, count, self.rows, lane))
        if not stay:
            self.rows += count

    def shape(self):
        return jax.ShapeDtypeStruct((-(-self.rows // 8) * 8, self.width), F32)

    def plain(self):
        whole = jnp.zeros(self.shape().shape, F32)
        for array, (start, count, row, lane) in zip(self.arrays, self.pieces):
            whole = whole.at[row : row + count, lane : lane + array.shape[1]].set(
                array[start : start + count]
            )
        return lax.psum(whole, AXES)


def hop_scratch(small):
    block = pltpu.VMEM((5,) + small.shape().shape, F32)
    return [block, block] + [pltpu.SemaphoreType.DMA((5,))] * 2


def tail_body(depth, starts, pieces, *refs):
    take = splitter(refs)
    count = len(starts)
    parts, small, (away,) = take(count), take(len(pieces)), take(1)
    owns, (total, back) = take(count), take(2)
    hop_refs, (send, recv) = take(4), take(2)
    place = Place(depth)
    carrier = Carrier(place, True, starts, parts, parts, owns, take(10 * count))
    hops = Hops(place, pieces, small, total, *hop_refs)
    across = remote(away, back, send.at[0], recv.at[0], place.over_y())
    carrier.step(0)
    hops.begin()
    for number in range(1, 4):
        hops.hop(number)
        carrier.step(number)
    hops.hop(4)
    across.start()
    hops.hop(5)
    carrier.end()
    across.wait()


def starts_of(parts):
    return [start for _, start, _ in parts]


def tail_sums(grid, number, parts, small, away):
    cubes, shapes, scratch = carried(grid, parts)
    count = len(small.arrays)
    result = pl.pallas_call(
        functools.partial(tail_body, grid.depth, starts_of(parts), small.pieces),
        in_specs=[VMEM_SPEC] * (len(parts) + count + 1),
        out_specs=[VMEM_SPEC] * (len(parts) + 2),
        out_shape=shapes + [small.shape(), jax.ShapeDtypeStruct(away.shape, away.dtype)],
        scratch_shapes=hop_scratch(small) + [pltpu.SemaphoreType.DMA((1,))] * 2 + scratch,
        compiler_params=stage_params(number),
        cost_estimate=stage_cost(20000000000),
        name="sum_rows",
    )(*cubes, *small.arrays, away)
    return result[:-2], result[-2], result[-1]


def norm_back_rows(e, unit, scale, gain):
    along = e * gain
    lanes = e.shape[-1]
    mean_along = jnp.sum(along, axis=-1, keepdims=True) * (1.0 / lanes)
    mean_unit = jnp.sum(along * unit, axis=-1, keepdims=True) * (1.0 / lanes)
    return scale * (along - mean_along - unit * mean_unit)


def column_sum(value):
    return jnp.sum(value, axis=0, keepdims=True)


def tie(value, *others):
    return lax.optimization_barrier((value, *others))[0]


class Near:
    def __init__(self, place, line, whole, other, send, recv):
        self.place, self.line, self.whole, self.other = place, line, whole, other
        self.send, self.recv = send, recv
        self.depth = line.shape[0]

    def pair(self, number, src, dst, target):
        return remote(src, dst, self.send.at[number], self.recv.at[number], target)

    def at(self, ref, dx, dy, low=0, size=None):
        x = 1 - self.place.x if dx else self.place.x
        y = 1 - self.place.y if dy else self.place.y
        view = ref.at[pl.ds(low, size or self.depth), x, y]
        return view.at[:, self.place.t] if len(ref.shape) == 6 else view

    def sides(self):
        dst = self.at(self.whole, 0, 0)
        return [
            self.pair(0, self.line, dst, self.place.over_x()),
            self.pair(1, self.line, dst, self.place.over_y()),
        ]

    def corners(self):
        half = self.depth // 2
        first = self.at(self.whole, 1, 0, 0, half)
        second = self.at(self.whole, 0, 1, half, half)
        return [
            self.pair(2, first, first, self.place.over_y()),
            self.pair(3, second, second, self.place.over_x()),
        ]

    def swap(self, number):
        if self.other is None:
            return []
        if number == 0:
            src, dst = self.line, self.at(self.other, 0, 0)
        else:
            dx, dy = number & 1, number >> 1
            src, dst = self.at(self.whole, dx, dy), self.at(self.other, dx, dy)
        return [self.pair(4 + number, src, dst, self.place.over_t())]

    def begin(self):
        for item in self.sides() + self.swap(0) + [self.keep()]:
            item.start()

    def keep(self):
        return pltpu.make_async_copy(self.line, self.at(self.whole, 0, 0), self.send.at[8])

    def middle(self):
        for item in self.sides():
            item.wait()
        for item in self.corners() + self.swap(1) + self.swap(2):
            item.start()

    def corner_in(self):
        for item in self.corners():
            item.wait()
        for item in self.swap(3):
            item.start()

    def end(self):
        for number in range(4):
            for item in self.swap(number):
                item.wait()
        self.keep().wait()


class Deep:
    def __init__(self, place, block, line, send, recv):
        self.place, self.block, self.line, self.send, self.recv = place, block, line, send, recv

    def copies(self):
        return [
            remote(
                self.block,
                self.line.at[self.place.z],
                self.send.at[k - 1],
                self.recv.at[k - 1],
                self.place.over_z(k),
            )
            for k in range(1, self.line.shape[0])
        ]

    def begin(self):
        for item in self.copies():
            item.start()
        self.line[self.place.z] = self.block[...]

    def end(self):
        for item in self.copies():
            item.wait()


def landing(line, both):
    depth, step_rows, lanes = line
    if both == "one":
        return [jax.ShapeDtypeStruct((depth, 2, 2, 2, step_rows, lanes), BF)]
    return [jax.ShapeDtypeStruct((depth, 2, 2, step_rows, lanes), BF)] * (2 if both else 1)


def landed(outs, both):
    whole = outs.pop(0)
    if both == "one":
        return whole, whole
    return whole, outs.pop(0) if both else None


class Load:
    def __init__(self, grid, near=(), swapped=(), deep=(), across=()):
        self.depth = grid.depth
        self.swapped = list(swapped)
        self.near_count, self.deep_count = len(near), len(deep)
        self.inputs = list(near) + list(deep) + list(across)
        self.across_count = len(across)
        self.shapes, self.scratch, self.specs = [], [], []
        for line, both in zip(near, swapped):
            shapes = landing(line.shape, both)
            self.shapes += shapes
            self.specs += [ANY_SPEC] * len(shapes)
            self.scratch += [pltpu.SemaphoreType.DMA((9,)), pltpu.SemaphoreType.DMA((8,))]
        for block in deep:
            self.shapes.append(jax.ShapeDtypeStruct((self.depth,) + block.shape, BF))
            self.specs.append(VMEM_SPEC)
            self.scratch += [pltpu.SemaphoreType.DMA((self.depth - 1,))] * 2

        for item in across:
            self.shapes.append(jax.ShapeDtypeStruct(item.shape, item.dtype))
            self.specs.append(VMEM_SPEC)
            self.scratch += [pltpu.SemaphoreType.DMA((1,))] * 2

    def results(self, arrays):
        arrays = list(arrays)
        flat = lambda item: item.reshape(-1, item.shape[-1])
        near = []
        for both in self.swapped:
            near.append([None if item is None else flat(item) for item in landed(arrays, both)])
        return near, arrays


class Loader:
    def __init__(self, place, cores, load, ins, outs, sems):
        self.place, self.cores, self.load = place, cores, load
        ins, outs, sems = list(ins), list(outs), list(sems)
        self.near = []
        for both in load.swapped:
            whole, other = landed(outs, both)
            self.near.append(Near(place, ins.pop(0), whole, other, sems.pop(0), sems.pop(0)))
        self.deep = [
            Deep(place, ins.pop(0), outs.pop(0), sems.pop(0), sems.pop(0))
            for _ in range(load.deep_count)
        ]
        self.across = []
        for _ in range(load.across_count):
            send, recv = sems.pop(0), sems.pop(0)
            self.across.append(
                remote(ins.pop(0), outs.pop(0), send.at[0], recv.at[0], place.over_y())
            )

    def begin(self):
        chips = bool(self.near or self.deep or self.across)
        if chips or self.cores:
            self.place.meet(chips, self.cores or bool(self.near))
        for item in self.near + self.deep:
            item.begin()
        for item in self.across:
            item.start()

    def middle(self):
        for item in self.near:
            item.middle()

    def end(self):
        for item in self.near:
            item.corner_in()
        for item in self.near:
            item.end()
        for item in self.deep:
            item.end()
        for item in self.across:
            item.wait()


def open_kernel(load, staging, refs, scratch):
    take = splitter(refs)
    in_refs = take(len(staging.ins))
    load_ins = take(len(load.inputs))
    out_refs = take(len(staging.outs))
    load_outs = take(len(load.shapes))
    scratch_refs = take(scratch)
    in_refs, out_refs = staging.open(in_refs, out_refs, take(staging.count()))
    return in_refs, out_refs, scratch_refs, (load_ins, load_outs, take(len(load.scratch)))


def kernel_call(body, number, ins, shapes, scratch, load, name, smem=0, cores=False):
    staging = Staging(smem, ins, shapes)
    result = pl.pallas_call(
        functools.partial(body, staging),
        in_specs=staging.in_specs() + [VMEM_SPEC] * len(load.inputs),
        out_specs=staging.out_specs() + load.specs,
        out_shape=list(shapes) + load.shapes,
        scratch_shapes=list(scratch) + staging.scratch() + load.scratch,
        compiler_params=stage_params(number, sends=cores or bool(load.inputs)),
        cost_estimate=stage_cost(20000000000),
        name=name,
    )(*ins, *load.inputs)
    return result[: len(shapes)], load.results(result[len(shapes) :])


def first_body(swapped, depth, next_count, *refs):
    take = splitter(refs)
    count = len(swapped)
    blocks, next_blocks = take(count), take(next_count)
    wholes = [landed(take(2 if both is True else 1), both) for both in swapped]
    next_lines = take(next_count)
    lines = take(count)
    place = Place(depth)
    deep = [Deep(place, blocks[i], lines[i], *take(2)) for i in range(count)]
    near = [Near(place, lines[i], *wholes[i], *take(2)) for i in range(count)]
    after = [Deep(place, next_blocks[i], next_lines[i], *take(2)) for i in range(next_count)]
    place.meet(True, True)
    for item in deep:
        item.begin()
    for one, two in zip(deep, near):
        one.end()
        two.begin()
    for item in after:
        item.begin()
    for item in near:
        item.middle()
    for item in near:
        item.corner_in()
    for item in near:
        item.end()
    for item in after:
        item.end()


def first_gather(grid, number, blocks, swapped, next_blocks):
    depth = grid.depth
    line = lambda item: (depth,) + item.shape
    shapes = []
    for item, both in zip(blocks, swapped):
        shapes += landing(line(item), both)
    specs = [ANY_SPEC] * len(shapes) + [VMEM_SPEC] * len(next_blocks)
    shapes += [jax.ShapeDtypeStruct(line(item), BF) for item in next_blocks]
    sems = lambda size: [pltpu.SemaphoreType.DMA((size,))] * 2
    scratch = [pltpu.VMEM(line(item), BF) for item in blocks]
    for _ in blocks:
        scratch += sems(depth - 1)
    for _ in blocks:
        scratch += [pltpu.SemaphoreType.DMA((9,)), pltpu.SemaphoreType.DMA((8,))]
    for _ in next_blocks:
        scratch += sems(depth - 1)
    arrays = list(
        pl.pallas_call(
            functools.partial(first_body, tuple(swapped), depth, len(next_blocks)),
            in_specs=[VMEM_SPEC] * (len(blocks) + len(next_blocks)),
            out_specs=specs,
            out_shape=shapes,
            scratch_shapes=scratch,
            compiler_params=stage_params(number),
            cost_estimate=stage_cost(20000000000),
            name="first_gather",
        )(*blocks, *next_blocks)
    )
    flat = lambda item: None if item is None else item.reshape(-1, item.shape[-1])
    near = [[flat(item) for item in landed(arrays, both)] for both in swapped]
    return near, arrays


def norm_rows(state, gain, shift):
    lanes = state.shape[-1]
    center = state - jnp.sum(state, axis=-1, keepdims=True) * (1.0 / lanes)
    spread = jnp.sum(center * center, axis=-1, keepdims=True) * (1.0 / lanes)
    scale = lax.rsqrt(spread + epsilon)
    unit = center * scale
    return (unit * gain + shift).astype(BF), unit, scale


def square_sum(value, valid):
    return jnp.sum(jnp.sum(value * value, axis=-1, keepdims=True) * valid, axis=0, keepdims=True)


def temporal_body(load, att_scale, layer, staging, *refs):
    ins, outs, scratch, loads = open_kernel(load, staging, refs, 3)
    state, valid, gain, shift, tri, tri_bias, merge0, merge1, merge_bias, mixing, mix_bias = ins
    out, unit, scale, normed, qkv, mine, swap, joined, sq = outs
    away, send, recv = scratch
    gain, shift = row_of(gain, 3 * layer), row_of(shift, 3 * layer)
    tri_bias = row_of(tri_bias, layer)
    merge_bias, mix_bias = row_of(merge_bias, 4 * layer), row_of(mix_bias, 4 * layer + 1)
    place = Place(load.depth)
    loader = Loader(place, True, load, *loads)
    frames, padded, width = state.shape
    loader.begin()
    staging.fetch()

    def norm_one(f, carry):
        low, u, s = norm_rows(state[f], gain[...], shift[...])
        normed[f] = low
        unit[f] = u
        scale[f] = s
        return carry

    lax.fori_loop(0, frames, norm_one, 0)
    own = normed.at[pl.ds(0, frames)]
    swap_normed = remote(
        own, normed.at[pl.ds(frames, frames)], send.at[0], recv.at[0], place.over_t()
    )
    swap_normed.start()

    def project(f, carry):
        qkv[f] = (dot_nn(normed[f], tri[...]) + tri_bias[...]).astype(BF)
        return carry

    lax.fori_loop(0, frames, project, 0)
    swap_normed.wait()
    lax.fori_loop(frames, 2 * frames, project, 0)
    tile = 16
    fix = temporal_fix(tile)

    def one(i, carry):
        at = pl.ds(pl.multiple_of(i * tile, tile), tile)

        def put(pair, value):
            cols = slice(pair * 128, pair * 128 + 128)
            both = value.reshape(2 * frames, tile, 128)
            mine[:, at, cols] = both[:frames]
            away[:, at, cols] = both[frames:]

        heads_forward(
            lambda part, pair: qkv[:, at, column(part, pair)].reshape(2 * frames * tile, 128),
            fix,
            att_scale,
            put,
        )
        return carry

    lax.fori_loop(0, padded // tile, one, 0)
    swap_mixed = remote(away, swap, send.at[1], recv.at[1], place.over_t())
    swap_mixed.start()
    loader.middle()
    swap_mixed.wait()

    def finish(f, carry):
        low = (
            dot_nt(mine[f], merge0[...]) + dot_nt(swap[f], merge1[...]) + merge_bias[...]
        ).astype(BF)
        joined[f] = low
        branch = dot_nn(low, mixing[...]) + mix_bias[...]
        out[f] = state[f] + branch
        return carry + square_sum(branch, valid[...])

    total = lax.fori_loop(0, frames, finish, jnp.zeros((1, 1), F32))
    sq[...] = jnp.broadcast_to(total, sq.shape)
    staging.flush()
    loader.end()


def temporal_stage(number, layer, state, valid, gain, shift, w, biases, load, att_scale):
    frames, padded, width = state.shape
    split = w["merge_t"][0].shape[1]
    shape = lambda dims, kind=BF: jax.ShapeDtypeStruct(dims, kind)
    ins = [state, valid, gain, shift, w["triple_t"], biases[0], *w["merge_t"], biases[1]]
    ins += [w["mixing"], biases[2]]
    return kernel_call(
        functools.partial(temporal_body, load, att_scale, layer),
        number,
        ins,
        [
            shape((frames, padded, width), F32),
            shape((frames, padded, width), F32),
            shape((frames, padded, 1), F32),
            shape((2 * frames, padded, width)),
            shape((2 * frames, padded, 3 * split)),
            shape((frames, padded, split)),
            shape((frames, padded, split)),
            shape((frames, padded, width)),
            shape((8, 128), F32),
        ],
        [pltpu.VMEM((frames, padded, split), BF)] + [pltpu.SemaphoreType.DMA((2,))] * 2,
        load,
        "temporal_forward",
        cores=True,
    )


def spatial_body(load, places, att_scale, layer, staging, *refs):
    ins, outs, scratch, loads = open_kernel(load, staging, refs, 0)
    count_ref, state, valid, gain, shift, tri0, tri1, bias0, bias1, merge0, merge1, out_bias = ins
    out, unit, scale, normed, qkv0, qkv1, mixed0, mixed1, sq = outs
    gain, shift = row_of(gain, 3 * layer + 1), row_of(shift, 3 * layer + 1)
    bias0, bias1 = row_of(bias0, layer), row_of(bias1, layer)
    out_bias = row_of(out_bias, 4 * layer + 2)
    place = Place(load.depth)
    loader = Loader(place, False, load, *loads)
    frames, padded, width = state.shape
    fix = spatial_fix(count_ref, padded, places)
    loader.begin()
    staging.fetch()

    def one(f, carry):
        low, u, s = norm_rows(state[f], gain[...], shift[...])
        normed[f] = low
        unit[f] = u
        scale[f] = s
        for tri, bias, qkv, mixed in (
            (tri0, bias0, qkv0, mixed0),
            (tri1, bias1, qkv1, mixed1),
        ):
            qkv[f] = (dot_nn(low, tri[...]) + bias[...]).astype(BF)

            def put(pair, value, mixed=mixed):
                mixed[f, :, pair * 128 : pair * 128 + 128] = value

            heads_forward(
                lambda part, pair, qkv=qkv: qkv[f, :, column(part, pair)], fix, att_scale, put
            )
        branch = dot_nt(mixed0[f], merge0[...]) + dot_nt(mixed1[f], merge1[...]) + out_bias[...]
        out[f] = state[f] + branch
        return carry + square_sum(branch, valid[...])

    cut = frames - 1
    total = lax.fori_loop(0, cut, one, jnp.zeros((1, 1), F32))
    loader.middle()
    total = lax.fori_loop(cut, frames, one, total)
    sq[...] = jnp.broadcast_to(total, sq.shape)
    staging.flush()
    loader.end()


def spatial_stage(number, layer, count_ref, state, valid, gain, shift, w, biases, load, places, att_scale):
    frames, padded, width = state.shape
    split = w["merge_s"][0].shape[1]
    shape = lambda dims, kind=BF: jax.ShapeDtypeStruct(dims, kind)
    ins = [count_ref, state, valid, gain, shift, *w["triple_s"], biases[0], biases[1]]
    ins += [*w["merge_s"], biases[2]]
    return kernel_call(
        functools.partial(spatial_body, load, places, att_scale, layer),
        number,
        ins,
        [
            shape((frames, padded, width), F32),
            shape((frames, padded, width), F32),
            shape((frames, padded, 1), F32),
            shape((frames, padded, width)),
            shape((frames, padded, 3 * split)),
            shape((frames, padded, 3 * split)),
            shape((frames, padded, split)),
            shape((frames, padded, split)),
            shape((8, 128), F32),
        ],
        [],
        load,
        "spatial_forward",
        1,
    )


def feed_body(load, layer, staging, *refs):
    ins, outs, scratch, loads = open_kernel(load, staging, refs, 0)
    state, valid, gain, shift, up0, up1, bias0, bias1, down0, down1, out_bias = ins
    out, unit, scale, normed, act0, act1, slope0, slope1, sq = outs
    gain, shift = row_of(gain, 3 * layer + 2), row_of(shift, 3 * layer + 2)
    bias0, bias1 = row_of(bias0, layer), row_of(bias1, layer)
    out_bias = row_of(out_bias, 4 * layer + 3)
    place = Place(load.depth)
    loader = Loader(place, False, load, *loads)
    frames, padded, width = state.shape
    loader.begin()
    staging.fetch()

    def one(f, carry):
        low, u, s = norm_rows(state[f], gain[...], shift[...])
        normed[f] = low
        unit[f] = u
        scale[f] = s
        branch = jnp.broadcast_to(out_bias[...], (padded, width))
        for up, bias, down, act, slope in (
            (up0, bias0, down0, act0, slope0),
            (up1, bias1, down1, act1, slope1),
        ):
            lanes = up.shape[1]
            piece = lanes // 3
            for number in range(3):
                cols = slice(number * piece, (number + 1) * piece)
                hidden = dot_nn(low, up[:, cols]) + bias[:, cols]
                below = 0.5 * (1.0 + lax.erf(hidden * root_half))
                act[f, :, cols] = (hidden * below).astype(BF)
                slope[f, :, cols] = (
                    below + hidden * gauss_scale * jnp.exp(-0.5 * hidden * hidden)
                ).astype(BF)
            branch = branch + dot_nt(act[f], down[...])
        value = state[f] + branch
        out[f] = value
        return (
            carry[0] + square_sum(branch, valid[...]),
            carry[1] + square_sum(value, valid[...]),
        )

    zero = jnp.zeros((1, 1), F32)
    cut = frames - 1
    total = lax.fori_loop(0, cut, one, (zero, zero))
    loader.middle()
    total = lax.fori_loop(cut, frames, one, total)
    sq[...] = jnp.broadcast_to(total[0], sq.shape)
    sq[0:1] = jnp.broadcast_to(total[1], (1, sq.shape[1]))
    staging.flush()
    loader.end()


def feed_stage(number, layer, state, valid, gain, shift, w, biases, load):
    frames, padded, width = state.shape
    hid = w["up"][0].shape[1]
    shape = lambda dims, kind=BF: jax.ShapeDtypeStruct(dims, kind)
    ins = [state, valid, gain, shift, *w["up"], biases[0], biases[1], *w["down"], biases[2]]
    return kernel_call(
        functools.partial(feed_body, load, layer),
        number,
        ins,
        [
            shape((frames, padded, width), F32),
            shape((frames, padded, width), F32),
            shape((frames, padded, 1), F32),
            shape((frames, padded, width)),
        ]
        + [shape((frames, padded, hid))] * 4
        + [shape((8, 128), F32)],
        [],
        load,
        "feed_forward",
    )


def feed_back_body(depth, starts, steps, layer, *refs):
    take = splitter(refs)
    count = len(starts)
    state, normed, unit, scale, gain = take(5)
    gain = row_of(gain, 3 * layer + 2)
    oth, own = take(4), take(4)
    parts = take(count)
    out, sums, g_up, g_down, h_own, h_oth = take(6)
    owns = take(count)
    r, rt, nt, bh, s_up, s_down, r_up, r_down, send, recv = take(10)
    place = Place(depth)
    carrier = Carrier(place, True, starts, parts, parts, owns, take(10 * count))
    frames, padded, width = state.shape
    rows_all = frames * padded
    i = pl.program_id(0)

    @pl.when(i == 0)
    def _():
        carrier.step(0)
        sums[...] = jnp.zeros_like(sums)

        def begin(f, carry):
            low = state[f].astype(BF)
            r[f] = low
            out[f] = jnp.zeros((padded, width), F32)
            return carry + column_sum(low.astype(F32))

        sums[2:3] = lax.fori_loop(0, frames, begin, jnp.zeros((1, width), F32))
        rt[...] = r[...].reshape(rows_all, width).T
        nt[...] = normed[...].reshape(rows_all, width).T

    def work(down, up, active, slope, h_sum):
        lanes = down.shape[1]

        value = dot_nn(r[...].reshape(rows_all, width), down[...])
        value = (value * slope[...].reshape(rows_all, lanes).astype(F32)).astype(BF)
        bh[...] = value.reshape(frames, padded, lanes)
        h_sum[...] = column_sum(value.astype(F32))
        out[...] += dot_nt(value, up[...]).reshape(frames, padded, width)
        return (
            dot_nn(nt[...], bh[...].reshape(rows_all, lanes)),
            dot_nn(rt[...], active[...].reshape(rows_all, lanes)),
        )

    def swaps(j):
        return [
            remote(s_up.at[j], r_up.at[j], send.at[0, j], recv.at[0, j], place.over_t()),
            remote(s_down.at[j], r_down.at[j], send.at[1, j], recv.at[1, j], place.over_t()),
        ]

    for number, at in ((1, 1), (2, 3), (3, 4)):
        if count:

            @pl.when(i == at)
            def _(number=number):
                carrier.step(number)

    @pl.when(i < steps)
    def _():
        up_part, down_part = work(*oth, h_oth)
        s_up[i] = up_part.astype(BF)
        s_down[i] = down_part.astype(BF)
        for item in swaps(i):
            item.start()

    @pl.when(i >= steps)
    def _():
        j = i - steps
        up_part, down_part = work(*own, h_own)
        for item in swaps(j):
            item.wait()
        g_up[...] = (up_part + r_up[j].astype(F32)).astype(BF)
        g_down[...] = (down_part + r_down[j].astype(F32)).astype(BF)

    @pl.when(i == 2 * steps - 1)
    def _():
        def finish(f, carry):
            e, u = out[f], unit[f]
            out[f] = state[f] + norm_back_rows(e, u, scale[f], gain[...])
            return (carry[0] + column_sum(e * u), carry[1] + column_sum(e))

        zero = jnp.zeros((1, width), F32)
        sums[0:1], sums[1:2] = lax.fori_loop(0, frames, finish, (zero, zero))
        carrier.end()


def feed_back(grid, number, layer, state, kept, gain, w, parts):
    frames, padded, width = state.shape
    hid = w["up"][0].shape[1]
    steps = 3
    lanes = hid // steps
    cubes, shapes, scratch = carried(grid, parts)
    whole = lambda item: pl.BlockSpec(
        item.shape, lambda i: (0,) * item.ndim, pipeline_mode=pl.Buffered(1)
    )
    first = lambda i: jnp.minimum(i, steps - 1)
    later = lambda i: jnp.maximum(i - steps, 0)

    def side(at):
        weight = pl.BlockSpec((width, lanes), lambda i: (0, at(i)))
        token = pl.BlockSpec((frames, padded, lanes), lambda i: (0, 0, at(i)))
        return [weight, weight, token, token]

    tokens = lambda item: item.reshape(frames, padded, hid)
    sides = [
        [w["down"][k], w["up"][k], tokens(kept["active"][k]), tokens(kept["slope"][k])]
        for k in (1, 0)
    ]
    fixed = [state, kept["normed_m"], kept["unit_m"], kept["scale_m"], gain]
    vec = lambda at: pl.BlockSpec((1, lanes), lambda i: (0, at(i)))
    result = pl.pallas_call(
        functools.partial(feed_back_body, grid.depth, starts_of(parts), steps, layer),
        grid=(2 * steps,),
        in_specs=[whole(item) for item in fixed]
        + side(first)
        + side(later)
        + [whole(item) for item in cubes],
        out_specs=[
            pl.BlockSpec((frames, padded, width), lambda i: (0, 0, 0)),
            pl.BlockSpec((8, width), lambda i: (0, 0)),
            pl.BlockSpec((width, lanes), lambda i: (0, later(i))),
            pl.BlockSpec((width, lanes), lambda i: (0, later(i))),
            vec(later),
            vec(first),
        ]
        + [pl.BlockSpec(item.shape, lambda i: (0, 0)) for item in shapes],
        out_shape=[
            jax.ShapeDtypeStruct((frames, padded, width), F32),
            jax.ShapeDtypeStruct((8, width), F32),
            jax.ShapeDtypeStruct((width, hid), BF),
            jax.ShapeDtypeStruct((width, hid), BF),
            jax.ShapeDtypeStruct((1, hid), F32),
            jax.ShapeDtypeStruct((1, hid), F32),
        ]
        + shapes,
        scratch_shapes=[
            pltpu.VMEM((frames, padded, width), BF),
            pltpu.VMEM((width, frames * padded), BF),
            pltpu.VMEM((width, frames * padded), BF),
            pltpu.VMEM((frames, padded, lanes), BF),
        ]
        + [pltpu.VMEM((steps, width, lanes), BF)] * 4
        + [pltpu.SemaphoreType.DMA((2, steps))] * 2
        + scratch,
        compiler_params=stage_params(number),
        cost_estimate=stage_cost(24000000000),
        name="feed_back",
    )(*fixed, *sides[0], *sides[1], *cubes)
    return result[0], result[1], result[2:4], (result[4], result[5]), result[6:]


def spatial_back_body(depth, starts, places, att_scale, layer, staging, *refs):
    take = splitter(refs)
    count = len(starts)
    in_refs, out_refs = take(14 + count), take(5 + count)
    own_scratch, sum_scratch = take(13), take(10 * count)
    sources = in_refs[14:]
    in_refs, out_refs = staging.open(in_refs, out_refs, take(staging.count()))
    take = splitter(in_refs + out_refs + own_scratch + sum_scratch)
    (count_ref, state, merge0, merge1, mixed0, mixed1, qkv0, qkv1) = take(8)
    tri0, tri1, normed, unit, scale, gain = take(6)
    gain = row_of(gain, 3 * layer + 1)
    parts = take(count)
    out, sums, q_sums, g_tri, g_merge = take(5)
    owns = take(count)
    r, bm0, bm1, b0, b1, rt, nt, s_tri, r_tri, s_merge, r_merge, send, recv = take(13)
    place = Place(depth)
    carrier = Carrier(place, True, starts, sources, parts, owns, take(10 * count), 3)
    frames, padded, width = state.shape
    rows_all = frames * padded
    split = merge0.shape[1]
    fix = spatial_fix(count_ref, padded, places)
    carrier.step(0)
    staging.fetch()

    def one(f, carry):
        low = state[f].astype(BF)
        r[f] = low
        for merge, bm, src, dst in ((merge0, bm0, qkv0, b0), (merge1, bm1, qkv1, b1)):
            bm[...] = dot_nn(low, merge[...]).astype(BF)

            def put(part, pair, value, dst=dst):
                dst[f, :, column(part, pair)] = value

            heads_backward(
                lambda part, pair, src=src: src[f, :, column(part, pair)],
                lambda pair, bm=bm: bm[:, pair * 128 : pair * 128 + 128],
                fix,
                att_scale,
                put,
            )
        return carry + column_sum(low.astype(F32))

    sums[...] = jnp.zeros_like(sums)
    q_sums[...] = jnp.zeros_like(q_sums)
    total = jnp.zeros((1, width), F32)
    total = lax.fori_loop(0, 2, one, total)
    carrier.step(1)
    total = lax.fori_loop(2, 3, one, total)
    carrier.step(2)
    sums[2:3] = lax.fori_loop(3, frames, one, total)
    rt[...] = r[...].reshape(rows_all, width).T
    nt[...] = normed[...].reshape(rows_all, width).T
    flat = lambda ref, part: ref[:, :, part * split : (part + 1) * split].reshape(rows_all, split)
    swap_tri = remote(s_tri, r_tri, send.at[0], recv.at[0], place.over_t())
    swap_merge = remote(s_merge, r_merge, send.at[1], recv.at[1], place.over_t())
    s_merge[...] = dot_nn(rt[...], mixed1[...]).astype(BF)
    swap_merge.start()
    for part in range(3):
        cols = slice(part * split, (part + 1) * split)
        s_tri[:, cols] = dot_nn(nt[...], flat(b1, part)).astype(BF)
    swap_tri.start()
    carrier.step(3)

    def finish(f, carry):
        e = dot_nt(b0[f], tri0[...]) + dot_nt(b1[f], tri1[...])
        u = unit[f]
        out[f] = state[f] + norm_back_rows(e, u, scale[f], gain[...])
        return (
            carry[0] + column_sum(e * u),
            carry[1] + column_sum(e),
            carry[2] + column_sum(b0[f].astype(F32)),
            carry[3] + column_sum(b1[f].astype(F32)),
        )

    zero, wide = jnp.zeros((1, width), F32), jnp.zeros((1, 3 * split), F32)
    sums[0:1], sums[1:2], mine, theirs = lax.fori_loop(
        0, frames, finish, (zero, zero, wide, wide)
    )
    carrier.step(4)
    for number, value in ((0, mine), (1, theirs)):
        q_sums[number : number + 1, :split] = value[:, :split]
        q_sums[number : number + 1, split:] = value[:, 2 * split :]
    swap_merge.wait()
    g_merge[...] = (dot_nn(rt[...], mixed0[...]) + r_merge[...].astype(F32)).astype(BF)
    swap_tri.wait()
    for part in range(3):
        cols = slice(part * split, (part + 1) * split)
        mine = dot_nn(nt[...], flat(b0, part))
        g_tri[:, cols] = (mine + r_tri[:, cols].astype(F32)).astype(BF)
    staging.flush(5)
    carrier.end()
    staging.flush_rest()


def spatial_back(grid, number, layer, count_ref, state, kept, gain, w, parts, places, att_scale):
    frames, padded, width = state.shape
    split = w["merge_s"][0].shape[1]
    cubes, shapes, scratch = carried(grid, parts)
    flat = [item.reshape(frames * padded, split) for item in kept["mixed_s"]]
    fixed = [count_ref, state, *w["merge_s"], *flat, *kept["qkv_s"], *w["triple_s"]]
    fixed += [kept["normed_s"], kept["unit_s"], kept["scale_s"], gain]
    ins = fixed + cubes
    outs = [
        jax.ShapeDtypeStruct((frames, padded, width), F32),
        jax.ShapeDtypeStruct((8, width), F32),
        jax.ShapeDtypeStruct((8, 2 * split), F32),
        jax.ShapeDtypeStruct((width, 3 * split), BF),
        jax.ShapeDtypeStruct((width, split), BF),
    ] + shapes
    staging = Staging(1, ins, outs)
    result = pl.pallas_call(
        functools.partial(
            spatial_back_body, grid.depth, starts_of(parts), places, att_scale, layer, staging
        ),
        in_specs=staging.in_specs(),
        out_specs=staging.out_specs(),
        out_shape=outs,
        scratch_shapes=[pltpu.VMEM((frames, padded, width), BF)]
        + [pltpu.VMEM((padded, split), BF)] * 2
        + [pltpu.VMEM((frames, padded, 3 * split), BF)] * 2
        + [pltpu.VMEM((width, frames * padded), BF)] * 2
        + [pltpu.VMEM((width, 3 * split), BF)] * 2
        + [pltpu.VMEM((width, split), BF)] * 2
        + [pltpu.SemaphoreType.DMA((2,))] * 2
        + scratch
        + staging.scratch(),
        compiler_params=stage_params(number),
        cost_estimate=stage_cost(24000000000),
        name="spatial_stage",
    )(*ins)
    return result[0], result[1], result[2], result[3:5], result[5:]


def temporal_back_body(depth, starts, att_scale, layer, staging, pieces, joined_mix, *refs):
    take = splitter(refs)
    count = len(starts)
    chained = 1 if pieces else 0
    in_refs, small = take(13 + count), take(len(pieces))
    out_refs, total = take(6 + count), take(chained)
    own_scratch, sum_scratch, hop_refs = take(13), take(10 * count), take(4 * chained)
    mix_refs = take(3) if joined_mix else None
    sources = in_refs[13:]
    in_refs, out_refs = staging.open(in_refs, out_refs, take(staging.count()))
    take = splitter(in_refs + out_refs + own_scratch + sum_scratch)
    state, mixing, joined, merge0, merge1, mine, swap, qkv, tri = take(9)
    normed, unit, scale, gain = take(4)
    gain = row_of(gain, 3 * layer)
    parts = take(count)
    out, sums, q_sums, g_tri, g_merge, g_mix = take(6)
    owns = take(count)
    r, bj, away, bm, b, nt, rt, s_merge, r_merge, s_back, r_back, send, recv = take(13)
    joins = len(g_mix.shape) == 3
    if joins:
        (whole_mix, s_mix, r_mix), shard_mix = mix_refs, g_mix
    place = Place(depth)
    carrier = Carrier(place, True, starts, sources, parts, owns, take(10 * count))
    frames, padded, width = state.shape
    rows_all = frames * padded
    split = merge0.shape[1]
    carrier.step(0)
    hops = Hops(place, pieces, small, *total, *hop_refs) if chained else None
    if chained:
        hops.begin()
    staging.fetch()

    def begin(f, carry):
        low = state[f].astype(BF)
        r[f] = low
        value = dot_nt(low, mixing[...]).astype(BF)
        bj[f] = value
        bm[f] = dot_nn(value, merge0[...]).astype(BF)
        away[f] = dot_nn(value, merge1[...]).astype(BF)
        return (carry[0] + column_sum(low.astype(F32)), carry[1] + column_sum(value.astype(F32)))

    sums[...] = jnp.zeros_like(sums)
    q_sums[...] = jnp.zeros_like(q_sums)
    zero = jnp.zeros((1, width), F32)
    sums[3:4], sums[2:3] = lax.fori_loop(0, frames, begin, (zero, zero))
    swap_bm = remote(
        away, bm.at[pl.ds(frames, frames)], send.at[0], recv.at[0], place.over_t()
    )
    swap_bm.start()
    carrier.step(1)
    rt[...] = bj[...].reshape(rows_all, width).T
    s_merge[...] = dot_nn(rt[...], swap[...].reshape(rows_all, split)).astype(BF)
    swap_merge = remote(s_merge, r_merge, send.at[1], recv.at[1], place.over_t())
    swap_merge.start()
    if chained:
        hops.hop(1)
    rt[...] = joined[...].reshape(rows_all, width).T
    for half in range(2):
        cols = slice(half * split, (half + 1) * split)
        mix_part = dot_nn(rt[...], r[:, :, cols].reshape(rows_all, split))
        (whole_mix if joins else g_mix)[:, cols] = mix_part
    if joins:
        blocks, step = shard_mix.shape[0], shard_mix.shape[1]

        def mix_rows(k, core):
            at = pl.multiple_of((2 * k + core) * step, 8)
            return whole_mix[pl.ds(at, step), :]

        for k in range(blocks):
            s_mix[k] = mix_rows(k, 1 - place.t).astype(BF)
        swap_mix = remote(s_mix, r_mix, send.at[3], recv.at[3], place.over_t())
        swap_mix.start()
    rt[...] = bj[...].reshape(rows_all, width).T
    swap_merge.wait()
    g_merge[...] = (dot_nn(rt[...], mine[...].reshape(rows_all, split)) + r_merge[...].astype(F32)).astype(BF)
    swap_bm.wait()
    tile = 16
    fix = temporal_fix(tile)

    def one(i, carry):
        at = pl.ds(pl.multiple_of(i * tile, tile), tile)

        def put(part, pair, value):
            b[:, at, column(part, pair)] = value.reshape(FRAMES, tile, 128)

        heads_backward(
            lambda part, pair: qkv[:, at, column(part, pair)].reshape(FRAMES * tile, 128),
            lambda pair: bm[:, at, pair * 128 : pair * 128 + 128].reshape(FRAMES * tile, 128),
            fix,
            att_scale,
            put,
        )
        return carry

    tiles = padded // tile
    lax.fori_loop(0, tiles // 3, one, 0)
    if joins:
        swap_mix.wait()
        for k in range(blocks):
            shard_mix[k] = (mix_rows(k, place.t) + r_mix[k].astype(F32)).astype(BF)
    carrier.step(2)
    if chained:
        hops.hop(2)
    lax.fori_loop(tiles // 3, 2 * tiles // 3, one, 0)
    if chained:
        hops.hop(3)
    lax.fori_loop(2 * tiles // 3, tiles, one, 0)
    carrier.step(3)

    def toward(f, carry):
        s_back[f] = dot_nt(b[f + frames], tri[...]).astype(BF)
        return carry

    lax.fori_loop(0, frames, toward, 0)
    swap_back = remote(s_back, r_back, send.at[2], recv.at[2], place.over_t())
    swap_back.start()
    if chained:
        hops.hop(4)
    nt[...] = normed[...].reshape(2 * rows_all, width).T
    for part in range(3):
        cols = slice(part * split, (part + 1) * split)
        g_tri[:, cols] = dot_nn(
            nt[...], b[:, :, cols].reshape(2 * rows_all, split)
        ).astype(BF)
    swap_back.wait()

    def finish(f, carry):
        e = dot_nt(b[f], tri[...]) + r_back[f].astype(F32)
        u = unit[f]
        out[f] = state[f] + norm_back_rows(e, u, scale[f], gain[...])
        both = column_sum(b[f].astype(F32)) + column_sum(b[f + frames].astype(F32))
        return (carry[0] + column_sum(e * u), carry[1] + column_sum(e), carry[2] + both)

    sums[0:1], sums[1:2], wide = lax.fori_loop(
        0, frames, finish, (zero, zero, jnp.zeros((1, 3 * split), F32))
    )
    q_sums[0:1, :split] = wide[:, :split]
    q_sums[0:1, split:] = wide[:, 2 * split :]
    if chained:
        hops.hop(5)
    staging.flush(6)
    carrier.end()
    staging.flush_rest()


def temporal_back(grid, number, layer, state, kept, gain, w, parts, att_scale, small=None):
    frames, padded, width = state.shape
    split = w["merge_t"][0].shape[1]
    cubes, shapes, scratch = carried(grid, parts)
    fixed = [state, w["mixing"], kept["joined"], *w["merge_t"], *kept["mixed_t"], kept["qkv_t"]]
    fixed += [w["triple_t"], kept["normed_t"], kept["unit_t"], kept["scale_t"], gain]
    ins = fixed + cubes
    outs = [
        jax.ShapeDtypeStruct((frames, padded, width), F32),
        jax.ShapeDtypeStruct((8, width), F32),
        jax.ShapeDtypeStruct((8, 2 * split), F32),
        jax.ShapeDtypeStruct((width, 3 * split), BF),
        jax.ShapeDtypeStruct((width, split), BF),
        jax.ShapeDtypeStruct((width, width), F32),
    ] + shapes
    mix_scratch = []
    if grid.direct:
        step = width // (4 * grid.depth) // 2
        outs[5] = jax.ShapeDtypeStruct((4 * grid.depth, step, width), BF)
        mix_scratch = [pltpu.VMEM((width, width), F32)]
        mix_scratch += [pltpu.VMEM((4 * grid.depth, step, width), BF)] * 2
    staging = Staging(0, ins, outs)
    pieces = small.pieces if small else []
    chained = 1 if small else 0
    result = pl.pallas_call(
        functools.partial(
            temporal_back_body, grid.depth, starts_of(parts), att_scale, layer, staging, pieces, grid.direct
        ),
        in_specs=staging.in_specs() + [VMEM_SPEC] * len(pieces),
        out_specs=staging.out_specs() + [VMEM_SPEC] * chained,
        out_shape=outs + ([small.shape()] if small else []),
        scratch_shapes=[pltpu.VMEM((frames, padded, width), BF)] * 2
        + [pltpu.VMEM((frames, padded, split), BF)]
        + [pltpu.VMEM((2 * frames, padded, split), BF)]
        + [pltpu.VMEM((2 * frames, padded, 3 * split), BF)]
        + [pltpu.VMEM((width, 2 * frames * padded), BF)]
        + [pltpu.VMEM((width, frames * padded), BF)]
        + [pltpu.VMEM((width, split), BF)] * 2
        + [pltpu.VMEM((frames, padded, width), BF)] * 2
        + [pltpu.SemaphoreType.DMA((4,))] * 2
        + scratch
        + (hop_scratch(small) if chained else [])
        + mix_scratch
        + staging.scratch(),
        compiler_params=stage_params(number, 60),
        cost_estimate=stage_cost(24000000000),
        name="temporal_stage",
    )(*ins, *(small.arrays if small else []))
    end = 6 + len(parts)
    return result[0], result[1], result[2], result[3:6], result[6:end], result[end:]


def plain_sums(parts):
    return [
        lax.psum_scatter(part.astype(F32), ("shard", "ctx"), scatter_dimension=0, tiled=True)
        for part in parts
    ]


def split_columns(value, widths):
    outs, start = [], 0
    for width in widths:
        outs.append(value[..., start : start + width])
        start += width
    return outs


def per_device(
    video_clips,
    cotangent,
    slot_clip,
    valid_places,
    norm_gain,
    norm_bias,
    triple_weight,
    entry_bias,
    merge_weight,
    branch_bias,
    mixing_weight,
    up_weight,
    up_bias,
    down_weight,
):
    grid = Grid()
    slots, frames_here, places_here, width = video_clips.shape
    places = places_here * 2
    padded = -(-places // 16) * 16
    scale = HEAD_DIM ** (-0.5)
    step_rows = triple_weight.shape[2]
    half_rows = step_rows // 2
    own_first = grid.t == 0
    straight = grid.t == grid.y

    clip_ids = jnp.arange(valid_places.shape[0], dtype=jnp.int32)
    my_clip = lax.dynamic_index_in_dim(slot_clip, grid.y, 0, keepdims=False)
    count = jnp.sum(jnp.where(my_clip == clip_ids, valid_places, 0)).astype(jnp.int32)
    valid_here = (jnp.arange(padded, dtype=jnp.int32) < count).astype(F32)[None, :, None]
    count_ref = count.reshape(1)

    def spread_in(value):
        mine = lax.dynamic_index_in_dim(value, grid.y, 0, keepdims=False)
        theirs = lax.dynamic_index_in_dim(value, 1 - grid.y, 0, keepdims=False)
        return spread_in_last(mine, grid.over_y(theirs))

    def spread_in_last(mine, got):
        keep = jnp.where(straight, mine, got)
        send = jnp.where(straight, got, mine)
        swap = grid.over_t(send)
        low = jnp.where(own_first, keep, swap)
        high = jnp.where(own_first, swap, keep)
        gap = jnp.zeros((frames_here, padded - places, width), mine.dtype)
        return jnp.concatenate([low, high, gap], axis=1)

    def spread_first(value):
        low = value[:, :places_here]
        high = value[:, places_here:places]
        keep = jnp.where(own_first, low, high)
        send = jnp.where(own_first, high, low)
        swap = grid.over_t(send)
        return jnp.where(straight, swap, keep), jnp.where(straight, keep, swap)

    def spread_last(got, mine):
        first = jnp.where(grid.y == 0, mine, got)
        second = jnp.where(grid.y == 0, got, mine)
        return jnp.stack([first, second])

    def spread_out(value):
        away, mine = spread_first(value)
        return spread_last(grid.over_y(away), mine)

    def pack_mix(item):
        return jnp.concatenate([item[..., : width // 2], item[..., width // 2 :]], axis=-2)

    def block_triple(layer, part):
        return [triple_weight[layer, part, :, i] for i in range(3)]

    def block_out(layer):
        return [merge_weight[layer, 0].T, pack_mix(mixing_weight[layer])]

    def block_s(layer):
        return block_triple(layer, 1) + [merge_weight[layer, 1].T]

    def block_m(layer):
        return [up_weight[layer], down_weight[layer].T]

    split = triple_weight.shape[-1]
    hid = up_weight.shape[-1]
    wide_t = (3 * split, split, width // 2)
    wide_s = (3 * split, split)
    wide_m = (hid, hid)

    def unpack_mix(item):
        cube = item.reshape(-1, 2, half_rows, width // 2)
        return jnp.concatenate([cube[:, 0], cube[:, 1]], axis=-1)

    def with_other(item):
        return (item, grid.over_t(item))

    def mixing_of(both):
        mix_own, mix_oth = [unpack_mix(item) for item in both]
        return jnp.stack(
            [jnp.where(own_first, mix_own, mix_oth), jnp.where(own_first, mix_oth, mix_own)],
            axis=1,
        ).reshape(width, width)

    def block_named(layer, name):
        if name == "triple_t":
            return jnp.concatenate(block_triple(layer, 0), axis=1)
        if name == "triple_s":
            return jnp.concatenate(block_triple(layer, 1), axis=1)
        if name == "merge_t":
            return merge_weight[layer, 0].T
        if name == "mix":
            return mixing_weight[layer] if grid.direct else pack_mix(mixing_weight[layer])
        if name == "merge_s":
            return merge_weight[layer, 1].T
        return block_m(layer)[0 if name == "up" else 1]

    gathered = [dict() for _ in range(LAYERS)]

    def settle(keys, near):
        for (layer, name), both in zip(keys, near):
            w = gathered[layer]
            if name == "triple_t":
                w[name] = both[0]
            elif name == "mix":
                w["mixing"] = both[0] if grid.direct else mixing_of(both)
            else:
                w[name] = both

    ahead = [
        [(0, "triple_t"), (0, "merge_t"), (0, "mix")],
        [(0, "triple_s"), (0, "merge_s"), (0, "up")],
        [(0, "down")],
        [(1, "triple_t"), (1, "merge_t"), (1, "mix")],
        [(1, "triple_s"), (1, "merge_s"), (1, "up")],
        [(1, "down")],
        [],
        [],
    ]
    named = lambda keys: [block_named(*key) for key in keys]
    modes = {"triple_t": False, "mix": "one"}
    modes_of = lambda keys: [modes.get(name, True) for _, name in keys]
    lines = {}
    if grid.direct:
        near, lines[1] = first_gather(
            grid, 7, named(ahead[0]), modes_of(ahead[0]), named(ahead[1])
        )
        settle(ahead[0], near)
    else:
        for keys in ahead:
            settle(
                keys,
                [
                    with_other(lax.all_gather(item, ("shard", "ctx"), axis=0, tiled=True))
                    for item in named(keys)
                ],
            )

    def load_at(index):
        across = [far_cotangent] if index == 3 * LAYERS - 1 and grid.direct else []
        if not grid.direct:
            return Load(grid)
        keys = ahead[index + 1]
        swapped = modes_of(keys)
        near = lines[index + 1] if keys else []
        return Load(grid, near, swapped, named(ahead[index + 2]), across)

    def loaded(index, got):
        near, new_lines = got
        if index == 3 * LAYERS - 1:
            lines["across"] = new_lines[0] if grid.direct else grid.over_y(far_cotangent)
        elif grid.direct:
            settle(ahead[index + 1], near)
            lines[index + 2] = new_lines

    small = jnp.concatenate([entry_bias[:, 1].reshape(LAYERS, -1), up_bias], axis=1)
    small_oth = grid.over_t(small)
    middle = jnp.zeros((LAYERS, split), F32)

    def query_value(both):
        return jnp.concatenate([both[:, :split], middle, both[:, split : 2 * split]], axis=1)

    gains, shifts = [item.reshape(3 * LAYERS, width) for item in (norm_gain, norm_bias)]
    biases = branch_bias.reshape(4 * LAYERS, width)
    bias_t = query_value(entry_bias[:, 0].reshape(LAYERS, -1))
    bias_s = [query_value(item) for item in (small, small_oth)]
    bias_m = [up_bias, small_oth[:, 2 * split :]]

    state = spread_in(video_clips).astype(F32)
    valid_rows = valid_here[0]
    low_cotangent = cotangent.astype(BF)
    near_cotangent = lax.dynamic_index_in_dim(low_cotangent, grid.y, 0, keepdims=False)
    far_cotangent = lax.dynamic_index_in_dim(low_cotangent, 1 - grid.y, 0, keepdims=False)
    stored = []
    squares = []
    for layer in range(LAYERS):
        w = gathered[layer]
        first = 3 * layer
        (state, unit_t, scale_t, normed_t, qkv_t, mine, swap, joined, sq_t), got = temporal_stage(
            8 + first,
            layer,
            state,
            valid_rows,
            gains,
            shifts,
            w,
            [bias_t, biases, biases],
            load_at(first),
            scale,
        )
        loaded(first, got)
        (state, unit_s, scale_s, normed_s, qkv0, qkv1, mixed0, mixed1, sq_s), got = spatial_stage(
            9 + first,
            layer,
            count_ref,
            state,
            valid_rows,
            gains,
            shifts,
            w,
            bias_s + [biases],
            load_at(first + 1),
            places,
            scale,
        )
        loaded(first + 1, got)
        (state, unit_m, scale_m, normed_m, act0, act1, slope0, slope1, sq_m), got = feed_stage(
            10 + first,
            layer,
            state,
            valid_rows,
            gains,
            shifts,
            w,
            bias_m + [biases],
            load_at(first + 2),
        )
        loaded(first + 2, got)
        squares.append((sq_t, sq_s, sq_m))
        stored.append(
            dict(
                unit_t=unit_t,
                scale_t=scale_t,
                normed_t=normed_t,
                qkv_t=qkv_t,
                mixed_t=(mine, swap),
                joined=joined,
                unit_s=unit_s,
                scale_s=scale_s,
                normed_s=normed_s,
                qkv_s=[qkv0, qkv1],
                mixed_s=[mixed0, mixed1],
                unit_m=unit_m,
                scale_m=scale_m,
                normed_m=normed_m,
                active=[act0, act1],
                slope=[slope0, slope1],
            )
        )
    upstream = spread_in_last(near_cotangent, lines["across"]).astype(F32) * valid_here
    block_output = spread_out(state.astype(BF))

    shards = [None] * LAYERS
    sums = {}
    vectors, half_rows_of = [None] * LAYERS, [None] * LAYERS
    waiting = None

    def both_cores(mine, theirs):
        return [jnp.where(own_first, mine, theirs), jnp.where(own_first, theirs, mine)]

    def carry_sums(names, parts):
        nonlocal waiting
        if not grid.direct:
            sums.update(
                zip(names, plain_sums([item[:, start : start + size] for item, start, size in parts]))
            )
            return
        waiting = (names, parts)

    def carried_parts():
        return waiting[1] if waiting else []

    def arrived_sums(result):
        nonlocal waiting
        if waiting:
            sums.update(zip(waiting[0], result))
        waiting = None

    for layer in range(LAYERS - 1, -1, -1):
        w, kept = gathered[layer], stored[layer]
        upstream, vec_m, parts_m, hidden_part, got = feed_back(
            grid, layer, layer, upstream, kept, gains, w, carried_parts()
        )
        arrived_sums(got)
        cut = hid // 2
        carry_sums(
            [("up_a", layer), ("up_b", layer), ("down_a", layer)],
            [(parts_m[0], 0, cut), (parts_m[0], cut, cut), (parts_m[1], 0, cut)],
        )
        upstream, vec_s, entry_s, parts_s, got = spatial_back(
            grid,
            2 + layer,
            layer,
            count_ref,
            upstream,
            kept,
            gains,
            w,
            carried_parts(),
            places,
            scale,
        )
        arrived_sums(got)
        carry_sums(
            [("triple_s", layer), ("down_b", layer), ("merge_s", layer)],
            [(parts_s[0], 0, 3 * split), (parts_m[1], cut, cut), (parts_s[1], 0, split)],
        )
        per_row = hid // width
        hidden_rows = [item.reshape(per_row, width) for item in hidden_part]
        half_rows_of[layer] = both_cores(
            jnp.concatenate([entry_s[:1], hidden_rows[0]]),
            jnp.concatenate([entry_s[1:2], hidden_rows[1]]),
        )
        vectors[layer] = [vec_s, vec_m]
        early = None
        if layer == 0:
            early = Small(width)
            for vec_pair in vectors:
                early.add(vec_pair[0], 0, 3)
                early.add(vec_pair[1], 0, 3)
            early.add(last_vec, 0, 4)
            for item in half_rows_of:
                early.add(item[0], 0, 3)
                early.add(item[1], 0, 3)
            for item in last_half:
                early.add(item, 0, 1)
            for sq_t, sq_s, sq_m in squares:
                for place_at, (item, start) in enumerate(
                    ((sq_t, 0), (sq_s, 0), (sq_m, 1), (sq_m, 0))
                ):
                    early.add(item, start, 1, 128 * place_at, place_at < 3)
        early_rows = early
        upstream, vec_t, entry_t, parts_t, got, early = temporal_back(
            grid,
            4 + layer,
            layer,
            upstream,
            kept,
            gains,
            w,
            carried_parts(),
            scale,
            early if grid.direct else None,
        )
        arrived_sums(got)
        if grid.direct:
            mix_sum = parts_t[2].reshape(width // 2, width)
        else:
            mix_part = parts_t[2].reshape(-1, 2, half_rows, width)
            mix_mine = lax.dynamic_index_in_dim(mix_part, grid.t, 1, keepdims=False)
            mix_theirs = lax.dynamic_index_in_dim(mix_part, 1 - grid.t, 1, keepdims=False)
            mix_got = grid.over_t(mix_theirs.astype(BF)).astype(F32)
            mix_sum = (mix_mine + mix_got).astype(BF).reshape(width // 2, width)
        carry_sums(
            [("triple_t", layer), ("merge_t", layer), ("mix", layer)],
            [(parts_t[0], 0, 3 * split), (parts_t[1], 0, split), (mix_sum, 0, width)],
        )
        last_vec = vec_t
        last_half = both_cores(entry_t[:1], jnp.zeros_like(entry_t[:1]))

    small = Small(width)
    small.add(last_vec, 0, 4)
    for item in last_half:
        small.add(item, 0, 1)
    out_low, out_ready = spread_first(upstream.astype(BF))
    if waiting:
        got, small, out_got = tail_sums(grid, 6, carried_parts(), small, out_low)
        arrived_sums(got)
        (early,) = early
    else:
        small, early = small.plain(), early_rows.plain()
        out_got = grid.over_y(out_low)
    input_grad = spread_last(out_got, out_ready).astype(F32)
    names = ("triple_t", "merge_t", "mix", "triple_s", "merge_s")
    for layer in range(LAYERS):
        up, down = [
            jnp.concatenate([sums[name + "_a", layer], sums[name + "_b", layer]], axis=1)
            for name in ("up", "down")
        ]
        shards[layer] = [sums[name, layer] for name in names] + [up, down]
    block = 6 * LAYERS
    pairs = early[:block].reshape(LAYERS, 2, 3, width)
    ends = jnp.stack([small[:4], early[block : block + 4]])
    gain_sum, shift_sum = [
        jnp.concatenate([ends[:, k : k + 1], pairs[:, :, k]], axis=1) for k in range(2)
    ]
    bias_sum = jnp.concatenate([ends[:, 2:4], pairs[:, :, 2]], axis=1)
    start = block + 4
    half_sums = early[start : start + 6 * LAYERS].reshape(LAYERS, 2, 3, width)
    end_sums = jnp.stack([small[4:6], early[start + 6 * LAYERS : start + 6 * LAYERS + 2]])
    half_sums = lax.dynamic_index_in_dim(half_sums, grid.t, 1, keepdims=False)
    end_sums = lax.dynamic_index_in_dim(end_sums, grid.t, 1, keepdims=False)
    entry_sum = jnp.stack([end_sums, half_sums[:, 0]], axis=1).reshape(LAYERS, 2, 2, split)
    hidden_sum = half_sums[:, 1:].reshape(LAYERS, hid)
    start = start + 6 * LAYERS + 2
    square_sums = early[start : start + LAYERS, : 4 * 128].reshape(LAYERS, 4, 128)[:, :, 0]
    tokens = FRAMES * width * jnp.sum(valid_places).astype(F32)
    root_squares = jnp.sqrt(square_sums / tokens)

    def triple_shape(item):
        return item.reshape(step_rows, 3, split)

    return (
        block_output,
        input_grad,
        gain_sum,
        shift_sum,
        jnp.stack([jnp.stack([triple_shape(s[0]), triple_shape(s[3])]) for s in shards]),
        entry_sum,
        jnp.stack([jnp.stack([s[1].T, s[4].T]) for s in shards]),
        bias_sum,
        jnp.stack([s[2] for s in shards]),
        jnp.stack([s[5] for s in shards]),
        hidden_sum,
        jnp.stack([s[6].T for s in shards]),
        root_squares,
    )


def solution(mesh):
    return jax.shard_map(
        per_device,
        mesh=mesh,
        in_specs=(
            P("shard", "ctx", "tp", None),
            P("shard", "ctx", "tp", None),
            P("shard"),
            P(),
            P(),
            P(),
            P(None, None, ("shard", "ctx"), None, "tp"),
            P(None, None, None, "tp"),
            P(None, None, "tp", ("shard", "ctx")),
            P(),
            P(None, ("shard", "ctx", "tp"), None),
            P(None, ("shard", "ctx"), "tp"),
            P(None, "tp"),
            P(None, "tp", ("shard", "ctx")),
        ),
        out_specs=(
            P("shard", "ctx", "tp", None),
            P("shard", "ctx", "tp", None),
            P(),
            P(),
            P(None, None, ("shard", "ctx"), None, "tp"),
            P(None, None, None, "tp"),
            P(None, None, "tp", ("shard", "ctx")),
            P(),
            P(None, ("shard", "ctx", "tp"), None),
            P(None, ("shard", "ctx"), "tp"),
            P(None, "tp"),
            P(None, "tp", ("shard", "ctx")),
            P(),
        ),
        check_vma=False,
    )
```
